32 devices in a mesh: scene: 2 (over x), frame: 16 (over z, y, core).
Axes of the slice: x: 2, y: 2, z: 4, core: 2. Of those that a mesh axis runs over, the one named last changes fastest.
Arguments:
- tokens: bfloat16 [2, 2304, 1024], P('scene', 'frame'), may hold values from -6 to 6
- patch_counts: int32 [2, 16], P('scene', 'frame'), may hold values from 43 to 139, as said below
- first_gain: bfloat16 [2, 1024], replicated, may hold values from 0.25 to 1.75
- first_shift: bfloat16 [2, 1024], replicated, may hold values from -3 to 3
- joint_weight: bfloat16 [2, 1024, 3072], replicated, may hold values from -0.1875 to 0.1875
- joint_bias: bfloat16 [2, 3072], replicated, may hold values from -3 to 3
- query_gain: bfloat16 [2, 64], replicated, may hold values from 0.796875 to 1.796875
- query_shift: bfloat16 [2, 64], replicated, may hold values from -3 to 3
- key_gain: bfloat16 [2, 64], replicated, may hold values from 0.796875 to 1.796875
- mixer_weight: bfloat16 [2, 1024, 1024], replicated, may hold values from -2 to 2
- mixer_bias: bfloat16 [2, 1024], replicated, may hold values from -3 to 3
- mixer_scale: bfloat16 [2, 1024], replicated, may hold values from 0.25 to 1.75
- second_gain: bfloat16 [2, 1024], replicated, may hold values from 0.25 to 1.75
- second_shift: bfloat16 [2, 1024], replicated, may hold values from -3 to 3
- inner_weight: bfloat16 [2, 1024, 4096], replicated, may hold values from -0.1875 to 0.1875
- inner_bias: bfloat16 [2, 4096], replicated, may hold values from -3 to 3
- outer_weight: bfloat16 [2, 4096, 1024], replicated, may hold values from -0.09375 to 0.09375
- outer_bias: bfloat16 [2, 1024], replicated, may hold values from -3 to 3
- outer_scale: bfloat16 [2, 1024], replicated, may hold values from 0.25 to 1.75
- cotangent: bfloat16 [2, 2304, 1024], P('scene', 'frame'), may hold values from -6 to 6
Outputs:
- layer_out: bfloat16 [2, 2304, 1024], P('scene', 'frame')
- grad_tokens: bfloat16 [2, 2304, 1024], P('scene', 'frame')
- grad_first_gain: float32 [2, 1024], replicated
- grad_first_shift: float32 [2, 1024], replicated
- grad_joint_weight: float32 [2, 1024, 3072], P(None, ('scene', 'frame'))
- grad_joint_bias: float32 [2, 3072], replicated
- grad_query_gain: float32 [2, 64], replicated
- grad_query_shift: float32 [2, 64], replicated
- grad_key_gain: float32 [2, 64], replicated
- grad_mixer_weight: float32 [2, 1024, 1024], P(None, ('scene', 'frame'))
- grad_mixer_bias: float32 [2, 1024], replicated
- grad_mixer_scale: float32 [2, 1024], replicated
- grad_second_gain: float32 [2, 1024], replicated
- grad_second_shift: float32 [2, 1024], replicated
- grad_inner_weight: float32 [2, 1024, 4096], P(None, ('scene', 'frame'))
- grad_inner_bias: float32 [2, 4096], replicated
- grad_outer_weight: float32 [2, 4096, 1024], P(None, ('scene', 'frame'))
- grad_outer_bias: float32 [2, 1024], replicated
- grad_outer_scale: float32 [2, 1024], replicated
The draws below stay inside these ranges and needn't reach their ends.
Inputs may be any that keep to these rules, and one draw needn't show every extreme that they name: `patch_counts`: A frame's 5 camera and register tokens and then its patches fill the first slots of its 144; in every scene some frame has the most patches and some the fewest.
All inputs are finite; a program needn't handle non-finite values.
Results may differ from the reference program's by a relative error of at most 0.014.
Values may be sent and summed in bfloat16 or wider, within the bound.
A program may use at most 384 MiB of HBM per device.

```python
import jax
import jax.numpy as jnp
from jax import lax

D = 1024
HEAD = 64
FF = 4096
TOK_DEV = 144
SPECIAL = 5
SCENES = 2
FRAMES = 16


def draw_patch_counts(key, part):
    lowest = TOK_DEV // 3 - SPECIAL
    highest = TOK_DEV - SPECIAL
    counts = jax.random.randint(key, (SCENES, FRAMES), lowest, highest + 1)
    places = jax.random.randint(jax.random.fold_in(key, 7), (SCENES, 1), 0, FRAMES)
    column = jnp.arange(FRAMES, dtype=jnp.int32)[None, :]
    counts = jnp.where(column == places, highest, counts)
    counts = jnp.where(column == (places + 1) % FRAMES, lowest, counts)
    return counts.astype(jnp.int32)


def shard_levels(key, shape, pieces, least, top_value):
    def one(axis_at, shards_of):
        steps = jax.random.uniform(jax.random.fold_in(jax.random.fold_in(key, 6), axis_at), (shards_of,), jnp.float32, least / len(pieces), top_value / len(pieces))
        return jnp.repeat(jnp.exp(steps), shape[axis_at] // shards_of).reshape((-1,) + (1,) * (len(shape) - axis_at - 1))

    level = one(*pieces[0])
    for cut in pieces[1:]:
        level = level * one(*cut)
    return level


def noise(key, shape, spread, reach, pieces=(), held_as=jnp.bfloat16):
    gain = shard_levels(key, shape, pieces, -0.22, 0.18) if pieces else 1.0
    entries = jax.random.normal(key, shape, jnp.float32) * spread * gain
    return jnp.minimum(jnp.maximum(entries, -reach), reach).astype(held_as)


def setup_inputs(seed: int = 0) -> dict:
    keys = jax.random.split(jax.random.key(seed), 21)
    tokens = noise(keys[0], (SCENES, FRAMES * TOK_DEV, D), 1.0, 6.0, ((0, 2), (1, 16)))
    patch_counts = draw_patch_counts(jax.random.fold_in(keys[20], 71), 0)
    first_gain = jnp.clip(1.0 + 0.15 * jax.random.normal(keys[2], (2, D), jnp.float32), 0.25, 1.75).astype(jnp.bfloat16)
    first_shift = noise(keys[3], (2, D), 0.3, 3.0)
    joint_weight = noise(keys[4], (2, D, 3 * D), D ** -0.5, 0.1875)
    joint_bias = noise(keys[5], (2, 3 * D), 0.3, 3.0)
    query_gain = jnp.clip(jax.random.uniform(keys[6], (2, HEAD), jnp.float32, 0.796875, 1.796875), 0.796875, 1.796875).astype(jnp.bfloat16)
    query_shift = noise(keys[7], (2, HEAD), 0.3, 3.0)
    key_gain = jnp.clip(jax.random.uniform(keys[8], (2, HEAD), jnp.float32, 0.796875, 1.796875), 0.796875, 1.796875).astype(jnp.bfloat16)
    mixer_weight = noise(keys[9], (2, D, D), (max(D // 128, 4)) ** -0.5, 2.0)
    mixer_bias = noise(keys[10], (2, D), 0.3, 3.0)
    mixer_scale = jnp.clip(1.0 + 0.15 * jax.random.normal(keys[11], (2, D), jnp.float32), 0.25, 1.75).astype(jnp.bfloat16)
    second_gain = jnp.clip(1.0 + 0.15 * jax.random.normal(keys[12], (2, D), jnp.float32), 0.25, 1.75).astype(jnp.bfloat16)
    second_shift = noise(keys[13], (2, D), 0.3, 3.0)
    inner_weight = noise(keys[14], (2, D, FF), D ** -0.5, 0.1875)
    inner_bias = noise(keys[15], (2, FF), 0.3, 3.0)
    outer_weight = noise(keys[16], (2, FF, D), FF ** -0.5, 0.09375)
    outer_bias = noise(keys[17], (2, D), 0.3, 3.0)
    outer_scale = jnp.clip(1.0 + 0.15 * jax.random.normal(keys[18], (2, D), jnp.float32), 0.25, 1.75).astype(jnp.bfloat16)
    cotangent = noise(keys[19], (SCENES, FRAMES * TOK_DEV, D), 1.0, 6.0, ((0, 2), (1, 16)))
    return dict(tokens=tokens, patch_counts=patch_counts, first_gain=first_gain, first_shift=first_shift, joint_weight=joint_weight, joint_bias=joint_bias, query_gain=query_gain, query_shift=query_shift, key_gain=key_gain, mixer_weight=mixer_weight, mixer_bias=mixer_bias, mixer_scale=mixer_scale, second_gain=second_gain, second_shift=second_shift, inner_weight=inner_weight, inner_bias=inner_bias, outer_weight=outer_weight, outer_bias=outer_bias, outer_scale=outer_scale, cotangent=cotangent)


@jax.custom_vjp
def low(v):
    return lax.optimization_barrier(v.astype(jnp.bfloat16)).astype(jnp.float32)

@jax.custom_vjp
def low_back(v):
    return v

def low_keep(v):
    return (low(v), None)

def low_pass(kept, grad):
    return (grad,)

def back_keep(v):
    return (v, None)

def back_low(kept, grad):
    return (low(grad),)
low.defvjp(low_keep, low_pass)
low_back.defvjp(back_keep, back_low)
exact_precision = lax.Precision.HIGHEST
norm_eps = 1e-06
head_eps = 1e-05
mask_depth = 1000000000.0

def layer_norm(inputs, norm_gain, norm_shift, epsilon):
    average = lax.optimization_barrier(jnp.mean(inputs, axis=-1, keepdims=True))
    centered = inputs - average
    variance = lax.optimization_barrier(jnp.mean(centered * centered, axis=-1, keepdims=True))
    return centered * lax.rsqrt(variance + epsilon) * norm_gain + norm_shift

def product(left_side, right_side):
    return jnp.dot(left_side, right_side, precision=exact_precision)

def attend(queries, key_heads, values, key_bias):
    score_scale = queries.shape[-1] ** (-0.5)
    dot_scores = jnp.einsum('qhe,khe->hqk', queries, key_heads, precision=exact_precision)
    scores = low_back(dot_scores * score_scale + key_bias[None, None, :])
    probability = jax.nn.softmax(scores, axis=-1)
    return jnp.einsum('hqk,khe->qhe', low(probability), values, precision=exact_precision)

def attend_rows(queries, key_heads, values, key_bias):
    query_count = queries.shape[0]
    block_size = 512 if query_count % 512 == 0 else query_count
    blocks = queries.reshape(query_count // block_size, block_size, queries.shape[1], queries.shape[2])

    def one_block(query_block):
        return attend(query_block, key_heads, values, key_bias)
    results = lax.map(jax.checkpoint(one_block), blocks)
    return results.reshape(queries.shape)

def block(stream, weights, mix):
    first_gain, first_shift, joint_weight, joint_bias, query_gain, query_shift, key_gain, mixer_weight, mixer_bias, mixer_scale, second_gain, second_shift, inner_weight, inner_bias, outer_weight, outer_bias, outer_scale = weights
    row_count, model_width = stream.shape
    head_size = query_gain.shape[0]
    head_count = model_width // head_size
    normed = low(layer_norm(stream, first_gain, first_shift, norm_eps))
    joined = low_back(product(normed, joint_weight) + joint_bias)
    joined_parts = joined.reshape(row_count, 3, head_count, head_size)
    queries = low(layer_norm(joined_parts[:, 0], query_gain, query_shift, head_eps))
    key_heads = low(layer_norm(joined_parts[:, 1], key_gain, 0.0, head_eps))
    values = low(joined_parts[:, 2])
    attended = mix(queries, key_heads, values).reshape(row_count, model_width)
    attended = low(low_back(attended))
    branch = low_back(product(attended, mixer_weight) + mixer_bias)
    middle = stream + mixer_scale * branch
    normed_mid = low(layer_norm(middle, second_gain, second_shift, norm_eps))
    hidden_pre = low_back(product(normed_mid, inner_weight) + inner_bias)
    hidden = low(jax.nn.gelu(hidden_pre, approximate=False))
    feed_out = low_back(product(hidden, outer_weight) + outer_bias)
    return middle + outer_scale * feed_out

def reference(tokens, patch_counts, first_gain, first_shift, joint_weight, joint_bias, query_gain, query_shift, key_gain, mixer_weight, mixer_bias, mixer_scale, second_gain, second_shift, inner_weight, inner_bias, outer_weight, outer_bias, outer_scale, cotangent):
    scenes, length, model_width = tokens.shape
    frames = patch_counts.shape[1]
    frame_rows = length // frames
    positions = jnp.arange(frame_rows, dtype=jnp.int32)
    valid = (positions[None, None, :] < (patch_counts + SPECIAL)[:, :, None]).astype(jnp.float32)
    key_bias = (valid - 1.0) * mask_depth
    frame_bias = key_bias.reshape(scenes * frames, frame_rows)
    scene_bias = key_bias.reshape(scenes, length)
    valid_rows = valid.reshape(scenes * length, 1)

    def frame_mix(queries, key_heads, values):
        head_shape = (scenes * frames, frame_rows, queries.shape[1], queries.shape[2])
        mixed_out = jax.vmap(attend)(queries.reshape(head_shape), key_heads.reshape(head_shape), values.reshape(head_shape), frame_bias)
        return mixed_out.reshape(queries.shape)

    def scene_mix(queries, key_heads, values):
        head_shape = (scenes, length, queries.shape[1], queries.shape[2])

        def one_scene(scene_part):
            return attend_rows(scene_part[0], scene_part[1], scene_part[2], scene_part[3])
        mixed_out = lax.map(one_scene, (queries.reshape(head_shape), key_heads.reshape(head_shape), values.reshape(head_shape), scene_bias))
        return mixed_out.reshape(queries.shape)
    params = tuple((param_array.astype(jnp.float32) for param_array in (first_gain, first_shift, joint_weight, joint_bias, query_gain, query_shift, key_gain, mixer_weight, mixer_bias, mixer_scale, second_gain, second_shift, inner_weight, inner_bias, outer_weight, outer_bias, outer_scale)))
    stream_in = tokens.astype(jnp.float32).reshape(scenes * length, model_width)

    def forward(stream, weights):
        first_block = block(stream, tuple((param_array[0] for param_array in weights)), frame_mix)
        second_block = block(first_block, tuple((param_array[1] for param_array in weights)), scene_mix)
        return second_block * valid_rows
    result, pullback = jax.vjp(forward, stream_in, params)
    grad_stream, grad_params = pullback(cotangent.astype(jnp.float32).reshape(scenes * length, model_width))
    layer_out = result.astype(jnp.bfloat16).reshape(tokens.shape)
    grad_tokens = grad_stream.astype(jnp.bfloat16).reshape(tokens.shape)
    return (layer_out, grad_tokens, grad_params[0], grad_params[1], grad_params[2], grad_params[3], grad_params[4], grad_params[5], grad_params[6], grad_params[7], grad_params[8], grad_params[9], grad_params[10], grad_params[11], grad_params[12], grad_params[13], grad_params[14], grad_params[15], grad_params[16])
```

```python
from functools import partial

import jax
import jax.numpy as jnp
from jax import lax
from jax.experimental import pallas as pl
from jax.experimental.pallas import tpu as pltpu
from jax.sharding import PartitionSpec as P

SPECIAL = 5
CHUNK = 512
LANES = 128
SLAB = 256
norm_eps = 1e-06
head_eps = 1e-05
closed_score = -10000.0
f32 = jnp.float32
bf16 = jnp.bfloat16


def nn(a, b):
    return lax.dot_general(a, b, (((1,), (0,)), ((), ())), preferred_element_type=f32)


def nt(a, b):
    return lax.dot_general(a, b, (((1,), (1,)), ((), ())), preferred_element_type=f32)


def tn(a, b):
    return lax.dot_general(a, b, (((0,), (0,)), ((), ())), preferred_element_type=f32)


def row(ref, index):
    return ref[...].astype(f32)[index : index + 1, :]


def col_sum(value):
    return jnp.sum(value, axis=0, keepdims=True)


def center_norm(value, eps):
    centered = value - jnp.mean(value, axis=-1, keepdims=True)
    spread = lax.rsqrt(jnp.mean(centered * centered, axis=-1, keepdims=True) + eps)
    return centered * spread, spread


def norm_back(grad_hat, hat, spread):
    mean_grad = jnp.mean(grad_hat, axis=-1, keepdims=True)
    mean_both = jnp.mean(grad_hat * hat, axis=-1, keepdims=True)
    return spread * (grad_hat - mean_grad - hat * mean_both)


def seg_matrix(width, head, value):
    shift = head.bit_length() - 1
    first = lax.shift_right_logical(lax.broadcasted_iota(jnp.int32, (width, width), 0), shift)
    second = lax.shift_right_logical(lax.broadcasted_iota(jnp.int32, (width, width), 1), shift)
    return jnp.where(first == second, value, 0.0).astype(bf16)


def seg_dot(value, matrix):
    high = value.astype(bf16)
    low = (value - high.astype(f32)).astype(bf16)
    return nn(high, matrix) + nn(low, matrix)


def seg_norm(value, mean_matrix):
    centered = value - seg_dot(value, mean_matrix)
    spread = lax.rsqrt(seg_dot(centered * centered, mean_matrix) + head_eps)
    return centered * spread, spread


def first_lanes(rows):
    return lax.broadcasted_iota(jnp.int32, (rows, LANES), 1) < LANES // 2


def turn(value):
    return pltpu.roll(value, LANES // 2, value.ndim - 1)


def pack_pair(slab):
    half = slab.shape[0] // 2
    top, bottom = slab[:half], slab[half:]
    low = first_lanes(half)
    return jnp.where(low, top, turn(bottom)), jnp.where(low, turn(top), bottom)


def unpack_pair(even, odd):
    low = first_lanes(even.shape[0])
    top = jnp.where(low, even, turn(odd))
    bottom = jnp.where(low, turn(even), odd)
    return jnp.concatenate([top, bottom], axis=0)


def erf(value):
    value = jnp.clip(value, -4.0, 4.0)
    square = value * value
    top = jnp.full_like(square, -2.72614225801306e-10)
    for coefficient in (
        2.77068142495902e-08,
        -2.10102402082508e-06,
        -5.69250639462346e-05,
        -7.34990630326855e-04,
        -2.95459980854025e-03,
        -1.60960333262415e-02,
    ):
        top = top * square + coefficient
    bottom = jnp.full_like(square, -1.45660718464996e-05)
    for coefficient in (
        -2.13374055278905e-04,
        -1.68282697438203e-03,
        -7.37332916720468e-03,
        -1.42647390514189e-02,
    ):
        bottom = bottom * square + coefficient
    return value * top / bottom


def full(shape):
    return pl.BlockSpec(shape, lambda *_: (0,) * len(shape))


def sds(shape, dtype):
    return jax.ShapeDtypeStruct(shape, dtype)


def call(body, name, grid, in_specs, out_specs, out_shape, scratch, flops, moved):
    return pl.pallas_call(
        body,
        name=name,
        out_shape=out_shape,
        grid_spec=pltpu.PrefetchScalarGridSpec(
            num_scalar_prefetch=1,
            grid=grid,
            in_specs=in_specs,
            out_specs=out_specs,
            scratch_shapes=scratch,
        ),
        cost_estimate=pl.CostEstimate(flops=flops, bytes_accessed=moved, transcendentals=0),
    )


def joint_body(
    block, packed, head, meta, x_ref, gain_ref, shift_ref, pattern_ref, w_ref, b_ref,
    own_ref, other_ref, pre_ref, out_ref, normed_ref, *stage
):
    step = pl.program_id(0)
    rows, width = normed_ref.shape
    per_part = width // CHUNK
    half = rows // 2

    @pl.when(step == 0)
    def _():
        hat, _ = center_norm(x_ref[...].astype(f32), norm_eps)
        normed = (hat * row(gain_ref, block) + row(shift_ref, block)).astype(bf16)
        normed_ref[...] = normed

        @pl.when(meta[0] == 0)
        def _():
            own_ref[...] = normed[:, : width // 2]
            other_ref[...] = normed[:, width // 2 :]

        @pl.when(meta[0] != 0)
        def _():
            own_ref[...] = normed[:, width // 2 :]
            other_ref[...] = normed[:, : width // 2]

        if packed:
            count = jnp.full((8, LANES), meta[3], jnp.int32).astype(f32)
            for place in range(stage[0].shape[0]):
                stage[0][place, 3 * half : 3 * half + 8, :] = count

    joined = nn(normed_ref[...], w_ref[0]) + row(b_ref, block)
    pattern = pattern_ref[...]

    def emit(part, values):
        if packed:
            base = (step - part * per_part) * (CHUNK // head)
            for slab in range(CHUNK // LANES):
                even, odd = pack_pair(values[:, slab * LANES : (slab + 1) * LANES])
                stage[0][base + 2 * slab, part * half : (part + 1) * half, :] = even
                stage[0][base + 2 * slab + 1, part * half : (part + 1) * half, :] = odd
        else:
            out_ref[...] = values.astype(bf16)

    def normed_heads(gain, shift):
        mean_matrix = seg_matrix(SLAB, head, 1.0 / head)
        pieces = []
        for slab in range(CHUNK // SLAB):
            hat, _ = seg_norm(joined[:, slab * SLAB : (slab + 1) * SLAB], mean_matrix)
            pieces.append(hat * gain if shift is None else hat * gain + shift)
        return jnp.concatenate(pieces, axis=1)

    scale = head ** (-0.5)

    @pl.when(step < per_part)
    def _():
        pre_ref[...] = joined
        emit(0, normed_heads(
            pattern[3 * block : 3 * block + 1] * scale,
            pattern[3 * block + 1 : 3 * block + 2] * scale,
        ))

    @pl.when((step >= per_part) & (step < 2 * per_part))
    def _():
        pre_ref[...] = joined
        emit(1, normed_heads(pattern[3 * block + 2 : 3 * block + 3], None))

    @pl.when(step >= 2 * per_part)
    def _():
        emit(2, joined)

    if packed:

        @pl.when(step == 3 * per_part - 1)
        def _():
            out_ref[...] = stage[0][...].astype(bf16)


def joint_forward(block, packed, head, meta, x, gain, shift, pattern, weight, bias):
    rows, width = x.shape
    per_part = width // CHUNK
    heads = width // head
    packed_rows = 3 * (rows // 2) + 8
    if packed:
        out_spec, out = full((heads, packed_rows, LANES)), sds((heads, packed_rows, LANES), bf16)
        extra = [pltpu.VMEM((heads, packed_rows, LANES), f32)]
    else:
        out_spec = pl.BlockSpec((rows, CHUNK), lambda j, m: (0, j))
        out = sds((rows, 3 * width), bf16)
        extra = []
    return call(
        partial(joint_body, block, packed, head),
        f"joint_forward_{block}",
        (3 * per_part,),
        [
            full((rows, width)),
            full(gain.shape),
            full(shift.shape),
            full(pattern.shape),
            pl.BlockSpec((1, width, CHUNK), lambda j, m: (block, 0, j)),
            pl.BlockSpec((2, CHUNK), lambda j, m: (0, j)),
        ],
        [
            full((rows, width // 2)),
            full((rows, width // 2)),
            pl.BlockSpec((rows, CHUNK), lambda j, m: (0, jnp.minimum(j, 2 * per_part - 1))),
            out_spec,
        ],
        [
            sds((rows, width // 2), bf16),
            sds((rows, width // 2), bf16),
            sds((rows, 2 * width), f32),
            out,
        ],
        [pltpu.VMEM((rows, width), bf16)] + extra,
        2 * rows * width * 3 * width,
        6 * width * width + 16 * rows * width,
    )(meta, x, gain, shift, pattern, weight, bias)


def lane_picks():
    lane = lax.broadcasted_iota(jnp.int32, (1, LANES), 1)
    low = jnp.where(lane < LANES // 2, 1.0, 0.0)
    return low.astype(bf16), (1.0 - low).astype(bf16)


def open_row(meta, rows):
    place = lax.broadcasted_iota(jnp.int32, (1, rows), 1)
    return jnp.where(place < meta[3] + SPECIAL, 0.0, closed_score)


def frame_body(meta, qkv_ref, out_ref):
    rows, width = out_ref.shape
    bias = open_row(meta, rows)
    picks = lane_picks()
    low = first_lanes(rows)
    for slab in range(width // LANES):
        at = slab * LANES
        queries = qkv_ref[:, at : at + LANES]
        keys = qkv_ref[:, width + at : width + at + LANES]
        values = qkv_ref[:, 2 * width + at : 2 * width + at + LANES]
        results = []
        for pick in picks:
            power = jnp.exp(nt(queries * pick, keys) + bias)
            probs = power / jnp.sum(power, axis=-1, keepdims=True)
            results.append(nn(probs.astype(bf16), values))
        out_ref[:, at : at + LANES] = jnp.where(low, results[0], results[1]).astype(bf16)


def frame_forward(meta, qkv):
    rows = qkv.shape[0]
    width = qkv.shape[1] // 3
    return call(
        frame_body,
        "frame_forward",
        (1,),
        [full(qkv.shape)],
        full((rows, width)),
        sds((rows, width), bf16),
        [],
        4 * rows * rows * width,
        8 * rows * width,
    )(meta, qkv)


def frame_back_body(meta, qkv_ref, grad_ref, out_ref):
    rows, width = grad_ref.shape
    bias = open_row(meta, rows)
    picks = lane_picks()
    low = first_lanes(rows)
    scale = (LANES // 2) ** (-0.5)
    for slab in range(width // LANES):
        at = slab * LANES
        queries = qkv_ref[:, at : at + LANES]
        keys = qkv_ref[:, width + at : width + at + LANES]
        values = qkv_ref[:, 2 * width + at : 2 * width + at + LANES]
        grads = grad_ref[:, at : at + LANES]
        found = []
        for pick in picks:
            power = jnp.exp(nt(queries * pick, keys) + bias)
            probs = power / jnp.sum(power, axis=-1, keepdims=True)
            grad_probs = nt(grads * pick, values)
            delta = jnp.sum(probs * grad_probs, axis=-1, keepdims=True)
            grad_scores = (probs * (grad_probs - delta)).astype(bf16)
            found.append((
                nn(grad_scores, keys) * scale,
                tn(grad_scores, queries),
                tn(probs.astype(bf16), grads),
            ))
        for part in range(3):
            out_ref[:, part * width + at : part * width + at + LANES] = jnp.where(
                low, found[0][part], found[1][part]
            )


def frame_backward(meta, qkv, grad):
    rows, width = grad.shape
    return call(
        frame_back_body,
        "frame_backward",
        (1,),
        [full(qkv.shape), full(grad.shape)],
        full((rows, 3 * width)),
        sds((rows, 3 * width), f32),
        [],
        10 * rows * rows * width,
        20 * rows * width,
    )(meta, qkv, grad)


def packed_part(ref, part, half):
    whole = ref[...].astype(f32)
    return whole[:, part * half : (part + 1) * half, :].reshape(-1, LANES)


def open_slots(ref, half):
    count = ref[...].astype(f32)[:, 3 * half : 3 * half + 8, :]
    count = jnp.concatenate([count] * (half // 8), axis=1)
    place = lax.broadcasted_iota(jnp.int32, count.shape, 1).astype(f32)
    return (
        (place < count + SPECIAL).reshape(-1, LANES),
        (place + half < count + SPECIAL).reshape(-1, LANES),
    )


def scene_body(half, span, meta, q_ref, kv_ref, att_ref, out_ref, log_ref, queries, keys, values):
    n = queries.shape[0] // 2
    m = keys.shape[0] // 2
    q = packed_part(q_ref, 0, half)
    low_n, low_m = first_lanes(n), first_lanes(m)
    queries[:n, :] = jnp.where(low_n, q, 0.0).astype(bf16)
    queries[n:, :] = jnp.where(low_n, turn(q), 0.0).astype(bf16)
    k = packed_part(kv_ref, 1, half)
    keys[:m, :] = k.astype(bf16)
    keys[m:, :] = turn(k).astype(bf16)
    v = packed_part(kv_ref, 2, half)
    open_low, open_high = open_slots(kv_ref, half)
    values[:m, :] = jnp.where(open_low, jnp.where(low_m, v, 1.0), 0.0).astype(bf16)
    values[m:, :] = jnp.where(open_high, jnp.where(low_m, turn(v), 1.0), 0.0).astype(bf16)
    low = first_lanes(LANES)

    @pl.loop(0, n // LANES)
    def _(piece):
        at = pl.multiple_of(piece * LANES, LANES)
        some = jnp.concatenate([queries[pl.ds(at, LANES), :], queries[pl.ds(n + at, LANES), :]], axis=0)
        total = jnp.zeros((2 * LANES, LANES), f32)
        for start in range(0, 2 * m, span):
            power = jnp.exp(nt(some, keys[start : start + span, :])).astype(bf16)
            total = total + nn(power, values[start : start + span, :])
        first, second = total[:LANES], total[LANES:]
        bottom = jnp.where(low, turn(first), second)
        result = jnp.where(low, first, turn(second)) / bottom
        att_ref[pl.ds(at, LANES), :] = result.astype(bf16)
        out_ref[pl.ds(at, LANES), :] = result
        log_ref[pl.ds(at, LANES), :] = jnp.log(bottom)


def scene_forward(meta, q_pack, kv_pack, half):
    n = q_pack.shape[0] * half
    m = kv_pack.shape[0] * half
    span = m // 2
    while span > 640:
        span = span // 2
    return call(
        partial(scene_body, half, span),
        "scene_forward",
        (1,),
        [full(q_pack.shape), full(kv_pack.shape)],
        [full((n, LANES))] * 3,
        [sds((n, LANES), bf16), sds((n, LANES), f32), sds((n, LANES), f32)],
        [
            pltpu.VMEM((2 * n, LANES), bf16),
            pltpu.VMEM((2 * m, LANES), bf16),
            pltpu.VMEM((2 * m, LANES), bf16),
        ],
        4 * 4 * n * m * LANES,
        20 * n * LANES,
    )(meta, q_pack, kv_pack)


def three_lanes(value, closed):
    lane = lax.broadcasted_iota(jnp.int32, value.shape, 1)
    base = LANES // 2
    high = value.astype(bf16).astype(f32)
    rest = value - high
    middle = rest.astype(bf16).astype(f32)
    last = rest - middle
    result = jnp.where(lane == base, high, jnp.where(lane == base + 1, middle, last))
    return jnp.where(lane < base + 3, result, jnp.where(lane == base + 3, closed, 0.0))


def scene_back_body(
    half, span, meta, q_ref, kv_ref, grad_ref, out_ref, log_ref,
    dq_ref, dk_ref, dv_ref, queries, keys, values, grads, turned
):
    n = queries.shape[0] // 2
    m = keys.shape[0] // 2
    low_n, low_m = first_lanes(n), first_lanes(m)
    base = LANES // 2
    q = packed_part(q_ref, 0, half)
    log = -log_ref[...]
    queries[:n, :] = jnp.where(low_n, q, three_lanes(turn(log), closed_score)).astype(bf16)
    queries[n:, :] = jnp.where(low_n, turn(q), three_lanes(log, closed_score)).astype(bf16)
    g = grad_ref[...].astype(f32)
    delta = -seg_dot(g * out_ref[...], seg_matrix(LANES, base, 1.0))
    grads[:n, :] = jnp.where(low_n, g, three_lanes(turn(delta), 0.0)).astype(bf16)
    grads[n:, :] = jnp.where(low_n, turn(g), three_lanes(delta, 0.0)).astype(bf16)
    lane = lax.broadcasted_iota(jnp.int32, (m, LANES), 1)
    ones = jnp.where(lane < base + 3, 1.0, 0.0)
    open_low, open_high = open_slots(kv_ref, half)
    k = packed_part(kv_ref, 1, half)
    for place, k_now, is_open in ((0, k, open_low), (m, turn(k), open_high)):
        tail = jnp.where((lane == base + 3) & jnp.logical_not(is_open), 1.0, ones)
        keys[place : place + m, :] = jnp.where(low_m, k_now, tail).astype(bf16)
    v = packed_part(kv_ref, 2, half)
    values[:m, :] = jnp.where(low_m, v, ones).astype(bf16)
    values[m:, :] = jnp.where(low_m, turn(v), ones).astype(bf16)
    turned[...] = jnp.zeros_like(turned)
    low = first_lanes(LANES)

    @pl.loop(0, m // LANES)
    def _(piece):
        at = pl.multiple_of(piece * LANES, LANES)
        key_part = jnp.concatenate([keys[pl.ds(at, LANES), :], keys[pl.ds(m + at, LANES), :]], axis=0)
        value_part = jnp.concatenate(
            [values[pl.ds(at, LANES), :], values[pl.ds(m + at, LANES), :]], axis=0
        )
        key_turned = jnp.transpose(key_part.astype(f32)).astype(bf16)
        dk = jnp.zeros((2 * LANES, LANES), f32)
        dv = jnp.zeros((2 * LANES, LANES), f32)
        for start in range(0, 2 * n, span):
            some = queries[start : start + span, :]
            some_grads = grads[start : start + span, :]
            probs = jnp.exp(nt(key_part, some))
            grad_scores = (probs * nt(value_part, some_grads)).astype(bf16)
            dv = dv + nn(probs.astype(bf16), some_grads)
            dk = dk + nn(grad_scores, some)
            turned[:, start : start + span] += nn(key_turned, grad_scores)
        dk_ref[pl.ds(at, LANES), :] = jnp.where(low, dk[:LANES], turn(dk[LANES:])).astype(bf16)
        dv_ref[pl.ds(at, LANES), :] = jnp.where(low, dv[:LANES], turn(dv[LANES:])).astype(bf16)

    scale = base ** (-0.5)
    for at in range(0, n, LANES):
        first = jnp.transpose(turned[:, at : at + LANES])
        second = jnp.transpose(turned[:, n + at : n + at + LANES])
        dq_ref[at : at + LANES, :] = (jnp.where(low, first, turn(second)) * scale).astype(bf16)


def scene_backward(meta, q_pack, kv_pack, grad, out, log, half):
    n = q_pack.shape[0] * half
    m = kv_pack.shape[0] * half
    span = n // 2
    while span > 640:
        span = span // 2
    return call(
        partial(scene_back_body, half, span),
        "scene_backward",
        (1,),
        [full(q_pack.shape), full(kv_pack.shape)] + [full((n, LANES))] * 3,
        [full((n, LANES)), full((m, LANES)), full((m, LANES))],
        [sds((n, LANES), bf16), sds((m, LANES), bf16), sds((m, LANES), bf16)],
        [
            pltpu.VMEM((2 * n, LANES), bf16),
            pltpu.VMEM((2 * m, LANES), bf16),
            pltpu.VMEM((2 * m, LANES), bf16),
            pltpu.VMEM((2 * n, LANES), bf16),
            pltpu.VMEM((LANES, 2 * n), f32),
        ],
        10 * 4 * n * m * LANES,
        30 * n * LANES,
    )(meta, q_pack, kv_pack, grad, out, log)


def feed_body(
    block, packed, meta, att_ref, x_ref, mixer_ref, mixer_bias, mixer_scale, gain_ref, shift_ref,
    inner_ref, inner_bias, outer_ref, outer_bias, outer_scale,
    own_ref, other_ref, middle_ref, branch_ref, feed_ref, slope_ref, out_ref, normed_ref, total_ref
):
    step = pl.program_id(0)
    steps = pl.num_programs(0)
    rows, width = middle_ref.shape
    hidden_half = own_ref.shape[1] - width
    half_steps = hidden_half // CHUNK
    mine = meta[0]

    def split(value, at):
        first, second = value[:, : width // 2], value[:, width // 2 :]

        @pl.when(mine == 0)
        def _():
            own_ref[:, at : at + width // 2] = first
            other_ref[:, at : at + width // 2] = second

        @pl.when(mine != 0)
        def _():
            own_ref[:, at : at + width // 2] = second
            other_ref[:, at : at + width // 2] = first

    @pl.when(step == 0)
    def _():
        if packed:
            pieces = []
            for pair in range(width // LANES):
                pieces.append(
                    unpack_pair(att_ref[2 * pair].astype(f32), att_ref[2 * pair + 1].astype(f32))
                )
            attended = jnp.concatenate(pieces, axis=1).astype(bf16)
        else:
            attended = att_ref[...]
        branch = nn(attended, mixer_ref[0]) + row(mixer_bias, block)
        middle = x_ref[...].astype(f32) + row(mixer_scale, block) * branch
        hat, _ = center_norm(middle, norm_eps)
        normed = (hat * row(gain_ref, block) + row(shift_ref, block)).astype(bf16)
        branch_ref[...] = branch
        middle_ref[...] = middle
        normed_ref[...] = normed
        split(normed, hidden_half)
        split(attended, hidden_half + width // 2)
        total_ref[...] = jnp.zeros_like(total_ref)

    pre = nn(normed_ref[...], inner_ref[0]) + row(inner_bias, block)
    share = 0.5 * (1.0 + erf(pre * (2.0 ** (-0.5))))
    slope_ref[...] = share + pre * jnp.exp(-0.5 * pre * pre) * 0.3989422804014327
    hidden = (pre * share).astype(bf16)
    place = pl.multiple_of(lax.rem(step, half_steps) * CHUNK, CHUNK)

    @pl.when(step // half_steps == mine)
    def _():
        own_ref[:, pl.ds(place, CHUNK)] = hidden

    @pl.when(step // half_steps != mine)
    def _():
        other_ref[:, pl.ds(place, CHUNK)] = hidden

    total_ref[...] += nn(hidden, outer_ref[0])

    @pl.when(step == steps - 1)
    def _():
        feed = total_ref[...] + row(outer_bias, block)
        feed_ref[...] = feed
        result = middle_ref[...] + row(outer_scale, block) * feed
        if packed:
            place = lax.broadcasted_iota(jnp.int32, result.shape, 0)
            result = jnp.where(place < meta[3] + SPECIAL, result, 0.0)
        out_ref[...] = result.astype(out_ref.dtype)


def feed_forward(block, packed, meta, att, x, mixer, mixer_bias, mixer_scale, gain, shift, inner, inner_bias, outer, outer_bias, outer_scale):
    rows, width = x.shape
    hidden = inner.shape[2]
    kept = hidden // 2 + width
    steps = hidden // CHUNK
    vector = full(gain.shape)
    return call(
        partial(feed_body, block, packed),
        f"feed_forward_{block}",
        (steps,),
        [
            full(att.shape),
            full((rows, width)),
            pl.BlockSpec((1, width, width), lambda j, m: (block, 0, 0)),
            vector, vector, vector, vector,
            pl.BlockSpec((1, width, CHUNK), lambda j, m: (block, 0, j)),
            pl.BlockSpec((2, CHUNK), lambda j, m: (0, j)),
            pl.BlockSpec((1, CHUNK, width), lambda j, m: (block, j, 0)),
            vector, vector,
        ],
        [full((rows, kept))] * 2
        + [full((rows, width))] * 3
        + [pl.BlockSpec((rows, CHUNK), lambda j, m: (0, j)), full((rows, width))],
        [sds((rows, kept), bf16)] * 2
        + [sds((rows, width), f32)] * 3
        + [sds((rows, hidden), f32), sds((rows, width), bf16 if packed else f32)],
        [pltpu.VMEM((rows, width), bf16), pltpu.VMEM((rows, width), f32)],
        2 * rows * width * (2 * hidden + width),
        4 * width * hidden + 4 * rows * hidden + 30 * rows * width,
    )(meta, att, x, mixer, mixer_bias, mixer_scale, gain, shift, inner, inner_bias, outer, outer_bias, outer_scale)


def feed_back_body(
    block, packed, meta, g_ref, feed_ref, slope_ref, middle_ref, branch_ref,
    outer_scale, gain_ref, mixer_scale, outer_ref, inner_ref, mixer_ref,
    grads_ref, g_middle_ref, g_att_ref, vector_ref, g_feed_ref, total_ref, *kept
):
    step = pl.program_id(0)
    steps = pl.num_programs(0)
    rows, width = middle_ref.shape
    half_steps = steps // 2

    def incoming():
        g = g_ref[...].astype(f32)
        if packed:
            place = lax.broadcasted_iota(jnp.int32, g.shape, 0)
            g = jnp.where(place < meta[3] + SPECIAL, g, 0.0)
        return g

    @pl.when(step == 0)
    def _():
        g = incoming()
        g_feed = (g * row(outer_scale, block)).astype(bf16)
        g_feed_ref[...] = g_feed
        grads_ref[0, :, : width // 2] = g_feed[:, : width // 2]
        grads_ref[1, :, : width // 2] = g_feed[:, width // 2 :]
        vector_ref[0:1, :] = col_sum(g * feed_ref[...])
        vector_ref[1:2, :] = col_sum(g_feed.astype(f32))
        total_ref[...] = jnp.zeros_like(total_ref)

    g_pre = (nt(g_feed_ref[...], outer_ref[0]) * slope_ref[...]).astype(bf16)
    grads_ref[step // half_steps, :, pl.ds(pl.multiple_of(width + lax.rem(step, half_steps) * CHUNK, CHUNK), CHUNK)] = g_pre
    per_row = width // CHUNK
    vector_ref[pl.ds(6 + step // per_row, 1), pl.ds(pl.multiple_of(lax.rem(step, per_row) * CHUNK, CHUNK), CHUNK)] = col_sum(g_pre.astype(f32))
    total_ref[...] += nt(g_pre, inner_ref[0])

    @pl.when(step == steps - 1)
    def _():
        hat, spread = center_norm(middle_ref[...], norm_eps)
        g_nm = total_ref[...]
        vector_ref[2:3, :] = col_sum(g_nm * hat)
        vector_ref[3:4, :] = col_sum(g_nm)
        g_middle = incoming() + norm_back(g_nm * row(gain_ref, block), hat, spread)
        g_middle_ref[...] = g_middle
        vector_ref[4:5, :] = col_sum(g_middle * branch_ref[...])
        g_branch = (g_middle * row(mixer_scale, block)).astype(bf16)
        vector_ref[5:6, :] = col_sum(g_branch.astype(f32))
        grads_ref[0, :, width // 2 : width] = g_branch[:, : width // 2]
        grads_ref[1, :, width // 2 : width] = g_branch[:, width // 2 :]
        g_att = nt(g_branch, mixer_ref[0])
        if packed:
            for pair in range(width // LANES):
                even, odd = pack_pair(g_att[:, pair * LANES : (pair + 1) * LANES])
                g_att_ref[2 * pair] = even.astype(bf16)
                g_att_ref[2 * pair + 1] = odd.astype(bf16)
        else:
            g_att_ref[...] = g_att.astype(bf16)


def feed_backward(block, packed, heads, meta, g, feed, slope, middle, branch, outer_scale, gain, mixer_scale, outer, inner, mixer):
    rows, width = middle.shape
    hidden = inner.shape[2]
    steps = hidden // CHUNK
    vector = full(gain.shape)
    vector_rows = 6 + hidden // width
    att_shape = (heads, rows // 2, LANES) if packed else (rows, width)
    return call(
        partial(feed_back_body, block, packed),
        f"feed_backward_{block}",
        (steps,),
        [
            full((rows, width)),
            full((rows, width)),
            pl.BlockSpec((rows, CHUNK), lambda j, m: (0, j)),
            full((rows, width)),
            full((rows, width)),
            vector, vector, vector,
            pl.BlockSpec((1, CHUNK, width), lambda j, m: (block, j, 0)),
            pl.BlockSpec((1, width, CHUNK), lambda j, m: (block, 0, j)),
            pl.BlockSpec((1, width, width), lambda j, m: (block, 0, 0)),
        ],
        [
            full((2, rows, width + hidden // 2)),
            full((rows, width)),
            full(att_shape),
            full((vector_rows, width)),
        ],
        [
            sds((2, rows, width + hidden // 2), bf16),
            sds((rows, width), f32),
            sds(att_shape, bf16),
            sds((vector_rows, width), f32),
        ],
        [pltpu.VMEM((rows, width), bf16), pltpu.VMEM((rows, width), f32)],
        2 * rows * width * (2 * hidden + width),
        4 * width * hidden + 8 * rows * hidden + 20 * rows * width,
    )(meta, g, feed, slope, middle, branch, outer_scale, gain, mixer_scale, outer, inner, mixer)


def joint_back_body(
    block, packed, head, meta, g_ref, pre_ref, x_ref, g_middle_ref, gain_ref, pattern_ref, w_ref,
    grads_ref, out_ref, vector_ref, total_ref
):
    step = pl.program_id(0)
    steps = pl.num_programs(0)
    rows, width = total_ref.shape
    per_part = width // CHUNK
    half_steps = steps // 2

    @pl.when(step == 0)
    def _():
        total_ref[...] = jnp.zeros_like(total_ref)
        vector_ref[...] = jnp.zeros_like(vector_ref)

    if packed:
        pieces = []
        for pair in range(CHUNK // LANES):
            pieces.append(
                unpack_pair(g_ref[2 * pair, 0].astype(f32), g_ref[2 * pair + 1, 0].astype(f32))
            )
        g = jnp.concatenate(pieces, axis=1)
    else:
        g = g_ref[...]
    pattern = pattern_ref[...]

    def finish(g_joined):
        rounded = g_joined.astype(bf16)
        grads_ref[step // half_steps, :, pl.ds(pl.multiple_of(lax.rem(step, half_steps) * CHUNK, CHUNK), CHUNK)] = rounded
        vector_ref[pl.ds(2 + step // per_part, 1), pl.ds(pl.multiple_of(lax.rem(step, per_part) * CHUNK, CHUNK), CHUNK)] = col_sum(rounded.astype(f32))
        total_ref[...] += nt(rounded, w_ref[0])

    def head_back(gain, gain_row, shift_row):
        mean_matrix = seg_matrix(SLAB, head, 1.0 / head)
        pieces = []
        for slab in range(CHUNK // SLAB):
            at = slab * SLAB
            g_now = g[:, at : at + SLAB]
            hat, spread = seg_norm(pre_ref[:, at : at + SLAB], mean_matrix)
            vector_ref[gain_row : gain_row + 1, at : at + SLAB] += col_sum(g_now * hat)
            if shift_row is not None:
                vector_ref[shift_row : shift_row + 1, at : at + SLAB] += col_sum(g_now)
            grad_hat = g_now * gain
            pieces.append(
                spread
                * (
                    grad_hat
                    - seg_dot(grad_hat, mean_matrix)
                    - hat * seg_dot(grad_hat * hat, mean_matrix)
                )
            )
        finish(jnp.concatenate(pieces, axis=1))

    @pl.when(step < per_part)
    def _():
        head_back(pattern[3 * block : 3 * block + 1], 5, 6)

    @pl.when((step >= per_part) & (step < 2 * per_part))
    def _():
        head_back(pattern[3 * block + 2 : 3 * block + 3], 7, None)

    @pl.when(step >= 2 * per_part)
    def _():
        finish(g)

    @pl.when(step == steps - 1)
    def _():
        hat, spread = center_norm(x_ref[...].astype(f32), norm_eps)
        g_normed = total_ref[...]
        vector_ref[0:1, :] = col_sum(g_normed * hat)
        vector_ref[1:2, :] = col_sum(g_normed)
        result = g_middle_ref[...] + norm_back(g_normed * row(gain_ref, block), hat, spread)
        out_ref[...] = result.astype(out_ref.dtype)


def joint_backward(block, packed, head, meta, g, pre, x, g_middle, gain, pattern, weight):
    rows, width = x.shape
    per_part = width // CHUNK
    if packed:
        g_spec = pl.BlockSpec(
            (CHUNK // head, 1, rows // 2, LANES),
            lambda j, m: (lax.rem(j, per_part), j // per_part, 0, 0),
        )
    else:
        g_spec = pl.BlockSpec((rows, CHUNK), lambda j, m: (0, j))
    return call(
        partial(joint_back_body, block, packed, head),
        f"joint_backward_{block}",
        (3 * per_part,),
        [
            g_spec,
            pl.BlockSpec((rows, CHUNK), lambda j, m: (0, jnp.minimum(j, 2 * per_part - 1))),
            full((rows, width)),
            full((rows, width)),
            full(gain.shape),
            full(pattern.shape),
            pl.BlockSpec((1, width, CHUNK), lambda j, m: (block, 0, j)),
        ],
        [full((2, rows, 3 * width // 2)), full((rows, width)), full((8, width))],
        [
            sds((2, rows, 3 * width // 2), bf16),
            sds((rows, width), f32 if packed else bf16),
            sds((8, width), f32),
        ],
        [pltpu.VMEM((rows, width), f32)],
        2 * rows * width * 3 * width,
        6 * width * width + 30 * rows * width,
    )(meta, g, pre, x, g_middle, gain, pattern, weight)


def product_body(plan, chips, meta, *refs):
    lefts, rights = refs[:4], refs[4:8]
    send_ref, keep_ref, left, right = refs[8:]
    rows = lefts[0].shape[0]
    for index in range(4):
        left[index * rows : (index + 1) * rows, :] = lefts[index][...]
        right[index * rows : (index + 1) * rows, :] = rights[index][0]
    odd = meta[2] == 1
    for left_at, left_width, right_at, offset in plan:
        deep = left_width // chips
        for start in range(0, left_width, CHUNK):
            value = tn(
                left[:, left_at + start : left_at + start + CHUNK],
                right[:, right_at : right_at + CHUNK],
            ).astype(f32)
            value = value.reshape(CHUNK // (2 * deep), 2, deep, CHUNK)
            first = start // (2 * deep)
            last = first + CHUNK // (2 * deep)
            keep_ref[first:last, offset : offset + deep, :] = jnp.where(odd, value[:, 1], value[:, 0]).astype(bf16)
            send_ref[first:last, offset : offset + deep, :] = jnp.where(odd, value[:, 0], value[:, 1]).astype(bf16)


def product(name, plan, chips, meta, lefts, rights):
    rows, left_width = lefts[0].shape
    right_width = rights[0].shape[2]
    deep = sum(piece[1] // chips for piece in plan)
    shape = (chips // 2, deep, CHUNK)
    half = pl.BlockSpec((1, rows, right_width), lambda i, m: (m[1], 0, 0))
    return call(
        partial(product_body, plan, chips),
        name,
        (1,),
        [full((rows, left_width))] * 4 + [half] * 4,
        [full(shape)] * 2,
        [sds(shape, bf16)] * 2,
        [pltpu.VMEM((4 * rows, left_width), bf16), pltpu.VMEM((4 * rows, right_width), bf16)],
        2 * 4 * rows * deep * chips * CHUNK,
        8 * rows * (left_width + right_width) + 2 * chips * deep * CHUNK,
    )(meta, *lefts, *rights)


def local(scenes, frames, tokens, patch_counts, first_gain, first_shift, joint_weight, joint_bias, query_gain, query_shift, key_gain, mixer_weight, mixer_bias, mixer_scale, second_gain, second_shift, inner_weight, inner_bias, outer_weight, outer_bias, outer_scale, cotangent):
    rows, width = tokens.shape[1:]
    half = rows // 2
    head = query_gain.shape[1]
    heads = width // head
    hidden = inner_weight.shape[2]
    chips = frames // 2
    parts = frames // heads
    scene = lax.axis_index("scene")
    frame = lax.axis_index("frame")
    core = lax.rem(frame, 2)
    meta = jnp.stack([scene, core, lax.rem(frame // 2, 2), patch_counts[0, 0]]).astype(jnp.int32)
    pattern = jnp.tile(
        jnp.stack([vector[block] for block in range(2) for vector in (query_gain, query_shift, key_gain)]).astype(f32),
        (1, SLAB // head),
    )
    everyone = [("scene", "frame")]

    def swap_scene(value):
        return lax.ppermute(value, "scene", [(s, s ^ 1) for s in range(scenes)])

    def swap_frame(value, bit):
        return lax.ppermute(value, "frame", [(f, f ^ bit) for f in range(frames)])

    groups = [[part * heads + place for place in range(heads)] for part in range(parts)]

    def exchange(value):
        if parts == 1:
            return lax.all_to_all(value, "frame", 0, 0, tiled=True)
        return lax.all_to_all(value, "frame", 0, 0, tiled=True, axis_index_groups=groups)

    def to_heads(value):
        if parts > 1:
            value = jnp.tile(value, (parts, 1, 1))
        everything = lax.all_to_all(value, "frame", 0, 0, tiled=True)
        if parts == 1:
            return everything, everything
        return lax.dynamic_slice_in_dim(everything, (frame // heads) * heads, heads, 0), everything

    def from_heads(dq, dk, dv):
        if parts == 1:
            value = jnp.stack([part.reshape(heads, half, LANES) for part in (dq, dk, dv)], axis=1)
            return exchange(value)
        dq = exchange(dq.reshape(heads, half, LANES))
        both = jnp.stack([part.reshape(frames, half, LANES) for part in (dk, dv)], axis=1)
        both = lax.all_to_all(both, "frame", 0, 0, tiled=True)
        both = both.astype(f32).reshape(parts, heads, 2, half, LANES).sum(0).astype(bf16)
        return jnp.concatenate([dq[:, None], both], axis=1)

    def share_left(own, other):
        beside = swap_scene(other)
        return (own, beside, swap_frame(own, 1), swap_frame(beside, 1))

    def share_right(own):
        beside = swap_scene(own)
        return (own, beside, swap_frame(own, 1), swap_frame(beside, 1))

    def scatter(send, keep):
        bit = 2
        while True:
            held = keep.astype(f32) + swap_frame(send, bit).astype(f32)
            bit = bit * 2
            if bit >= frames:
                return held[0]
            place = lax.rem(frame // bit, 2)
            pairs = held.astype(bf16).reshape((held.shape[0] // 2, 2) + held.shape[1:])
            send = lax.dynamic_index_in_dim(pairs, 1 - place, 1, keepdims=False)
            keep = lax.dynamic_index_in_dim(pairs, place, 1, keepdims=False)

    def core_blocks(held, at, deep, pieces):
        return held[at : at + deep * pieces].reshape(pieces, 2, deep // 2, CHUNK)

    def both_halves(mine, theirs):
        first = jnp.where(core == 0, mine, theirs)
        second = jnp.where(core == 0, theirs, mine)
        return jnp.concatenate([first, second], axis=1)

    def finish(held, layout):
        own, away = [], []
        for deep, pieces, at in layout:
            blocks = core_blocks(held, at, deep, pieces)
            own.append(lax.dynamic_index_in_dim(blocks, core, 1, keepdims=False))
            away.append(lax.dynamic_index_in_dim(blocks, 1 - core, 1, keepdims=False).astype(bf16).reshape(-1, CHUNK))
        came = swap_frame(jnp.concatenate(away, axis=0), 1).astype(f32)
        at = 0
        results = []
        for (deep, pieces, _), mine in zip(layout, own):
            size = pieces * deep // 2
            theirs = came[at : at + size].reshape(pieces, deep // 2, CHUNK)
            at += size
            mine = jnp.transpose(mine, (1, 0, 2)).reshape(deep // 2, pieces * CHUNK)
            theirs = jnp.transpose(theirs, (1, 0, 2)).reshape(deep // 2, pieces * CHUNK)
            results.append(both_halves(mine, theirs))
        return results

    deep_outer = hidden // 2 // chips
    deep_rest = width // 2 // chips
    pieces_inner = hidden // 2 // CHUNK
    pieces_joint = 3 * width // 2 // CHUNK
    plan_feed = [(0, hidden // 2, 0, 0)]
    plan_feed += [
        (hidden // 2, width // 2, width + piece * CHUNK, deep_outer + piece * deep_rest)
        for piece in range(pieces_inner)
    ]
    at_mixer = deep_outer + pieces_inner * deep_rest
    plan_feed += [(hidden // 2 + width // 2, width // 2, width // 2, at_mixer)]
    plan_joint = [(0, width // 2, piece * CHUNK, piece * deep_rest) for piece in range(pieces_joint)]
    layout_feed = [(deep_outer, 1, 0), (deep_rest, pieces_inner, deep_outer), (deep_rest, 1, at_mixer)]
    layout_joint = [(deep_rest, pieces_joint, 0)]

    x0 = tokens[0]
    feed_params = (mixer_weight, mixer_bias, mixer_scale, second_gain, second_shift, inner_weight, inner_bias, outer_weight, outer_bias, outer_scale)
    back_params = (outer_scale, second_gain, mixer_scale, outer_weight, inner_weight, mixer_weight)

    own0, other0, pre0, qkv0 = joint_forward(0, False, head, meta, x0, first_gain, first_shift, pattern, joint_weight, joint_bias)
    left_joint0 = share_left(own0, other0)
    att0 = frame_forward(meta, qkv0)
    own, other, middle0, branch0, feed0, slope0, x1 = feed_forward(0, False, meta, att0, x0, *feed_params)
    left_feed0 = share_left(own, other)
    own1, other1, pre1, pack1 = joint_forward(1, True, head, meta, x1, first_gain, first_shift, pattern, joint_weight, joint_bias)
    left_joint1 = share_left(own1, other1)
    q_pack, kv_pack = to_heads(pack1)
    att_heads, att_full, att_log = scene_forward(meta, q_pack, kv_pack, half)
    att1 = exchange(att_heads.reshape(heads, half, LANES))
    own, other, middle1, branch1, feed1, slope1, layer_out = feed_forward(1, True, meta, att1, x1, *feed_params)
    left_feed1 = share_left(own, other)

    grads, g_middle1, g_att1, vector_feed1 = feed_backward(1, True, heads, meta, cotangent[0], feed1, slope1, middle1, branch1, *back_params)
    send_feed1, keep_feed1 = product("product_feed_1", plan_feed, chips, meta, left_feed1, share_right(grads))
    grad_heads = exchange(g_att1)
    dq, dk, dv = scene_backward(meta, q_pack, kv_pack, grad_heads.reshape(heads * half, LANES), att_full, att_log, half)
    g_qkv1 = from_heads(dq, dk, dv)
    grads, g1, vector_joint1 = joint_backward(1, True, head, meta, g_qkv1, pre1, x1, g_middle1, first_gain, pattern, joint_weight)
    send_joint1, keep_joint1 = product("product_joint_1", plan_joint, chips, meta, left_joint1, share_right(grads))

    grads, g_middle0, g_att0, vector_feed0 = feed_backward(0, False, heads, meta, g1, feed0, slope0, middle0, branch0, *back_params)
    send_feed0, keep_feed0 = product("product_feed_0", plan_feed, chips, meta, left_feed0, share_right(grads))
    g_qkv0 = frame_backward(meta, qkv0, g_att0)
    grads, g0, vector_joint0 = joint_backward(0, False, head, meta, g_qkv0, pre0, x0, g_middle0, first_gain, pattern, joint_weight)
    send_joint0, keep_joint0 = product("product_joint_0", plan_joint, chips, meta, left_joint0, share_right(grads))

    outer1, inner1, mixer1 = finish(scatter(send_feed1, keep_feed1), layout_feed)
    (joint1,) = finish(scatter(send_joint1, keep_joint1), layout_joint)
    outer0, inner0, mixer0 = finish(scatter(send_feed0, keep_feed0), layout_feed)
    (joint0,) = finish(scatter(send_joint0, keep_joint0), layout_joint)

    vectors = jnp.concatenate([vector_feed0, vector_joint0, vector_feed1, vector_joint1], axis=0)
    vectors = lax.psum(vectors, ("scene", "frame")).reshape(2, -1, width)
    at_joint = vector_feed0.shape[0]

    def folded(index):
        return vectors[:, at_joint + index].reshape(2, heads, head).sum(1)

    return (
        layer_out[None],
        g0[None],
        vectors[:, at_joint],
        vectors[:, at_joint + 1],
        jnp.stack([joint0, joint1]),
        vectors[:, at_joint + 2 : at_joint + 5].reshape(2, 3 * width),
        folded(5),
        folded(6),
        folded(7),
        jnp.stack([mixer0, mixer1]),
        vectors[:, 5],
        vectors[:, 4],
        vectors[:, 2],
        vectors[:, 3],
        jnp.stack([inner0, inner1]),
        vectors[:, 6:at_joint].reshape(2, hidden),
        jnp.stack([outer0, outer1]),
        vectors[:, 1],
        vectors[:, 0],
    )


def solution(mesh):
    tokens_spec = P("scene", "frame", None)
    shard = P(None, ("scene", "frame"), None)
    in_specs = (tokens_spec, P("scene", "frame")) + (P(),) * 17 + (tokens_spec,)
    out_specs = (
        tokens_spec, tokens_spec, P(), P(), shard, P(), P(), P(), P(), shard,
        P(), P(), P(), P(), shard, P(), shard, P(), P(),
    )
    body = partial(local, mesh.shape["scene"], mesh.shape["frame"])
    return jax.shard_map(body, mesh=mesh, in_specs=in_specs, out_specs=out_specs, check_vma=False)
```

```python
from functools import partial

import jax
import jax.numpy as jnp
from jax import lax
from jax.experimental import pallas as pl
from jax.experimental.pallas import tpu as pltpu
from jax.sharding import PartitionSpec as P

SPECIAL = 5
CHUNK = 512
LANES = 128
SLAB = 256
norm_eps = 1e-06
head_eps = 1e-05
closed_score = -10000.0
f32 = jnp.float32
bf16 = jnp.bfloat16


def nn(a, b):
    return lax.dot_general(a, b, (((1,), (0,)), ((), ())), preferred_element_type=f32)


def nt(a, b):
    return lax.dot_general(a, b, (((1,), (1,)), ((), ())), preferred_element_type=f32)


def tn(a, b):
    return lax.dot_general(a, b, (((0,), (0,)), ((), ())), preferred_element_type=f32)


def row(ref, index):
    return ref[...].astype(f32)[index : index + 1, :]


def col_sum(value):
    return jnp.sum(value, axis=0, keepdims=True)


def center_norm(value, eps):
    centered = value - jnp.mean(value, axis=-1, keepdims=True)
    spread = lax.rsqrt(jnp.mean(centered * centered, axis=-1, keepdims=True) + eps)
    return centered * spread, spread


def norm_back(grad_hat, hat, spread):
    mean_grad = jnp.mean(grad_hat, axis=-1, keepdims=True)
    mean_both = jnp.mean(grad_hat * hat, axis=-1, keepdims=True)
    return spread * (grad_hat - mean_grad - hat * mean_both)


def seg_matrix(width, head, value):
    shift = head.bit_length() - 1
    first = lax.shift_right_logical(lax.broadcasted_iota(jnp.int32, (width, width), 0), shift)
    second = lax.shift_right_logical(lax.broadcasted_iota(jnp.int32, (width, width), 1), shift)
    return jnp.where(first == second, value, 0.0).astype(bf16)


def seg_dot(value, matrix):
    high = value.astype(bf16)
    low = (value - high.astype(f32)).astype(bf16)
    return nn(high, matrix) + nn(low, matrix)


def seg_norm(value, mean_matrix):
    centered = value - seg_dot(value, mean_matrix)
    spread = lax.rsqrt(seg_dot(centered * centered, mean_matrix) + head_eps)
    return centered * spread, spread


def first_lanes(rows):
    return lax.broadcasted_iota(jnp.int32, (rows, LANES), 1) < LANES // 2


def turn(value):
    return pltpu.roll(value, LANES // 2, value.ndim - 1)


def pack_pair(slab):
    half = slab.shape[0] // 2
    top, bottom = slab[:half], slab[half:]
    low = first_lanes(half)
    return jnp.where(low, top, turn(bottom)), jnp.where(low, turn(top), bottom)


def unpack_pair(even, odd):
    low = first_lanes(even.shape[0])
    top = jnp.where(low, even, turn(odd))
    bottom = jnp.where(low, turn(even), odd)
    return jnp.concatenate([top, bottom], axis=0)


def erf(value):
    value = jnp.clip(value, -4.0, 4.0)
    square = value * value
    top = jnp.full_like(square, -2.72614225801306e-10)
    for coefficient in (
        2.77068142495902e-08,
        -2.10102402082508e-06,
        -5.69250639462346e-05,
        -7.34990630326855e-04,
        -2.95459980854025e-03,
        -1.60960333262415e-02,
    ):
        top = top * square + coefficient
    bottom = jnp.full_like(square, -1.45660718464996e-05)
    for coefficient in (
        -2.13374055278905e-04,
        -1.68282697438203e-03,
        -7.37332916720468e-03,
        -1.42647390514189e-02,
    ):
        bottom = bottom * square + coefficient
    return value * top / bottom


def full(shape):
    return pl.BlockSpec(shape, lambda *_: (0,) * len(shape))


def sds(shape, dtype):
    return jax.ShapeDtypeStruct(shape, dtype)


def call(body, name, grid, in_specs, out_specs, out_shape, scratch, flops, moved):
    return pl.pallas_call(
        body,
        name=name,
        out_shape=out_shape,
        grid_spec=pltpu.PrefetchScalarGridSpec(
            num_scalar_prefetch=1,
            grid=grid,
            in_specs=in_specs,
            out_specs=out_specs,
            scratch_shapes=scratch,
        ),
        cost_estimate=pl.CostEstimate(flops=flops, bytes_accessed=moved, transcendentals=0),
    )


def joint_body(
    block, packed, head, meta, x_ref, gain_ref, shift_ref, pattern_ref, w_ref, b_ref,
    own_ref, other_ref, pre_ref, out_ref, normed_ref, *stage
):
    step = pl.program_id(0)
    rows, width = normed_ref.shape
    per_part = width // CHUNK
    half = rows // 2

    @pl.when(step == 0)
    def _():
        hat, _ = center_norm(x_ref[...].astype(f32), norm_eps)
        normed = (hat * row(gain_ref, block) + row(shift_ref, block)).astype(bf16)
        normed_ref[...] = normed

        @pl.when(meta[0] == 0)
        def _():
            own_ref[...] = normed[:, : width // 2]
            other_ref[...] = normed[:, width // 2 :]

        @pl.when(meta[0] != 0)
        def _():
            own_ref[...] = normed[:, width // 2 :]
            other_ref[...] = normed[:, : width // 2]

        if packed:
            count = jnp.full((8, LANES), meta[3], jnp.int32).astype(f32)
            for place in range(stage[0].shape[0]):
                stage[0][place, 3 * half : 3 * half + 8, :] = count

    joined = nn(normed_ref[...], w_ref[0]) + row(b_ref, block)
    pattern = pattern_ref[...]

    def emit(part, values):
        if packed:
            base = (step - part * per_part) * (CHUNK // head)
            for slab in range(CHUNK // LANES):
                even, odd = pack_pair(values[:, slab * LANES : (slab + 1) * LANES])
                stage[0][base + 2 * slab, part * half : (part + 1) * half, :] = even
                stage[0][base + 2 * slab + 1, part * half : (part + 1) * half, :] = odd
        else:
            out_ref[...] = values.astype(bf16)

    def normed_heads(gain, shift):
        mean_matrix = seg_matrix(SLAB, head, 1.0 / head)
        pieces = []
        for slab in range(CHUNK // SLAB):
            hat, _ = seg_norm(joined[:, slab * SLAB : (slab + 1) * SLAB], mean_matrix)
            pieces.append(hat * gain if shift is None else hat * gain + shift)
        return jnp.concatenate(pieces, axis=1)

    scale = head ** (-0.5)

    @pl.when(step < per_part)
    def _():
        pre_ref[...] = joined
        emit(0, normed_heads(
            pattern[3 * block : 3 * block + 1] * scale,
            pattern[3 * block + 1 : 3 * block + 2] * scale,
        ))

    @pl.when((step >= per_part) & (step < 2 * per_part))
    def _():
        pre_ref[...] = joined
        emit(1, normed_heads(pattern[3 * block + 2 : 3 * block + 3], None))

    @pl.when(step >= 2 * per_part)
    def _():
        emit(2, joined)

    if packed:

        @pl.when(step == 3 * per_part - 1)
        def _():
            out_ref[...] = stage[0][...].astype(bf16)


def joint_forward(block, packed, head, meta, x, gain, shift, pattern, weight, bias):
    rows, width = x.shape
    per_part = width // CHUNK
    heads = width // head
    packed_rows = 3 * (rows // 2) + 8
    if packed:
        out_spec, out = full((heads, packed_rows, LANES)), sds((heads, packed_rows, LANES), bf16)
        extra = [pltpu.VMEM((heads, packed_rows, LANES), f32)]
    else:
        out_spec = pl.BlockSpec((rows, CHUNK), lambda j, m: (0, j))
        out = sds((rows, 3 * width), bf16)
        extra = []
    return call(
        partial(joint_body, block, packed, head),
        f"joint_forward_{block}",
        (3 * per_part,),
        [
            full((rows, width)),
            full(gain.shape),
            full(shift.shape),
            full(pattern.shape),
            pl.BlockSpec((1, width, CHUNK), lambda j, m: (block, 0, j)),
            pl.BlockSpec((2, CHUNK), lambda j, m: (0, j)),
        ],
        [
            full((rows, width // 2)),
            full((rows, width // 2)),
            pl.BlockSpec((rows, CHUNK), lambda j, m: (0, jnp.minimum(j, 2 * per_part - 1))),
            out_spec,
        ],
        [
            sds((rows, width // 2), bf16),
            sds((rows, width // 2), bf16),
            sds((rows, 2 * width), f32),
            out,
        ],
        [pltpu.VMEM((rows, width), bf16)] + extra,
        2 * rows * width * 3 * width,
        6 * width * width + 16 * rows * width,
    )(meta, x, gain, shift, pattern, weight, bias)


def lane_picks():
    lane = lax.broadcasted_iota(jnp.int32, (1, LANES), 1)
    low = jnp.where(lane < LANES // 2, 1.0, 0.0)
    return low.astype(bf16), (1.0 - low).astype(bf16)


def open_row(meta, rows):
    place = lax.broadcasted_iota(jnp.int32, (1, rows), 1)
    return jnp.where(place < meta[3] + SPECIAL, 0.0, closed_score)


def frame_body(meta, qkv_ref, out_ref):
    rows, width = out_ref.shape
    bias = open_row(meta, rows)
    picks = lane_picks()
    low = first_lanes(rows)
    for slab in range(width // LANES):
        at = slab * LANES
        queries = qkv_ref[:, at : at + LANES]
        keys = qkv_ref[:, width + at : width + at + LANES]
        values = qkv_ref[:, 2 * width + at : 2 * width + at + LANES]
        results = []
        for pick in picks:
            power = jnp.exp(nt(queries * pick, keys) + bias)
            probs = power / jnp.sum(power, axis=-1, keepdims=True)
            results.append(nn(probs.astype(bf16), values))
        out_ref[:, at : at + LANES] = jnp.where(low, results[0], results[1]).astype(bf16)


def frame_forward(meta, qkv):
    rows = qkv.shape[0]
    width = qkv.shape[1] // 3
    return call(
        frame_body,
        "frame_forward",
        (1,),
        [full(qkv.shape)],
        full((rows, width)),
        sds((rows, width), bf16),
        [],
        4 * rows * rows * width,
        8 * rows * width,
    )(meta, qkv)


def frame_back_body(meta, qkv_ref, grad_ref, out_ref):
    rows, width = grad_ref.shape
    bias = open_row(meta, rows)
    picks = lane_picks()
    low = first_lanes(rows)
    scale = (LANES // 2) ** (-0.5)
    for slab in range(width // LANES):
        at = slab * LANES
        queries = qkv_ref[:, at : at + LANES]
        keys = qkv_ref[:, width + at : width + at + LANES]
        values = qkv_ref[:, 2 * width + at : 2 * width + at + LANES]
        grads = grad_ref[:, at : at + LANES]
        found = []
        for pick in picks:
            power = jnp.exp(nt(queries * pick, keys) + bias)
            probs = power / jnp.sum(power, axis=-1, keepdims=True)
            grad_probs = nt(grads * pick, values)
            delta = jnp.sum(probs * grad_probs, axis=-1, keepdims=True)
            grad_scores = (probs * (grad_probs - delta)).astype(bf16)
            found.append((
                nn(grad_scores, keys) * scale,
                tn(grad_scores, queries),
                tn(probs.astype(bf16), grads),
            ))
        for part in range(3):
            out_ref[:, part * width + at : part * width + at + LANES] = jnp.where(
                low, found[0][part], found[1][part]
            )


def frame_backward(meta, qkv, grad):
    rows, width = grad.shape
    return call(
        frame_back_body,
        "frame_backward",
        (1,),
        [full(qkv.shape), full(grad.shape)],
        full((rows, 3 * width)),
        sds((rows, 3 * width), f32),
        [],
        10 * rows * rows * width,
        20 * rows * width,
    )(meta, qkv, grad)


def packed_part(ref, part, half):
    whole = ref[...].astype(f32)
    return whole[:, part * half : (part + 1) * half, :].reshape(-1, LANES)


def open_slots(ref, half):
    count = ref[...].astype(f32)[:, 3 * half : 3 * half + 8, :]
    count = jnp.concatenate([count] * (half // 8), axis=1)
    place = lax.broadcasted_iota(jnp.int32, count.shape, 1).astype(f32)
    return (
        (place < count + SPECIAL).reshape(-1, LANES),
        (place + half < count + SPECIAL).reshape(-1, LANES),
    )


def scene_body(half, span, meta, q_ref, kv_ref, att_ref, out_ref, log_ref, queries, keys, values):
    n = queries.shape[0] // 2
    m = keys.shape[0] // 2
    q = packed_part(q_ref, 0, half)
    low_n, low_m = first_lanes(n), first_lanes(m)
    queries[:n, :] = jnp.where(low_n, q, 0.0).astype(bf16)
    queries[n:, :] = jnp.where(low_n, turn(q), 0.0).astype(bf16)
    k = packed_part(kv_ref, 1, half)
    keys[:m, :] = k.astype(bf16)
    keys[m:, :] = turn(k).astype(bf16)
    v = packed_part(kv_ref, 2, half)
    open_low, open_high = open_slots(kv_ref, half)
    values[:m, :] = jnp.where(open_low, jnp.where(low_m, v, 1.0), 0.0).astype(bf16)
    values[m:, :] = jnp.where(open_high, jnp.where(low_m, turn(v), 1.0), 0.0).astype(bf16)
    low = first_lanes(LANES)

    @pl.loop(0, n // LANES)
    def _(piece):
        at = pl.multiple_of(piece * LANES, LANES)
        some = jnp.concatenate([queries[pl.ds(at, LANES), :], queries[pl.ds(n + at, LANES), :]], axis=0)
        total = jnp.zeros((2 * LANES, LANES), f32)
        for start in range(0, 2 * m, span):
            power = jnp.exp(nt(some, keys[start : start + span, :])).astype(bf16)
            total = total + nn(power, values[start : start + span, :])
        first, second = total[:LANES], total[LANES:]
        bottom = jnp.where(low, turn(first), second)
        result = jnp.where(low, first, turn(second)) / bottom
        att_ref[pl.ds(at, LANES), :] = result.astype(bf16)
        out_ref[pl.ds(at, LANES), :] = result
        log_ref[pl.ds(at, LANES), :] = jnp.log(bottom)


def scene_forward(meta, q_pack, kv_pack, half):
    n = q_pack.shape[0] * half
    m = kv_pack.shape[0] * half
    span = m // 2
    while span > 640:
        span = span // 2
    return call(
        partial(scene_body, half, span),
        "scene_forward",
        (1,),
        [full(q_pack.shape), full(kv_pack.shape)],
        [full((n, LANES))] * 3,
        [sds((n, LANES), bf16), sds((n, LANES), f32), sds((n, LANES), f32)],
        [
            pltpu.VMEM((2 * n, LANES), bf16),
            pltpu.VMEM((2 * m, LANES), bf16),
            pltpu.VMEM((2 * m, LANES), bf16),
        ],
        4 * 4 * n * m * LANES,
        20 * n * LANES,
    )(meta, q_pack, kv_pack)


def three_lanes(value, closed):
    lane = lax.broadcasted_iota(jnp.int32, value.shape, 1)
    base = LANES // 2
    high = value.astype(bf16).astype(f32)
    rest = value - high
    middle = rest.astype(bf16).astype(f32)
    last = rest - middle
    result = jnp.where(lane == base, high, jnp.where(lane == base + 1, middle, last))
    return jnp.where(lane < base + 3, result, jnp.where(lane == base + 3, closed, 0.0))


def scene_back_body(
    half, span, meta, q_ref, kv_ref, grad_ref, out_ref, log_ref,
    dq_ref, dk_ref, dv_ref, queries, keys, values, grads, turned
):
    n = queries.shape[0] // 2
    m = keys.shape[0] // 2
    low_n, low_m = first_lanes(n), first_lanes(m)
    base = LANES // 2
    q = packed_part(q_ref, 0, half)
    log = -log_ref[...]
    queries[:n, :] = jnp.where(low_n, q, three_lanes(turn(log), closed_score)).astype(bf16)
    queries[n:, :] = jnp.where(low_n, turn(q), three_lanes(log, closed_score)).astype(bf16)
    g = grad_ref[...].astype(f32)
    delta = -seg_dot(g * out_ref[...], seg_matrix(LANES, base, 1.0))
    grads[:n, :] = jnp.where(low_n, g, three_lanes(turn(delta), 0.0)).astype(bf16)
    grads[n:, :] = jnp.where(low_n, turn(g), three_lanes(delta, 0.0)).astype(bf16)
    lane = lax.broadcasted_iota(jnp.int32, (m, LANES), 1)
    ones = jnp.where(lane < base + 3, 1.0, 0.0)
    open_low, open_high = open_slots(kv_ref, half)
    k = packed_part(kv_ref, 1, half)
    for place, k_now, is_open in ((0, k, open_low), (m, turn(k), open_high)):
        tail = jnp.where((lane == base + 3) & jnp.logical_not(is_open), 1.0, ones)
        keys[place : place + m, :] = jnp.where(low_m, k_now, tail).astype(bf16)
    v = packed_part(kv_ref, 2, half)
    values[:m, :] = jnp.where(low_m, v, ones).astype(bf16)
    values[m:, :] = jnp.where(low_m, turn(v), ones).astype(bf16)
    turned[...] = jnp.zeros_like(turned)
    low = first_lanes(LANES)

    @pl.loop(0, m // LANES)
    def _(piece):
        at = pl.multiple_of(piece * LANES, LANES)
        key_part = jnp.concatenate([keys[pl.ds(at, LANES), :], keys[pl.ds(m + at, LANES), :]], axis=0)
        value_part = jnp.concatenate(
            [values[pl.ds(at, LANES), :], values[pl.ds(m + at, LANES), :]], axis=0
        )
        key_turned = jnp.transpose(key_part.astype(f32)).astype(bf16)
        dk = jnp.zeros((2 * LANES, LANES), f32)
        dv = jnp.zeros((2 * LANES, LANES), f32)
        for start in range(0, 2 * n, span):
            some = queries[start : start + span, :]
            some_grads = grads[start : start + span, :]
            probs = jnp.exp(nt(key_part, some))
            grad_scores = (probs * nt(value_part, some_grads)).astype(bf16)
            dv = dv + nn(probs.astype(bf16), some_grads)
            dk = dk + nn(grad_scores, some)
            turned[:, start : start + span] += nn(key_turned, grad_scores)
        dk_ref[pl.ds(at, LANES), :] = jnp.where(low, dk[:LANES], turn(dk[LANES:])).astype(bf16)
        dv_ref[pl.ds(at, LANES), :] = jnp.where(low, dv[:LANES], turn(dv[LANES:])).astype(bf16)

    scale = base ** (-0.5)
    for at in range(0, n, LANES):
        first = jnp.transpose(turned[:, at : at + LANES])
        second = jnp.transpose(turned[:, n + at : n + at + LANES])
        dq_ref[at : at + LANES, :] = (jnp.where(low, first, turn(second)) * scale).astype(bf16)


def scene_backward(meta, q_pack, kv_pack, grad, out, log, half):
    n = q_pack.shape[0] * half
    m = kv_pack.shape[0] * half
    span = n // 2
    while span > 640:
        span = span // 2
    return call(
        partial(scene_back_body, half, span),
        "scene_backward",
        (1,),
        [full(q_pack.shape), full(kv_pack.shape)] + [full((n, LANES))] * 3,
        [full((n, LANES)), full((m, LANES)), full((m, LANES))],
        [sds((n, LANES), bf16), sds((m, LANES), bf16), sds((m, LANES), bf16)],
        [
            pltpu.VMEM((2 * n, LANES), bf16),
            pltpu.VMEM((2 * m, LANES), bf16),
            pltpu.VMEM((2 * m, LANES), bf16),
            pltpu.VMEM((2 * n, LANES), bf16),
            pltpu.VMEM((LANES, 2 * n), f32),
        ],
        10 * 4 * n * m * LANES,
        30 * n * LANES,
    )(meta, q_pack, kv_pack, grad, out, log)


def feed_body(
    block, packed, meta, att_ref, x_ref, mixer_ref, mixer_bias, mixer_scale, gain_ref, shift_ref,
    inner_ref, inner_bias, outer_ref, outer_bias, outer_scale,
    own_ref, other_ref, middle_ref, branch_ref, feed_ref, slope_ref, out_ref, normed_ref, total_ref
):
    step = pl.program_id(0)
    steps = pl.num_programs(0)
    rows, width = middle_ref.shape
    hidden_half = own_ref.shape[1] - width
    half_steps = hidden_half // CHUNK
    mine = meta[0]

    def split(value, at):
        first, second = value[:, : width // 2], value[:, width // 2 :]

        @pl.when(mine == 0)
        def _():
            own_ref[:, at : at + width // 2] = first
            other_ref[:, at : at + width // 2] = second

        @pl.when(mine != 0)
        def _():
            own_ref[:, at : at + width // 2] = second
            other_ref[:, at : at + width // 2] = first

    @pl.when(step == 0)
    def _():
        if packed:
            pieces = []
            for pair in range(width // LANES):
                pieces.append(
                    unpack_pair(att_ref[2 * pair].astype(f32), att_ref[2 * pair + 1].astype(f32))
                )
            attended = jnp.concatenate(pieces, axis=1).astype(bf16)
        else:
            attended = att_ref[...]
        branch = nn(attended, mixer_ref[0]) + row(mixer_bias, block)
        middle = x_ref[...].astype(f32) + row(mixer_scale, block) * branch
        hat, _ = center_norm(middle, norm_eps)
        normed = (hat * row(gain_ref, block) + row(shift_ref, block)).astype(bf16)
        branch_ref[...] = branch
        middle_ref[...] = middle
        normed_ref[...] = normed
        split(normed, hidden_half)
        split(attended, hidden_half + width // 2)
        total_ref[...] = jnp.zeros_like(total_ref)

    pre = nn(normed_ref[...], inner_ref[0]) + row(inner_bias, block)
    share = 0.5 * (1.0 + erf(pre * (2.0 ** (-0.5))))
    slope_ref[...] = share + pre * jnp.exp(-0.5 * pre * pre) * 0.3989422804014327
    hidden = (pre * share).astype(bf16)
    place = pl.multiple_of(lax.rem(step, half_steps) * CHUNK, CHUNK)

    @pl.when(step // half_steps == mine)
    def _():
        own_ref[:, pl.ds(place, CHUNK)] = hidden

    @pl.when(step // half_steps != mine)
    def _():
        other_ref[:, pl.ds(place, CHUNK)] = hidden

    total_ref[...] += nn(hidden, outer_ref[0])

    @pl.when(step == steps - 1)
    def _():
        feed = total_ref[...] + row(outer_bias, block)
        feed_ref[...] = feed
        result = middle_ref[...] + row(outer_scale, block) * feed
        if packed:
            place = lax.broadcasted_iota(jnp.int32, result.shape, 0)
            result = jnp.where(place < meta[3] + SPECIAL, result, 0.0)
        out_ref[...] = result.astype(out_ref.dtype)


def feed_forward(block, packed, meta, att, x, mixer, mixer_bias, mixer_scale, gain, shift, inner, inner_bias, outer, outer_bias, outer_scale):
    rows, width = x.shape
    hidden = inner.shape[2]
    kept = hidden // 2 + width
    steps = hidden // CHUNK
    vector = full(gain.shape)
    return call(
        partial(feed_body, block, packed),
        f"feed_forward_{block}",
        (steps,),
        [
            full(att.shape),
            full((rows, width)),
            pl.BlockSpec((1, width, width), lambda j, m: (block, 0, 0)),
            vector, vector, vector, vector,
            pl.BlockSpec((1, width, CHUNK), lambda j, m: (block, 0, j)),
            pl.BlockSpec((2, CHUNK), lambda j, m: (0, j)),
            pl.BlockSpec((1, CHUNK, width), lambda j, m: (block, j, 0)),
            vector, vector,
        ],
        [full((rows, kept))] * 2
        + [full((rows, width))] * 3
        + [pl.BlockSpec((rows, CHUNK), lambda j, m: (0, j)), full((rows, width))],
        [sds((rows, kept), bf16)] * 2
        + [sds((rows, width), f32)] * 3
        + [sds((rows, hidden), f32), sds((rows, width), bf16 if packed else f32)],
        [pltpu.VMEM((rows, width), bf16), pltpu.VMEM((rows, width), f32)],
        2 * rows * width * (2 * hidden + width),
        4 * width * hidden + 4 * rows * hidden + 30 * rows * width,
    )(meta, att, x, mixer, mixer_bias, mixer_scale, gain, shift, inner, inner_bias, outer, outer_bias, outer_scale)


def feed_back_body(
    block, packed, meta, g_ref, feed_ref, slope_ref, middle_ref, branch_ref,
    outer_scale, gain_ref, mixer_scale, outer_ref, inner_ref, mixer_ref,
    grads_ref, g_middle_ref, g_att_ref, vector_ref, g_feed_ref, total_ref, *kept
):
    step = pl.program_id(0)
    steps = pl.num_programs(0)
    rows, width = middle_ref.shape
    half_steps = steps // 2

    def incoming():
        g = g_ref[...].astype(f32)
        if packed:
            place = lax.broadcasted_iota(jnp.int32, g.shape, 0)
            g = jnp.where(place < meta[3] + SPECIAL, g, 0.0)
        return g

    @pl.when(step == 0)
    def _():
        g = incoming()
        g_feed = (g * row(outer_scale, block)).astype(bf16)
        g_feed_ref[...] = g_feed
        grads_ref[0, :, : width // 2] = g_feed[:, : width // 2]
        grads_ref[1, :, : width // 2] = g_feed[:, width // 2 :]
        vector_ref[0:1, :] = col_sum(g * feed_ref[...])
        vector_ref[1:2, :] = col_sum(g_feed.astype(f32))
        total_ref[...] = jnp.zeros_like(total_ref)

    g_pre = (nt(g_feed_ref[...], outer_ref[0]) * slope_ref[...]).astype(bf16)
    grads_ref[step // half_steps, :, pl.ds(pl.multiple_of(width + lax.rem(step, half_steps) * CHUNK, CHUNK), CHUNK)] = g_pre
    per_row = width // CHUNK
    vector_ref[pl.ds(6 + step // per_row, 1), pl.ds(pl.multiple_of(lax.rem(step, per_row) * CHUNK, CHUNK), CHUNK)] = col_sum(g_pre.astype(f32))
    total_ref[...] += nt(g_pre, inner_ref[0])

    @pl.when(step == steps - 1)
    def _():
        hat, spread = center_norm(middle_ref[...], norm_eps)
        g_nm = total_ref[...]
        vector_ref[2:3, :] = col_sum(g_nm * hat)
        vector_ref[3:4, :] = col_sum(g_nm)
        g_middle = incoming() + norm_back(g_nm * row(gain_ref, block), hat, spread)
        g_middle_ref[...] = g_middle
        vector_ref[4:5, :] = col_sum(g_middle * branch_ref[...])
        g_branch = (g_middle * row(mixer_scale, block)).astype(bf16)
        vector_ref[5:6, :] = col_sum(g_branch.astype(f32))
        grads_ref[0, :, width // 2 : width] = g_branch[:, : width // 2]
        grads_ref[1, :, width // 2 : width] = g_branch[:, width // 2 :]
        g_att = nt(g_branch, mixer_ref[0])
        if packed:
            for pair in range(width // LANES):
                even, odd = pack_pair(g_att[:, pair * LANES : (pair + 1) * LANES])
                g_att_ref[2 * pair] = even.astype(bf16)
                g_att_ref[2 * pair + 1] = odd.astype(bf16)
        else:
            g_att_ref[...] = g_att.astype(bf16)


def feed_backward(block, packed, heads, meta, g, feed, slope, middle, branch, outer_scale, gain, mixer_scale, outer, inner, mixer):
    rows, width = middle.shape
    hidden = inner.shape[2]
    steps = hidden // CHUNK
    vector = full(gain.shape)
    vector_rows = 6 + hidden // width
    att_shape = (heads, rows // 2, LANES) if packed else (rows, width)
    return call(
        partial(feed_back_body, block, packed),
        f"feed_backward_{block}",
        (steps,),
        [
            full((rows, width)),
            full((rows, width)),
            pl.BlockSpec((rows, CHUNK), lambda j, m: (0, j)),
            full((rows, width)),
            full((rows, width)),
            vector, vector, vector,
            pl.BlockSpec((1, CHUNK, width), lambda j, m: (block, j, 0)),
            pl.BlockSpec((1, width, CHUNK), lambda j, m: (block, 0, j)),
            pl.BlockSpec((1, width, width), lambda j, m: (block, 0, 0)),
        ],
        [
            full((2, rows, width + hidden // 2)),
            full((rows, width)),
            full(att_shape),
            full((vector_rows, width)),
        ],
        [
            sds((2, rows, width + hidden // 2), bf16),
            sds((rows, width), f32),
            sds(att_shape, bf16),
            sds((vector_rows, width), f32),
        ],
        [pltpu.VMEM((rows, width), bf16), pltpu.VMEM((rows, width), f32)],
        2 * rows * width * (2 * hidden + width),
        4 * width * hidden + 8 * rows * hidden + 20 * rows * width,
    )(meta, g, feed, slope, middle, branch, outer_scale, gain, mixer_scale, outer, inner, mixer)


def joint_back_body(
    block, packed, head, meta, g_ref, pre_ref, x_ref, g_middle_ref, gain_ref, pattern_ref, w_ref,
    grads_ref, out_ref, vector_ref, total_ref
):
    step = pl.program_id(0)
    steps = pl.num_programs(0)
    rows, width = total_ref.shape
    per_part = width // CHUNK
    half_steps = steps // 2

    @pl.when(step == 0)
    def _():
        total_ref[...] = jnp.zeros_like(total_ref)
        vector_ref[...] = jnp.zeros_like(vector_ref)

    if packed:
        pieces = []
        for pair in range(CHUNK // LANES):
            pieces.append(
                unpack_pair(g_ref[2 * pair, 0].astype(f32), g_ref[2 * pair + 1, 0].astype(f32))
            )
        g = jnp.concatenate(pieces, axis=1)
    else:
        g = g_ref[...]
    pattern = pattern_ref[...]

    def finish(g_joined):
        rounded = g_joined.astype(bf16)
        grads_ref[step // half_steps, :, pl.ds(pl.multiple_of(lax.rem(step, half_steps) * CHUNK, CHUNK), CHUNK)] = rounded
        vector_ref[pl.ds(2 + step // per_part, 1), pl.ds(pl.multiple_of(lax.rem(step, per_part) * CHUNK, CHUNK), CHUNK)] = col_sum(rounded.astype(f32))
        total_ref[...] += nt(rounded, w_ref[0])

    def head_back(gain, gain_row, shift_row):
        mean_matrix = seg_matrix(SLAB, head, 1.0 / head)
        pieces = []
        for slab in range(CHUNK // SLAB):
            at = slab * SLAB
            g_now = g[:, at : at + SLAB]
            hat, spread = seg_norm(pre_ref[:, at : at + SLAB], mean_matrix)
            vector_ref[gain_row : gain_row + 1, at : at + SLAB] += col_sum(g_now * hat)
            if shift_row is not None:
                vector_ref[shift_row : shift_row + 1, at : at + SLAB] += col_sum(g_now)
            grad_hat = g_now * gain
            pieces.append(
                spread
                * (
                    grad_hat
                    - seg_dot(grad_hat, mean_matrix)
                    - hat * seg_dot(grad_hat * hat, mean_matrix)
                )
            )
        finish(jnp.concatenate(pieces, axis=1))

    @pl.when(step < per_part)
    def _():
        head_back(pattern[3 * block : 3 * block + 1], 5, 6)

    @pl.when((step >= per_part) & (step < 2 * per_part))
    def _():
        head_back(pattern[3 * block + 2 : 3 * block + 3], 7, None)

    @pl.when(step >= 2 * per_part)
    def _():
        finish(g)

    @pl.when(step == steps - 1)
    def _():
        hat, spread = center_norm(x_ref[...].astype(f32), norm_eps)
        g_normed = total_ref[...]
        vector_ref[0:1, :] = col_sum(g_normed * hat)
        vector_ref[1:2, :] = col_sum(g_normed)
        result = g_middle_ref[...] + norm_back(g_normed * row(gain_ref, block), hat, spread)
        out_ref[...] = result.astype(out_ref.dtype)


def joint_backward(block, packed, head, meta, g, pre, x, g_middle, gain, pattern, weight):
    rows, width = x.shape
    per_part = width // CHUNK
    if packed:
        g_spec = pl.BlockSpec(
            (CHUNK // head, 1, rows // 2, LANES),
            lambda j, m: (lax.rem(j, per_part), j // per_part, 0, 0),
        )
    else:
        g_spec = pl.BlockSpec((rows, CHUNK), lambda j, m: (0, j))
    return call(
        partial(joint_back_body, block, packed, head),
        f"joint_backward_{block}",
        (3 * per_part,),
        [
            g_spec,
            pl.BlockSpec((rows, CHUNK), lambda j, m: (0, jnp.minimum(j, 2 * per_part - 1))),
            full((rows, width)),
            full((rows, width)),
            full(gain.shape),
            full(pattern.shape),
            pl.BlockSpec((1, width, CHUNK), lambda j, m: (block, 0, j)),
        ],
        [full((2, rows, 3 * width // 2)), full((rows, width)), full((8, width))],
        [
            sds((2, rows, 3 * width // 2), bf16),
            sds((rows, width), f32 if packed else bf16),
            sds((8, width), f32),
        ],
        [pltpu.VMEM((rows, width), f32)],
        2 * rows * width * 3 * width,
        6 * width * width + 30 * rows * width,
    )(meta, g, pre, x, g_middle, gain, pattern, weight)


MESH = pl.DeviceIdType.MESH


def peers_of(frames):
    scene = lax.axis_index("scene")
    frame = lax.axis_index("frame")
    bits = []
    bit = 1
    while bit < frames:
        value = lax.rem(frame // bit, 2)
        bits.append((value, (scene, frame + bit * (1 - 2 * value))))
        bit *= 2
    core, core_peer = bits[0]
    scene_peer = (1 - scene, frame)
    cross_peer = (1 - scene, core_peer[1])
    return core, core_peer, scene_peer, cross_peer, bits[1:]


def enter(targets):
    barrier = pltpu.get_barrier_semaphore()
    for target in targets:
        pl.semaphore_signal(barrier, inc=1, device_id=target, device_id_type=MESH)
    pl.semaphore_wait(barrier, len(targets))


def collect_body(frames, blocks, hidden_half, width, meta, *refs):
    count = 2 + 8
    inputs, refs = refs[: blocks * count], refs[blocks * count :]
    vector_in, refs = refs[0], refs[1:]
    out_ref, vector_out, refs = refs[0], refs[1], refs[2:]
    own, came, acts, hids, parts, last, sums, refs = (
        refs[0], refs[1], refs[2], refs[3], refs[4], refs[5], refs[6], refs[7:]
    )
    stages = len(refs) - 9
    steps, refs = refs[:stages], refs[stages:]
    load_sem, g_send, g_recv, p_send, p_recv, f_send, f_recv, v_send, v_recv = refs
    rows = own.shape[2]
    chips = frames // 2
    n_outer = 4
    n_inner = hidden_half // CHUNK
    n_joint = 3 * (width // 2) // CHUNK
    per_block = n_outer + n_inner + 1 + n_joint
    n_pieces = 1 + n_inner + 1 + n_joint
    total = blocks * per_block
    half = width // 2
    core, core_peer, scene_peer, cross_peer, bits = peers_of(frames)

    loads = []

    def load(source, target):
        copy = pltpu.make_async_copy(source, target, load_sem.at[len(loads)])
        copy.start()
        loads.append(copy)

    for block in range(blocks):
        feed_g, joint_g = inputs[block * count], inputs[block * count + 1]
        pre_lanes = hidden_half
        load(feed_g.at[:, :, pl.ds(0, half)], own.at[block, :, :, pl.ds(0, half)])
        load(feed_g.at[:, :, pl.ds(width, pre_lanes)], own.at[block, :, :, pl.ds(half, pre_lanes)])
        load(feed_g.at[:, :, pl.ds(half, half)], own.at[block, :, :, pl.ds(half + pre_lanes, half)])
        load(joint_g, own.at[block, :, :, pl.ds(width + pre_lanes, 3 * half)])
    first_loads = len(loads)
    for block in range(blocks):
        for place in range(4):
            feed_x, joint_x = inputs[block * count + 2 + place], inputs[block * count + 6 + place]
            load(feed_x.at[:, pl.ds(0, hidden_half)], hids.at[block, place])
            load(feed_x.at[:, pl.ds(hidden_half, width)], acts.at[block, place, :, pl.ds(0, width)])
            load(joint_x, acts.at[block, place, :, pl.ds(width, half)])

    enter([core_peer, scene_peer, cross_peer] + [peer for _, peer in bits])
    for copy in loads[:first_loads]:
        copy.wait()

    def piece_copy(block, piece, which):
        lanes = pl.ds(pl.multiple_of(piece * CHUNK, CHUNK), CHUNK)
        target = (scene_peer, core_peer, cross_peer)[which]
        side = core if which == 0 else 1 - core
        return pltpu.make_async_remote_copy(
            src_ref=own.at[block, side, :, lanes],
            dst_ref=came.at[block, which, :, lanes],
            send_sem=g_send.at[block, which, piece],
            recv_sem=g_recv.at[block, which, piece],
            device_id=target,
            device_id_type=MESH,
        )

    ahead = 3

    def start_pieces(index):
        block = index // per_block
        unit = lax.rem(index, per_block)

        @pl.when((index < total) & ((unit == 0) | (unit >= n_outer)))
        def _():
            piece = jnp.where(unit == 0, 0, unit - (n_outer - 1))
            for which in range(3):
                piece_copy(block, piece, which).start()

    @pl.loop(0, ahead)
    def _(index):
        start_pieces(index)

    for copy in loads[first_loads:]:
        copy.wait()

    vector_peers = [core_peer, scene_peer] + [peer for _, peer in bits]
    sums[0] = vector_in[...]

    def vector_copy(stage):
        return pltpu.make_async_remote_copy(
            src_ref=sums.at[2 * stage],
            dst_ref=sums.at[2 * stage + 1],
            send_sem=v_send.at[stage],
            recv_sem=v_recv.at[stage],
            device_id=vector_peers[stage],
            device_id_type=MESH,
        )

    def vector_step(stage):
        vector_copy(stage).wait()
        result = sums[2 * stage] + sums[2 * stage + 1]
        if stage + 1 < len(vector_peers):
            sums[2 * stage + 2] = result
        else:
            vector_out[...] = result

    def stage_pieces(stage, index):
        value, peer = bits[stage]
        source = parts if stage == 0 else steps[stage - 1]
        for pair in range(chips >> (stage + 1)):
            yield pltpu.make_async_remote_copy(
                src_ref=source.at[index, 2 * pair + 1 - value],
                dst_ref=steps[stage].at[index, pair],
                send_sem=p_send.at[stage, index],
                recv_sem=p_recv.at[stage, index],
                device_id=peer,
                device_id_type=MESH,
            )

    def stage_start(stage, index):
        for copy in stage_pieces(stage, index):
            copy.start()

    def stage_whole(stage, index):
        return pltpu.make_async_remote_copy(
            src_ref=steps[stage].at[index],
            dst_ref=steps[stage].at[index],
            send_sem=p_send.at[stage, index],
            recv_sem=p_recv.at[stage, index],
            device_id=bits[stage][1],
            device_id_type=MESH,
        )

    def last_copy(index):
        return pltpu.make_async_remote_copy(
            src_ref=steps[stages - 1].at[index, 0, 1 - core],
            dst_ref=last.at[index],
            send_sem=f_send.at[index],
            recv_sem=f_recv.at[index],
            device_id=core_peer,
            device_id_type=MESH,
        )

    def multiply(index):
        block = index // per_block
        unit = lax.rem(index, per_block)

        def wait_piece(piece):
            for which in range(3):
                piece_copy(block, piece, which).wait_recv()

        def gathered(lanes):
            return jnp.concatenate(
                [own[block, core, :, lanes]] + [came[block, which, :, lanes] for which in range(3)], axis=0
            )

        @pl.when(unit < n_outer)
        def _():
            @pl.when(unit == 0)
            def _():
                wait_piece(0)

            left = jnp.concatenate([hids[block, place] for place in range(4)], axis=0)
            right = gathered(pl.ds(pl.multiple_of(unit * LANES, LANES), LANES))
            value = tn(left, right)
            deep = hidden_half // chips // 8
            value = value.reshape(chips, 2, 4, deep, LANES)
            value = jnp.concatenate([value[:, :, turn] for turn in range(4)], axis=-1)
            parts[index] = value.astype(bf16)

        @pl.when(unit >= n_outer)
        def _():
            piece = unit - (n_outer - 1)
            wait_piece(piece)
            place = jnp.where(unit >= n_outer + n_inner, 1, 0) + jnp.where(unit >= n_outer + n_inner + 1, 1, 0)
            lanes = pl.ds(pl.multiple_of(place * half, half), half)
            left = jnp.concatenate([acts[block, source, :, lanes] for source in range(4)], axis=0)
            value = tn(left, gathered(pl.ds(pl.multiple_of(piece * CHUNK, CHUNK), CHUNK)))
            parts[index] = value.reshape(chips, 2, half // chips // 2, CHUNK).astype(bf16)

    def add(stage, index):
        stage_whole(stage, index).wait_recv()
        value = bits[stage][0]
        source = parts if stage == 0 else steps[stage - 1]
        for pair in range(chips >> (stage + 1)):
            held = source[index, 2 * pair + value].astype(f32) + steps[stage][index, pair].astype(f32)
            if stage + 1 == stages:
                out_ref[index, core] = jnp.where(core == 0, held[0], held[1])
            steps[stage][index, pair] = held.astype(bf16)

    def close(index):
        last_copy(index).wait_recv()
        out_ref[index, 1 - core] = last[index].astype(f32)

    n_vector = len(vector_peers)
    vector_copy(0).start()
    lags = [2 + 2 * stage for stage in range(stages)]
    ends = lags[-1] + 2

    @pl.loop(0, total + ends)
    def _(turn_at):
        @pl.when(turn_at < total)
        def _():
            multiply(turn_at)

        for stage in range(stages):
            index = turn_at - lags[stage]

            @pl.when((index >= 0) & (index < total))
            def _():
                add(stage, index)

        for stage in range(n_vector):

            @pl.when(turn_at == 2 * stage + 1)
            def _():
                vector_step(stage)

        index_last = turn_at - ends

        @pl.when((index_last >= 0) & (index_last < total))
        def _():
            close(index_last)

        for stage in range(stages):
            index = turn_at - lags[stage]

            @pl.when((index >= 0) & (index < total))
            def _():
                if stage + 1 < stages:
                    stage_start(stage + 1, index)
                else:
                    last_copy(index).start()

        for stage in range(1, n_vector):

            @pl.when(turn_at == 2 * stage - 1)
            def _():
                vector_copy(stage).start()

        @pl.when(turn_at < total)
        def _():
            stage_start(0, turn_at)

        start_pieces(turn_at + ahead)

    @pl.loop(0, total)
    def _(index):
        for stage in range(stages):
            stage_whole(stage, index).wait_send()
        last_copy(index).wait_send()

    for block in range(blocks):

        @pl.loop(0, n_pieces)
        def _(piece):
            for which in range(3):
                piece_copy(block, piece, which).wait_send()


def collect(frames, meta, groups, vector):
    blocks = len(groups)
    flat = []
    for feed_g, joint_g, feed_x, joint_x in groups:
        flat += [feed_g, joint_g, *feed_x, *joint_x]
    rows = flat[0].shape[1]
    half = flat[1].shape[2] // 3
    width = 2 * half
    hidden_half = flat[0].shape[2] - width
    chips = frames // 2
    stages = chips.bit_length() - 1
    n_inner = hidden_half // CHUNK
    n_joint = 3 * half // CHUNK
    per_block = 4 + n_inner + 1 + n_joint
    n_pieces = 2 + n_inner + n_joint
    total = blocks * per_block
    deep = half // chips // 2
    any_space = pl.BlockSpec(memory_space=pl.ANY)
    n_vector = 2 + stages
    dma = pltpu.SemaphoreType.DMA
    moved = 12 * total * chips * deep * CHUNK
    return pl.pallas_call(
        partial(collect_body, frames, blocks, hidden_half, width),
        name="collect",
        out_shape=[sds((total, 2, deep, CHUNK), f32), sds(vector.shape, f32)],
        grid_spec=pltpu.PrefetchScalarGridSpec(
            num_scalar_prefetch=1,
            grid=(1,),
            in_specs=[any_space] * len(flat) + [full(vector.shape)],
            out_specs=[full((total, 2, deep, CHUNK)), full(vector.shape)],
            scratch_shapes=[
                pltpu.VMEM((blocks, 2, rows, n_pieces * CHUNK), bf16),
                pltpu.VMEM((blocks, 3, rows, n_pieces * CHUNK), bf16),
                pltpu.VMEM((blocks, 4, rows, 3 * half), bf16),
                pltpu.VMEM((blocks, 4, rows, hidden_half), bf16),
                pltpu.VMEM((total, chips, 2, deep, CHUNK), bf16),
                pltpu.VMEM((total, deep, CHUNK), bf16),
                pltpu.VMEM((2 * n_vector,) + vector.shape, f32),
            ]
            + [pltpu.VMEM((total, chips >> (stage + 1), 2, deep, CHUNK), bf16) for stage in range(stages)]
            + [
                dma((blocks * 16,)),
                dma((blocks, 3, n_pieces)),
                dma((blocks, 3, n_pieces)),
                dma((stages, total)),
                dma((stages, total)),
                dma((total,)),
                dma((total,)),
                dma((n_vector,)),
                dma((n_vector,)),
            ],
        ),
        compiler_params=pltpu.CompilerParams(
            collective_id=0, has_side_effects=True, vmem_limit_bytes=64 * 1024 * 1024 - 65536
        ),
        cost_estimate=pl.CostEstimate(flops=2 * 4 * rows * total * chips * 2 * deep * CHUNK, bytes_accessed=moved, transcendentals=0),
    )(meta, *flat, vector)


def local(scenes, frames, tokens, patch_counts, first_gain, first_shift, joint_weight, joint_bias, query_gain, query_shift, key_gain, mixer_weight, mixer_bias, mixer_scale, second_gain, second_shift, inner_weight, inner_bias, outer_weight, outer_bias, outer_scale, cotangent):
    rows, width = tokens.shape[1:]
    half = rows // 2
    head = query_gain.shape[1]
    heads = width // head
    hidden = inner_weight.shape[2]
    chips = frames // 2
    parts = frames // heads
    scene = lax.axis_index("scene")
    frame = lax.axis_index("frame")
    core = lax.rem(frame, 2)
    meta = jnp.stack([scene, core, lax.rem(frame // 2, 2), patch_counts[0, 0]]).astype(jnp.int32)
    pattern = jnp.tile(
        jnp.stack([vector[block] for block in range(2) for vector in (query_gain, query_shift, key_gain)]).astype(f32),
        (1, SLAB // head),
    )

    def swap_scene(value):
        return lax.ppermute(value, "scene", [(s, s ^ 1) for s in range(scenes)])

    def swap_frame(value, bit):
        return lax.ppermute(value, "frame", [(f, f ^ bit) for f in range(frames)])

    groups = [[part * heads + place for place in range(heads)] for part in range(parts)]

    def exchange(value):
        if parts == 1:
            return lax.all_to_all(value, "frame", 0, 0, tiled=True)
        return lax.all_to_all(value, "frame", 0, 0, tiled=True, axis_index_groups=groups)

    def to_heads(value):
        if parts > 1:
            value = jnp.tile(value, (parts, 1, 1))
        everything = lax.all_to_all(value, "frame", 0, 0, tiled=True)
        if parts == 1:
            return everything, everything
        return lax.dynamic_slice_in_dim(everything, (frame // heads) * heads, heads, 0), everything

    def from_heads(dq, dk, dv):
        if parts == 1:
            value = jnp.stack([part.reshape(heads, half, LANES) for part in (dq, dk, dv)], axis=1)
            return exchange(value)
        dq = exchange(dq.reshape(heads, half, LANES))
        both = jnp.stack([part.reshape(frames, half, LANES) for part in (dk, dv)], axis=1)
        both = lax.all_to_all(both, "frame", 0, 0, tiled=True)
        both = both.astype(f32).reshape(parts, heads, 2, half, LANES).sum(0).astype(bf16)
        return jnp.concatenate([dq[:, None], both], axis=1)

    def share_left(own, other):
        beside = swap_scene(other)
        return (own, beside, swap_frame(own, 1), swap_frame(beside, 1))

    x0 = tokens[0]
    feed_params = (mixer_weight, mixer_bias, mixer_scale, second_gain, second_shift, inner_weight, inner_bias, outer_weight, outer_bias, outer_scale)
    back_params = (outer_scale, second_gain, mixer_scale, outer_weight, inner_weight, mixer_weight)

    own0, other0, pre0, qkv0 = joint_forward(0, False, head, meta, x0, first_gain, first_shift, pattern, joint_weight, joint_bias)
    left_joint0 = share_left(own0, other0)
    att0 = frame_forward(meta, qkv0)
    own, other, middle0, branch0, feed0, slope0, x1 = feed_forward(0, False, meta, att0, x0, *feed_params)
    left_feed0 = share_left(own, other)
    own1, other1, pre1, pack1 = joint_forward(1, True, head, meta, x1, first_gain, first_shift, pattern, joint_weight, joint_bias)
    left_joint1 = share_left(own1, other1)
    q_pack, kv_pack = to_heads(pack1)
    att_heads, att_full, att_log = scene_forward(meta, q_pack, kv_pack, half)
    att1 = exchange(att_heads.reshape(heads, half, LANES))
    own, other, middle1, branch1, feed1, slope1, layer_out = feed_forward(1, True, meta, att1, x1, *feed_params)
    left_feed1 = share_left(own, other)

    g_feed1, g_middle1, g_att1, vector_feed1 = feed_backward(1, True, heads, meta, cotangent[0], feed1, slope1, middle1, branch1, *back_params)
    grad_heads = exchange(g_att1)
    dq, dk, dv = scene_backward(meta, q_pack, kv_pack, grad_heads.reshape(heads * half, LANES), att_full, att_log, half)
    g_qkv1 = from_heads(dq, dk, dv)
    g_joint1, g1, vector_joint1 = joint_backward(1, True, head, meta, g_qkv1, pre1, x1, g_middle1, first_gain, pattern, joint_weight)

    g_feed0, g_middle0, g_att0, vector_feed0 = feed_backward(0, False, heads, meta, g1, feed0, slope0, middle0, branch0, *back_params)
    g_qkv0 = frame_backward(meta, qkv0, g_att0)
    g_joint0, g0, vector_joint0 = joint_backward(0, False, head, meta, g_qkv0, pre0, x0, g_middle0, first_gain, pattern, joint_weight)

    vectors = jnp.concatenate([vector_feed0, vector_joint0, vector_feed1, vector_joint1], axis=0)
    pieces, vectors = collect(
        frames,
        meta,
        [(g_feed1, g_joint1, left_feed1, left_joint1), (g_feed0, g_joint0, left_feed0, left_joint0)],
        vectors,
    )
    pieces = pieces[:].reshape((2, -1) + pieces.shape[1:])[::-1]
    n_inner = hidden // 2 // CHUNK
    deep = pieces.shape[3]

    def laid_out(first, last):
        some = jnp.transpose(pieces[:, first:last], (0, 3, 2, 1, 4))
        return some.reshape(2, deep, -1)

    outer = pieces[:, :4].reshape(2, 4, 2, deep, 4, LANES)
    outer = jnp.transpose(outer, (0, 4, 3, 2, 1, 5)).reshape(2, 4 * deep, width)
    inner = laid_out(4, 4 + n_inner)
    mixer = laid_out(4 + n_inner, 5 + n_inner)
    joint = laid_out(5 + n_inner, pieces.shape[1])
    vectors = vectors.reshape(2, -1, width)
    at_joint = vector_feed0.shape[0]

    def folded(index):
        return vectors[:, at_joint + index].reshape(2, heads, head).sum(1)

    return (
        layer_out[None],
        g0[None],
        vectors[:, at_joint],
        vectors[:, at_joint + 1],
        joint,
        vectors[:, at_joint + 2 : at_joint + 5].reshape(2, 3 * width),
        folded(5),
        folded(6),
        folded(7),
        mixer,
        vectors[:, 5],
        vectors[:, 4],
        vectors[:, 2],
        vectors[:, 3],
        inner,
        vectors[:, 6:at_joint].reshape(2, hidden),
        outer,
        vectors[:, 1],
        vectors[:, 0],
    )


def solution(mesh):
    tokens_spec = P("scene", "frame", None)
    shard = P(None, ("scene", "frame"), None)
    in_specs = (tokens_spec, P("scene", "frame")) + (P(),) * 17 + (tokens_spec,)
    out_specs = (
        tokens_spec, tokens_spec, P(), P(), shard, P(), P(), P(), P(), shard,
        P(), P(), P(), P(), shard, P(), shard, P(), P(),
    )
    body = partial(local, mesh.shape["scene"], mesh.shape["frame"])
    return jax.shard_map(body, mesh=mesh, in_specs=in_specs, out_specs=out_specs, check_vma=False)
```

```python
from functools import partial

import jax
import jax.numpy as jnp
from jax import lax
from jax.experimental import pallas as pl
from jax.experimental.pallas import tpu as pltpu
from jax.sharding import PartitionSpec as P

SPECIAL = 5
CHUNK = 512
LANES = 128
SLAB = 256
norm_eps = 1e-06
head_eps = 1e-05
closed_score = -10000.0
f32 = jnp.float32
bf16 = jnp.bfloat16


def nn(a, b):
    return lax.dot_general(a, b, (((1,), (0,)), ((), ())), preferred_element_type=f32)


def nt(a, b):
    return lax.dot_general(a, b, (((1,), (1,)), ((), ())), preferred_element_type=f32)


def tn(a, b):
    return lax.dot_general(a, b, (((0,), (0,)), ((), ())), preferred_element_type=f32)


def row(ref, index):
    return ref[...].astype(f32)[index : index + 1, :]


def col_sum(value):
    return jnp.sum(value, axis=0, keepdims=True)


def center_norm(value, eps):
    centered = value - jnp.mean(value, axis=-1, keepdims=True)
    spread = lax.rsqrt(jnp.mean(centered * centered, axis=-1, keepdims=True) + eps)
    return centered * spread, spread


def norm_back(grad_hat, hat, spread):
    mean_grad = jnp.mean(grad_hat, axis=-1, keepdims=True)
    mean_both = jnp.mean(grad_hat * hat, axis=-1, keepdims=True)
    return spread * (grad_hat - mean_grad - hat * mean_both)


def seg_matrix(width, head, value):
    shift = head.bit_length() - 1
    first = lax.shift_right_logical(lax.broadcasted_iota(jnp.int32, (width, width), 0), shift)
    second = lax.shift_right_logical(lax.broadcasted_iota(jnp.int32, (width, width), 1), shift)
    return jnp.where(first == second, value, 0.0).astype(bf16)


def seg_dot(value, matrix):
    high = value.astype(bf16)
    low = (value - high.astype(f32)).astype(bf16)
    return nn(high, matrix) + nn(low, matrix)


def seg_norm(value, mean_matrix):
    centered = value - seg_dot(value, mean_matrix)
    spread = lax.rsqrt(seg_dot(centered * centered, mean_matrix) + head_eps)
    return centered * spread, spread


def first_lanes(rows):
    return lax.broadcasted_iota(jnp.int32, (rows, LANES), 1) < LANES // 2


def turn(value):
    return pltpu.roll(value, LANES // 2, value.ndim - 1)


def pack_pair(slab):
    half = slab.shape[0] // 2
    top, bottom = slab[:half], slab[half:]
    low = first_lanes(half)
    return jnp.where(low, top, turn(bottom)), jnp.where(low, turn(top), bottom)


def unpack_pair(even, odd):
    low = first_lanes(even.shape[0])
    top = jnp.where(low, even, turn(odd))
    bottom = jnp.where(low, turn(even), odd)
    return jnp.concatenate([top, bottom], axis=0)


def erf(value):
    value = jnp.clip(value, -4.0, 4.0)
    square = value * value
    top = jnp.full_like(square, -2.72614225801306e-10)
    for coefficient in (
        2.77068142495902e-08,
        -2.10102402082508e-06,
        -5.69250639462346e-05,
        -7.34990630326855e-04,
        -2.95459980854025e-03,
        -1.60960333262415e-02,
    ):
        top = top * square + coefficient
    bottom = jnp.full_like(square, -1.45660718464996e-05)
    for coefficient in (
        -2.13374055278905e-04,
        -1.68282697438203e-03,
        -7.37332916720468e-03,
        -1.42647390514189e-02,
    ):
        bottom = bottom * square + coefficient
    return value * top / bottom


def full(shape):
    return pl.BlockSpec(shape, lambda *_: (0,) * len(shape))


def sds(shape, dtype):
    return jax.ShapeDtypeStruct(shape, dtype)


def call(body, name, grid, in_specs, out_specs, out_shape, scratch, flops, moved):
    return pl.pallas_call(
        body,
        name=name,
        out_shape=out_shape,
        grid_spec=pltpu.PrefetchScalarGridSpec(
            num_scalar_prefetch=1,
            grid=grid,
            in_specs=in_specs,
            out_specs=out_specs,
            scratch_shapes=scratch,
        ),
        cost_estimate=pl.CostEstimate(flops=flops, bytes_accessed=moved, transcendentals=0),
    )


def joint_body(
    block, packed, head, meta, x_ref, gain_ref, shift_ref, pattern_ref, w_ref, b_ref,
    own_ref, other_ref, pre_ref, out_ref, normed_ref, *stage
):
    step = pl.program_id(0)
    rows, width = normed_ref.shape
    per_part = width // CHUNK
    half = rows // 2

    @pl.when(step == 0)
    def _():
        hat, _ = center_norm(x_ref[...].astype(f32), norm_eps)
        normed = (hat * row(gain_ref, block) + row(shift_ref, block)).astype(bf16)
        normed_ref[...] = normed

        @pl.when(meta[0] == 0)
        def _():
            own_ref[...] = normed[:, : width // 2]
            other_ref[...] = normed[:, width // 2 :]

        @pl.when(meta[0] != 0)
        def _():
            own_ref[...] = normed[:, width // 2 :]
            other_ref[...] = normed[:, : width // 2]

        if packed:
            count = jnp.full((8, LANES), meta[3], jnp.int32).astype(f32)
            for place in range(stage[0].shape[0]):
                stage[0][place, 3 * half : 3 * half + 8, :] = count

    joined = nn(normed_ref[...], w_ref[0]) + row(b_ref, block)
    pattern = pattern_ref[...]

    def emit(part, values):
        if packed:
            base = (step - part * per_part) * (CHUNK // head)
            for slab in range(CHUNK // LANES):
                even, odd = pack_pair(values[:, slab * LANES : (slab + 1) * LANES])
                stage[0][base + 2 * slab, part * half : (part + 1) * half, :] = even
                stage[0][base + 2 * slab + 1, part * half : (part + 1) * half, :] = odd
        else:
            out_ref[...] = values.astype(bf16)

    def normed_heads(gain, shift):
        mean_matrix = seg_matrix(SLAB, head, 1.0 / head)
        pieces = []
        for slab in range(CHUNK // SLAB):
            hat, _ = seg_norm(joined[:, slab * SLAB : (slab + 1) * SLAB], mean_matrix)
            pieces.append(hat * gain if shift is None else hat * gain + shift)
        return jnp.concatenate(pieces, axis=1)

    scale = head ** (-0.5)

    @pl.when(step < per_part)
    def _():
        pre_ref[...] = joined
        emit(0, normed_heads(
            pattern[3 * block : 3 * block + 1] * scale,
            pattern[3 * block + 1 : 3 * block + 2] * scale,
        ))

    @pl.when((step >= per_part) & (step < 2 * per_part))
    def _():
        pre_ref[...] = joined
        emit(1, normed_heads(pattern[3 * block + 2 : 3 * block + 3], None))

    @pl.when(step >= 2 * per_part)
    def _():
        emit(2, joined)

    if packed:

        @pl.when(step == 3 * per_part - 1)
        def _():
            out_ref[...] = stage[0][...].astype(bf16)


def joint_forward(block, packed, head, meta, x, gain, shift, pattern, weight, bias):
    rows, width = x.shape
    per_part = width // CHUNK
    heads = width // head
    packed_rows = 3 * (rows // 2) + 8
    if packed:
        out_spec, out = full((heads, packed_rows, LANES)), sds((heads, packed_rows, LANES), bf16)
        extra = [pltpu.VMEM((heads, packed_rows, LANES), f32)]
    else:
        out_spec = pl.BlockSpec((rows, CHUNK), lambda j, m: (0, j))
        out = sds((rows, 3 * width), bf16)
        extra = []
    return call(
        partial(joint_body, block, packed, head),
        f"joint_forward_{block}",
        (3 * per_part,),
        [
            full((rows, width)),
            full(gain.shape),
            full(shift.shape),
            full(pattern.shape),
            pl.BlockSpec((1, width, CHUNK), lambda j, m: (block, 0, j)),
            pl.BlockSpec((2, CHUNK), lambda j, m: (0, j)),
        ],
        [
            full((rows, width // 2)),
            full((rows, width // 2)),
            pl.BlockSpec((rows, CHUNK), lambda j, m: (0, jnp.minimum(j, 2 * per_part - 1))),
            out_spec,
        ],
        [
            sds((rows, width // 2), bf16),
            sds((rows, width // 2), bf16),
            sds((rows, 2 * width), f32),
            out,
        ],
        [pltpu.VMEM((rows, width), bf16)] + extra,
        2 * rows * width * 3 * width,
        6 * width * width + 16 * rows * width,
    )(meta, x, gain, shift, pattern, weight, bias)


def lane_picks():
    lane = lax.broadcasted_iota(jnp.int32, (1, LANES), 1)
    low = jnp.where(lane < LANES // 2, 1.0, 0.0)
    return low.astype(bf16), (1.0 - low).astype(bf16)


def open_row(meta, rows):
    place = lax.broadcasted_iota(jnp.int32, (1, rows), 1)
    return jnp.where(place < meta[3] + SPECIAL, 0.0, closed_score)


def frame_body(meta, qkv_ref, out_ref):
    rows, width = out_ref.shape
    bias = open_row(meta, rows)
    picks = lane_picks()
    low = first_lanes(rows)
    for slab in range(width // LANES):
        at = slab * LANES
        queries = qkv_ref[:, at : at + LANES]
        keys = qkv_ref[:, width + at : width + at + LANES]
        values = qkv_ref[:, 2 * width + at : 2 * width + at + LANES]
        results = []
        for pick in picks:
            power = jnp.exp(nt(queries * pick, keys) + bias)
            probs = power / jnp.sum(power, axis=-1, keepdims=True)
            results.append(nn(probs.astype(bf16), values))
        out_ref[:, at : at + LANES] = jnp.where(low, results[0], results[1]).astype(bf16)


def frame_forward(meta, qkv):
    rows = qkv.shape[0]
    width = qkv.shape[1] // 3
    return call(
        frame_body,
        "frame_forward",
        (1,),
        [full(qkv.shape)],
        full((rows, width)),
        sds((rows, width), bf16),
        [],
        4 * rows * rows * width,
        8 * rows * width,
    )(meta, qkv)


def frame_back_body(meta, qkv_ref, grad_ref, out_ref):
    rows, width = grad_ref.shape
    bias = open_row(meta, rows)
    picks = lane_picks()
    low = first_lanes(rows)
    scale = (LANES // 2) ** (-0.5)
    for slab in range(width // LANES):
        at = slab * LANES
        queries = qkv_ref[:, at : at + LANES]
        keys = qkv_ref[:, width + at : width + at + LANES]
        values = qkv_ref[:, 2 * width + at : 2 * width + at + LANES]
        grads = grad_ref[:, at : at + LANES]
        found = []
        for pick in picks:
            power = jnp.exp(nt(queries * pick, keys) + bias)
            probs = power / jnp.sum(power, axis=-1, keepdims=True)
            grad_probs = nt(grads * pick, values)
            delta = jnp.sum(probs * grad_probs, axis=-1, keepdims=True)
            grad_scores = (probs * (grad_probs - delta)).astype(bf16)
            found.append((
                nn(grad_scores, keys) * scale,
                tn(grad_scores, queries),
                tn(probs.astype(bf16), grads),
            ))
        for part in range(3):
            out_ref[:, part * width + at : part * width + at + LANES] = jnp.where(
                low, found[0][part], found[1][part]
            )


def frame_backward(meta, qkv, grad):
    rows, width = grad.shape
    return call(
        frame_back_body,
        "frame_backward",
        (1,),
        [full(qkv.shape), full(grad.shape)],
        full((rows, 3 * width)),
        sds((rows, 3 * width), f32),
        [],
        10 * rows * rows * width,
        20 * rows * width,
    )(meta, qkv, grad)


def packed_part(value, part, half):
    whole = value.astype(f32)
    return whole[:, part * half : (part + 1) * half, :].reshape(-1, LANES)


def open_slots(value, half):
    count = value.astype(f32)[:, 3 * half : 3 * half + 8, :]
    count = jnp.concatenate([count] * (half // 8), axis=1)
    place = lax.broadcasted_iota(jnp.int32, count.shape, 1).astype(f32)
    return (
        (place < count + SPECIAL).reshape(-1, LANES),
        (place + half < count + SPECIAL).reshape(-1, LANES),
    )


MESH = pl.DeviceIdType.MESH


def peers_of(frames):
    scene = lax.axis_index("scene")
    frame = lax.axis_index("frame")
    bits = []
    bit = 1
    while bit < frames:
        value = lax.rem(frame // bit, 2)
        bits.append((value, (scene, frame + bit * (1 - 2 * value))))
        bit *= 2
    core, core_peer = bits[0]
    scene_peer = (1 - scene, frame)
    cross_peer = (1 - scene, core_peer[1])
    return core, core_peer, scene_peer, cross_peer, bits[1:]


def enter(targets):
    barrier = pltpu.get_barrier_semaphore()
    for target in targets:
        pl.semaphore_signal(barrier, inc=1, device_id=target, device_id_type=MESH)
    pl.semaphore_wait(barrier, len(targets))


def enter_scene(frames):
    barrier = pltpu.get_barrier_semaphore()
    _, _, scene_peer, cross_peer, _ = peers_of(frames)
    scene = lax.axis_index("scene")
    frame = lax.axis_index("frame")
    for target in (scene_peer, cross_peer):
        pl.semaphore_signal(barrier, inc=1, device_id=target, device_id_type=MESH)

    @pl.loop(1, frames)
    def _(offset):
        pl.semaphore_signal(
            barrier, inc=1, device_id=(scene, lax.rem(frame + offset, frames)), device_id_type=MESH
        )

    pl.semaphore_wait(barrier, frames + 1)


def remote(source, target, send, recv, device):
    return pltpu.make_async_remote_copy(
        src_ref=source, dst_ref=target, send_sem=send, recv_sem=recv, device_id=device, device_id_type=MESH
    )


class Share:
    def __init__(self, frames, pairs, outs, send, recv):
        _, core_peer, scene_peer, _, _ = peers_of(frames)
        self.first, self.second = [], []
        for index, ((own, other), out) in enumerate(zip(pairs, outs)):
            self.first.append(remote(other, out.at[0], send.at[3 * index], recv.at[3 * index], scene_peer))
            self.first.append(remote(own, out.at[1], send.at[3 * index + 1], recv.at[3 * index + 1], core_peer))
            self.second.append(
                remote(out.at[0], out.at[2], send.at[3 * index + 2], recv.at[3 * index + 2], core_peer)
            )

    def start(self):
        for copy in self.first:
            copy.start()

    def relay(self):
        for index, copy in enumerate(self.second):
            self.first[2 * index].wait_recv()
            copy.start()

    def close(self):
        for index, copy in enumerate(self.second):
            self.first[2 * index].wait_send()
            self.first[2 * index + 1].wait()
            copy.wait()


def scene_body(
    frames, half, span, n_share, meta, pack_ref, *refs
):
    heads = pack_ref.shape[0]
    pairs = [(refs[2 * index], refs[2 * index + 1]) for index in range(n_share)]
    refs = refs[2 * n_share :]
    att_ref, kept_ref, out_ref, log_ref = refs[:4]
    outs, refs = refs[4 : 4 + n_share], refs[4 + n_share :]
    queries, keys, values, sent, a_send, a_recv, b_send, b_recv, s_send, s_recv, own_sem = refs
    n = queries.shape[0] // 2
    m = keys.shape[0] // 2
    scene = lax.axis_index("scene")
    frame = lax.axis_index("frame")
    part = frame // heads
    own = pltpu.make_async_copy(pack_ref.at[lax.rem(frame, heads)], kept_ref.at[frame], own_sem)
    own.start()
    share = Share(frames, pairs, outs, s_send, s_recv)
    enter_scene(frames)

    def to_head(offset):
        target = lax.rem(frame + offset, frames)
        return remote(
            pack_ref.at[lax.rem(target, heads)], kept_ref.at[frame], a_send.at[offset], a_recv.at[offset], (scene, target)
        )

    @pl.loop(1, frames)
    def _(offset):
        to_head(offset).start()

    share.start()
    own.wait()

    @pl.loop(1, frames)
    def _(offset):
        to_head(offset).wait_recv()

    first = pl.multiple_of(part * heads, heads)
    q = packed_part(kept_ref[pl.ds(first, heads)], 0, half)
    low_n, low_m = first_lanes(n), first_lanes(m)
    queries[:n, :] = jnp.where(low_n, q, 0.0).astype(bf16)
    queries[n:, :] = jnp.where(low_n, turn(q), 0.0).astype(bf16)
    k = packed_part(kept_ref[...], 1, half)
    keys[:m, :] = k.astype(bf16)
    keys[m:, :] = turn(k).astype(bf16)
    v = packed_part(kept_ref[...], 2, half)
    open_low, open_high = open_slots(kept_ref[...], half)
    values[:m, :] = jnp.where(open_low, jnp.where(low_m, v, 1.0), 0.0).astype(bf16)
    values[m:, :] = jnp.where(open_high, jnp.where(low_m, turn(v), 1.0), 0.0).astype(bf16)
    low = first_lanes(LANES)

    @pl.loop(0, n // LANES)
    def _(piece):
        at = pl.multiple_of(piece * LANES, LANES)
        some = jnp.concatenate([queries[pl.ds(at, LANES), :], queries[pl.ds(n + at, LANES), :]], axis=0)
        total = jnp.zeros((2 * LANES, LANES), f32)
        for start in range(0, 2 * m, span):
            power = jnp.exp(nt(some, keys[start : start + span, :])).astype(bf16)
            total = total + nn(power, values[start : start + span, :])
        first, second = total[:LANES], total[LANES:]
        bottom = jnp.where(low, turn(first), second)
        result = jnp.where(low, first, turn(second)) / bottom
        out_ref[pl.ds(at, LANES), :] = result
        log_ref[pl.ds(at, LANES), :] = jnp.log(bottom)

    share.relay()
    sent[...] = out_ref[...].reshape(heads, half, LANES).astype(bf16)
    place = lax.rem(frame, heads)

    def from_head(offset):
        target = lax.rem(place + offset, heads)
        return remote(
            sent.at[target], att_ref.at[place], b_send.at[offset], b_recv.at[offset], (scene, part * heads + target)
        )

    @pl.loop(1, heads)
    def _(offset):
        from_head(offset).start()

    att_ref[place] = sent[place]

    @pl.loop(1, frames)
    def _(offset):
        to_head(offset).wait_send()

    @pl.loop(1, heads)
    def _(offset):
        from_head(offset).wait()

    share.close()


any_space = pl.BlockSpec(memory_space=pl.ANY)
vmem_space = pl.BlockSpec(memory_space=pltpu.VMEM)
dma = pltpu.SemaphoreType.DMA


def scene_forward(frames, meta, pack, half, pairs):
    heads = pack.shape[0]
    n = heads * half
    m = frames * half
    span = m // 2
    while span > 640:
        span = span // 2
    flat = [value for pair in pairs for value in pair]
    results = pl.pallas_call(
        partial(scene_body, frames, half, span, len(pairs)),
        name="scene_forward",
        out_shape=[
            sds((heads, half, LANES), bf16),
            sds((frames,) + pack.shape[1:], bf16),
            sds((n, LANES), f32),
            sds((n, LANES), f32),
        ]
        + [sds((3,) + own.shape, bf16) for own, _ in pairs],
        grid_spec=pltpu.PrefetchScalarGridSpec(
            num_scalar_prefetch=1,
            grid=(1,),
            in_specs=[vmem_space] + [any_space] * len(flat),
            out_specs=[vmem_space] * 4 + [any_space] * len(pairs),
            scratch_shapes=[
                pltpu.VMEM((2 * n, LANES), bf16),
                pltpu.VMEM((2 * m, LANES), bf16),
                pltpu.VMEM((2 * m, LANES), bf16),
                pltpu.VMEM((heads, half, LANES), bf16),
                dma((frames,)),
                dma((frames,)),
                dma((heads,)),
                dma((heads,)),
                dma((3 * len(pairs),)),
                dma((3 * len(pairs),)),
                dma(()),
            ],
        ),
        compiler_params=pltpu.CompilerParams(collective_id=1, has_side_effects=True),
        cost_estimate=pl.CostEstimate(flops=16 * n * m * LANES, bytes_accessed=20 * n * LANES, transcendentals=0),
    )(meta, pack, *flat)
    return results[0], results[1], results[2], results[3], results[4:]


def three_lanes(value, closed):
    lane = lax.broadcasted_iota(jnp.int32, value.shape, 1)
    base = LANES // 2
    high = value.astype(bf16).astype(f32)
    rest = value - high
    middle = rest.astype(bf16).astype(f32)
    last = rest - middle
    result = jnp.where(lane == base, high, jnp.where(lane == base + 1, middle, last))
    return jnp.where(lane < base + 3, result, jnp.where(lane == base + 3, closed, 0.0))


def scene_back_body(frames, half, span, n_share, meta, kept_ref, grad_ref, out_ref, log_ref, *refs):
    heads = grad_ref.shape[0]
    pairs = [(refs[2 * index], refs[2 * index + 1]) for index in range(n_share)]
    refs = refs[2 * n_share :]
    back_ref, outs, refs = refs[0], refs[1 : 1 + n_share], refs[1 + n_share :]
    queries, keys, values, grads, turned, came, dk_ref, dv_ref, sent_q, sent_kv = refs[:10]
    a_send, a_recv, b_send, b_recv, c_send, c_recv, s_send, s_recv = refs[10:]
    n = queries.shape[0] // 2
    m = keys.shape[0] // 2
    scene = lax.axis_index("scene")
    frame = lax.axis_index("frame")
    part = frame // heads
    place = lax.rem(frame, heads)
    share = Share(frames, pairs, outs, s_send, s_recv)
    enter_scene(frames)

    def to_head(offset):
        target = lax.rem(place + offset, heads)
        return remote(
            grad_ref.at[target], came.at[place], a_send.at[offset], a_recv.at[offset], (scene, part * heads + target)
        )

    @pl.loop(1, heads)
    def _(offset):
        to_head(offset).start()

    share.start()
    came[place] = grad_ref[place]
    first = pl.multiple_of(part * heads, heads)
    low_n, low_m = first_lanes(n), first_lanes(m)
    base = LANES // 2
    q = packed_part(kept_ref[pl.ds(first, heads)], 0, half)
    log = -log_ref[...]
    queries[:n, :] = jnp.where(low_n, q, three_lanes(turn(log), closed_score)).astype(bf16)
    queries[n:, :] = jnp.where(low_n, turn(q), three_lanes(log, closed_score)).astype(bf16)
    lane = lax.broadcasted_iota(jnp.int32, (m, LANES), 1)
    ones = jnp.where(lane < base + 3, 1.0, 0.0)
    open_low, open_high = open_slots(kept_ref[...], half)
    k = packed_part(kept_ref[...], 1, half)
    for place_at, k_now, is_open in ((0, k, open_low), (m, turn(k), open_high)):
        tail = jnp.where((lane == base + 3) & jnp.logical_not(is_open), 1.0, ones)
        keys[place_at : place_at + m, :] = jnp.where(low_m, k_now, tail).astype(bf16)
    v = packed_part(kept_ref[...], 2, half)
    values[:m, :] = jnp.where(low_m, v, ones).astype(bf16)
    values[m:, :] = jnp.where(low_m, turn(v), ones).astype(bf16)
    turned[...] = jnp.zeros_like(turned)
    low = first_lanes(LANES)

    @pl.loop(1, heads)
    def _(offset):
        to_head(offset).wait_recv()

    g = came[...].astype(f32).reshape(n, LANES)
    delta = -seg_dot(g * out_ref[...], seg_matrix(LANES, base, 1.0))
    grads[:n, :] = jnp.where(low_n, g, three_lanes(turn(delta), 0.0)).astype(bf16)
    grads[n:, :] = jnp.where(low_n, turn(g), three_lanes(delta, 0.0)).astype(bf16)

    @pl.loop(0, m // LANES)
    def _(piece):
        at = pl.multiple_of(piece * LANES, LANES)
        key_part = jnp.concatenate([keys[pl.ds(at, LANES), :], keys[pl.ds(m + at, LANES), :]], axis=0)
        value_part = jnp.concatenate(
            [values[pl.ds(at, LANES), :], values[pl.ds(m + at, LANES), :]], axis=0
        )
        key_turned = jnp.transpose(key_part.astype(f32)).astype(bf16)
        dk = jnp.zeros((2 * LANES, LANES), f32)
        dv = jnp.zeros((2 * LANES, LANES), f32)
        for start in range(0, 2 * n, span):
            some = queries[start : start + span, :]
            some_grads = grads[start : start + span, :]
            probs = jnp.exp(nt(key_part, some))
            grad_scores = (probs * nt(value_part, some_grads)).astype(bf16)
            dv = dv + nn(probs.astype(bf16), some_grads)
            dk = dk + nn(grad_scores, some)
            turned[:, start : start + span] += nn(key_turned, grad_scores)
        dk_ref[pl.ds(at, LANES), :] = jnp.where(low, dk[:LANES], turn(dk[LANES:]))
        dv_ref[pl.ds(at, LANES), :] = jnp.where(low, dv[:LANES], turn(dv[LANES:]))

    share.relay()
    sent_kv[:, 0] = dk_ref[...].reshape(frames, half, LANES).astype(bf16)
    sent_kv[:, 1] = dv_ref[...].reshape(frames, half, LANES).astype(bf16)

    def back_kv(offset):
        target = lax.rem(frame + offset, frames)
        return remote(
            sent_kv.at[target], back_ref.at[frame, pl.ds(1, 2)], b_send.at[offset], b_recv.at[offset], (scene, target)
        )

    @pl.loop(1, frames)
    def _(offset):
        back_kv(offset).start()

    scale = base ** (-0.5)
    rows = []
    for at in range(0, n, LANES):
        first = jnp.transpose(turned[:, at : at + LANES])
        second = jnp.transpose(turned[:, n + at : n + at + LANES])
        rows.append(jnp.where(low, first, turn(second)) * scale)
    sent_q[...] = jnp.concatenate(rows, axis=0).reshape(heads, half, LANES).astype(bf16)

    def back_q(offset):
        target = lax.rem(place + offset, heads)
        return remote(
            sent_q.at[target], back_ref.at[frame, 0], c_send.at[offset], c_recv.at[offset], (scene, part * heads + target)
        )

    back_ref[frame, 1] = sent_kv[frame, 0]
    back_ref[frame, 2] = sent_kv[frame, 1]

    @pl.loop(1, heads)
    def _(offset):
        back_q(offset).start()

    back_ref[frame, 0] = sent_q[place]

    @pl.loop(1, heads)
    def _(offset):
        to_head(offset).wait_send()

    @pl.loop(1, frames)
    def _(offset):
        back_kv(offset).wait()

    @pl.loop(1, heads)
    def _(offset):
        back_q(offset).wait()

    share.close()


def scene_backward(frames, meta, kept, grad, out, log, half, pairs):
    heads = grad.shape[0]
    n = heads * half
    m = frames * half
    span = n // 2
    while span > 640:
        span = span // 2
    flat = [value for pair in pairs for value in pair]
    results = pl.pallas_call(
        partial(scene_back_body, frames, half, span, len(pairs)),
        name="scene_backward",
        out_shape=[sds((frames, 3, half, LANES), bf16)] + [sds((3,) + own.shape, bf16) for own, _ in pairs],
        grid_spec=pltpu.PrefetchScalarGridSpec(
            num_scalar_prefetch=1,
            grid=(1,),
            in_specs=[vmem_space] * 4 + [any_space] * len(flat),
            out_specs=[vmem_space] + [any_space] * len(pairs),
            scratch_shapes=[
                pltpu.VMEM((2 * n, LANES), bf16),
                pltpu.VMEM((2 * m, LANES), bf16),
                pltpu.VMEM((2 * m, LANES), bf16),
                pltpu.VMEM((2 * n, LANES), bf16),
                pltpu.VMEM((LANES, 2 * n), f32),
                pltpu.VMEM((heads, half, LANES), bf16),
                pltpu.VMEM((m, LANES), f32),
                pltpu.VMEM((m, LANES), f32),
                pltpu.VMEM((heads, half, LANES), bf16),
                pltpu.VMEM((frames, 2, half, LANES), bf16),
                dma((heads,)),
                dma((heads,)),
                dma((frames,)),
                dma((frames,)),
                dma((heads,)),
                dma((heads,)),
                dma((3 * len(pairs),)),
                dma((3 * len(pairs),)),
            ],
        ),
        compiler_params=pltpu.CompilerParams(collective_id=2, has_side_effects=True),
        cost_estimate=pl.CostEstimate(flops=40 * n * m * LANES, bytes_accessed=30 * n * LANES, transcendentals=0),
    )(meta, kept, grad, out, log, *flat)
    back = results[0]
    if frames > heads:
        place = lax.axis_index("frame") // heads * heads
        dq = lax.dynamic_slice(back, (place, 0, 0, 0), (heads, 1, half, LANES))
        both = back.reshape(frames // heads, heads, 3, half, LANES)[:, :, 1:].astype(f32).sum(0)
        back = jnp.concatenate([dq, both.astype(bf16)], axis=1)
    return back, results[1:]


def feed_body(
    block, packed, meta, att_ref, x_ref, mixer_ref, mixer_bias, mixer_scale, gain_ref, shift_ref,
    inner_ref, inner_bias, outer_ref, outer_bias, outer_scale,
    own_ref, other_ref, middle_ref, branch_ref, feed_ref, slope_ref, out_ref, normed_ref, total_ref
):
    step = pl.program_id(0)
    steps = pl.num_programs(0)
    rows, width = middle_ref.shape
    hidden_half = own_ref.shape[1] - width
    half_steps = hidden_half // CHUNK
    mine = meta[0]

    def split(value, at):
        first, second = value[:, : width // 2], value[:, width // 2 :]

        @pl.when(mine == 0)
        def _():
            own_ref[:, at : at + width // 2] = first
            other_ref[:, at : at + width // 2] = second

        @pl.when(mine != 0)
        def _():
            own_ref[:, at : at + width // 2] = second
            other_ref[:, at : at + width // 2] = first

    @pl.when(step == 0)
    def _():
        if packed:
            pieces = []
            for pair in range(width // LANES):
                pieces.append(
                    unpack_pair(att_ref[2 * pair].astype(f32), att_ref[2 * pair + 1].astype(f32))
                )
            attended = jnp.concatenate(pieces, axis=1).astype(bf16)
        else:
            attended = att_ref[...]
        branch = nn(attended, mixer_ref[0]) + row(mixer_bias, block)
        middle = x_ref[...].astype(f32) + row(mixer_scale, block) * branch
        hat, _ = center_norm(middle, norm_eps)
        normed = (hat * row(gain_ref, block) + row(shift_ref, block)).astype(bf16)
        branch_ref[...] = branch
        middle_ref[...] = middle
        normed_ref[...] = normed
        split(normed, hidden_half)
        split(attended, hidden_half + width // 2)
        total_ref[...] = jnp.zeros_like(total_ref)

    pre = nn(normed_ref[...], inner_ref[0]) + row(inner_bias, block)
    share = 0.5 * (1.0 + erf(pre * (2.0 ** (-0.5))))
    slope_ref[...] = share + pre * jnp.exp(-0.5 * pre * pre) * 0.3989422804014327
    hidden = (pre * share).astype(bf16)
    place = pl.multiple_of(lax.rem(step, half_steps) * CHUNK, CHUNK)

    @pl.when(step // half_steps == mine)
    def _():
        own_ref[:, pl.ds(place, CHUNK)] = hidden

    @pl.when(step // half_steps != mine)
    def _():
        other_ref[:, pl.ds(place, CHUNK)] = hidden

    total_ref[...] += nn(hidden, outer_ref[0])

    @pl.when(step == steps - 1)
    def _():
        feed = total_ref[...] + row(outer_bias, block)
        feed_ref[...] = feed
        result = middle_ref[...] + row(outer_scale, block) * feed
        if packed:
            place = lax.broadcasted_iota(jnp.int32, result.shape, 0)
            result = jnp.where(place < meta[3] + SPECIAL, result, 0.0)
        out_ref[...] = result.astype(out_ref.dtype)


def feed_forward(block, packed, meta, att, x, mixer, mixer_bias, mixer_scale, gain, shift, inner, inner_bias, outer, outer_bias, outer_scale):
    rows, width = x.shape
    hidden = inner.shape[2]
    kept = hidden // 2 + width
    steps = hidden // CHUNK
    vector = full(gain.shape)
    return call(
        partial(feed_body, block, packed),
        f"feed_forward_{block}",
        (steps,),
        [
            full(att.shape),
            full((rows, width)),
            pl.BlockSpec((1, width, width), lambda j, m: (block, 0, 0)),
            vector, vector, vector, vector,
            pl.BlockSpec((1, width, CHUNK), lambda j, m: (block, 0, j)),
            pl.BlockSpec((2, CHUNK), lambda j, m: (0, j)),
            pl.BlockSpec((1, CHUNK, width), lambda j, m: (block, j, 0)),
            vector, vector,
        ],
        [full((rows, kept))] * 2
        + [full((rows, width))] * 3
        + [pl.BlockSpec((rows, CHUNK), lambda j, m: (0, j)), full((rows, width))],
        [sds((rows, kept), bf16)] * 2
        + [sds((rows, width), f32)] * 3
        + [sds((rows, hidden), f32), sds((rows, width), bf16 if packed else f32)],
        [pltpu.VMEM((rows, width), bf16), pltpu.VMEM((rows, width), f32)],
        2 * rows * width * (2 * hidden + width),
        4 * width * hidden + 4 * rows * hidden + 30 * rows * width,
    )(meta, att, x, mixer, mixer_bias, mixer_scale, gain, shift, inner, inner_bias, outer, outer_bias, outer_scale)


def feed_back_body(
    block, packed, meta, g_ref, feed_ref, slope_ref, middle_ref, branch_ref,
    outer_scale, gain_ref, mixer_scale, outer_ref, inner_ref, mixer_ref,
    grads_ref, g_middle_ref, g_att_ref, vector_ref, g_feed_ref, total_ref, *kept
):
    step = pl.program_id(0)
    steps = pl.num_programs(0)
    rows, width = middle_ref.shape
    half_steps = steps // 2

    def incoming():
        g = g_ref[...].astype(f32)
        if packed:
            place = lax.broadcasted_iota(jnp.int32, g.shape, 0)
            g = jnp.where(place < meta[3] + SPECIAL, g, 0.0)
        return g

    @pl.when(step == 0)
    def _():
        g = incoming()
        g_feed = (g * row(outer_scale, block)).astype(bf16)
        g_feed_ref[...] = g_feed
        grads_ref[0, :, : width // 2] = g_feed[:, : width // 2]
        grads_ref[1, :, : width // 2] = g_feed[:, width // 2 :]
        vector_ref[0:1, :] = col_sum(g * feed_ref[...])
        vector_ref[1:2, :] = col_sum(g_feed.astype(f32))
        total_ref[...] = jnp.zeros_like(total_ref)

    g_pre = (nt(g_feed_ref[...], outer_ref[0]) * slope_ref[...]).astype(bf16)
    grads_ref[step // half_steps, :, pl.ds(pl.multiple_of(width + lax.rem(step, half_steps) * CHUNK, CHUNK), CHUNK)] = g_pre
    per_row = width // CHUNK
    vector_ref[pl.ds(6 + step // per_row, 1), pl.ds(pl.multiple_of(lax.rem(step, per_row) * CHUNK, CHUNK), CHUNK)] = col_sum(g_pre.astype(f32))
    total_ref[...] += nt(g_pre, inner_ref[0])

    @pl.when(step == steps - 1)
    def _():
        hat, spread = center_norm(middle_ref[...], norm_eps)
        g_nm = total_ref[...]
        vector_ref[2:3, :] = col_sum(g_nm * hat)
        vector_ref[3:4, :] = col_sum(g_nm)
        g_middle = incoming() + norm_back(g_nm * row(gain_ref, block), hat, spread)
        g_middle_ref[...] = g_middle
        vector_ref[4:5, :] = col_sum(g_middle * branch_ref[...])
        g_branch = (g_middle * row(mixer_scale, block)).astype(bf16)
        vector_ref[5:6, :] = col_sum(g_branch.astype(f32))
        grads_ref[0, :, width // 2 : width] = g_branch[:, : width // 2]
        grads_ref[1, :, width // 2 : width] = g_branch[:, width // 2 :]
        g_att = nt(g_branch, mixer_ref[0])
        if packed:
            for pair in range(width // LANES):
                even, odd = pack_pair(g_att[:, pair * LANES : (pair + 1) * LANES])
                g_att_ref[2 * pair] = even.astype(bf16)
                g_att_ref[2 * pair + 1] = odd.astype(bf16)
        else:
            g_att_ref[...] = g_att.astype(bf16)


def feed_backward(block, packed, heads, meta, g, feed, slope, middle, branch, outer_scale, gain, mixer_scale, outer, inner, mixer):
    rows, width = middle.shape
    hidden = inner.shape[2]
    steps = hidden // CHUNK
    vector = full(gain.shape)
    vector_rows = 6 + hidden // width
    att_shape = (heads, rows // 2, LANES) if packed else (rows, width)
    return call(
        partial(feed_back_body, block, packed),
        f"feed_backward_{block}",
        (steps,),
        [
            full((rows, width)),
            full((rows, width)),
            pl.BlockSpec((rows, CHUNK), lambda j, m: (0, j)),
            full((rows, width)),
            full((rows, width)),
            vector, vector, vector,
            pl.BlockSpec((1, CHUNK, width), lambda j, m: (block, j, 0)),
            pl.BlockSpec((1, width, CHUNK), lambda j, m: (block, 0, j)),
            pl.BlockSpec((1, width, width), lambda j, m: (block, 0, 0)),
        ],
        [
            full((2, rows, width + hidden // 2)),
            full((rows, width)),
            full(att_shape),
            full((vector_rows, width)),
        ],
        [
            sds((2, rows, width + hidden // 2), bf16),
            sds((rows, width), f32),
            sds(att_shape, bf16),
            sds((vector_rows, width), f32),
        ],
        [pltpu.VMEM((rows, width), bf16), pltpu.VMEM((rows, width), f32)],
        2 * rows * width * (2 * hidden + width),
        4 * width * hidden + 8 * rows * hidden + 20 * rows * width,
    )(meta, g, feed, slope, middle, branch, outer_scale, gain, mixer_scale, outer, inner, mixer)


def joint_back_body(
    block, packed, head, meta, g_ref, pre_ref, x_ref, g_middle_ref, gain_ref, pattern_ref, w_ref,
    grads_ref, out_ref, vector_ref, total_ref
):
    step = pl.program_id(0)
    steps = pl.num_programs(0)
    rows, width = total_ref.shape
    per_part = width // CHUNK
    half_steps = steps // 2

    @pl.when(step == 0)
    def _():
        total_ref[...] = jnp.zeros_like(total_ref)
        vector_ref[...] = jnp.zeros_like(vector_ref)

    if packed:
        pieces = []
        for pair in range(CHUNK // LANES):
            pieces.append(
                unpack_pair(g_ref[2 * pair, 0].astype(f32), g_ref[2 * pair + 1, 0].astype(f32))
            )
        g = jnp.concatenate(pieces, axis=1)
    else:
        g = g_ref[...]
    pattern = pattern_ref[...]

    def finish(g_joined):
        rounded = g_joined.astype(bf16)
        grads_ref[step // half_steps, :, pl.ds(pl.multiple_of(lax.rem(step, half_steps) * CHUNK, CHUNK), CHUNK)] = rounded
        vector_ref[pl.ds(2 + step // per_part, 1), pl.ds(pl.multiple_of(lax.rem(step, per_part) * CHUNK, CHUNK), CHUNK)] = col_sum(rounded.astype(f32))
        total_ref[...] += nt(rounded, w_ref[0])

    def head_back(gain, gain_row, shift_row):
        mean_matrix = seg_matrix(SLAB, head, 1.0 / head)
        pieces = []
        for slab in range(CHUNK // SLAB):
            at = slab * SLAB
            g_now = g[:, at : at + SLAB]
            hat, spread = seg_norm(pre_ref[:, at : at + SLAB], mean_matrix)
            vector_ref[gain_row : gain_row + 1, at : at + SLAB] += col_sum(g_now * hat)
            if shift_row is not None:
                vector_ref[shift_row : shift_row + 1, at : at + SLAB] += col_sum(g_now)
            grad_hat = g_now * gain
            pieces.append(
                spread
                * (
                    grad_hat
                    - seg_dot(grad_hat, mean_matrix)
                    - hat * seg_dot(grad_hat * hat, mean_matrix)
                )
            )
        finish(jnp.concatenate(pieces, axis=1))

    @pl.when(step < per_part)
    def _():
        head_back(pattern[3 * block : 3 * block + 1], 5, 6)

    @pl.when((step >= per_part) & (step < 2 * per_part))
    def _():
        head_back(pattern[3 * block + 2 : 3 * block + 3], 7, None)

    @pl.when(step >= 2 * per_part)
    def _():
        finish(g)

    @pl.when(step == steps - 1)
    def _():
        hat, spread = center_norm(x_ref[...].astype(f32), norm_eps)
        g_normed = total_ref[...]
        vector_ref[0:1, :] = col_sum(g_normed * hat)
        vector_ref[1:2, :] = col_sum(g_normed)
        result = g_middle_ref[...] + norm_back(g_normed * row(gain_ref, block), hat, spread)
        out_ref[...] = result.astype(out_ref.dtype)


def joint_backward(block, packed, head, meta, g, pre, x, g_middle, gain, pattern, weight):
    rows, width = x.shape
    per_part = width // CHUNK
    if packed:
        g_spec = pl.BlockSpec(
            (CHUNK // head, 1, rows // 2, LANES),
            lambda j, m: (lax.rem(j, per_part), j // per_part, 0, 0),
        )
    else:
        g_spec = pl.BlockSpec((rows, CHUNK), lambda j, m: (0, j))
    return call(
        partial(joint_back_body, block, packed, head),
        f"joint_backward_{block}",
        (3 * per_part,),
        [
            g_spec,
            pl.BlockSpec((rows, CHUNK), lambda j, m: (0, jnp.minimum(j, 2 * per_part - 1))),
            full((rows, width)),
            full((rows, width)),
            full(gain.shape),
            full(pattern.shape),
            pl.BlockSpec((1, width, CHUNK), lambda j, m: (block, 0, j)),
        ],
        [full((2, rows, 3 * width // 2)), full((rows, width)), full((8, width))],
        [
            sds((2, rows, 3 * width // 2), bf16),
            sds((rows, width), f32 if packed else bf16),
            sds((8, width), f32),
        ],
        [pltpu.VMEM((rows, width), f32)],
        2 * rows * width * 3 * width,
        6 * width * width + 30 * rows * width,
    )(meta, g, pre, x, g_middle, gain, pattern, weight)


def collect_body(frames, blocks, hidden_half, width, meta, *refs):
    count = 2 + 4
    inputs, refs = refs[: blocks * count], refs[blocks * count :]
    vector_in, refs = refs[0], refs[1:]
    out_ref, vector_out, refs = refs[0], refs[1], refs[2:]
    own, came, acts, hids, parts, last, sums, refs = (
        refs[0], refs[1], refs[2], refs[3], refs[4], refs[5], refs[6], refs[7:]
    )
    stages = len(refs) - 9
    steps, refs = refs[:stages], refs[stages:]
    load_sem, g_send, g_recv, p_send, p_recv, f_send, f_recv, v_send, v_recv = refs
    rows = own.shape[2]
    chips = frames // 2
    n_outer = 4
    n_inner = hidden_half // CHUNK
    n_joint = 3 * (width // 2) // CHUNK
    per_block = n_outer + n_inner + 1 + n_joint
    n_pieces = 1 + n_inner + 1 + n_joint
    total = blocks * per_block
    half = width // 2
    core, core_peer, scene_peer, cross_peer, bits = peers_of(frames)

    loads = []

    def load(source, target):
        copy = pltpu.make_async_copy(source, target, load_sem.at[len(loads)])
        copy.start()
        loads.append(copy)

    for block in range(blocks):
        feed_g, joint_g = inputs[block * count], inputs[block * count + 1]
        pre_lanes = hidden_half
        load(feed_g.at[:, :, pl.ds(0, half)], own.at[block, :, :, pl.ds(0, half)])
        load(feed_g.at[:, :, pl.ds(width, pre_lanes)], own.at[block, :, :, pl.ds(half, pre_lanes)])
        load(feed_g.at[:, :, pl.ds(half, half)], own.at[block, :, :, pl.ds(half + pre_lanes, half)])
        load(joint_g, own.at[block, :, :, pl.ds(width + pre_lanes, 3 * half)])
    first_loads = len(loads)
    for block in range(blocks):
        for place in range(4):
            feed_x, joint_x = inputs[block * count + 2], inputs[block * count + 4]
            if place:
                feed_x = inputs[block * count + 3].at[place - 1]
                joint_x = inputs[block * count + 5].at[place - 1]
            load(feed_x.at[:, pl.ds(0, hidden_half)], hids.at[block, place])
            load(feed_x.at[:, pl.ds(hidden_half, width)], acts.at[block, place, :, pl.ds(0, width)])
            load(joint_x, acts.at[block, place, :, pl.ds(width, half)])

    enter([core_peer, scene_peer, cross_peer] + [peer for _, peer in bits])
    for copy in loads[:first_loads]:
        copy.wait()

    def piece_copy(block, piece, which):
        lanes = pl.ds(pl.multiple_of(piece * CHUNK, CHUNK), CHUNK)
        target = (scene_peer, core_peer, cross_peer)[which]
        side = core if which == 0 else 1 - core
        return pltpu.make_async_remote_copy(
            src_ref=own.at[block, side, :, lanes],
            dst_ref=came.at[block, which, :, lanes],
            send_sem=g_send.at[block, which, piece],
            recv_sem=g_recv.at[block, which, piece],
            device_id=target,
            device_id_type=MESH,
        )

    ahead = 3

    def start_pieces(index):
        block = index // per_block
        unit = lax.rem(index, per_block)

        @pl.when((index < total) & ((unit == 0) | (unit >= n_outer)))
        def _():
            piece = jnp.where(unit == 0, 0, unit - (n_outer - 1))
            for which in range(3):
                piece_copy(block, piece, which).start()

    @pl.loop(0, ahead)
    def _(index):
        start_pieces(index)

    for copy in loads[first_loads:]:
        copy.wait()

    vector_peers = [core_peer, scene_peer] + [peer for _, peer in bits]
    sums[0] = vector_in[...]

    def vector_copy(stage):
        return pltpu.make_async_remote_copy(
            src_ref=sums.at[2 * stage],
            dst_ref=sums.at[2 * stage + 1],
            send_sem=v_send.at[stage],
            recv_sem=v_recv.at[stage],
            device_id=vector_peers[stage],
            device_id_type=MESH,
        )

    def vector_step(stage):
        vector_copy(stage).wait()
        result = sums[2 * stage] + sums[2 * stage + 1]
        if stage + 1 < len(vector_peers):
            sums[2 * stage + 2] = result
        else:
            vector_out[...] = result

    def stage_pieces(stage, index):
        value, peer = bits[stage]
        source = parts if stage == 0 else steps[stage - 1]
        for pair in range(chips >> (stage + 1)):
            yield pltpu.make_async_remote_copy(
                src_ref=source.at[index, 2 * pair + 1 - value],
                dst_ref=steps[stage].at[index, pair],
                send_sem=p_send.at[stage, index],
                recv_sem=p_recv.at[stage, index],
                device_id=peer,
                device_id_type=MESH,
            )

    def stage_start(stage, index):
        for copy in stage_pieces(stage, index):
            copy.start()

    def stage_whole(stage, index):
        return pltpu.make_async_remote_copy(
            src_ref=steps[stage].at[index],
            dst_ref=steps[stage].at[index],
            send_sem=p_send.at[stage, index],
            recv_sem=p_recv.at[stage, index],
            device_id=bits[stage][1],
            device_id_type=MESH,
        )

    def last_copy(index):
        return pltpu.make_async_remote_copy(
            src_ref=steps[stages - 1].at[index, 0, 1 - core],
            dst_ref=last.at[index],
            send_sem=f_send.at[index],
            recv_sem=f_recv.at[index],
            device_id=core_peer,
            device_id_type=MESH,
        )

    def multiply(index):
        block = index // per_block
        unit = lax.rem(index, per_block)

        def wait_piece(piece):
            for which in range(3):
                piece_copy(block, piece, which).wait_recv()

        def gathered(lanes):
            return jnp.concatenate(
                [own[block, core, :, lanes]] + [came[block, which, :, lanes] for which in range(3)], axis=0
            )

        @pl.when(unit < n_outer)
        def _():
            @pl.when(unit == 0)
            def _():
                wait_piece(0)

            left = jnp.concatenate([hids[block, place] for place in range(4)], axis=0)
            right = gathered(pl.ds(pl.multiple_of(unit * LANES, LANES), LANES))
            value = tn(left, right)
            deep = hidden_half // chips // 8
            value = value.reshape(chips, 2, 4, deep, LANES)
            value = jnp.concatenate([value[:, :, turn] for turn in range(4)], axis=-1)
            parts[index] = value.astype(bf16)

        @pl.when(unit >= n_outer)
        def _():
            piece = unit - (n_outer - 1)
            wait_piece(piece)
            place = jnp.where(unit >= n_outer + n_inner, 1, 0) + jnp.where(unit >= n_outer + n_inner + 1, 1, 0)
            lanes = pl.ds(pl.multiple_of(place * half, half), half)
            left = jnp.concatenate([acts[block, source, :, lanes] for source in range(4)], axis=0)
            value = tn(left, gathered(pl.ds(pl.multiple_of(piece * CHUNK, CHUNK), CHUNK)))
            parts[index] = value.reshape(chips, 2, half // chips // 2, CHUNK).astype(bf16)

    def add(stage, index):
        stage_whole(stage, index).wait_recv()
        value = bits[stage][0]
        source = parts if stage == 0 else steps[stage - 1]
        for pair in range(chips >> (stage + 1)):
            held = source[index, 2 * pair + value].astype(f32) + steps[stage][index, pair].astype(f32)
            if stage + 1 == stages:
                out_ref[index, core] = jnp.where(core == 0, held[0], held[1])
            steps[stage][index, pair] = held.astype(bf16)

    def close(index):
        last_copy(index).wait_recv()
        out_ref[index, 1 - core] = last[index].astype(f32)

    n_vector = len(vector_peers)
    vector_copy(0).start()
    lags = [2 + 2 * stage for stage in range(stages)]
    ends = lags[-1] + 2

    @pl.loop(0, total + ends)
    def _(turn_at):
        @pl.when(turn_at < total)
        def _():
            multiply(turn_at)

        for stage in range(stages):
            index = turn_at - lags[stage]

            @pl.when((index >= 0) & (index < total))
            def _():
                add(stage, index)

        for stage in range(n_vector):

            @pl.when(turn_at == 2 * stage + 1)
            def _():
                vector_step(stage)

        index_last = turn_at - ends

        @pl.when((index_last >= 0) & (index_last < total))
        def _():
            close(index_last)

        for stage in range(stages):
            index = turn_at - lags[stage]

            @pl.when((index >= 0) & (index < total))
            def _():
                if stage + 1 < stages:
                    stage_start(stage + 1, index)
                else:
                    last_copy(index).start()

        for stage in range(1, n_vector):

            @pl.when(turn_at == 2 * stage - 1)
            def _():
                vector_copy(stage).start()

        @pl.when(turn_at < total)
        def _():
            stage_start(0, turn_at)

        start_pieces(turn_at + ahead)

    @pl.loop(0, total)
    def _(index):
        for stage in range(stages):
            stage_whole(stage, index).wait_send()
        last_copy(index).wait_send()

    for block in range(blocks):

        @pl.loop(0, n_pieces)
        def _(piece):
            for which in range(3):
                piece_copy(block, piece, which).wait_send()


def collect(frames, meta, groups, vector):
    blocks = len(groups)
    flat = []
    for group in groups:
        flat += group
    rows = flat[0].shape[1]
    half = flat[1].shape[2] // 3
    width = 2 * half
    hidden_half = flat[0].shape[2] - width
    chips = frames // 2
    stages = chips.bit_length() - 1
    n_inner = hidden_half // CHUNK
    n_joint = 3 * half // CHUNK
    per_block = 4 + n_inner + 1 + n_joint
    n_pieces = 2 + n_inner + n_joint
    total = blocks * per_block
    deep = half // chips // 2
    n_vector = 2 + stages
    moved = 12 * total * chips * deep * CHUNK
    return pl.pallas_call(
        partial(collect_body, frames, blocks, hidden_half, width),
        name="collect",
        out_shape=[sds((total, 2, deep, CHUNK), f32), sds(vector.shape, f32)],
        grid_spec=pltpu.PrefetchScalarGridSpec(
            num_scalar_prefetch=1,
            grid=(1,),
            in_specs=[any_space] * len(flat) + [full(vector.shape)],
            out_specs=[full((total, 2, deep, CHUNK)), full(vector.shape)],
            scratch_shapes=[
                pltpu.VMEM((blocks, 2, rows, n_pieces * CHUNK), bf16),
                pltpu.VMEM((blocks, 3, rows, n_pieces * CHUNK), bf16),
                pltpu.VMEM((blocks, 4, rows, 3 * half), bf16),
                pltpu.VMEM((blocks, 4, rows, hidden_half), bf16),
                pltpu.VMEM((total, chips, 2, deep, CHUNK), bf16),
                pltpu.VMEM((total, deep, CHUNK), bf16),
                pltpu.VMEM((2 * n_vector,) + vector.shape, f32),
            ]
            + [pltpu.VMEM((total, chips >> (stage + 1), 2, deep, CHUNK), bf16) for stage in range(stages)]
            + [
                dma((blocks * 16,)),
                dma((blocks, 3, n_pieces)),
                dma((blocks, 3, n_pieces)),
                dma((stages, total)),
                dma((stages, total)),
                dma((total,)),
                dma((total,)),
                dma((n_vector,)),
                dma((n_vector,)),
            ],
        ),
        compiler_params=pltpu.CompilerParams(
            collective_id=0, has_side_effects=True, vmem_limit_bytes=64 * 1024 * 1024 - 65536
        ),
        cost_estimate=pl.CostEstimate(flops=2 * 4 * rows * total * chips * 2 * deep * CHUNK, bytes_accessed=moved, transcendentals=0),
    )(meta, *flat, vector)


def local(scenes, frames, tokens, patch_counts, first_gain, first_shift, joint_weight, joint_bias, query_gain, query_shift, key_gain, mixer_weight, mixer_bias, mixer_scale, second_gain, second_shift, inner_weight, inner_bias, outer_weight, outer_bias, outer_scale, cotangent):
    rows, width = tokens.shape[1:]
    half = rows // 2
    head = query_gain.shape[1]
    heads = width // head
    hidden = inner_weight.shape[2]
    chips = frames // 2
    scene = lax.axis_index("scene")
    frame = lax.axis_index("frame")
    core = lax.rem(frame, 2)
    meta = jnp.stack([scene, core, lax.rem(frame // 2, 2), patch_counts[0, 0]]).astype(jnp.int32)
    pattern = jnp.tile(
        jnp.stack([vector[block] for block in range(2) for vector in (query_gain, query_shift, key_gain)]).astype(f32),
        (1, SLAB // head),
    )

    x0 = tokens[0]
    feed_params = (mixer_weight, mixer_bias, mixer_scale, second_gain, second_shift, inner_weight, inner_bias, outer_weight, outer_bias, outer_scale)
    back_params = (outer_scale, second_gain, mixer_scale, outer_weight, inner_weight, mixer_weight)

    own0, other0, pre0, qkv0 = joint_forward(0, False, head, meta, x0, first_gain, first_shift, pattern, joint_weight, joint_bias)
    att0 = frame_forward(meta, qkv0)
    own_feed0, other_feed0, middle0, branch0, feed0, slope0, x1 = feed_forward(0, False, meta, att0, x0, *feed_params)
    own1, other1, pre1, pack1 = joint_forward(1, True, head, meta, x1, first_gain, first_shift, pattern, joint_weight, joint_bias)
    att1, kept1, att_full, att_log, (left_joint0, left_feed0, left_joint1) = scene_forward(
        frames, meta, pack1, half, [(own0, other0), (own_feed0, other_feed0), (own1, other1)]
    )
    own_feed1, other_feed1, middle1, branch1, feed1, slope1, layer_out = feed_forward(1, True, meta, att1, x1, *feed_params)

    g_feed1, g_middle1, g_att1, vector_feed1 = feed_backward(1, True, heads, meta, cotangent[0], feed1, slope1, middle1, branch1, *back_params)
    g_qkv1, (left_feed1,) = scene_backward(frames, meta, kept1, g_att1, att_full, att_log, half, [(own_feed1, other_feed1)])
    g_joint1, g1, vector_joint1 = joint_backward(1, True, head, meta, g_qkv1, pre1, x1, g_middle1, first_gain, pattern, joint_weight)

    g_feed0, g_middle0, g_att0, vector_feed0 = feed_backward(0, False, heads, meta, g1, feed0, slope0, middle0, branch0, *back_params)
    g_qkv0 = frame_backward(meta, qkv0, g_att0)
    g_joint0, g0, vector_joint0 = joint_backward(0, False, head, meta, g_qkv0, pre0, x0, g_middle0, first_gain, pattern, joint_weight)

    vectors = jnp.concatenate([vector_feed0, vector_joint0, vector_feed1, vector_joint1], axis=0)
    pieces, vectors = collect(
        frames,
        meta,
        [
            (g_feed1, g_joint1, own_feed1, left_feed1, own1, left_joint1),
            (g_feed0, g_joint0, own_feed0, left_feed0, own0, left_joint0),
        ],
        vectors,
    )
    pieces = pieces[:].reshape((2, -1) + pieces.shape[1:])[::-1]
    n_inner = hidden // 2 // CHUNK
    deep = pieces.shape[3]

    def laid_out(first, last):
        some = jnp.transpose(pieces[:, first:last], (0, 3, 2, 1, 4))
        return some.reshape(2, deep, -1)

    outer = pieces[:, :4].reshape(2, 4, 2, deep, 4, LANES)
    outer = jnp.transpose(outer, (0, 4, 3, 2, 1, 5)).reshape(2, 4 * deep, width)
    inner = laid_out(4, 4 + n_inner)
    mixer = laid_out(4 + n_inner, 5 + n_inner)
    joint = laid_out(5 + n_inner, pieces.shape[1])
    vectors = vectors.reshape(2, -1, width)
    at_joint = vector_feed0.shape[0]

    def folded(index):
        return vectors[:, at_joint + index].reshape(2, heads, head).sum(1)

    return (
        layer_out[None],
        g0[None],
        vectors[:, at_joint],
        vectors[:, at_joint + 1],
        joint,
        vectors[:, at_joint + 2 : at_joint + 5].reshape(2, 3 * width),
        folded(5),
        folded(6),
        folded(7),
        mixer,
        vectors[:, 5],
        vectors[:, 4],
        vectors[:, 2],
        vectors[:, 3],
        inner,
        vectors[:, 6:at_joint].reshape(2, hidden),
        outer,
        vectors[:, 1],
        vectors[:, 0],
    )


def solution(mesh):
    tokens_spec = P("scene", "frame", None)
    shard = P(None, ("scene", "frame"), None)
    in_specs = (tokens_spec, P("scene", "frame")) + (P(),) * 17 + (tokens_spec,)
    out_specs = (
        tokens_spec, tokens_spec, P(), P(), shard, P(), P(), P(), P(), shard,
        P(), P(), P(), P(), shard, P(), shard, P(), P(),
    )
    body = partial(local, mesh.shape["scene"], mesh.shape["frame"])
    return jax.shard_map(body, mesh=mesh, in_specs=in_specs, out_specs=out_specs, check_vma=False)
```

```python
from functools import partial

import jax
import jax.numpy as jnp
from jax import lax
from jax.experimental import pallas as pl
from jax.experimental.pallas import tpu as pltpu
from jax.sharding import PartitionSpec as P

SPECIAL = 5
CHUNK = 512
LANES = 128
SLAB = 256
SHARED_PIECES = 4
SWAP_EVERY = 4
AHEAD = 3
LAG = 3
VECTOR_LAG = 3
norm_eps = 1e-06
head_eps = 1e-05
closed_score = -10000.0
f32 = jnp.float32
bf16 = jnp.bfloat16


def nn(a, b):
    return lax.dot_general(a, b, (((1,), (0,)), ((), ())), preferred_element_type=f32)


def nt(a, b):
    return lax.dot_general(a, b, (((1,), (1,)), ((), ())), preferred_element_type=f32)


def tn(a, b):
    return lax.dot_general(a, b, (((0,), (0,)), ((), ())), preferred_element_type=f32)


def row(ref, index):
    return ref[...].astype(f32)[index : index + 1, :]


def col_sum(value):
    return jnp.sum(value, axis=0, keepdims=True)


def center_norm(value, eps):
    centered = value - jnp.mean(value, axis=-1, keepdims=True)
    spread = lax.rsqrt(jnp.mean(centered * centered, axis=-1, keepdims=True) + eps)
    return centered * spread, spread


def norm_back(grad_hat, hat, spread):
    mean_grad = jnp.mean(grad_hat, axis=-1, keepdims=True)
    mean_both = jnp.mean(grad_hat * hat, axis=-1, keepdims=True)
    return spread * (grad_hat - mean_grad - hat * mean_both)


def seg_matrix(width, head, value):
    shift = head.bit_length() - 1
    first = lax.shift_right_logical(lax.broadcasted_iota(jnp.int32, (width, width), 0), shift)
    second = lax.shift_right_logical(lax.broadcasted_iota(jnp.int32, (width, width), 1), shift)
    return jnp.where(first == second, value, 0.0).astype(bf16)


def seg_dot(value, matrix):
    high = value.astype(bf16)
    low = (value - high.astype(f32)).astype(bf16)
    return nn(high, matrix) + nn(low, matrix)


def seg_norm(value, mean_matrix):
    centered = value - seg_dot(value, mean_matrix)
    spread = lax.rsqrt(seg_dot(centered * centered, mean_matrix) + head_eps)
    return centered * spread, spread


def first_lanes(rows):
    return lax.broadcasted_iota(jnp.int32, (rows, LANES), 1) < LANES // 2


def turn(value):
    return pltpu.roll(value, LANES // 2, value.ndim - 1)


def pack_pair(slab):
    half = slab.shape[0] // 2
    top, bottom = slab[:half], slab[half:]
    low = first_lanes(half)
    return jnp.where(low, top, turn(bottom)), jnp.where(low, turn(top), bottom)


def unpack_pair(even, odd):
    low = first_lanes(even.shape[0])
    top = jnp.where(low, even, turn(odd))
    bottom = jnp.where(low, turn(even), odd)
    return jnp.concatenate([top, bottom], axis=0)


def erf(value):
    value = jnp.clip(value, -4.0, 4.0)
    square = value * value
    top = jnp.full_like(square, -2.72614225801306e-10)
    for coefficient in (
        2.77068142495902e-08,
        -2.10102402082508e-06,
        -5.69250639462346e-05,
        -7.34990630326855e-04,
        -2.95459980854025e-03,
        -1.60960333262415e-02,
    ):
        top = top * square + coefficient
    bottom = jnp.full_like(square, -1.45660718464996e-05)
    for coefficient in (
        -2.13374055278905e-04,
        -1.68282697438203e-03,
        -7.37332916720468e-03,
        -1.42647390514189e-02,
    ):
        bottom = bottom * square + coefficient
    return value * top / bottom


def full(shape):
    return pl.BlockSpec(shape, lambda *_: (0,) * len(shape))


def sds(shape, dtype):
    return jax.ShapeDtypeStruct(shape, dtype)


def call(body, name, grid, in_specs, out_specs, out_shape, scratch, flops, moved):
    return pl.pallas_call(
        body,
        name=name,
        out_shape=out_shape,
        grid_spec=pltpu.PrefetchScalarGridSpec(
            num_scalar_prefetch=1,
            grid=grid,
            in_specs=in_specs,
            out_specs=out_specs,
            scratch_shapes=scratch,
        ),
        cost_estimate=pl.CostEstimate(flops=flops, bytes_accessed=moved, transcendentals=0),
    )


def joint_body(
    block, packed, head, meta, x_ref, gain_ref, shift_ref, pattern_ref, w_ref, b_ref,
    own_ref, other_ref, pre_ref, out_ref, normed_ref, *stage
):
    step = pl.program_id(0)
    rows, width = normed_ref.shape
    per_part = width // CHUNK
    half = rows // 2

    @pl.when(step == 0)
    def _():
        hat, _ = center_norm(x_ref[...].astype(f32), norm_eps)
        normed = (hat * row(gain_ref, block) + row(shift_ref, block)).astype(bf16)
        normed_ref[...] = normed

        @pl.when(meta[0] == 0)
        def _():
            own_ref[...] = normed[:, : width // 2]
            other_ref[...] = normed[:, width // 2 :]

        @pl.when(meta[0] != 0)
        def _():
            own_ref[...] = normed[:, width // 2 :]
            other_ref[...] = normed[:, : width // 2]

        if packed:
            count = jnp.full((8, LANES), meta[3], jnp.int32).astype(f32)
            for place in range(stage[0].shape[0]):
                stage[0][place, 3 * half : 3 * half + 8, :] = count

    joined = nn(normed_ref[...], w_ref[0]) + row(b_ref, block)
    pattern = pattern_ref[...]

    def emit(part, values):
        if packed:
            base = (step - part * per_part) * (CHUNK // head)
            for slab in range(CHUNK // LANES):
                even, odd = pack_pair(values[:, slab * LANES : (slab + 1) * LANES])
                stage[0][base + 2 * slab, part * half : (part + 1) * half, :] = even
                stage[0][base + 2 * slab + 1, part * half : (part + 1) * half, :] = odd
        else:
            out_ref[...] = values.astype(bf16)

    def normed_heads(gain, shift):
        mean_matrix = seg_matrix(SLAB, head, 1.0 / head)
        pieces = []
        for slab in range(CHUNK // SLAB):
            hat, _ = seg_norm(joined[:, slab * SLAB : (slab + 1) * SLAB], mean_matrix)
            pieces.append(hat * gain if shift is None else hat * gain + shift)
        return jnp.concatenate(pieces, axis=1)

    scale = head ** (-0.5)

    @pl.when(step < per_part)
    def _():
        pre_ref[...] = joined
        emit(0, normed_heads(
            pattern[3 * block : 3 * block + 1] * scale,
            pattern[3 * block + 1 : 3 * block + 2] * scale,
        ))

    @pl.when((step >= per_part) & (step < 2 * per_part))
    def _():
        pre_ref[...] = joined
        emit(1, normed_heads(pattern[3 * block + 2 : 3 * block + 3], None))

    @pl.when(step >= 2 * per_part)
    def _():
        emit(2, joined)

    if packed:

        @pl.when(step == 3 * per_part - 1)
        def _():
            out_ref[...] = stage[0][...].astype(bf16)


def joint_forward(block, packed, head, meta, x, gain, shift, pattern, weight, bias):
    rows, width = x.shape
    per_part = width // CHUNK
    heads = width // head
    packed_rows = 3 * (rows // 2) + 8
    if packed:
        out_spec, out = full((heads, packed_rows, LANES)), sds((heads, packed_rows, LANES), bf16)
        extra = [pltpu.VMEM((heads, packed_rows, LANES), f32)]
    else:
        out_spec = pl.BlockSpec((rows, CHUNK), lambda j, m: (0, j))
        out = sds((rows, 3 * width), bf16)
        extra = []
    return call(
        partial(joint_body, block, packed, head),
        f"joint_forward_{block}",
        (3 * per_part,),
        [
            full((rows, width)),
            full(gain.shape),
            full(shift.shape),
            full(pattern.shape),
            pl.BlockSpec((1, width, CHUNK), lambda j, m: (block, 0, j)),
            pl.BlockSpec((2, CHUNK), lambda j, m: (0, j)),
        ],
        [
            full((rows, width // 2)),
            full((rows, width // 2)),
            pl.BlockSpec((rows, CHUNK), lambda j, m: (0, jnp.minimum(j, 2 * per_part - 1))),
            out_spec,
        ],
        [
            sds((rows, width // 2), bf16),
            sds((rows, width // 2), bf16),
            sds((rows, 2 * width), f32),
            out,
        ],
        [pltpu.VMEM((rows, width), bf16)] + extra,
        2 * rows * width * 3 * width,
        6 * width * width + 16 * rows * width,
    )(meta, x, gain, shift, pattern, weight, bias)


def lane_picks():
    lane = lax.broadcasted_iota(jnp.int32, (1, LANES), 1)
    low = jnp.where(lane < LANES // 2, 1.0, 0.0)
    return low.astype(bf16), (1.0 - low).astype(bf16)


def open_row(meta, rows):
    place = lax.broadcasted_iota(jnp.int32, (1, rows), 1)
    return jnp.where(place < meta[3] + SPECIAL, 0.0, closed_score)


def frame_body(meta, qkv_ref, out_ref):
    rows, width = out_ref.shape
    bias = open_row(meta, rows)
    picks = lane_picks()
    low = first_lanes(rows)
    for slab in range(width // LANES):
        at = slab * LANES
        queries = qkv_ref[:, at : at + LANES]
        keys = qkv_ref[:, width + at : width + at + LANES]
        values = qkv_ref[:, 2 * width + at : 2 * width + at + LANES]
        results = []
        for pick in picks:
            power = jnp.exp(nt(queries * pick, keys) + bias)
            probs = power / jnp.sum(power, axis=-1, keepdims=True)
            results.append(nn(probs.astype(bf16), values))
        out_ref[:, at : at + LANES] = jnp.where(low, results[0], results[1]).astype(bf16)


def frame_forward(meta, qkv):
    rows = qkv.shape[0]
    width = qkv.shape[1] // 3
    return call(
        frame_body,
        "frame_forward",
        (1,),
        [full(qkv.shape)],
        full((rows, width)),
        sds((rows, width), bf16),
        [],
        4 * rows * rows * width,
        8 * rows * width,
    )(meta, qkv)


def frame_back_slab(at, meta, qkv_ref, grad_ref, out_ref):
    rows, width = grad_ref.shape
    bias = open_row(meta, rows)
    scale = (LANES // 2) ** (-0.5)

    def lanes(part):
        return pl.ds(pl.multiple_of(part * width + at, LANES), LANES)

    queries = qkv_ref[:, lanes(0)]
    keys = qkv_ref[:, lanes(1)]
    values = qkv_ref[:, lanes(2)]
    grads = grad_ref[:, lanes(0)]
    found = []
    for pick in lane_picks():
        power = jnp.exp(nt(queries * pick, keys) + bias)
        probs = power / jnp.sum(power, axis=-1, keepdims=True)
        grad_probs = nt(grads * pick, values)
        delta = jnp.sum(probs * grad_probs, axis=-1, keepdims=True)
        grad_scores = (probs * (grad_probs - delta)).astype(bf16)
        found.append((
            nn(grad_scores, keys) * scale,
            tn(grad_scores, queries),
            tn(probs.astype(bf16), grads),
        ))
    low = first_lanes(rows)
    for part in range(3):
        out_ref[:, lanes(part)] = jnp.where(low, found[0][part], found[1][part])


def packed_part(value, part, half):
    whole = value.astype(f32)
    return whole[:, part * half : (part + 1) * half, :].reshape(-1, LANES)


def open_slots(value, half):
    count = value.astype(f32)[:, 3 * half : 3 * half + 8, :]
    count = jnp.concatenate([count] * (half // 8), axis=1)
    place = lax.broadcasted_iota(jnp.int32, count.shape, 1).astype(f32)
    return (
        (place < count + SPECIAL).reshape(-1, LANES),
        (place + half < count + SPECIAL).reshape(-1, LANES),
    )


MESH = pl.DeviceIdType.MESH


def peers_of(frames):
    scene = lax.axis_index("scene")
    frame = lax.axis_index("frame")
    bits = []
    bit = 1
    while bit < frames:
        value = lax.rem(frame // bit, 2)
        bits.append((value, (scene, frame + bit * (1 - 2 * value))))
        bit *= 2
    core, core_peer = bits[0]
    scene_peer = (1 - scene, frame)
    cross_peer = (1 - scene, core_peer[1])
    return core, core_peer, scene_peer, cross_peer, bits[1:]


def enter(targets):
    barrier = pltpu.get_barrier_semaphore()
    for target in targets:
        pl.semaphore_signal(barrier, inc=1, device_id=target, device_id_type=MESH)
    pl.semaphore_wait(barrier, len(targets))


def enter_scene(frames):
    barrier = pltpu.get_barrier_semaphore()
    _, _, scene_peer, cross_peer, _ = peers_of(frames)
    scene = lax.axis_index("scene")
    frame = lax.axis_index("frame")
    for target in (scene_peer, cross_peer):
        pl.semaphore_signal(barrier, inc=1, device_id=target, device_id_type=MESH)

    @pl.loop(1, frames)
    def _(offset):
        pl.semaphore_signal(
            barrier, inc=1, device_id=(scene, lax.rem(frame + offset, frames)), device_id_type=MESH
        )

    pl.semaphore_wait(barrier, frames + 1)


def remote(source, target, send, recv, device):
    return pltpu.make_async_remote_copy(
        src_ref=source, dst_ref=target, send_sem=send, recv_sem=recv, device_id=device, device_id_type=MESH
    )


class Share:
    def __init__(self, frames, pairs, outs, send, recv):
        _, core_peer, scene_peer, _, _ = peers_of(frames)
        self.first, self.second = [], []
        for index, ((own, other), out) in enumerate(zip(pairs, outs)):
            self.first.append(remote(other, out.at[0], send.at[3 * index], recv.at[3 * index], scene_peer))
            self.first.append(remote(own, out.at[1], send.at[3 * index + 1], recv.at[3 * index + 1], core_peer))
            self.second.append(
                remote(out.at[0], out.at[2], send.at[3 * index + 2], recv.at[3 * index + 2], core_peer)
            )

    def start(self):
        for copy in self.first:
            copy.start()

    def relay(self):
        for index, copy in enumerate(self.second):
            self.first[2 * index].wait_recv()
            copy.start()

    def close(self):
        for index, copy in enumerate(self.second):
            self.first[2 * index].wait_send()
            self.first[2 * index + 1].wait()
            copy.wait()


def scene_body(
    frames, half, span, n_share, meta, pack_ref, *refs
):
    heads = pack_ref.shape[0]
    pairs = [(refs[2 * index], refs[2 * index + 1]) for index in range(n_share)]
    refs = refs[2 * n_share :]
    att_ref, kept_ref, out_ref, log_ref = refs[:4]
    outs, refs = refs[4 : 4 + n_share], refs[4 + n_share :]
    queries, keys, values, sent, a_send, a_recv, b_send, b_recv, s_send, s_recv, own_sem = refs
    n = queries.shape[0] // 2
    m = keys.shape[0] // 2
    scene = lax.axis_index("scene")
    frame = lax.axis_index("frame")
    part = frame // heads
    own = pltpu.make_async_copy(pack_ref.at[lax.rem(frame, heads)], kept_ref.at[frame], own_sem)
    own.start()
    share = Share(frames, pairs, outs, s_send, s_recv)
    enter_scene(frames)

    def to_head(offset):
        target = lax.rem(frame + offset, frames)
        return remote(
            pack_ref.at[lax.rem(target, heads)], kept_ref.at[frame], a_send.at[offset], a_recv.at[offset], (scene, target)
        )

    @pl.loop(1, frames)
    def _(offset):
        to_head(offset).start()

    share.start()
    own.wait()

    @pl.loop(1, frames)
    def _(offset):
        to_head(offset).wait_recv()

    first = pl.multiple_of(part * heads, heads)
    q = packed_part(kept_ref[pl.ds(first, heads)], 0, half)
    low_n, low_m = first_lanes(n), first_lanes(m)
    queries[:n, :] = jnp.where(low_n, q, 0.0).astype(bf16)
    queries[n:, :] = jnp.where(low_n, turn(q), 0.0).astype(bf16)
    k = packed_part(kept_ref[...], 1, half)
    keys[:m, :] = k.astype(bf16)
    keys[m:, :] = turn(k).astype(bf16)
    v = packed_part(kept_ref[...], 2, half)
    open_low, open_high = open_slots(kept_ref[...], half)
    values[:m, :] = jnp.where(open_low, jnp.where(low_m, v, 1.0), 0.0).astype(bf16)
    values[m:, :] = jnp.where(open_high, jnp.where(low_m, turn(v), 1.0), 0.0).astype(bf16)
    low = first_lanes(LANES)

    @pl.loop(0, n // LANES)
    def _(piece):
        at = pl.multiple_of(piece * LANES, LANES)
        some = jnp.concatenate([queries[pl.ds(at, LANES), :], queries[pl.ds(n + at, LANES), :]], axis=0)
        total = jnp.zeros((2 * LANES, LANES), f32)
        for start in range(0, 2 * m, span):
            power = jnp.exp(nt(some, keys[start : start + span, :])).astype(bf16)
            total = total + nn(power, values[start : start + span, :])
        first, second = total[:LANES], total[LANES:]
        bottom = jnp.where(low, turn(first), second)
        result = jnp.where(low, first, turn(second)) / bottom
        out_ref[pl.ds(at, LANES), :] = result
        log_ref[pl.ds(at, LANES), :] = jnp.log(bottom)

    share.relay()
    sent[...] = out_ref[...].reshape(heads, half, LANES).astype(bf16)
    place = lax.rem(frame, heads)

    def from_head(offset):
        target = lax.rem(place + offset, heads)
        return remote(
            sent.at[target], att_ref.at[place], b_send.at[offset], b_recv.at[offset], (scene, part * heads + target)
        )

    @pl.loop(1, heads)
    def _(offset):
        from_head(offset).start()

    att_ref[place] = sent[place]

    @pl.loop(1, frames)
    def _(offset):
        to_head(offset).wait_send()

    @pl.loop(1, heads)
    def _(offset):
        from_head(offset).wait()

    share.close()


any_space = pl.BlockSpec(memory_space=pl.ANY)
vmem_space = pl.BlockSpec(memory_space=pltpu.VMEM)
dma = pltpu.SemaphoreType.DMA


def scene_forward(frames, meta, pack, half, pairs):
    heads = pack.shape[0]
    n = heads * half
    m = frames * half
    span = m // 2
    while span > 640:
        span = span // 2
    flat = [value for pair in pairs for value in pair]
    results = pl.pallas_call(
        partial(scene_body, frames, half, span, len(pairs)),
        name="scene_forward",
        out_shape=[
            sds((heads, half, LANES), bf16),
            sds((frames,) + pack.shape[1:], bf16),
            sds((n, LANES), f32),
            sds((n, LANES), f32),
        ]
        + [sds((3,) + own.shape, bf16) for own, _ in pairs],
        grid_spec=pltpu.PrefetchScalarGridSpec(
            num_scalar_prefetch=1,
            grid=(1,),
            in_specs=[vmem_space] + [any_space] * len(flat),
            out_specs=[vmem_space] * 4 + [any_space] * len(pairs),
            scratch_shapes=[
                pltpu.VMEM((2 * n, LANES), bf16),
                pltpu.VMEM((2 * m, LANES), bf16),
                pltpu.VMEM((2 * m, LANES), bf16),
                pltpu.VMEM((heads, half, LANES), bf16),
                dma((frames,)),
                dma((frames,)),
                dma((heads,)),
                dma((heads,)),
                dma((3 * len(pairs),)),
                dma((3 * len(pairs),)),
                dma(()),
            ],
        ),
        compiler_params=pltpu.CompilerParams(collective_id=1, has_side_effects=True),
        cost_estimate=pl.CostEstimate(flops=16 * n * m * LANES, bytes_accessed=20 * n * LANES, transcendentals=0),
    )(meta, pack, *flat)
    return results[0], results[1], results[2], results[3], results[4:]


def three_lanes(value, closed):
    lane = lax.broadcasted_iota(jnp.int32, value.shape, 1)
    base = LANES // 2
    high = value.astype(bf16).astype(f32)
    rest = value - high
    middle = rest.astype(bf16).astype(f32)
    last = rest - middle
    result = jnp.where(lane == base, high, jnp.where(lane == base + 1, middle, last))
    return jnp.where(lane < base + 3, result, jnp.where(lane == base + 3, closed, 0.0))


def gradient_copies(frames, own, came, send, recv, lanes):
    core, core_peer, scene_peer, cross_peer, _ = peers_of(frames)
    targets = ((core, scene_peer), (1 - core, core_peer), (1 - core, cross_peer))
    return [
        remote(own.at[side, :, lanes], came.at[which, :, lanes], send.at[which], recv.at[which], peer)
        for which, (side, peer) in enumerate(targets)
    ]


def scene_back_body(frames, half, span, n_share, shared, meta, kept_ref, grad_ref, out_ref, log_ref, feed_ref, *refs):
    heads = grad_ref.shape[0]
    pairs = [(refs[2 * index], refs[2 * index + 1]) for index in range(n_share)]
    refs = refs[2 * n_share :]
    back_ref, feed_came, outs, refs = refs[0], refs[1], refs[2 : 2 + n_share], refs[2 + n_share :]
    queries, keys, values, grads, turned, came, dk_ref, dv_ref, sent_q, sent_kv = refs[:10]
    a_send, a_recv, b_send, b_recv, c_send, c_recv, s_send, s_recv, g_send, g_recv = refs[10:]
    n = queries.shape[0] // 2
    m = keys.shape[0] // 2
    scene = lax.axis_index("scene")
    frame = lax.axis_index("frame")
    part = frame // heads
    place = lax.rem(frame, heads)
    share = Share(frames, pairs, outs, s_send, s_recv)
    feed_copies = gradient_copies(frames, feed_ref, feed_came, g_send, g_recv, pl.ds(0, shared))
    enter_scene(frames)

    def to_head(offset):
        target = lax.rem(place + offset, heads)
        return remote(
            grad_ref.at[target], came.at[place], a_send.at[offset], a_recv.at[offset], (scene, part * heads + target)
        )

    @pl.loop(1, heads)
    def _(offset):
        to_head(offset).start()

    share.start()
    for copy in feed_copies:
        copy.start()
    came[place] = grad_ref[place]
    first = pl.multiple_of(part * heads, heads)
    low_n, low_m = first_lanes(n), first_lanes(m)
    base = LANES // 2
    q = packed_part(kept_ref[pl.ds(first, heads)], 0, half)
    log = -log_ref[...]
    queries[:n, :] = jnp.where(low_n, q, three_lanes(turn(log), closed_score)).astype(bf16)
    queries[n:, :] = jnp.where(low_n, turn(q), three_lanes(log, closed_score)).astype(bf16)
    lane = lax.broadcasted_iota(jnp.int32, (m, LANES), 1)
    ones = jnp.where(lane < base + 3, 1.0, 0.0)
    open_low, open_high = open_slots(kept_ref[...], half)
    k = packed_part(kept_ref[...], 1, half)
    for place_at, k_now, is_open in ((0, k, open_low), (m, turn(k), open_high)):
        tail = jnp.where((lane == base + 3) & jnp.logical_not(is_open), 1.0, ones)
        keys[place_at : place_at + m, :] = jnp.where(low_m, k_now, tail).astype(bf16)
    v = packed_part(kept_ref[...], 2, half)
    values[:m, :] = jnp.where(low_m, v, ones).astype(bf16)
    values[m:, :] = jnp.where(low_m, turn(v), ones).astype(bf16)
    turned[...] = jnp.zeros_like(turned)
    low = first_lanes(LANES)

    @pl.loop(1, heads)
    def _(offset):
        to_head(offset).wait_recv()

    g = came[...].astype(f32).reshape(n, LANES)
    delta = -seg_dot(g * out_ref[...], seg_matrix(LANES, base, 1.0))
    grads[:n, :] = jnp.where(low_n, g, three_lanes(turn(delta), 0.0)).astype(bf16)
    grads[n:, :] = jnp.where(low_n, turn(g), three_lanes(delta, 0.0)).astype(bf16)

    @pl.loop(0, m // LANES)
    def _(piece):
        at = pl.multiple_of(piece * LANES, LANES)
        key_part = jnp.concatenate([keys[pl.ds(at, LANES), :], keys[pl.ds(m + at, LANES), :]], axis=0)
        value_part = jnp.concatenate(
            [values[pl.ds(at, LANES), :], values[pl.ds(m + at, LANES), :]], axis=0
        )
        key_turned = jnp.transpose(key_part.astype(f32)).astype(bf16)
        dk = jnp.zeros((2 * LANES, LANES), f32)
        dv = jnp.zeros((2 * LANES, LANES), f32)
        for start in range(0, 2 * n, span):
            some = queries[start : start + span, :]
            some_grads = grads[start : start + span, :]
            probs = jnp.exp(nt(key_part, some))
            grad_scores = (probs * nt(value_part, some_grads)).astype(bf16)
            dv = dv + nn(probs.astype(bf16), some_grads)
            dk = dk + nn(grad_scores, some)
            turned[:, start : start + span] += nn(key_turned, grad_scores)
        dk_ref[pl.ds(at, LANES), :] = jnp.where(low, dk[:LANES], turn(dk[LANES:]))
        dv_ref[pl.ds(at, LANES), :] = jnp.where(low, dv[:LANES], turn(dv[LANES:]))

    share.relay()
    sent_kv[:, 0] = dk_ref[...].reshape(frames, half, LANES).astype(bf16)
    sent_kv[:, 1] = dv_ref[...].reshape(frames, half, LANES).astype(bf16)

    def back_kv(offset):
        target = lax.rem(frame + offset, frames)
        return remote(
            sent_kv.at[target], back_ref.at[frame, pl.ds(1, 2)], b_send.at[offset], b_recv.at[offset], (scene, target)
        )

    @pl.loop(1, frames)
    def _(offset):
        back_kv(offset).start()

    scale = base ** (-0.5)
    rows = []
    for at in range(0, n, LANES):
        first = jnp.transpose(turned[:, at : at + LANES])
        second = jnp.transpose(turned[:, n + at : n + at + LANES])
        rows.append(jnp.where(low, first, turn(second)) * scale)
    sent_q[...] = jnp.concatenate(rows, axis=0).reshape(heads, half, LANES).astype(bf16)

    def back_q(offset):
        target = lax.rem(place + offset, heads)
        return remote(
            sent_q.at[target], back_ref.at[frame, 0], c_send.at[offset], c_recv.at[offset], (scene, part * heads + target)
        )

    back_ref[frame, 1] = sent_kv[frame, 0]
    back_ref[frame, 2] = sent_kv[frame, 1]

    @pl.loop(1, heads)
    def _(offset):
        back_q(offset).start()

    back_ref[frame, 0] = sent_q[place]

    @pl.loop(1, heads)
    def _(offset):
        to_head(offset).wait_send()

    @pl.loop(1, frames)
    def _(offset):
        back_kv(offset).wait()

    @pl.loop(1, heads)
    def _(offset):
        back_q(offset).wait()

    share.close()
    for copy in feed_copies:
        copy.wait()


def scene_backward(frames, meta, kept, grad, out, log, half, pairs, feed_grads, shared):
    heads = grad.shape[0]
    n = heads * half
    m = frames * half
    span = n // 2
    while span > 640:
        span = span // 2
    flat = [value for pair in pairs for value in pair]
    results = pl.pallas_call(
        partial(scene_back_body, frames, half, span, len(pairs), shared),
        name="scene_backward",
        out_shape=[sds((frames, 3, half, LANES), bf16), sds((3,) + feed_grads.shape[1:], bf16)]
        + [sds((3,) + own.shape, bf16) for own, _ in pairs],
        grid_spec=pltpu.PrefetchScalarGridSpec(
            num_scalar_prefetch=1,
            grid=(1,),
            in_specs=[vmem_space] * 4 + [any_space] * (1 + len(flat)),
            out_specs=[vmem_space] + [any_space] * (1 + len(pairs)),
            scratch_shapes=[
                pltpu.VMEM((2 * n, LANES), bf16),
                pltpu.VMEM((2 * m, LANES), bf16),
                pltpu.VMEM((2 * m, LANES), bf16),
                pltpu.VMEM((2 * n, LANES), bf16),
                pltpu.VMEM((LANES, 2 * n), f32),
                pltpu.VMEM((heads, half, LANES), bf16),
                pltpu.VMEM((m, LANES), f32),
                pltpu.VMEM((m, LANES), f32),
                pltpu.VMEM((heads, half, LANES), bf16),
                pltpu.VMEM((frames, 2, half, LANES), bf16),
                dma((heads,)),
                dma((heads,)),
                dma((frames,)),
                dma((frames,)),
                dma((heads,)),
                dma((heads,)),
                dma((3 * len(pairs),)),
                dma((3 * len(pairs),)),
                dma((3,)),
                dma((3,)),
            ],
        ),
        compiler_params=pltpu.CompilerParams(collective_id=2, has_side_effects=True),
        cost_estimate=pl.CostEstimate(flops=40 * n * m * LANES, bytes_accessed=30 * n * LANES, transcendentals=0),
    )(meta, kept, grad, out, log, feed_grads, *flat)
    back = results[0]
    if frames > heads:
        place = lax.axis_index("frame") // heads * heads
        dq = lax.dynamic_slice(back, (place, 0, 0, 0), (heads, 1, half, LANES))
        both = back.reshape(frames // heads, heads, 3, half, LANES)[:, :, 1:].astype(f32).sum(0)
        back = jnp.concatenate([dq, both.astype(bf16)], axis=1)
    return back, results[1], results[2:]


def feed_body(
    block, packed, meta, att_ref, x_ref, mixer_ref, mixer_bias, mixer_scale, gain_ref, shift_ref,
    inner_ref, inner_bias, outer_ref, outer_bias, outer_scale,
    own_ref, other_ref, middle_ref, branch_ref, feed_ref, slope_ref, out_ref, normed_ref, total_ref
):
    step = pl.program_id(0)
    steps = pl.num_programs(0)
    rows, width = middle_ref.shape
    hidden_half = own_ref.shape[1] - width
    half_steps = hidden_half // CHUNK
    mine = meta[0]

    def split(value, at):
        first, second = value[:, : width // 2], value[:, width // 2 :]

        @pl.when(mine == 0)
        def _():
            own_ref[:, at : at + width // 2] = first
            other_ref[:, at : at + width // 2] = second

        @pl.when(mine != 0)
        def _():
            own_ref[:, at : at + width // 2] = second
            other_ref[:, at : at + width // 2] = first

    @pl.when(step == 0)
    def _():
        if packed:
            pieces = []
            for pair in range(width // LANES):
                pieces.append(
                    unpack_pair(att_ref[2 * pair].astype(f32), att_ref[2 * pair + 1].astype(f32))
                )
            attended = jnp.concatenate(pieces, axis=1).astype(bf16)
        else:
            attended = att_ref[...]
        branch = nn(attended, mixer_ref[0]) + row(mixer_bias, block)
        middle = x_ref[...].astype(f32) + row(mixer_scale, block) * branch
        hat, _ = center_norm(middle, norm_eps)
        normed = (hat * row(gain_ref, block) + row(shift_ref, block)).astype(bf16)
        branch_ref[...] = branch
        middle_ref[...] = middle
        normed_ref[...] = normed
        split(normed, hidden_half)
        split(attended, hidden_half + width // 2)
        total_ref[...] = jnp.zeros_like(total_ref)

    pre = nn(normed_ref[...], inner_ref[0]) + row(inner_bias, block)
    share = 0.5 * (1.0 + erf(pre * (2.0 ** (-0.5))))
    slope_ref[...] = share + pre * jnp.exp(-0.5 * pre * pre) * 0.3989422804014327
    hidden = (pre * share).astype(bf16)
    place = pl.multiple_of(lax.rem(step, half_steps) * CHUNK, CHUNK)

    @pl.when(step // half_steps == mine)
    def _():
        own_ref[:, pl.ds(place, CHUNK)] = hidden

    @pl.when(step // half_steps != mine)
    def _():
        other_ref[:, pl.ds(place, CHUNK)] = hidden

    total_ref[...] += nn(hidden, outer_ref[0])

    @pl.when(step == steps - 1)
    def _():
        feed = total_ref[...] + row(outer_bias, block)
        feed_ref[...] = feed
        result = middle_ref[...] + row(outer_scale, block) * feed
        if packed:
            place = lax.broadcasted_iota(jnp.int32, result.shape, 0)
            result = jnp.where(place < meta[3] + SPECIAL, result, 0.0)
        out_ref[...] = result.astype(out_ref.dtype)


def feed_forward(block, packed, meta, att, x, mixer, mixer_bias, mixer_scale, gain, shift, inner, inner_bias, outer, outer_bias, outer_scale):
    rows, width = x.shape
    hidden = inner.shape[2]
    kept = hidden // 2 + width
    steps = hidden // CHUNK
    vector = full(gain.shape)
    return call(
        partial(feed_body, block, packed),
        f"feed_forward_{block}",
        (steps,),
        [
            full(att.shape),
            full((rows, width)),
            pl.BlockSpec((1, width, width), lambda j, m: (block, 0, 0)),
            vector, vector, vector, vector,
            pl.BlockSpec((1, width, CHUNK), lambda j, m: (block, 0, j)),
            pl.BlockSpec((2, CHUNK), lambda j, m: (0, j)),
            pl.BlockSpec((1, CHUNK, width), lambda j, m: (block, j, 0)),
            vector, vector,
        ],
        [full((rows, kept))] * 2
        + [full((rows, width))] * 3
        + [pl.BlockSpec((rows, CHUNK), lambda j, m: (0, j)), full((rows, width))],
        [sds((rows, kept), bf16)] * 2
        + [sds((rows, width), f32)] * 3
        + [sds((rows, hidden), f32), sds((rows, width), bf16 if packed else f32)],
        [pltpu.VMEM((rows, width), bf16), pltpu.VMEM((rows, width), f32)],
        2 * rows * width * (2 * hidden + width),
        4 * width * hidden + 4 * rows * hidden + 30 * rows * width,
    )(meta, att, x, mixer, mixer_bias, mixer_scale, gain, shift, inner, inner_bias, outer, outer_bias, outer_scale)


def feed_back_core(
    block, packed, step, steps, chunk, meta, g_ref, feed_ref, slope_ref, middle_ref, branch_ref,
    outer_scale, gain_ref, mixer_scale, outer_ref, inner_ref, mixer_ref,
    grads_ref, g_middle_ref, g_att_ref, vector_ref, g_feed_ref, total_ref
):
    rows, width = total_ref.shape
    half_steps = steps // 2
    at_branch = width // 2 + half_steps * CHUNK

    def incoming():
        g = g_ref[...].astype(f32)
        if packed:
            place = lax.broadcasted_iota(jnp.int32, g.shape, 0)
            g = jnp.where(place < meta[3] + SPECIAL, g, 0.0)
        return g

    @pl.when(step == 0)
    def _():
        g = incoming()
        g_feed = (g * row(outer_scale, block)).astype(bf16)
        g_feed_ref[...] = g_feed
        grads_ref[0, :, : width // 2] = g_feed[:, : width // 2]
        grads_ref[1, :, : width // 2] = g_feed[:, width // 2 :]
        vector_ref[0:1, :] = col_sum(g * feed_ref[...])
        vector_ref[1:2, :] = col_sum(g_feed.astype(f32))
        total_ref[...] = jnp.zeros_like(total_ref)

    g_pre = (nt(g_feed_ref[...], outer_ref[0]) * slope_ref[...]).astype(bf16)
    place = pl.multiple_of(width // 2 + lax.rem(chunk, half_steps) * CHUNK, CHUNK)
    grads_ref[chunk // half_steps, :, pl.ds(place, CHUNK)] = g_pre
    per_row = width // CHUNK
    lanes = pl.ds(pl.multiple_of(lax.rem(chunk, per_row) * CHUNK, CHUNK), CHUNK)
    vector_ref[pl.ds(6 + chunk // per_row, 1), lanes] = col_sum(g_pre.astype(f32))
    total_ref[...] += nt(g_pre, inner_ref[0])

    @pl.when(step == steps - 1)
    def _():
        hat, spread = center_norm(middle_ref[...], norm_eps)
        g_nm = total_ref[...]
        vector_ref[2:3, :] = col_sum(g_nm * hat)
        vector_ref[3:4, :] = col_sum(g_nm)
        g_middle = incoming() + norm_back(g_nm * row(gain_ref, block), hat, spread)
        g_middle_ref[...] = g_middle
        vector_ref[4:5, :] = col_sum(g_middle * branch_ref[...])
        g_branch = (g_middle * row(mixer_scale, block)).astype(bf16)
        vector_ref[5:6, :] = col_sum(g_branch.astype(f32))
        grads_ref[0, :, at_branch : at_branch + width // 2] = g_branch[:, : width // 2]
        grads_ref[1, :, at_branch : at_branch + width // 2] = g_branch[:, width // 2 :]
        g_att = nt(g_branch, mixer_ref[0])
        if packed:
            for pair in range(width // LANES):
                even, odd = pack_pair(g_att[:, pair * LANES : (pair + 1) * LANES])
                g_att_ref[2 * pair] = even.astype(bf16)
                g_att_ref[2 * pair + 1] = odd.astype(bf16)
        else:
            g_att_ref[...] = g_att.astype(bf16)


def feed_back_body(block, packed, meta, *refs):
    step = pl.program_id(0)
    feed_back_core(block, packed, step, pl.num_programs(0), step, meta, *refs)


def feed_backward(block, packed, heads, meta, g, feed, slope, middle, branch, outer_scale, gain, mixer_scale, outer, inner, mixer):
    rows, width = middle.shape
    hidden = inner.shape[2]
    steps = hidden // CHUNK
    vector = full(gain.shape)
    vector_rows = 6 + hidden // width
    att_shape = (heads, rows // 2, LANES) if packed else (rows, width)
    return call(
        partial(feed_back_body, block, packed),
        f"feed_backward_{block}",
        (steps,),
        [
            full((rows, width)),
            full((rows, width)),
            pl.BlockSpec((rows, CHUNK), lambda j, m: (0, j)),
            full((rows, width)),
            full((rows, width)),
            vector, vector, vector,
            pl.BlockSpec((1, CHUNK, width), lambda j, m: (block, j, 0)),
            pl.BlockSpec((1, width, CHUNK), lambda j, m: (block, 0, j)),
            pl.BlockSpec((1, width, width), lambda j, m: (block, 0, 0)),
        ],
        [
            full((2, rows, width + hidden // 2)),
            full((rows, width)),
            full(att_shape),
            full((vector_rows, width)),
        ],
        [
            sds((2, rows, width + hidden // 2), bf16),
            sds((rows, width), f32),
            sds(att_shape, bf16),
            sds((vector_rows, width), f32),
        ],
        [pltpu.VMEM((rows, width), bf16), pltpu.VMEM((rows, width), f32)],
        2 * rows * width * (2 * hidden + width),
        4 * width * hidden + 8 * rows * hidden + 20 * rows * width,
    )(meta, g, feed, slope, middle, branch, outer_scale, gain, mixer_scale, outer, inner, mixer)


def joint_back_core(
    block, head, step, steps, chunk, g, pre_ref, x_ref, g_middle_ref, gain_ref, pattern_ref, w_ref,
    grads_ref, at_joined, out_ref, vector_ref, total_ref
):
    rows, width = total_ref.shape
    per_part = width // CHUNK
    half_steps = steps // 2

    @pl.when(step == 0)
    def _():
        total_ref[...] = jnp.zeros_like(total_ref)

    pattern = pattern_ref[...]
    in_row = pl.ds(pl.multiple_of(lax.rem(chunk, per_part) * CHUNK, CHUNK), CHUNK)

    def finish(g_joined):
        rounded = g_joined.astype(bf16)
        place = pl.multiple_of(at_joined + lax.rem(chunk, half_steps) * CHUNK, CHUNK)
        grads_ref[chunk // half_steps, :, pl.ds(place, CHUNK)] = rounded
        vector_ref[pl.ds(2 + chunk // per_part, 1), in_row] = col_sum(rounded.astype(f32))
        total_ref[...] += nt(rounded, w_ref[0])

    def head_back(gain, gain_row, shift_row):
        mean_matrix = seg_matrix(SLAB, head, 1.0 / head)
        pieces = []
        for slab in range(CHUNK // SLAB):
            at = slab * SLAB
            g_now = g[:, at : at + SLAB]
            hat, spread = seg_norm(pre_ref[:, at : at + SLAB], mean_matrix)
            vector_ref[gain_row : gain_row + 1, at : at + SLAB] += col_sum(g_now * hat)
            if shift_row is not None:
                vector_ref[shift_row : shift_row + 1, at : at + SLAB] += col_sum(g_now)
            grad_hat = g_now * gain
            pieces.append(
                spread
                * (
                    grad_hat
                    - seg_dot(grad_hat, mean_matrix)
                    - hat * seg_dot(grad_hat * hat, mean_matrix)
                )
            )
        finish(jnp.concatenate(pieces, axis=1))

    @pl.when(chunk < per_part)
    def _():
        head_back(pattern[3 * block : 3 * block + 1], 5, 6)

    @pl.when((chunk >= per_part) & (chunk < 2 * per_part))
    def _():
        head_back(pattern[3 * block + 2 : 3 * block + 3], 7, None)

    @pl.when(chunk >= 2 * per_part)
    def _():
        finish(g)

    @pl.when(step == steps - 1)
    def _():
        hat, spread = center_norm(x_ref[...].astype(f32), norm_eps)
        g_normed = total_ref[...]
        vector_ref[0:1, :] = col_sum(g_normed * hat)
        vector_ref[1:2, :] = col_sum(g_normed)
        result = g_middle_ref[...] + norm_back(g_normed * row(gain_ref, block), hat, spread)
        out_ref[...] = result.astype(out_ref.dtype)


class Rows:
    def __init__(self, ref, lead, base):
        self.ref, self.lead, self.base = ref, lead, base

    def at(self, key):
        rows, lanes = key
        if isinstance(rows, slice):
            rows = slice(rows.start + self.base, rows.stop + self.base)
        else:
            rows = pl.ds(rows.start + self.base, rows.size)
        return self.lead, rows, lanes

    def __getitem__(self, key):
        return self.ref[self.at(key)]

    def __setitem__(self, key, value):
        self.ref[self.at(key)] = value


class Plan:
    def __init__(self, frames, rows, width, hidden):
        self.half = width // 2
        self.hidden_half = hidden // 2
        self.chips = frames // 2
        self.stages = self.chips.bit_length() - 1
        self.deep = self.half // self.chips // 2
        self.n_outer = CHUNK // LANES
        self.n_inner = self.hidden_half // CHUNK
        self.n_joint = 3 * self.half // CHUNK
        self.per_block = self.n_outer + self.n_inner + 1 + self.n_joint
        self.n_pieces = self.n_inner + self.n_joint + 2
        self.total = 2 * self.per_block
        self.joint_steps = 2 * self.n_joint
        self.feed_steps = 2 * self.n_inner
        self.slabs = 4
        self.frame_steps = width // LANES // self.slabs
        self.feed_at = self.joint_steps
        self.frame_at = self.feed_at + self.feed_steps
        self.joint_at = self.frame_at + self.frame_steps
        self.compute_end = self.joint_at + self.joint_steps
        self.leave = []
        for piece in range(SHARED_PIECES, 1 + self.n_inner + 1):
            self.leave.append((1 + piece - SHARED_PIECES, 0, piece))
        at_joined = 2 + self.n_inner
        for piece in range(self.n_joint):
            self.leave.append((2 + 2 * piece, 0, at_joined + piece))
        self.leave.append((self.feed_at + 1, 1, 0))
        for piece in range(self.n_inner):
            self.leave.append((self.feed_at + 2 + 2 * piece, 1, 1 + piece))
        self.leave.append((self.frame_at + 1, 1, 1 + self.n_inner))
        for piece in range(self.n_joint):
            self.leave.append((self.joint_at + 2 + 2 * piece, 1, at_joined + piece))
        first = 1
        for slot, block, piece in self.leave:
            unit = 0 if piece == 0 else piece + self.n_outer - 1
            first = max(first, slot + AHEAD - block * self.per_block - unit)
        self.first = first
        self.ring = 12
        self.lags = [LAG * (stage + 1) for stage in range(self.stages)]
        self.end_lag = self.lags[-1] + 2
        self.n_vector = 2 + self.stages
        self.slots = max(
            self.first + self.total + self.end_lag, self.compute_end + VECTOR_LAG * self.n_vector + 1
        )


def rear_body(plan, frames, head, meta, *refs):
    (
        back_ref, pre1_ref, x1_ref, g_middle1_ref, gain_ref, pattern_ref, joint_ref,
        outer_scale, second_gain, mixer_scale, outer_ref, inner_ref, slope_ref, pre0_ref,
        mixer_in, feed_in, middle_in, branch_in, qkv_in, x0_in,
        feed_g, came_in, feed_x1, feed_three1, joint_x1, joint_three1, feed_x0, feed_three0, joint_x0, joint_three0,
        vector_in,
    ) = refs[:31]
    tokens_ref, outer_out, inner_out, mixer_out, joint_out, vector_out = refs[31:37]
    (
        own, came, acts, hids, act_turned, hid_turned, parts, last, sums,
        mixer, feed0, middle0, branch0, qkv0, x0,
        g1, g_middle0, g_att0, g_feed, g_qkv, total_sum,
    ) = refs[37:58]
    steps = refs[58 : 58 + plan.stages]
    load_sem, act_sem, hid_sem, g_send, g_recv, p_send, p_recv, f_send, f_recv, v_send, v_recv = refs[58 + plan.stages :]
    slot = pl.program_id(0)
    rows = own.shape[2]
    half, hidden_half, chips, total = plan.half, plan.hidden_half, plan.chips, plan.total
    width = 2 * half
    per_block, n_outer, n_inner = plan.per_block, plan.n_outer, plan.n_inner
    at_joined = (2 + n_inner) * CHUNK
    core, core_peer, scene_peer, cross_peer, bits = peers_of(frames)
    vector_rows = 6 + hidden_half * 2 // width
    section = vector_rows + 8

    sources = [
        (feed_g, own.at[0, :, :, pl.ds(0, at_joined)]),
        (came_in.at[:, :, pl.ds(0, SHARED_PIECES * CHUNK)], came.at[0, :, :, pl.ds(0, SHARED_PIECES * CHUNK)]),
        (feed_in, feed0),
        (mixer_in.at[pl.ds(0, 1)], mixer),
        (middle_in, middle0),
        (branch_in, branch0),
        (qkv_in, qkv0),
        (x0_in, x0),
    ]

    def load(index):
        return pltpu.make_async_copy(sources[index][0], sources[index][1], load_sem.at[index])

    def act_loads(block):
        feed_x, feed_three, joint_x, joint_three = (
            (feed_x1, feed_three1, joint_x1, joint_three1),
            (feed_x0, feed_three0, joint_x0, joint_three0),
        )[block]
        copies = []
        for place in range(4):
            feed_from = feed_x if place == 0 else feed_three.at[place - 1]
            joint_from = joint_x if place == 0 else joint_three.at[place - 1]
            copies.append(pltpu.make_async_copy(
                feed_from.at[:, pl.ds(hidden_half, width)], acts.at[place, :, pl.ds(0, width)], act_sem.at[2 * place]
            ))
            copies.append(pltpu.make_async_copy(
                joint_from, acts.at[place, :, pl.ds(width, half)], act_sem.at[2 * place + 1]
            ))
        return copies

    def hid_loads(block):
        feed_x, feed_three = ((feed_x1, feed_three1), (feed_x0, feed_three0))[block]
        return [
            pltpu.make_async_copy(
                (feed_x if place == 0 else feed_three.at[place - 1]).at[:, pl.ds(0, hidden_half)],
                hids.at[place],
                hid_sem.at[place],
            )
            for place in range(4)
        ]

    def piece_copy(block, piece, which):
        lanes = pl.ds(pl.multiple_of(piece * CHUNK, CHUNK), CHUNK)
        side = core if which == 0 else 1 - core
        return remote(
            own.at[block, side, :, lanes],
            came.at[block, which, :, lanes],
            g_send.at[block, which, piece],
            g_recv.at[block, which, piece],
            (scene_peer, core_peer, cross_peer)[which],
        )

    @pl.when(slot == 0)
    def _():
        load(0).start()
        for copy in hid_loads(0):
            copy.start()
        load(1).start()
        for copy in act_loads(0):
            copy.start()
        for index in range(2, len(sources)):
            load(index).start()
        sums[0] = jnp.zeros(sums.shape[1:], f32)
        for index in range(vector_rows):
            sums[0, section + index : section + index + 1, :] = vector_in[index : index + 1, :]
        enter([core_peer, scene_peer, cross_peer] + [peer for _, peer in bits])
        load(0).wait()
        for copy in hid_loads(0):
            copy.wait()
        load(1).wait()
        for copy in act_loads(0):
            copy.wait()

    def spread(step, steps_of):
        return lax.rem(step, 2) * (steps_of // 2) + step // 2

    @pl.when(slot < plan.joint_steps)
    def _():
        pieces = []
        for pair in range(CHUNK // LANES):
            pieces.append(
                unpack_pair(back_ref[2 * pair, 0].astype(f32), back_ref[2 * pair + 1, 0].astype(f32))
            )
        joint_back_core(
            1, head, slot, plan.joint_steps, spread(slot, plan.joint_steps), jnp.concatenate(pieces, axis=1),
            pre1_ref, x1_ref, g_middle1_ref, gain_ref, pattern_ref, joint_ref,
            own.at[0], at_joined, g1, Rows(sums, 0, section + vector_rows), total_sum,
        )

    @pl.when(slot == plan.feed_at)
    def _():
        for index in range(2, len(sources)):
            load(index).wait()

    @pl.when((slot >= plan.feed_at) & (slot < plan.frame_at))
    def _():
        step = slot - plan.feed_at
        feed_back_core(
            0, False, step, plan.feed_steps, spread(step, plan.feed_steps), meta, g1, feed0, slope_ref, middle0, branch0,
            outer_scale, second_gain, mixer_scale, outer_ref, inner_ref, mixer,
            own.at[1], g_middle0, g_att0, Rows(sums, 0, 0), g_feed, total_sum,
        )

    @pl.when((slot >= plan.frame_at) & (slot < plan.joint_at))
    def _():
        @pl.loop(0, plan.slabs)
        def _(slab):
            at = ((slot - plan.frame_at) * plan.slabs + slab) * LANES
            frame_back_slab(at, meta, qkv0, g_att0, g_qkv)

    @pl.when((slot >= plan.joint_at) & (slot < plan.compute_end))
    def _():
        step = slot - plan.joint_at
        chunk = spread(step, plan.joint_steps)
        joint_back_core(
            0, head, step, plan.joint_steps, chunk,
            g_qkv[:, pl.ds(pl.multiple_of(chunk * CHUNK, CHUNK), CHUNK)],
            pre0_ref, x0, g_middle0, gain_ref, pattern_ref, joint_ref,
            own.at[1], at_joined, tokens_ref, Rows(sums, 0, vector_rows), total_sum,
        )

    def swapped(index):
        return lax.rem(index, SWAP_EVERY) == 1

    def way(stage, index):
        value, peer = bits[stage]
        if stage > 1:
            return value, peer
        other_value, other_peer = bits[1 - stage]
        changed = swapped(index)
        return jnp.where(changed, other_value, value), (peer[0], jnp.where(changed, other_peer[1], peer[1]))

    def stage_start(stage, index):
        value, peer = way(stage, index)
        source = parts if stage == 0 else steps[stage - 1]
        held = lax.rem(index, plan.ring)
        for pair in range(chips >> (stage + 1)):
            remote(
                source.at[held, 2 * pair + 1 - value],
                steps[stage].at[held, pair],
                p_send.at[stage, held],
                p_recv.at[stage, held],
                peer,
            ).start()

    def stage_whole(stage, index):
        held = lax.rem(index, plan.ring)
        return remote(
            steps[stage].at[held], steps[stage].at[held], p_send.at[stage, held], p_recv.at[stage, held], way(stage, index)[1]
        )

    def last_copy(index):
        held = lax.rem(index, plan.ring)
        return remote(
            steps[-1].at[held, 0, 1 - core], last.at[held], f_send.at[held], f_recv.at[held], core_peer
        )

    def store(index, value):
        changed = swapped(index)
        held = lax.rem(index, plan.ring)

        @pl.when(jnp.logical_not(changed))
        def _():
            parts[held] = value.astype(bf16)

        @pl.when(changed)
        def _():
            pairs = value.reshape((chips // 4, 2, 2) + value.shape[1:])
            pairs = jnp.stack([pairs[:, :, place] for place in range(2)], axis=1)
            parts[held] = pairs.reshape(value.shape).astype(bf16)

    def multiply(index):
        block = index // per_block
        unit = lax.rem(index, per_block)

        def wait_piece(piece):
            @pl.when((block > 0) | (piece >= SHARED_PIECES))
            def _():
                for which in range(3):
                    piece_copy(block, piece, which).wait_recv()

        def gathered(lanes):
            return jnp.concatenate(
                [own[block, core, :, lanes]] + [came[block, which, :, lanes] for which in range(3)], axis=0
            )

        @pl.when(unit < n_outer)
        def _():
            @pl.when(unit == 0)
            def _():
                wait_piece(0)
                hid_turned[...] = jnp.transpose(jnp.concatenate([hids[place] for place in range(4)], axis=0))

            right = gathered(pl.ds(pl.multiple_of(unit * LANES, LANES), LANES))
            value = nn(hid_turned[...], right)
            value = value.reshape(chips, 2, 4, plan.deep, LANES)
            store(index, jnp.concatenate([value[:, :, place] for place in range(4)], axis=-1))

        @pl.when(unit >= n_outer)
        def _():
            piece = unit - (n_outer - 1)
            wait_piece(piece)

            for place, at in enumerate((n_outer, n_outer + n_inner, n_outer + n_inner + 1)):

                @pl.when(unit == at)
                def _():
                    left = [acts[source, :, place * half : (place + 1) * half] for source in range(4)]
                    act_turned[...] = jnp.transpose(jnp.concatenate(left, axis=0))

            value = nn(act_turned[...], gathered(pl.ds(pl.multiple_of(piece * CHUNK, CHUNK), CHUNK)))
            store(index, value.reshape(chips, 2, plan.deep, CHUNK))

    def put(index, side, value):
        block = 1 - index // per_block
        unit = lax.rem(index, per_block)

        @pl.when(unit < n_outer)
        def _():
            lanes = pl.ds(pl.multiple_of(side * half + unit * LANES, LANES), LANES)
            for place in range(4):
                outer_out[block, place * plan.deep : (place + 1) * plan.deep, lanes] = (
                    value[:, place * LANES : (place + 1) * LANES]
                )

        def wide(first, count, target):
            @pl.when((unit >= first) & (unit < first + count))
            def _():
                lanes = pl.ds(pl.multiple_of((side * count + unit - first) * CHUNK, CHUNK), CHUNK)
                target[block, :, lanes] = value

        wide(n_outer, n_inner, inner_out)
        wide(n_outer + n_inner, 1, mixer_out)
        wide(n_outer + n_inner + 1, plan.n_joint, joint_out)

    def add(stage, index):
        stage_whole(stage, index).wait()
        value = way(stage, index)[0]
        held = lax.rem(index, plan.ring)
        source = parts if stage == 0 else steps[stage - 1]
        for pair in range(chips >> (stage + 1)):
            result = source[held, 2 * pair + value].astype(f32) + steps[stage][held, pair].astype(f32)
            if stage + 1 == plan.stages:
                put(index, core, jnp.where(core == 0, result[0], result[1]))
            steps[stage][held, pair] = result.astype(bf16)

    def close(index):
        last_copy(index).wait()
        put(index, 1 - core, last[lax.rem(index, plan.ring)].astype(f32))

    def when_due(lag, action):
        index = slot - plan.first - lag

        @pl.when((index >= 0) & (index < total))
        def _():
            action(index)

    vector_peers = [core_peer, scene_peer] + [peer for _, peer in bits]

    def vector_copy(stage):
        return remote(
            sums.at[2 * stage], sums.at[2 * stage + 1], v_send.at[stage], v_recv.at[stage], vector_peers[stage]
        )

    when_due(0, multiply)
    for stage in range(plan.stages):
        when_due(plan.lags[stage], partial(add, stage))
    when_due(plan.end_lag, close)

    for stage in range(plan.n_vector):

        @pl.when(slot == plan.compute_end + VECTOR_LAG * (stage + 1))
        def _():
            vector_copy(stage).wait()
            result = sums[2 * stage] + sums[2 * stage + 1]
            if stage + 1 < plan.n_vector:
                sums[2 * stage + 2] = result
            else:
                vector_out[...] = result

    for stage in range(plan.stages - 1):
        when_due(plan.lags[stage], partial(stage_start, stage + 1))
    when_due(plan.lags[-1], lambda index: last_copy(index).start())
    when_due(0, partial(stage_start, 0))

    for at, block, piece in plan.leave:

        @pl.when(slot == at)
        def _():
            for which in range(3):
                piece_copy(block, piece, which).start()

    for stage in range(plan.n_vector):

        @pl.when(slot == plan.compute_end + VECTOR_LAG * stage)
        def _():
            vector_copy(stage).start()

    @pl.when(slot == plan.first + 1)
    def _():
        for copy in hid_loads(1):
            copy.start()

    @pl.when(slot == plan.first + per_block - 1)
    def _():
        for copy in hid_loads(1):
            copy.wait()

    @pl.when(slot == plan.first + n_outer + n_inner + 1)
    def _():
        for copy in act_loads(1):
            copy.start()

    @pl.when(slot == plan.first + per_block + n_outer - 1)
    def _():
        for copy in act_loads(1):
            copy.wait()

    @pl.when(slot == plan.slots - 1)
    def _():
        for at, block, piece in plan.leave:
            for which in range(3):
                piece_copy(block, piece, which).wait_send()


def rear(frames, head, meta, back, pre1, x1, g_middle1, gain, pattern, joint, outer_scale, second_gain, mixer_scale, outer, inner, slope0, pre0, mixer, feed0, middle0, branch0, qkv0, x0, feed_g1, came1, shares, vector1):
    rows, width = x1.shape
    hidden = inner.shape[2]
    half = width // 2
    plan = Plan(frames, rows, width, hidden)
    per_part = width // CHUNK
    vector_rows = vector1.shape[0]
    n_vector_rows = 2 * (vector_rows + 8)

    def clip(value, size):
        return jnp.minimum(jnp.maximum(value, 0), size - 1)

    def spread(step, steps):
        return lax.rem(step, 2) * (steps // 2) + step // 2

    def chunk1(slot):
        return spread(clip(slot, plan.joint_steps), plan.joint_steps)

    def chunk0(slot):
        return spread(clip(slot - plan.joint_at, plan.joint_steps), plan.joint_steps)

    def chunk_feed(slot):
        return spread(clip(slot - plan.feed_at, plan.feed_steps), plan.feed_steps)

    def back_map(slot, m):
        chunk = chunk1(slot)
        return (lax.rem(chunk, per_part), chunk // per_part, 0, 0)

    def joint_map(slot, m):
        late = slot >= plan.feed_at
        return (jnp.where(late, 0, 1), 0, jnp.where(late, chunk0(slot), chunk1(slot)))

    once = dict(pipeline_mode=pl.Buffered(1))
    single = lambda shape: pl.BlockSpec(shape, lambda *_: (0,) * len(shape), **once)
    out_shape = [
        sds((rows, width), bf16),
        sds((2, 4 * plan.deep, width), f32),
        sds((2, plan.deep, hidden), f32),
        sds((2, plan.deep, width), f32),
        sds((2, plan.deep, 3 * width), f32),
        sds((n_vector_rows, width), f32),
    ]
    container = (plan.ring, plan.chips, 2, plan.deep, CHUNK)
    return pl.pallas_call(
        partial(rear_body, plan, frames, head),
        name="rear",
        out_shape=out_shape,
        grid_spec=pltpu.PrefetchScalarGridSpec(
            num_scalar_prefetch=1,
            grid=(plan.slots,),
            in_specs=[
                pl.BlockSpec((CHUNK // head, 1, rows // 2, LANES), back_map),
                pl.BlockSpec((rows, CHUNK), lambda j, m: (0, jnp.minimum(chunk1(j), 2 * per_part - 1))),
                single(x1.shape),
                single(g_middle1.shape),
                single(gain.shape),
                single(pattern.shape),
                pl.BlockSpec((1, width, CHUNK), joint_map),
                single(outer_scale.shape),
                single(second_gain.shape),
                single(mixer_scale.shape),
                pl.BlockSpec((1, CHUNK, width), lambda j, m: (0, chunk_feed(j), 0)),
                pl.BlockSpec((1, width, CHUNK), lambda j, m: (0, 0, chunk_feed(j))),
                pl.BlockSpec((rows, CHUNK), lambda j, m: (0, chunk_feed(j))),
                pl.BlockSpec((rows, CHUNK), lambda j, m: (0, jnp.minimum(chunk0(j), 2 * per_part - 1))),
            ]
            + [any_space] * 16
            + [single(vector1.shape)],
            out_specs=[vmem_space] * len(out_shape),
            scratch_shapes=[
                pltpu.VMEM((2, 2, rows, plan.n_pieces * CHUNK), bf16),
                pltpu.VMEM((2, 3, rows, plan.n_pieces * CHUNK), bf16),
                pltpu.VMEM((4, rows, 3 * half), bf16),
                pltpu.VMEM((4, rows, plan.hidden_half), bf16),
                pltpu.VMEM((half, 4 * rows), bf16),
                pltpu.VMEM((plan.hidden_half, 4 * rows), bf16),
                pltpu.VMEM(container, bf16),
                pltpu.VMEM((plan.ring, plan.deep, CHUNK), bf16),
                pltpu.VMEM((2 * plan.n_vector, n_vector_rows, width), f32),
                pltpu.VMEM((1, width, width), bf16),
                pltpu.VMEM((rows, width), f32),
                pltpu.VMEM((rows, width), f32),
                pltpu.VMEM((rows, width), f32),
                pltpu.VMEM((rows, 3 * width), bf16),
                pltpu.VMEM((rows, width), bf16),
                pltpu.VMEM((rows, width), f32),
                pltpu.VMEM((rows, width), f32),
                pltpu.VMEM((rows, width), bf16),
                pltpu.VMEM((rows, width), bf16),
                pltpu.VMEM((rows, 3 * width), f32),
                pltpu.VMEM((rows, width), f32),
            ]
            + [pltpu.VMEM((plan.ring, plan.chips >> (stage + 1)) + container[2:], bf16) for stage in range(plan.stages)]
            + [
                dma((8,)),
                dma((8,)),
                dma((4,)),
                dma((2, 3, plan.n_pieces)),
                dma((2, 3, plan.n_pieces)),
                dma((plan.stages, plan.ring)),
                dma((plan.stages, plan.ring)),
                dma((plan.ring,)),
                dma((plan.ring,)),
                dma((plan.n_vector,)),
                dma((plan.n_vector,)),
            ],
        ),
        compiler_params=pltpu.CompilerParams(
            collective_id=0, has_side_effects=True, vmem_limit_bytes=64 * 1024 * 1024 - 65536
        ),
        cost_estimate=pl.CostEstimate(flops=2 * rows * width * hidden * 20, bytes_accessed=60 * width * hidden, transcendentals=0),
    )(
        meta, back, pre1, x1, g_middle1, gain, pattern, joint, outer_scale, second_gain, mixer_scale, outer, inner, slope0, pre0,
        mixer, feed0, middle0, branch0, qkv0, x0, feed_g1, came1, *shares, vector1,
    )


def local(scenes, frames, tokens, patch_counts, first_gain, first_shift, joint_weight, joint_bias, query_gain, query_shift, key_gain, mixer_weight, mixer_bias, mixer_scale, second_gain, second_shift, inner_weight, inner_bias, outer_weight, outer_bias, outer_scale, cotangent):
    rows, width = tokens.shape[1:]
    half = rows // 2
    head = query_gain.shape[1]
    heads = width // head
    hidden = inner_weight.shape[2]
    chips = frames // 2
    scene = lax.axis_index("scene")
    frame = lax.axis_index("frame")
    core = lax.rem(frame, 2)
    meta = jnp.stack([scene, core, lax.rem(frame // 2, 2), patch_counts[0, 0]]).astype(jnp.int32)
    pattern = jnp.tile(
        jnp.stack([vector[block] for block in range(2) for vector in (query_gain, query_shift, key_gain)]).astype(f32),
        (1, SLAB // head),
    )

    x0 = tokens[0]
    feed_params = (mixer_weight, mixer_bias, mixer_scale, second_gain, second_shift, inner_weight, inner_bias, outer_weight, outer_bias, outer_scale)
    back_params = (outer_scale, second_gain, mixer_scale, outer_weight, inner_weight, mixer_weight)

    own0, other0, pre0, qkv0 = joint_forward(0, False, head, meta, x0, first_gain, first_shift, pattern, joint_weight, joint_bias)
    att0 = frame_forward(meta, qkv0)
    own_feed0, other_feed0, middle0, branch0, feed0, slope0, x1 = feed_forward(0, False, meta, att0, x0, *feed_params)
    own1, other1, pre1, pack1 = joint_forward(1, True, head, meta, x1, first_gain, first_shift, pattern, joint_weight, joint_bias)
    att1, kept1, att_full, att_log, (left_joint0, left_feed0, left_joint1) = scene_forward(
        frames, meta, pack1, half, [(own0, other0), (own_feed0, other_feed0), (own1, other1)]
    )
    own_feed1, other_feed1, middle1, branch1, feed1, slope1, layer_out = feed_forward(1, True, meta, att1, x1, *feed_params)

    g_feed1, g_middle1, g_att1, vector_feed1 = feed_backward(1, True, heads, meta, cotangent[0], feed1, slope1, middle1, branch1, *back_params)
    shared = SHARED_PIECES * CHUNK
    g_qkv1, came_feed1, (left_feed1,) = scene_backward(
        frames, meta, kept1, g_att1, att_full, att_log, half, [(own_feed1, other_feed1)], g_feed1, shared
    )
    g0, outer, inner, mixer, joint, vectors = rear(
        frames, head, meta, g_qkv1, pre1, x1, g_middle1, first_gain, pattern, joint_weight,
        outer_scale, second_gain, mixer_scale, outer_weight, inner_weight, slope0, pre0,
        mixer_weight, feed0, middle0, branch0, qkv0, x0, g_feed1, came_feed1,
        [own_feed1, left_feed1, own1, left_joint1, own_feed0, left_feed0, own0, left_joint0], vector_feed1,
    )
    vectors = vectors.reshape(2, -1, width)
    at_joint = vector_feed1.shape[0]

    def folded(index):
        return vectors[:, at_joint + index].reshape(2, heads, head).sum(1)

    return (
        layer_out[None],
        g0[None],
        vectors[:, at_joint],
        vectors[:, at_joint + 1],
        joint,
        vectors[:, at_joint + 2 : at_joint + 5].reshape(2, 3 * width),
        folded(5),
        folded(6),
        folded(7),
        mixer,
        vectors[:, 5],
        vectors[:, 4],
        vectors[:, 2],
        vectors[:, 3],
        inner,
        vectors[:, 6:at_joint].reshape(2, hidden),
        outer,
        vectors[:, 1],
        vectors[:, 0],
    )


def solution(mesh):
    tokens_spec = P("scene", "frame", None)
    shard = P(None, ("scene", "frame"), None)
    in_specs = (tokens_spec, P("scene", "frame")) + (P(),) * 17 + (tokens_spec,)
    out_specs = (
        tokens_spec, tokens_spec, P(), P(), shard, P(), P(), P(), P(), shard,
        P(), P(), P(), P(), shard, P(), shard, P(), P(),
    )
    body = partial(local, mesh.shape["scene"], mesh.shape["frame"])
    return jax.shard_map(body, mesh=mesh, in_specs=in_specs, out_specs=out_specs, check_vma=False)
```

```python
from functools import partial

import jax
import jax.numpy as jnp
from jax import lax
from jax.experimental import pallas as pl
from jax.experimental.pallas import tpu as pltpu
from jax.sharding import PartitionSpec as P

SPECIAL = 5
CHUNK = 512
LANES = 128
SLAB = 256
SHARED_PIECES = 3
SWAP_EVERY = 3
AHEAD = 2
LAG = 3
VECTOR_LAG = 3
norm_eps = 1e-06
head_eps = 1e-05
closed_score = -10000.0
f32 = jnp.float32
bf16 = jnp.bfloat16


def nn(a, b):
    return lax.dot_general(a, b, (((1,), (0,)), ((), ())), preferred_element_type=f32)


def nt(a, b):
    return lax.dot_general(a, b, (((1,), (1,)), ((), ())), preferred_element_type=f32)


def tn(a, b):
    return lax.dot_general(a, b, (((0,), (0,)), ((), ())), preferred_element_type=f32)


def row(ref, index):
    return ref[...].astype(f32)[index : index + 1, :]


def col_sum(value):
    return jnp.sum(value, axis=0, keepdims=True)


def center_norm(value, eps):
    centered = value - jnp.mean(value, axis=-1, keepdims=True)
    spread = lax.rsqrt(jnp.mean(centered * centered, axis=-1, keepdims=True) + eps)
    return centered * spread, spread


def norm_back(grad_hat, hat, spread):
    mean_grad = jnp.mean(grad_hat, axis=-1, keepdims=True)
    mean_both = jnp.mean(grad_hat * hat, axis=-1, keepdims=True)
    return spread * (grad_hat - mean_grad - hat * mean_both)


def seg_matrix(width, head, value):
    shift = head.bit_length() - 1
    first = lax.shift_right_logical(lax.broadcasted_iota(jnp.int32, (width, width), 0), shift)
    second = lax.shift_right_logical(lax.broadcasted_iota(jnp.int32, (width, width), 1), shift)
    return jnp.where(first == second, value, 0.0).astype(bf16)


def seg_dot(value, matrix):
    high = value.astype(bf16)
    low = (value - high.astype(f32)).astype(bf16)
    return nn(high, matrix) + nn(low, matrix)


def seg_norm(value, mean_matrix):
    centered = value - seg_dot(value, mean_matrix)
    spread = lax.rsqrt(seg_dot(centered * centered, mean_matrix) + head_eps)
    return centered * spread, spread


def first_lanes(rows):
    return lax.broadcasted_iota(jnp.int32, (rows, LANES), 1) < LANES // 2


def turn(value):
    return pltpu.roll(value, LANES // 2, value.ndim - 1)


def pack_pair(slab):
    half = slab.shape[0] // 2
    top, bottom = slab[:half], slab[half:]
    low = first_lanes(half)
    return jnp.where(low, top, turn(bottom)), jnp.where(low, turn(top), bottom)


def unpack_pair(even, odd):
    low = first_lanes(even.shape[0])
    top = jnp.where(low, even, turn(odd))
    bottom = jnp.where(low, turn(even), odd)
    return jnp.concatenate([top, bottom], axis=0)


def erf(value):
    value = jnp.clip(value, -4.0, 4.0)
    square = value * value
    top = jnp.full_like(square, -2.72614225801306e-10)
    for coefficient in (
        2.77068142495902e-08,
        -2.10102402082508e-06,
        -5.69250639462346e-05,
        -7.34990630326855e-04,
        -2.95459980854025e-03,
        -1.60960333262415e-02,
    ):
        top = top * square + coefficient
    bottom = jnp.full_like(square, -1.45660718464996e-05)
    for coefficient in (
        -2.13374055278905e-04,
        -1.68282697438203e-03,
        -7.37332916720468e-03,
        -1.42647390514189e-02,
    ):
        bottom = bottom * square + coefficient
    return value * top / bottom


def full(shape):
    return pl.BlockSpec(shape, lambda *_: (0,) * len(shape))


def sds(shape, dtype):
    return jax.ShapeDtypeStruct(shape, dtype)


def call(body, name, grid, in_specs, out_specs, out_shape, scratch, flops, moved):
    return pl.pallas_call(
        body,
        name=name,
        out_shape=out_shape,
        grid_spec=pltpu.PrefetchScalarGridSpec(
            num_scalar_prefetch=1,
            grid=grid,
            in_specs=in_specs,
            out_specs=out_specs,
            scratch_shapes=scratch,
        ),
        cost_estimate=pl.CostEstimate(flops=flops, bytes_accessed=moved, transcendentals=0),
    )


def joint_body(
    block, packed, head, meta, x_ref, gain_ref, shift_ref, pattern_ref, w_ref, b_ref,
    own_ref, other_ref, pre_ref, out_ref, normed_ref, *stage
):
    step = pl.program_id(0)
    rows, width = normed_ref.shape
    per_part = width // CHUNK
    half = rows // 2

    @pl.when(step == 0)
    def _():
        hat, _ = center_norm(x_ref[...].astype(f32), norm_eps)
        normed = (hat * row(gain_ref, block) + row(shift_ref, block)).astype(bf16)
        normed_ref[...] = normed

        @pl.when(meta[0] == 0)
        def _():
            own_ref[...] = normed[:, : width // 2]
            other_ref[...] = normed[:, width // 2 :]

        @pl.when(meta[0] != 0)
        def _():
            own_ref[...] = normed[:, width // 2 :]
            other_ref[...] = normed[:, : width // 2]

        if packed:
            count = jnp.full((8, LANES), meta[3], jnp.int32).astype(f32)
            for place in range(stage[0].shape[0]):
                stage[0][place, 3 * half : 3 * half + 8, :] = count

    joined = nn(normed_ref[...], w_ref[0]) + row(b_ref, block)
    pattern = pattern_ref[...]

    def emit(part, values):
        if packed:
            base = (step - part * per_part) * (CHUNK // head)
            for slab in range(CHUNK // LANES):
                even, odd = pack_pair(values[:, slab * LANES : (slab + 1) * LANES])
                stage[0][base + 2 * slab, part * half : (part + 1) * half, :] = even
                stage[0][base + 2 * slab + 1, part * half : (part + 1) * half, :] = odd
        else:
            out_ref[...] = values.astype(bf16)

    def normed_heads(gain, shift):
        mean_matrix = seg_matrix(SLAB, head, 1.0 / head)
        pieces = []
        for slab in range(CHUNK // SLAB):
            hat, _ = seg_norm(joined[:, slab * SLAB : (slab + 1) * SLAB], mean_matrix)
            pieces.append(hat * gain if shift is None else hat * gain + shift)
        return jnp.concatenate(pieces, axis=1)

    scale = head ** (-0.5)

    @pl.when(step < per_part)
    def _():
        pre_ref[...] = joined
        emit(0, normed_heads(
            pattern[3 * block : 3 * block + 1] * scale,
            pattern[3 * block + 1 : 3 * block + 2] * scale,
        ))

    @pl.when((step >= per_part) & (step < 2 * per_part))
    def _():
        pre_ref[...] = joined
        emit(1, normed_heads(pattern[3 * block + 2 : 3 * block + 3], None))

    @pl.when(step >= 2 * per_part)
    def _():
        emit(2, joined)

    if packed:

        @pl.when(step == 3 * per_part - 1)
        def _():
            out_ref[...] = stage[0][...].astype(bf16)


def joint_forward(block, packed, head, meta, x, gain, shift, pattern, weight, bias):
    rows, width = x.shape
    per_part = width // CHUNK
    heads = width // head
    packed_rows = 3 * (rows // 2) + 8
    if packed:
        out_spec, out = full((heads, packed_rows, LANES)), sds((heads, packed_rows, LANES), bf16)
        extra = [pltpu.VMEM((heads, packed_rows, LANES), f32)]
    else:
        out_spec = pl.BlockSpec((rows, CHUNK), lambda j, m: (0, j))
        out = sds((rows, 3 * width), bf16)
        extra = []
    return call(
        partial(joint_body, block, packed, head),
        f"joint_forward_{block}",
        (3 * per_part,),
        [
            full((rows, width)),
            full(gain.shape),
            full(shift.shape),
            full(pattern.shape),
            pl.BlockSpec((1, width, CHUNK), lambda j, m: (block, 0, j)),
            pl.BlockSpec((2, CHUNK), lambda j, m: (0, j)),
        ],
        [
            full((rows, width // 2)),
            full((rows, width // 2)),
            pl.BlockSpec((rows, CHUNK), lambda j, m: (0, jnp.minimum(j, 2 * per_part - 1))),
            out_spec,
        ],
        [
            sds((rows, width // 2), bf16),
            sds((rows, width // 2), bf16),
            sds((rows, 2 * width), f32),
            out,
        ],
        [pltpu.VMEM((rows, width), bf16)] + extra,
        2 * rows * width * 3 * width,
        6 * width * width + 16 * rows * width,
    )(meta, x, gain, shift, pattern, weight, bias)


def lane_picks():
    lane = lax.broadcasted_iota(jnp.int32, (1, LANES), 1)
    low = jnp.where(lane < LANES // 2, 1.0, 0.0)
    return low.astype(bf16), (1.0 - low).astype(bf16)


def open_row(meta, rows):
    place = lax.broadcasted_iota(jnp.int32, (1, rows), 1)
    return jnp.where(place < meta[3] + SPECIAL, 0.0, closed_score)


def frame_body(meta, qkv_ref, out_ref):
    rows, width = out_ref.shape
    bias = open_row(meta, rows)
    picks = lane_picks()
    low = first_lanes(rows)
    for slab in range(width // LANES):
        at = slab * LANES
        queries = qkv_ref[:, at : at + LANES]
        keys = qkv_ref[:, width + at : width + at + LANES]
        values = qkv_ref[:, 2 * width + at : 2 * width + at + LANES]
        results = []
        for pick in picks:
            power = jnp.exp(nt(queries * pick, keys) + bias)
            probs = power / jnp.sum(power, axis=-1, keepdims=True)
            results.append(nn(probs.astype(bf16), values))
        out_ref[:, at : at + LANES] = jnp.where(low, results[0], results[1]).astype(bf16)


def frame_forward(meta, qkv):
    rows = qkv.shape[0]
    width = qkv.shape[1] // 3
    return call(
        frame_body,
        "frame_forward",
        (1,),
        [full(qkv.shape)],
        full((rows, width)),
        sds((rows, width), bf16),
        [],
        4 * rows * rows * width,
        8 * rows * width,
    )(meta, qkv)


def frame_back_slab(at, meta, qkv_ref, grad_ref, out_ref):
    rows, width = grad_ref.shape
    bias = open_row(meta, rows)
    scale = (LANES // 2) ** (-0.5)

    def lanes(part):
        return pl.ds(pl.multiple_of(part * width + at, LANES), LANES)

    queries = qkv_ref[:, lanes(0)]
    keys = qkv_ref[:, lanes(1)]
    values = qkv_ref[:, lanes(2)]
    grads = grad_ref[:, lanes(0)]
    found = []
    for pick in lane_picks():
        power = jnp.exp(nt(queries * pick, keys) + bias)
        probs = power / jnp.sum(power, axis=-1, keepdims=True)
        grad_probs = nt(grads * pick, values)
        delta = jnp.sum(probs * grad_probs, axis=-1, keepdims=True)
        grad_scores = (probs * (grad_probs - delta)).astype(bf16)
        found.append((
            nn(grad_scores, keys) * scale,
            tn(grad_scores, queries),
            tn(probs.astype(bf16), grads),
        ))
    low = first_lanes(rows)
    for part in range(3):
        out_ref[:, lanes(part)] = jnp.where(low, found[0][part], found[1][part])


def packed_part(value, part, half):
    whole = value.astype(f32)
    return whole[:, part * half : (part + 1) * half, :].reshape(-1, LANES)


def open_slots(value, half):
    count = value.astype(f32)[:, 3 * half : 3 * half + 8, :]
    count = jnp.concatenate([count] * (half // 8), axis=1)
    place = lax.broadcasted_iota(jnp.int32, count.shape, 1).astype(f32)
    return (
        (place < count + SPECIAL).reshape(-1, LANES),
        (place + half < count + SPECIAL).reshape(-1, LANES),
    )


MESH = pl.DeviceIdType.MESH


def peers_of(frames):
    scene = lax.axis_index("scene")
    frame = lax.axis_index("frame")
    bits = []
    bit = 1
    while bit < frames:
        value = lax.rem(frame // bit, 2)
        bits.append((value, (scene, frame + bit * (1 - 2 * value))))
        bit *= 2
    core, core_peer = bits[0]
    scene_peer = (1 - scene, frame)
    cross_peer = (1 - scene, core_peer[1])
    return core, core_peer, scene_peer, cross_peer, bits[1:]


def enter(targets):
    barrier = pltpu.get_barrier_semaphore()
    for target in targets:
        pl.semaphore_signal(barrier, inc=1, device_id=target, device_id_type=MESH)
    pl.semaphore_wait(barrier, len(targets))


def enter_scene(frames):
    barrier = pltpu.get_barrier_semaphore()
    _, _, scene_peer, cross_peer, _ = peers_of(frames)
    scene = lax.axis_index("scene")
    frame = lax.axis_index("frame")
    for target in (scene_peer, cross_peer):
        pl.semaphore_signal(barrier, inc=1, device_id=target, device_id_type=MESH)

    @pl.loop(1, frames)
    def _(offset):
        pl.semaphore_signal(
            barrier, inc=1, device_id=(scene, lax.rem(frame + offset, frames)), device_id_type=MESH
        )

    pl.semaphore_wait(barrier, frames + 1)


def remote(source, target, send, recv, device):
    return pltpu.make_async_remote_copy(
        src_ref=source, dst_ref=target, send_sem=send, recv_sem=recv, device_id=device, device_id_type=MESH
    )


class Share:
    def __init__(self, frames, pairs, outs, send, recv):
        _, core_peer, scene_peer, _, _ = peers_of(frames)
        self.first, self.second = [], []
        for index, ((own, other), out) in enumerate(zip(pairs, outs)):
            self.first.append(remote(other, out.at[0], send.at[3 * index], recv.at[3 * index], scene_peer))
            self.first.append(remote(own, out.at[1], send.at[3 * index + 1], recv.at[3 * index + 1], core_peer))
            self.second.append(
                remote(out.at[0], out.at[2], send.at[3 * index + 2], recv.at[3 * index + 2], core_peer)
            )

    def start(self):
        for copy in self.first:
            copy.start()

    def relay(self):
        for index, copy in enumerate(self.second):
            self.first[2 * index].wait_recv()
            copy.start()

    def close(self):
        for index, copy in enumerate(self.second):
            self.first[2 * index].wait_send()
            self.first[2 * index + 1].wait()
            copy.wait()


def scene_body(
    frames, half, span, n_share, meta, pack_ref, *refs
):
    heads = pack_ref.shape[0]
    pairs = [(refs[2 * index], refs[2 * index + 1]) for index in range(n_share)]
    refs = refs[2 * n_share :]
    att_ref, kept_ref, out_ref, log_ref = refs[:4]
    outs, refs = refs[4 : 4 + n_share], refs[4 + n_share :]
    queries, keys, values, sent, a_send, a_recv, b_send, b_recv, s_send, s_recv, own_sem = refs
    n = queries.shape[0] // 2
    m = keys.shape[0] // 2
    scene = lax.axis_index("scene")
    frame = lax.axis_index("frame")
    part = frame // heads
    own = pltpu.make_async_copy(pack_ref.at[lax.rem(frame, heads)], kept_ref.at[frame], own_sem)
    own.start()
    share = Share(frames, pairs, outs, s_send, s_recv)
    enter_scene(frames)

    def to_head(offset):
        target = lax.rem(frame + offset, frames)
        return remote(
            pack_ref.at[lax.rem(target, heads)], kept_ref.at[frame], a_send.at[offset], a_recv.at[offset], (scene, target)
        )

    @pl.loop(1, frames)
    def _(offset):
        to_head(offset).start()

    share.start()
    own.wait()

    @pl.loop(1, frames)
    def _(offset):
        to_head(offset).wait_recv()

    first = pl.multiple_of(part * heads, heads)
    q = packed_part(kept_ref[pl.ds(first, heads)], 0, half)
    low_n, low_m = first_lanes(n), first_lanes(m)
    queries[:n, :] = jnp.where(low_n, q, 0.0).astype(bf16)
    queries[n:, :] = jnp.where(low_n, turn(q), 0.0).astype(bf16)
    k = packed_part(kept_ref[...], 1, half)
    keys[:m, :] = k.astype(bf16)
    keys[m:, :] = turn(k).astype(bf16)
    v = packed_part(kept_ref[...], 2, half)
    open_low, open_high = open_slots(kept_ref[...], half)
    values[:m, :] = jnp.where(open_low, jnp.where(low_m, v, 1.0), 0.0).astype(bf16)
    values[m:, :] = jnp.where(open_high, jnp.where(low_m, turn(v), 1.0), 0.0).astype(bf16)
    low = first_lanes(LANES)

    pair = 2 * half
    place = lax.rem(frame, heads)
    low = first_lanes(pair)
    pieces = heads // 2

    def from_head(target):
        return remote(
            sent.at[target], att_ref.at[place], b_send.at[target], b_recv.at[place], (scene, part * heads + target)
        )

    def turned(piece):
        return lax.rem(piece + place // 2 + 1, pieces)

    def send(piece):
        for index in range(2):
            target = 2 * turned(piece) + index

            @pl.when(target != place)
            def _():
                from_head(target).start()

    @pl.loop(0, pieces)
    def _(piece):
        @pl.when(piece > 0)
        def _():
            send(piece - 1)

        at = pl.multiple_of(turned(piece) * pair, pair)
        some = jnp.concatenate([queries[pl.ds(at, pair), :], queries[pl.ds(n + at, pair), :]], axis=0)
        total = jnp.zeros((2 * pair, LANES), f32)
        for start in range(0, 2 * m, span):
            power = jnp.exp(nt(some, keys[start : start + span, :])).astype(bf16)
            total = total + nn(power, values[start : start + span, :])
        first, second = total[:pair], total[pair:]
        bottom = jnp.where(low, turn(first), second)
        result = jnp.where(low, first, turn(second)) / bottom
        sent[pl.ds(2 * turned(piece), 2)] = result.reshape(2, half, LANES).astype(bf16)
        out_ref[pl.ds(at, pair), :] = result
        log_ref[pl.ds(at, pair), :] = jnp.log(bottom)

    share.relay()
    send(pieces - 1)
    att_ref[place] = sent[place]

    @pl.loop(1, frames)
    def _(offset):
        to_head(offset).wait_send()

    @pl.loop(1, heads)
    def _(offset):
        other = lax.rem(place + offset, heads)
        from_head(other).wait_send()
        remote(
            sent.at[other], att_ref.at[other], b_send.at[other], b_recv.at[other], (scene, part * heads + other)
        ).wait_recv()

    share.close()


any_space = pl.BlockSpec(memory_space=pl.ANY)
vmem_space = pl.BlockSpec(memory_space=pltpu.VMEM)
dma = pltpu.SemaphoreType.DMA


def scene_forward(frames, meta, pack, half, pairs):
    heads = pack.shape[0]
    n = heads * half
    m = frames * half
    span = m // 2
    while span > 640:
        span = span // 2
    flat = [value for pair in pairs for value in pair]
    results = pl.pallas_call(
        partial(scene_body, frames, half, span, len(pairs)),
        name="scene_forward",
        out_shape=[
            sds((heads, half, LANES), bf16),
            sds((frames,) + pack.shape[1:], bf16),
            sds((n, LANES), f32),
            sds((n, LANES), f32),
        ]
        + [sds((3,) + own.shape, bf16) for own, _ in pairs],
        grid_spec=pltpu.PrefetchScalarGridSpec(
            num_scalar_prefetch=1,
            grid=(1,),
            in_specs=[vmem_space] + [any_space] * len(flat),
            out_specs=[vmem_space] * 4 + [any_space] * len(pairs),
            scratch_shapes=[
                pltpu.VMEM((2 * n, LANES), bf16),
                pltpu.VMEM((2 * m, LANES), bf16),
                pltpu.VMEM((2 * m, LANES), bf16),
                pltpu.VMEM((heads, half, LANES), bf16),
                dma((frames,)),
                dma((frames,)),
                dma((heads,)),
                dma((heads,)),
                dma((3 * len(pairs),)),
                dma((3 * len(pairs),)),
                dma(()),
            ],
        ),
        compiler_params=pltpu.CompilerParams(collective_id=1, has_side_effects=True),
        cost_estimate=pl.CostEstimate(flops=16 * n * m * LANES, bytes_accessed=20 * n * LANES, transcendentals=0),
    )(meta, pack, *flat)
    return results[0], results[1], results[2], results[3], results[4:]


def three_lanes(value, closed):
    lane = lax.broadcasted_iota(jnp.int32, value.shape, 1)
    base = LANES // 2
    high = value.astype(bf16).astype(f32)
    rest = value - high
    middle = rest.astype(bf16).astype(f32)
    last = rest - middle
    result = jnp.where(lane == base, high, jnp.where(lane == base + 1, middle, last))
    return jnp.where(lane < base + 3, result, jnp.where(lane == base + 3, closed, 0.0))


def gradient_copies(frames, own, came, send, recv, lanes):
    core, core_peer, scene_peer, cross_peer, _ = peers_of(frames)
    targets = ((core, scene_peer), (1 - core, core_peer), (1 - core, cross_peer))
    return [
        remote(own.at[side, :, lanes], came.at[which, :, lanes], send.at[which], recv.at[which], peer)
        for which, (side, peer) in enumerate(targets)
    ]


def scene_back_body(frames, half, span, n_share, shared, meta, kept_ref, grad_ref, out_ref, log_ref, feed_ref, *refs):
    heads = grad_ref.shape[0]
    pairs = [(refs[2 * index], refs[2 * index + 1]) for index in range(n_share)]
    refs = refs[2 * n_share :]
    back_ref, feed_came, outs, refs = refs[0], refs[1], refs[2 : 2 + n_share], refs[2 + n_share :]
    queries, keys, values, grads, turned, came, sent_q, sent_kv = refs[:8]
    a_send, a_recv, b_send, b_recv, c_send, c_recv, s_send, s_recv, g_send, g_recv = refs[8:]
    n = queries.shape[0] // 2
    m = keys.shape[0] // 2
    scene = lax.axis_index("scene")
    frame = lax.axis_index("frame")
    part = frame // heads
    place = lax.rem(frame, heads)
    share = Share(frames, pairs, outs, s_send, s_recv)
    feed_copies = gradient_copies(frames, feed_ref, feed_came, g_send, g_recv, pl.ds(0, shared))
    enter_scene(frames)

    def to_head(offset):
        target = lax.rem(place + offset, heads)
        return remote(
            grad_ref.at[target], came.at[place], a_send.at[offset], a_recv.at[offset], (scene, part * heads + target)
        )

    @pl.loop(1, heads)
    def _(offset):
        to_head(offset).start()

    share.start()
    for copy in feed_copies:
        copy.start()
    came[place] = grad_ref[place]
    first = pl.multiple_of(part * heads, heads)
    low_n, low_m = first_lanes(n), first_lanes(m)
    base = LANES // 2
    q = packed_part(kept_ref[pl.ds(first, heads)], 0, half)
    log = -log_ref[...]
    queries[:n, :] = jnp.where(low_n, q, three_lanes(turn(log), closed_score)).astype(bf16)
    queries[n:, :] = jnp.where(low_n, turn(q), three_lanes(log, closed_score)).astype(bf16)
    lane = lax.broadcasted_iota(jnp.int32, (m, LANES), 1)
    ones = jnp.where(lane < base + 3, 1.0, 0.0)
    open_low, open_high = open_slots(kept_ref[...], half)
    k = packed_part(kept_ref[...], 1, half)
    for place_at, k_now, is_open in ((0, k, open_low), (m, turn(k), open_high)):
        tail = jnp.where((lane == base + 3) & jnp.logical_not(is_open), 1.0, ones)
        keys[place_at : place_at + m, :] = jnp.where(low_m, k_now, tail).astype(bf16)
    v = packed_part(kept_ref[...], 2, half)
    values[:m, :] = jnp.where(low_m, v, ones).astype(bf16)
    values[m:, :] = jnp.where(low_m, turn(v), ones).astype(bf16)
    turned[...] = jnp.zeros_like(turned)
    low = first_lanes(LANES)

    @pl.loop(1, heads)
    def _(offset):
        to_head(offset).wait_recv()

    g = came[...].astype(f32).reshape(n, LANES)
    delta = -seg_dot(g * out_ref[...], seg_matrix(LANES, base, 1.0))
    grads[:n, :] = jnp.where(low_n, g, three_lanes(turn(delta), 0.0)).astype(bf16)
    grads[n:, :] = jnp.where(low_n, turn(g), three_lanes(delta, 0.0)).astype(bf16)

    pair = 2 * half
    low_pair = first_lanes(pair)
    pieces = frames // 2

    def back_kv(target):
        return remote(
            sent_kv.at[target], back_ref.at[frame, pl.ds(1, 2)], b_send.at[target], b_recv.at[frame], (scene, target)
        )

    def turned_to(piece):
        return lax.rem(piece + frame // 2 + 1, pieces)

    def send(piece):
        for index in range(2):
            target = 2 * turned_to(piece) + index

            @pl.when(target != frame)
            def _():
                back_kv(target).start()

    @pl.loop(0, pieces)
    def _(piece):
        @pl.when(piece > 0)
        def _():
            send(piece - 1)

        at = pl.multiple_of(turned_to(piece) * pair, pair)
        key_part = jnp.concatenate([keys[pl.ds(at, pair), :], keys[pl.ds(m + at, pair), :]], axis=0)
        value_part = jnp.concatenate([values[pl.ds(at, pair), :], values[pl.ds(m + at, pair), :]], axis=0)
        key_turned = jnp.transpose(key_part.astype(f32)).astype(bf16)
        dk = jnp.zeros((2 * pair, LANES), f32)
        dv = jnp.zeros((2 * pair, LANES), f32)
        for start in range(0, 2 * n, span):
            some = queries[start : start + span, :]
            some_grads = grads[start : start + span, :]
            probs = jnp.exp(nt(key_part, some))
            grad_scores = (probs * nt(value_part, some_grads)).astype(bf16)
            dv = dv + nn(probs.astype(bf16), some_grads)
            dk = dk + nn(grad_scores, some)
            turned[:, start : start + span] += nn(key_turned, grad_scores)
        dk = jnp.where(low_pair, dk[:pair], turn(dk[pair:])).reshape(2, half, LANES)
        dv = jnp.where(low_pair, dv[:pair], turn(dv[pair:])).reshape(2, half, LANES)
        sent_kv[pl.ds(2 * turned_to(piece), 2), 0] = dk.astype(bf16)
        sent_kv[pl.ds(2 * turned_to(piece), 2), 1] = dv.astype(bf16)

    share.relay()
    send(pieces - 1)

    scale = base ** (-0.5)
    rows = []
    for at in range(0, n, LANES):
        first = jnp.transpose(turned[:, at : at + LANES])
        second = jnp.transpose(turned[:, n + at : n + at + LANES])
        rows.append(jnp.where(low, first, turn(second)) * scale)
    sent_q[...] = jnp.concatenate(rows, axis=0).reshape(heads, half, LANES).astype(bf16)

    def back_q(offset):
        target = lax.rem(place + offset, heads)
        return remote(
            sent_q.at[target], back_ref.at[frame, 0], c_send.at[offset], c_recv.at[offset], (scene, part * heads + target)
        )

    back_ref[frame, 1] = sent_kv[frame, 0]
    back_ref[frame, 2] = sent_kv[frame, 1]

    @pl.loop(1, heads)
    def _(offset):
        back_q(offset).start()

    back_ref[frame, 0] = sent_q[place]

    @pl.loop(1, heads)
    def _(offset):
        to_head(offset).wait_send()

    @pl.loop(1, frames)
    def _(offset):
        other = lax.rem(frame + offset, frames)
        back_kv(other).wait_send()
        remote(
            sent_kv.at[other], back_ref.at[other, pl.ds(1, 2)], b_send.at[other], b_recv.at[other], (scene, other)
        ).wait_recv()

    @pl.loop(1, heads)
    def _(offset):
        back_q(offset).wait()

    share.close()
    for copy in feed_copies:
        copy.wait()


def scene_backward(frames, meta, kept, grad, out, log, half, pairs, feed_grads, shared):
    heads = grad.shape[0]
    n = heads * half
    m = frames * half
    span = n // 2
    while span > 640:
        span = span // 2
    flat = [value for pair in pairs for value in pair]
    results = pl.pallas_call(
        partial(scene_back_body, frames, half, span, len(pairs), shared),
        name="scene_backward",
        out_shape=[sds((frames, 3, half, LANES), bf16), sds((3,) + feed_grads.shape[1:], bf16)]
        + [sds((3,) + own.shape, bf16) for own, _ in pairs],
        grid_spec=pltpu.PrefetchScalarGridSpec(
            num_scalar_prefetch=1,
            grid=(1,),
            in_specs=[vmem_space] * 4 + [any_space] * (1 + len(flat)),
            out_specs=[vmem_space] + [any_space] * (1 + len(pairs)),
            scratch_shapes=[
                pltpu.VMEM((2 * n, LANES), bf16),
                pltpu.VMEM((2 * m, LANES), bf16),
                pltpu.VMEM((2 * m, LANES), bf16),
                pltpu.VMEM((2 * n, LANES), bf16),
                pltpu.VMEM((LANES, 2 * n), f32),
                pltpu.VMEM((heads, half, LANES), bf16),
                pltpu.VMEM((heads, half, LANES), bf16),
                pltpu.VMEM((frames, 2, half, LANES), bf16),
                dma((heads,)),
                dma((heads,)),
                dma((frames,)),
                dma((frames,)),
                dma((heads,)),
                dma((heads,)),
                dma((3 * len(pairs),)),
                dma((3 * len(pairs),)),
                dma((3,)),
                dma((3,)),
            ],
        ),
        compiler_params=pltpu.CompilerParams(collective_id=2, has_side_effects=True),
        cost_estimate=pl.CostEstimate(flops=40 * n * m * LANES, bytes_accessed=30 * n * LANES, transcendentals=0),
    )(meta, kept, grad, out, log, feed_grads, *flat)
    back = results[0]
    if frames > heads:
        place = lax.axis_index("frame") // heads * heads
        dq = lax.dynamic_slice(back, (place, 0, 0, 0), (heads, 1, half, LANES))
        both = back.reshape(frames // heads, heads, 3, half, LANES)[:, :, 1:].astype(f32).sum(0)
        back = jnp.concatenate([dq, both.astype(bf16)], axis=1)
    return back, results[1], results[2:]


def feed_body(
    block, packed, meta, att_ref, x_ref, mixer_ref, mixer_bias, mixer_scale, gain_ref, shift_ref,
    inner_ref, inner_bias, outer_ref, outer_bias, outer_scale,
    own_ref, other_ref, middle_ref, branch_ref, feed_ref, slope_ref, out_ref, normed_ref, total_ref
):
    step = pl.program_id(0)
    steps = pl.num_programs(0)
    rows, width = middle_ref.shape
    hidden_half = own_ref.shape[1] - width
    half_steps = hidden_half // CHUNK
    mine = meta[0]

    def split(value, at):
        first, second = value[:, : width // 2], value[:, width // 2 :]

        @pl.when(mine == 0)
        def _():
            own_ref[:, at : at + width // 2] = first
            other_ref[:, at : at + width // 2] = second

        @pl.when(mine != 0)
        def _():
            own_ref[:, at : at + width // 2] = second
            other_ref[:, at : at + width // 2] = first

    @pl.when(step == 0)
    def _():
        if packed:
            pieces = []
            for pair in range(width // LANES):
                pieces.append(
                    unpack_pair(att_ref[2 * pair].astype(f32), att_ref[2 * pair + 1].astype(f32))
                )
            attended = jnp.concatenate(pieces, axis=1).astype(bf16)
        else:
            attended = att_ref[...]
        branch = nn(attended, mixer_ref[0]) + row(mixer_bias, block)
        middle = x_ref[...].astype(f32) + row(mixer_scale, block) * branch
        hat, _ = center_norm(middle, norm_eps)
        normed = (hat * row(gain_ref, block) + row(shift_ref, block)).astype(bf16)
        branch_ref[...] = branch
        middle_ref[...] = middle
        normed_ref[...] = normed
        split(normed, hidden_half)
        split(attended, hidden_half + width // 2)
        total_ref[...] = jnp.zeros_like(total_ref)

    pre = nn(normed_ref[...], inner_ref[0]) + row(inner_bias, block)
    share = 0.5 * (1.0 + erf(pre * (2.0 ** (-0.5))))
    slope_ref[...] = share + pre * jnp.exp(-0.5 * pre * pre) * 0.3989422804014327
    hidden = (pre * share).astype(bf16)
    place = pl.multiple_of(lax.rem(step, half_steps) * CHUNK, CHUNK)

    @pl.when(step // half_steps == mine)
    def _():
        own_ref[:, pl.ds(place, CHUNK)] = hidden

    @pl.when(step // half_steps != mine)
    def _():
        other_ref[:, pl.ds(place, CHUNK)] = hidden

    total_ref[...] += nn(hidden, outer_ref[0])

    @pl.when(step == steps - 1)
    def _():
        feed = total_ref[...] + row(outer_bias, block)
        feed_ref[...] = feed
        result = middle_ref[...] + row(outer_scale, block) * feed
        if packed:
            place = lax.broadcasted_iota(jnp.int32, result.shape, 0)
            result = jnp.where(place < meta[3] + SPECIAL, result, 0.0)
        out_ref[...] = result.astype(out_ref.dtype)


def feed_forward(block, packed, meta, att, x, mixer, mixer_bias, mixer_scale, gain, shift, inner, inner_bias, outer, outer_bias, outer_scale):
    rows, width = x.shape
    hidden = inner.shape[2]
    kept = hidden // 2 + width
    steps = hidden // CHUNK
    vector = full(gain.shape)
    return call(
        partial(feed_body, block, packed),
        f"feed_forward_{block}",
        (steps,),
        [
            full(att.shape),
            full((rows, width)),
            pl.BlockSpec((1, width, width), lambda j, m: (block, 0, 0)),
            vector, vector, vector, vector,
            pl.BlockSpec((1, width, CHUNK), lambda j, m: (block, 0, j)),
            pl.BlockSpec((2, CHUNK), lambda j, m: (0, j)),
            pl.BlockSpec((1, CHUNK, width), lambda j, m: (block, j, 0)),
            vector, vector,
        ],
        [full((rows, kept))] * 2
        + [full((rows, width))] * 3
        + [pl.BlockSpec((rows, CHUNK), lambda j, m: (0, j)), full((rows, width))],
        [sds((rows, kept), bf16)] * 2
        + [sds((rows, width), f32)] * 3
        + [sds((rows, hidden), f32), sds((rows, width), bf16 if packed else f32)],
        [pltpu.VMEM((rows, width), bf16), pltpu.VMEM((rows, width), f32)],
        2 * rows * width * (2 * hidden + width),
        4 * width * hidden + 4 * rows * hidden + 30 * rows * width,
    )(meta, att, x, mixer, mixer_bias, mixer_scale, gain, shift, inner, inner_bias, outer, outer_bias, outer_scale)


def feed_back_core(
    block, packed, step, steps, chunk, meta, g_ref, feed_ref, slope_ref, middle_ref, branch_ref,
    outer_scale, gain_ref, mixer_scale, outer_ref, inner_ref, mixer_ref,
    grads_ref, g_middle_ref, g_att_ref, vector_ref, g_feed_ref, total_ref
):
    rows, width = total_ref.shape
    half_steps = steps // 2
    at_branch = width // 2 + half_steps * CHUNK

    def incoming():
        g = g_ref[...].astype(f32)
        if packed:
            place = lax.broadcasted_iota(jnp.int32, g.shape, 0)
            g = jnp.where(place < meta[3] + SPECIAL, g, 0.0)
        return g

    @pl.when(step == 0)
    def _():
        g = incoming()
        g_feed = (g * row(outer_scale, block)).astype(bf16)
        g_feed_ref[...] = g_feed
        grads_ref[0, :, : width // 2] = g_feed[:, : width // 2]
        grads_ref[1, :, : width // 2] = g_feed[:, width // 2 :]
        vector_ref[0:1, :] = col_sum(g * feed_ref[...])
        vector_ref[1:2, :] = col_sum(g_feed.astype(f32))
        total_ref[...] = jnp.zeros_like(total_ref)

    g_pre = (nt(g_feed_ref[...], outer_ref[0]) * slope_ref[...]).astype(bf16)
    place = pl.multiple_of(width // 2 + lax.rem(chunk, half_steps) * CHUNK, CHUNK)
    grads_ref[chunk // half_steps, :, pl.ds(place, CHUNK)] = g_pre
    per_row = width // CHUNK
    lanes = pl.ds(pl.multiple_of(lax.rem(chunk, per_row) * CHUNK, CHUNK), CHUNK)
    vector_ref[pl.ds(6 + chunk // per_row, 1), lanes] = col_sum(g_pre.astype(f32))
    total_ref[...] += nt(g_pre, inner_ref[0])

    @pl.when(step == steps - 1)
    def _():
        hat, spread = center_norm(middle_ref[...], norm_eps)
        g_nm = total_ref[...]
        vector_ref[2:3, :] = col_sum(g_nm * hat)
        vector_ref[3:4, :] = col_sum(g_nm)
        g_middle = incoming() + norm_back(g_nm * row(gain_ref, block), hat, spread)
        g_middle_ref[...] = g_middle
        vector_ref[4:5, :] = col_sum(g_middle * branch_ref[...])
        g_branch = (g_middle * row(mixer_scale, block)).astype(bf16)
        vector_ref[5:6, :] = col_sum(g_branch.astype(f32))
        grads_ref[0, :, at_branch : at_branch + width // 2] = g_branch[:, : width // 2]
        grads_ref[1, :, at_branch : at_branch + width // 2] = g_branch[:, width // 2 :]
        g_att = nt(g_branch, mixer_ref[0])
        if packed:
            for pair in range(width // LANES):
                even, odd = pack_pair(g_att[:, pair * LANES : (pair + 1) * LANES])
                g_att_ref[2 * pair] = even.astype(bf16)
                g_att_ref[2 * pair + 1] = odd.astype(bf16)
        else:
            g_att_ref[...] = g_att.astype(bf16)


def feed_back_body(block, packed, meta, *refs):
    step = pl.program_id(0)
    feed_back_core(block, packed, step, pl.num_programs(0), step, meta, *refs)


def feed_backward(block, packed, heads, meta, g, feed, slope, middle, branch, outer_scale, gain, mixer_scale, outer, inner, mixer):
    rows, width = middle.shape
    hidden = inner.shape[2]
    steps = hidden // CHUNK
    vector = full(gain.shape)
    vector_rows = 6 + hidden // width
    att_shape = (heads, rows // 2, LANES) if packed else (rows, width)
    return call(
        partial(feed_back_body, block, packed),
        f"feed_backward_{block}",
        (steps,),
        [
            full((rows, width)),
            full((rows, width)),
            pl.BlockSpec((rows, CHUNK), lambda j, m: (0, j)),
            full((rows, width)),
            full((rows, width)),
            vector, vector, vector,
            pl.BlockSpec((1, CHUNK, width), lambda j, m: (block, j, 0)),
            pl.BlockSpec((1, width, CHUNK), lambda j, m: (block, 0, j)),
            pl.BlockSpec((1, width, width), lambda j, m: (block, 0, 0)),
        ],
        [
            full((2, rows, width + hidden // 2)),
            full((rows, width)),
            full(att_shape),
            full((vector_rows, width)),
        ],
        [
            sds((2, rows, width + hidden // 2), bf16),
            sds((rows, width), f32),
            sds(att_shape, bf16),
            sds((vector_rows, width), f32),
        ],
        [pltpu.VMEM((rows, width), bf16), pltpu.VMEM((rows, width), f32)],
        2 * rows * width * (2 * hidden + width),
        4 * width * hidden + 8 * rows * hidden + 20 * rows * width,
    )(meta, g, feed, slope, middle, branch, outer_scale, gain, mixer_scale, outer, inner, mixer)


def joint_back_core(
    block, head, step, steps, chunk, g, pre_ref, x_ref, g_middle_ref, gain_ref, pattern_ref, w_ref,
    grads_ref, at_joined, out_ref, vector_ref, total_ref
):
    rows, width = total_ref.shape
    per_part = width // CHUNK
    half_steps = steps // 2

    @pl.when(step == 0)
    def _():
        total_ref[...] = jnp.zeros_like(total_ref)

    pattern = pattern_ref[...]
    in_row = pl.ds(pl.multiple_of(lax.rem(chunk, per_part) * CHUNK, CHUNK), CHUNK)

    def finish(g_joined):
        rounded = g_joined.astype(bf16)
        place = pl.multiple_of(at_joined + lax.rem(chunk, half_steps) * CHUNK, CHUNK)
        grads_ref[chunk // half_steps, :, pl.ds(place, CHUNK)] = rounded
        vector_ref[pl.ds(2 + chunk // per_part, 1), in_row] = col_sum(rounded.astype(f32))
        total_ref[...] += nt(rounded, w_ref[0])

    def head_back(gain, gain_row, shift_row):
        mean_matrix = seg_matrix(SLAB, head, 1.0 / head)
        pieces = []
        for slab in range(CHUNK // SLAB):
            at = slab * SLAB
            g_now = g[:, at : at + SLAB]
            hat, spread = seg_norm(pre_ref[:, at : at + SLAB], mean_matrix)
            vector_ref[gain_row : gain_row + 1, at : at + SLAB] += col_sum(g_now * hat)
            if shift_row is not None:
                vector_ref[shift_row : shift_row + 1, at : at + SLAB] += col_sum(g_now)
            grad_hat = g_now * gain
            pieces.append(
                spread
                * (
                    grad_hat
                    - seg_dot(grad_hat, mean_matrix)
                    - hat * seg_dot(grad_hat * hat, mean_matrix)
                )
            )
        finish(jnp.concatenate(pieces, axis=1))

    @pl.when(chunk < per_part)
    def _():
        head_back(pattern[3 * block : 3 * block + 1], 5, 6)

    @pl.when((chunk >= per_part) & (chunk < 2 * per_part))
    def _():
        head_back(pattern[3 * block + 2 : 3 * block + 3], 7, None)

    @pl.when(chunk >= 2 * per_part)
    def _():
        finish(g)

    @pl.when(step == steps - 1)
    def _():
        hat, spread = center_norm(x_ref[...].astype(f32), norm_eps)
        g_normed = total_ref[...]
        vector_ref[0:1, :] = col_sum(g_normed * hat)
        vector_ref[1:2, :] = col_sum(g_normed)
        result = g_middle_ref[...] + norm_back(g_normed * row(gain_ref, block), hat, spread)
        out_ref[...] = result.astype(out_ref.dtype)


class Rows:
    def __init__(self, ref, lead, base):
        self.ref, self.lead, self.base = ref, lead, base

    def at(self, key):
        rows, lanes = key
        if isinstance(rows, slice):
            rows = slice(rows.start + self.base, rows.stop + self.base)
        else:
            rows = pl.ds(rows.start + self.base, rows.size)
        return self.lead, rows, lanes

    def __getitem__(self, key):
        return self.ref[self.at(key)]

    def __setitem__(self, key, value):
        self.ref[self.at(key)] = value


class Plan:
    def __init__(self, frames, rows, width, hidden):
        self.half = width // 2
        self.hidden_half = hidden // 2
        self.chips = frames // 2
        self.stages = self.chips.bit_length() - 1
        self.deep = self.half // self.chips // 2
        self.n_outer = CHUNK // LANES
        self.n_inner = self.hidden_half // CHUNK
        self.n_joint = 3 * self.half // CHUNK
        self.per_block = self.n_outer + self.n_inner + 1 + self.n_joint
        self.n_pieces = self.n_inner + self.n_joint + 2
        self.total = 2 * self.per_block
        self.joint_steps = 2 * self.n_joint
        self.feed_steps = 2 * self.n_inner
        self.slabs = 4
        self.frame_steps = width // LANES // self.slabs
        self.feed_at = self.joint_steps
        self.frame_at = self.feed_at + self.feed_steps
        self.joint_at = self.frame_at + self.frame_steps
        self.compute_end = self.joint_at + self.joint_steps
        self.leave = []
        for piece in range(SHARED_PIECES, 1 + self.n_inner + 1):
            self.leave.append((1 + piece - SHARED_PIECES, 0, piece))
        at_joined = 2 + self.n_inner
        for piece in range(self.n_joint):
            self.leave.append((2 + 2 * piece, 0, at_joined + piece))
        self.leave.append((self.feed_at + 1, 1, 0))
        for piece in range(self.n_inner):
            self.leave.append((self.feed_at + 2 + 2 * piece, 1, 1 + piece))
        self.leave.append((self.frame_at + 1, 1, 1 + self.n_inner))
        for piece in range(self.n_joint):
            self.leave.append((self.joint_at + 2 + 2 * piece, 1, at_joined + piece))
        first = 1
        for slot, block, piece in self.leave:
            unit = 0 if piece == 0 else piece + self.n_outer - 1
            first = max(first, slot + AHEAD - block * self.per_block - unit)
        self.first = first
        self.ring = 12
        self.lags = [LAG * (stage + 1) for stage in range(self.stages)]
        self.end_lag = self.lags[-1] + 2
        self.n_vector = 2 + self.stages
        self.slots = max(
            self.first + self.total + self.end_lag, self.compute_end + VECTOR_LAG * self.n_vector + 1
        )


def rear_body(plan, frames, head, meta, *refs):
    (
        back_ref, pre1_ref, x1_ref, g_middle1_ref, gain_ref, pattern_ref, joint_ref,
        outer_scale, second_gain, mixer_scale, outer_ref, inner_ref, slope_ref, pre0_ref,
        mixer_in, feed_in, middle_in, branch_in, qkv_in, x0_in,
        feed_g, came_in, feed_x1, feed_three1, joint_x1, joint_three1, feed_x0, feed_three0, joint_x0, joint_three0,
        vector_in,
    ) = refs[:31]
    tokens_ref, outer_out, inner_out, mixer_out, joint_out, vector_out = refs[31:37]
    (
        own, came, acts, hids, act_turned, hid_turned, parts, last, sums,
        mixer, feed0, middle0, branch0, qkv0, x0,
        g1, g_middle0, g_att0, g_feed, g_qkv, total_sum,
    ) = refs[37:58]
    steps = refs[58 : 58 + plan.stages]
    load_sem, act_sem, hid_sem, g_send, g_recv, p_send, p_recv, f_send, f_recv, v_send, v_recv = refs[58 + plan.stages :]
    slot = pl.program_id(0)
    rows = own.shape[2]
    half, hidden_half, chips, total = plan.half, plan.hidden_half, plan.chips, plan.total
    width = 2 * half
    per_block, n_outer, n_inner = plan.per_block, plan.n_outer, plan.n_inner
    at_joined = (2 + n_inner) * CHUNK
    core, core_peer, scene_peer, cross_peer, bits = peers_of(frames)
    vector_rows = 6 + hidden_half * 2 // width
    section = vector_rows + 8

    sources = [
        (feed_g, own.at[0, :, :, pl.ds(0, at_joined)]),
        (came_in.at[:, :, pl.ds(0, SHARED_PIECES * CHUNK)], came.at[0, :, :, pl.ds(0, SHARED_PIECES * CHUNK)]),
        (feed_in, feed0),
        (mixer_in.at[pl.ds(0, 1)], mixer),
        (middle_in, middle0),
        (branch_in, branch0),
        (qkv_in, qkv0),
        (x0_in, x0),
    ]

    def load(index):
        return pltpu.make_async_copy(sources[index][0], sources[index][1], load_sem.at[index])

    def act_loads(block):
        feed_x, feed_three, joint_x, joint_three = (
            (feed_x1, feed_three1, joint_x1, joint_three1),
            (feed_x0, feed_three0, joint_x0, joint_three0),
        )[block]
        copies = []
        for place in range(4):
            feed_from = feed_x if place == 0 else feed_three.at[place - 1]
            joint_from = joint_x if place == 0 else joint_three.at[place - 1]
            copies.append(pltpu.make_async_copy(
                feed_from.at[:, pl.ds(hidden_half, width)], acts.at[place, :, pl.ds(0, width)], act_sem.at[2 * place]
            ))
            copies.append(pltpu.make_async_copy(
                joint_from, acts.at[place, :, pl.ds(width, half)], act_sem.at[2 * place + 1]
            ))
        return copies

    def hid_loads(block):
        feed_x, feed_three = ((feed_x1, feed_three1), (feed_x0, feed_three0))[block]
        return [
            pltpu.make_async_copy(
                (feed_x if place == 0 else feed_three.at[place - 1]).at[:, pl.ds(0, hidden_half)],
                hids.at[place],
                hid_sem.at[place],
            )
            for place in range(4)
        ]

    def piece_copy(block, piece, which):
        lanes = pl.ds(pl.multiple_of(piece * CHUNK, CHUNK), CHUNK)
        side = core if which == 0 else 1 - core
        return remote(
            own.at[block, side, :, lanes],
            came.at[block, which, :, lanes],
            g_send.at[block, which, piece],
            g_recv.at[block, which, piece],
            (scene_peer, core_peer, cross_peer)[which],
        )

    @pl.when(slot == 0)
    def _():
        load(0).start()
        for copy in hid_loads(0):
            copy.start()
        load(1).start()
        for copy in act_loads(0):
            copy.start()
        for index in range(2, len(sources)):
            load(index).start()
        sums[0] = jnp.zeros(sums.shape[1:], f32)
        for index in range(vector_rows):
            sums[0, section + index : section + index + 1, :] = vector_in[index : index + 1, :]
        enter([core_peer, scene_peer, cross_peer] + [peer for _, peer in bits])
        load(0).wait()
        for copy in hid_loads(0):
            copy.wait()
        load(1).wait()
        for copy in act_loads(0):
            copy.wait()

    def spread(step, steps_of):
        return lax.rem(step, 2) * (steps_of // 2) + step // 2

    @pl.when(slot < plan.joint_steps)
    def _():
        pieces = []
        for pair in range(CHUNK // LANES):
            pieces.append(
                unpack_pair(back_ref[2 * pair, 0].astype(f32), back_ref[2 * pair + 1, 0].astype(f32))
            )
        joint_back_core(
            1, head, slot, plan.joint_steps, spread(slot, plan.joint_steps), jnp.concatenate(pieces, axis=1),
            pre1_ref, x1_ref, g_middle1_ref, gain_ref, pattern_ref, joint_ref,
            own.at[0], at_joined, g1, Rows(sums, 0, section + vector_rows), total_sum,
        )

    @pl.when(slot == plan.feed_at)
    def _():
        for index in range(2, len(sources)):
            load(index).wait()

    @pl.when((slot >= plan.feed_at) & (slot < plan.frame_at))
    def _():
        step = slot - plan.feed_at
        feed_back_core(
            0, False, step, plan.feed_steps, spread(step, plan.feed_steps), meta, g1, feed0, slope_ref, middle0, branch0,
            outer_scale, second_gain, mixer_scale, outer_ref, inner_ref, mixer,
            own.at[1], g_middle0, g_att0, Rows(sums, 0, 0), g_feed, total_sum,
        )

    @pl.when((slot >= plan.frame_at) & (slot < plan.joint_at))
    def _():
        @pl.loop(0, plan.slabs)
        def _(slab):
            at = ((slot - plan.frame_at) * plan.slabs + slab) * LANES
            frame_back_slab(at, meta, qkv0, g_att0, g_qkv)

    @pl.when((slot >= plan.joint_at) & (slot < plan.compute_end))
    def _():
        step = slot - plan.joint_at
        chunk = spread(step, plan.joint_steps)
        joint_back_core(
            0, head, step, plan.joint_steps, chunk,
            g_qkv[:, pl.ds(pl.multiple_of(chunk * CHUNK, CHUNK), CHUNK)],
            pre0_ref, x0, g_middle0, gain_ref, pattern_ref, joint_ref,
            own.at[1], at_joined, tokens_ref, Rows(sums, 0, vector_rows), total_sum,
        )

    def swapped(index):
        return lax.rem(index, SWAP_EVERY) == 1

    def way(stage, index):
        value, peer = bits[stage]
        if stage > 1:
            return value, peer
        other_value, other_peer = bits[1 - stage]
        changed = swapped(index)
        return jnp.where(changed, other_value, value), (peer[0], jnp.where(changed, other_peer[1], peer[1]))

    def stage_start(stage, index):
        value, peer = way(stage, index)
        source = parts if stage == 0 else steps[stage - 1]
        held = lax.rem(index, plan.ring)
        for pair in range(chips >> (stage + 1)):
            remote(
                source.at[held, 2 * pair + 1 - value],
                steps[stage].at[held, pair],
                p_send.at[stage, held],
                p_recv.at[stage, held],
                peer,
            ).start()

    def stage_whole(stage, index):
        held = lax.rem(index, plan.ring)
        return remote(
            steps[stage].at[held], steps[stage].at[held], p_send.at[stage, held], p_recv.at[stage, held], way(stage, index)[1]
        )

    def last_copy(index):
        held = lax.rem(index, plan.ring)
        return remote(
            steps[-1].at[held, 0, 1 - core], last.at[held], f_send.at[held], f_recv.at[held], core_peer
        )

    def store(index, value):
        changed = swapped(index)
        held = lax.rem(index, plan.ring)

        @pl.when(jnp.logical_not(changed))
        def _():
            parts[held] = value.astype(bf16)

        @pl.when(changed)
        def _():
            pairs = value.reshape((chips // 4, 2, 2) + value.shape[1:])
            pairs = jnp.stack([pairs[:, :, place] for place in range(2)], axis=1)
            parts[held] = pairs.reshape(value.shape).astype(bf16)

    def multiply(index):
        block = index // per_block
        unit = lax.rem(index, per_block)

        def wait_piece(piece):
            @pl.when((block > 0) | (piece >= SHARED_PIECES))
            def _():
                for which in range(3):
                    piece_copy(block, piece, which).wait_recv()

        def gathered(lanes):
            return jnp.concatenate(
                [own[block, core, :, lanes]] + [came[block, which, :, lanes] for which in range(3)], axis=0
            )

        @pl.when(unit < n_outer)
        def _():
            @pl.when(unit == 0)
            def _():
                wait_piece(0)
                hid_turned[...] = jnp.transpose(jnp.concatenate([hids[place] for place in range(4)], axis=0))

            right = gathered(pl.ds(pl.multiple_of(unit * LANES, LANES), LANES))
            value = nn(hid_turned[...], right)
            value = value.reshape(chips, 2, 4, plan.deep, LANES)
            store(index, jnp.concatenate([value[:, :, place] for place in range(4)], axis=-1))

        @pl.when(unit >= n_outer)
        def _():
            piece = unit - (n_outer - 1)
            wait_piece(piece)

            for place, at in enumerate((n_outer, n_outer + n_inner, n_outer + n_inner + 1)):

                @pl.when(unit == at)
                def _():
                    left = [acts[source, :, place * half : (place + 1) * half] for source in range(4)]
                    act_turned[...] = jnp.transpose(jnp.concatenate(left, axis=0))

            value = nn(act_turned[...], gathered(pl.ds(pl.multiple_of(piece * CHUNK, CHUNK), CHUNK)))
            store(index, value.reshape(chips, 2, plan.deep, CHUNK))

    def put(index, side, value):
        block = 1 - index // per_block
        unit = lax.rem(index, per_block)

        @pl.when(unit < n_outer)
        def _():
            lanes = pl.ds(pl.multiple_of(side * half + unit * LANES, LANES), LANES)
            for place in range(4):
                outer_out[block, place * plan.deep : (place + 1) * plan.deep, lanes] = (
                    value[:, place * LANES : (place + 1) * LANES]
                )

        def wide(first, count, target):
            @pl.when((unit >= first) & (unit < first + count))
            def _():
                lanes = pl.ds(pl.multiple_of((side * count + unit - first) * CHUNK, CHUNK), CHUNK)
                target[block, :, lanes] = value

        wide(n_outer, n_inner, inner_out)
        wide(n_outer + n_inner, 1, mixer_out)
        wide(n_outer + n_inner + 1, plan.n_joint, joint_out)

    def add(stage, index):
        stage_whole(stage, index).wait()
        value = way(stage, index)[0]
        held = lax.rem(index, plan.ring)
        source = parts if stage == 0 else steps[stage - 1]
        for pair in range(chips >> (stage + 1)):
            result = source[held, 2 * pair + value].astype(f32) + steps[stage][held, pair].astype(f32)
            if stage + 1 == plan.stages:
                put(index, core, jnp.where(core == 0, result[0], result[1]))
            steps[stage][held, pair] = result.astype(bf16)

    def close(index):
        last_copy(index).wait()
        put(index, 1 - core, last[lax.rem(index, plan.ring)].astype(f32))

    def when_due(lag, action):
        index = slot - plan.first - lag

        @pl.when((index >= 0) & (index < total))
        def _():
            action(index)

    vector_peers = [core_peer, scene_peer] + [peer for _, peer in bits]

    def vector_copy(stage):
        return remote(
            sums.at[2 * stage], sums.at[2 * stage + 1], v_send.at[stage], v_recv.at[stage], vector_peers[stage]
        )

    when_due(0, multiply)
    for stage in range(plan.stages):
        when_due(plan.lags[stage], partial(add, stage))
    when_due(plan.end_lag, close)

    for stage in range(plan.n_vector):

        @pl.when(slot == plan.compute_end + VECTOR_LAG * (stage + 1))
        def _():
            vector_copy(stage).wait()
            result = sums[2 * stage] + sums[2 * stage + 1]
            if stage + 1 < plan.n_vector:
                sums[2 * stage + 2] = result
            else:
                vector_out[...] = result

    for stage in range(plan.stages - 1):
        when_due(plan.lags[stage], partial(stage_start, stage + 1))
    when_due(plan.lags[-1], lambda index: last_copy(index).start())
    when_due(0, partial(stage_start, 0))

    for at, block, piece in plan.leave:

        @pl.when(slot == at)
        def _():
            for which in range(3):
                piece_copy(block, piece, which).start()

    for stage in range(plan.n_vector):

        @pl.when(slot == plan.compute_end + VECTOR_LAG * stage)
        def _():
            vector_copy(stage).start()

    @pl.when(slot == plan.first + 1)
    def _():
        for copy in hid_loads(1):
            copy.start()

    @pl.when(slot == plan.first + per_block - 1)
    def _():
        for copy in hid_loads(1):
            copy.wait()

    @pl.when(slot == plan.first + n_outer + n_inner + 1)
    def _():
        for copy in act_loads(1):
            copy.start()

    @pl.when(slot == plan.first + per_block + n_outer - 1)
    def _():
        for copy in act_loads(1):
            copy.wait()

    @pl.when(slot == plan.slots - 1)
    def _():
        for at, block, piece in plan.leave:
            for which in range(3):
                piece_copy(block, piece, which).wait_send()


def rear(frames, head, meta, back, pre1, x1, g_middle1, gain, pattern, joint, outer_scale, second_gain, mixer_scale, outer, inner, slope0, pre0, mixer, feed0, middle0, branch0, qkv0, x0, feed_g1, came1, shares, vector1):
    rows, width = x1.shape
    hidden = inner.shape[2]
    half = width // 2
    plan = Plan(frames, rows, width, hidden)
    per_part = width // CHUNK
    vector_rows = vector1.shape[0]
    n_vector_rows = 2 * (vector_rows + 8)

    def clip(value, size):
        return jnp.minimum(jnp.maximum(value, 0), size - 1)

    def spread(step, steps):
        return lax.rem(step, 2) * (steps // 2) + step // 2

    def chunk1(slot):
        return spread(clip(slot, plan.joint_steps), plan.joint_steps)

    def chunk0(slot):
        return spread(clip(slot - plan.joint_at, plan.joint_steps), plan.joint_steps)

    def chunk_feed(slot):
        return spread(clip(slot - plan.feed_at, plan.feed_steps), plan.feed_steps)

    def back_map(slot, m):
        chunk = chunk1(slot)
        return (lax.rem(chunk, per_part), chunk // per_part, 0, 0)

    def joint_map(slot, m):
        late = slot >= plan.feed_at
        return (jnp.where(late, 0, 1), 0, jnp.where(late, chunk0(slot), chunk1(slot)))

    once = dict(pipeline_mode=pl.Buffered(1))
    single = lambda shape: pl.BlockSpec(shape, lambda *_: (0,) * len(shape), **once)
    out_shape = [
        sds((rows, width), bf16),
        sds((2, 4 * plan.deep, width), f32),
        sds((2, plan.deep, hidden), f32),
        sds((2, plan.deep, width), f32),
        sds((2, plan.deep, 3 * width), f32),
        sds((n_vector_rows, width), f32),
    ]
    container = (plan.ring, plan.chips, 2, plan.deep, CHUNK)
    return pl.pallas_call(
        partial(rear_body, plan, frames, head),
        name="rear",
        out_shape=out_shape,
        grid_spec=pltpu.PrefetchScalarGridSpec(
            num_scalar_prefetch=1,
            grid=(plan.slots,),
            in_specs=[
                pl.BlockSpec((CHUNK // head, 1, rows // 2, LANES), back_map),
                pl.BlockSpec((rows, CHUNK), lambda j, m: (0, jnp.minimum(chunk1(j), 2 * per_part - 1))),
                single(x1.shape),
                single(g_middle1.shape),
                single(gain.shape),
                single(pattern.shape),
                pl.BlockSpec((1, width, CHUNK), joint_map),
                single(outer_scale.shape),
                single(second_gain.shape),
                single(mixer_scale.shape),
                pl.BlockSpec((1, CHUNK, width), lambda j, m: (0, chunk_feed(j), 0)),
                pl.BlockSpec((1, width, CHUNK), lambda j, m: (0, 0, chunk_feed(j))),
                pl.BlockSpec((rows, CHUNK), lambda j, m: (0, chunk_feed(j))),
                pl.BlockSpec((rows, CHUNK), lambda j, m: (0, jnp.minimum(chunk0(j), 2 * per_part - 1))),
            ]
            + [any_space] * 16
            + [single(vector1.shape)],
            out_specs=[vmem_space] * len(out_shape),
            scratch_shapes=[
                pltpu.VMEM((2, 2, rows, plan.n_pieces * CHUNK), bf16),
                pltpu.VMEM((2, 3, rows, plan.n_pieces * CHUNK), bf16),
                pltpu.VMEM((4, rows, 3 * half), bf16),
                pltpu.VMEM((4, rows, plan.hidden_half), bf16),
                pltpu.VMEM((half, 4 * rows), bf16),
                pltpu.VMEM((plan.hidden_half, 4 * rows), bf16),
                pltpu.VMEM(container, bf16),
                pltpu.VMEM((plan.ring, plan.deep, CHUNK), bf16),
                pltpu.VMEM((2 * plan.n_vector, n_vector_rows, width), f32),
                pltpu.VMEM((1, width, width), bf16),
                pltpu.VMEM((rows, width), f32),
                pltpu.VMEM((rows, width), f32),
                pltpu.VMEM((rows, width), f32),
                pltpu.VMEM((rows, 3 * width), bf16),
                pltpu.VMEM((rows, width), bf16),
                pltpu.VMEM((rows, width), f32),
                pltpu.VMEM((rows, width), f32),
                pltpu.VMEM((rows, width), bf16),
                pltpu.VMEM((rows, width), bf16),
                pltpu.VMEM((rows, 3 * width), f32),
                pltpu.VMEM((rows, width), f32),
            ]
            + [pltpu.VMEM((plan.ring, plan.chips >> (stage + 1)) + container[2:], bf16) for stage in range(plan.stages)]
            + [
                dma((8,)),
                dma((8,)),
                dma((4,)),
                dma((2, 3, plan.n_pieces)),
                dma((2, 3, plan.n_pieces)),
                dma((plan.stages, plan.ring)),
                dma((plan.stages, plan.ring)),
                dma((plan.ring,)),
                dma((plan.ring,)),
                dma((plan.n_vector,)),
                dma((plan.n_vector,)),
            ],
        ),
        compiler_params=pltpu.CompilerParams(
            collective_id=0, has_side_effects=True, vmem_limit_bytes=64 * 1024 * 1024 - 65536
        ),
        cost_estimate=pl.CostEstimate(flops=2 * rows * width * hidden * 20, bytes_accessed=60 * width * hidden, transcendentals=0),
    )(
        meta, back, pre1, x1, g_middle1, gain, pattern, joint, outer_scale, second_gain, mixer_scale, outer, inner, slope0, pre0,
        mixer, feed0, middle0, branch0, qkv0, x0, feed_g1, came1, *shares, vector1,
    )


def finish_body(heads, meta, vectors_ref, *refs):
    count = 5
    large_in, large_out = refs[:count], refs[count : 2 * count]
    (
        first_gain, first_shift, joint_bias, query_gain, query_shift, key_gain, mixer_bias, mixer_scale,
        second_gain, second_shift, inner_bias, outer_bias, outer_scale,
    ) = refs[2 * count : -1]
    sem = refs[-1]
    copies = [
        pltpu.make_async_copy(source, target, sem.at[index])
        for index, (source, target) in enumerate(zip(large_in, large_out))
    ]
    for copy in copies:
        copy.start()
    width = first_gain.shape[1]
    head = query_gain.shape[1]
    feed_rows = 6 + inner_bias.shape[1] // width
    for block in range(2):
        base = block * (feed_rows + 8)
        rows = vectors_ref[base : base + feed_rows + 8, :]

        def pick(index):
            return rows[index : index + 1, :]

        def at(index):
            return pick(feed_rows + index)

        def fold(value):
            total = value[:, :LANES]
            for place in range(1, width // LANES):
                total = total + value[:, place * LANES : (place + 1) * LANES]
            return (total + turn(total))[:, :head]

        here = slice(block, block + 1)
        for target, index in (
            (outer_scale, 0), (outer_bias, 1), (second_gain, 2), (second_shift, 3), (mixer_scale, 4), (mixer_bias, 5),
        ):
            target[here, :] = pick(index)
        for index in range(inner_bias.shape[1] // width):
            inner_bias[here, index * width : (index + 1) * width] = pick(6 + index)
        first_gain[here, :] = at(0)
        first_shift[here, :] = at(1)
        for index in range(3):
            joint_bias[here, index * width : (index + 1) * width] = at(2 + index)
        query_gain[here, :] = fold(at(5))
        query_shift[here, :] = fold(at(6))
        key_gain[here, :] = fold(at(7))
    for copy in copies:
        copy.wait()


def finish(heads, meta, vectors, large):
    width = vectors.shape[1]
    head = width // heads
    hidden = large[2].shape[2]
    sizes = [width, width, 3 * width, head, head, head, width, width, width, width, hidden, width, width]
    return pl.pallas_call(
        partial(finish_body, heads),
        name="finish",
        out_shape=[sds(value.shape, value.dtype) for value in large] + [sds((2, size), f32) for size in sizes],
        grid_spec=pltpu.PrefetchScalarGridSpec(
            num_scalar_prefetch=1,
            grid=(1,),
            in_specs=[vmem_space] * 6,
            out_specs=[any_space] * 5 + [full((2, size)) for size in sizes],
            scratch_shapes=[dma((5,))],
        ),
    )(meta, vectors, *large)


def local(scenes, frames, tokens, patch_counts, first_gain, first_shift, joint_weight, joint_bias, query_gain, query_shift, key_gain, mixer_weight, mixer_bias, mixer_scale, second_gain, second_shift, inner_weight, inner_bias, outer_weight, outer_bias, outer_scale, cotangent):
    rows, width = tokens.shape[1:]
    half = rows // 2
    head = query_gain.shape[1]
    heads = width // head
    hidden = inner_weight.shape[2]
    chips = frames // 2
    scene = lax.axis_index("scene")
    frame = lax.axis_index("frame")
    core = lax.rem(frame, 2)
    meta = jnp.stack([scene, core, lax.rem(frame // 2, 2), patch_counts[0, 0]]).astype(jnp.int32)
    pattern = jnp.tile(
        jnp.stack([vector[block] for block in range(2) for vector in (query_gain, query_shift, key_gain)]).astype(f32),
        (1, SLAB // head),
    )

    x0 = tokens[0]
    feed_params = (mixer_weight, mixer_bias, mixer_scale, second_gain, second_shift, inner_weight, inner_bias, outer_weight, outer_bias, outer_scale)
    back_params = (outer_scale, second_gain, mixer_scale, outer_weight, inner_weight, mixer_weight)

    own0, other0, pre0, qkv0 = joint_forward(0, False, head, meta, x0, first_gain, first_shift, pattern, joint_weight, joint_bias)
    att0 = frame_forward(meta, qkv0)
    own_feed0, other_feed0, middle0, branch0, feed0, slope0, x1 = feed_forward(0, False, meta, att0, x0, *feed_params)
    own1, other1, pre1, pack1 = joint_forward(1, True, head, meta, x1, first_gain, first_shift, pattern, joint_weight, joint_bias)
    att1, kept1, att_full, att_log, (left_joint0, left_feed0, left_joint1) = scene_forward(
        frames, meta, pack1, half, [(own0, other0), (own_feed0, other_feed0), (own1, other1)]
    )
    own_feed1, other_feed1, middle1, branch1, feed1, slope1, layer_out = feed_forward(1, True, meta, att1, x1, *feed_params)

    g_feed1, g_middle1, g_att1, vector_feed1 = feed_backward(1, True, heads, meta, cotangent[0], feed1, slope1, middle1, branch1, *back_params)
    shared = SHARED_PIECES * CHUNK
    g_qkv1, came_feed1, (left_feed1,) = scene_backward(
        frames, meta, kept1, g_att1, att_full, att_log, half, [(own_feed1, other_feed1)], g_feed1, shared
    )
    g0, outer, inner, mixer, joint, vectors = rear(
        frames, head, meta, g_qkv1, pre1, x1, g_middle1, first_gain, pattern, joint_weight,
        outer_scale, second_gain, mixer_scale, outer_weight, inner_weight, slope0, pre0,
        mixer_weight, feed0, middle0, branch0, qkv0, x0, g_feed1, came_feed1,
        [own_feed1, left_feed1, own1, left_joint1, own_feed0, left_feed0, own0, left_joint0], vector_feed1,
    )
    (
        g0, outer, inner, mixer, joint,
        grad_first_gain, grad_first_shift, grad_joint_bias, grad_query_gain, grad_query_shift, grad_key_gain,
        grad_mixer_bias, grad_mixer_scale, grad_second_gain, grad_second_shift, grad_inner_bias, grad_outer_bias, grad_outer_scale,
    ) = finish(heads, meta, vectors, (g0, outer, inner, mixer, joint))
    return (
        layer_out[None], g0[None],
        grad_first_gain, grad_first_shift, joint, grad_joint_bias, grad_query_gain, grad_query_shift, grad_key_gain,
        mixer, grad_mixer_bias, grad_mixer_scale, grad_second_gain, grad_second_shift,
        inner, grad_inner_bias, outer, grad_outer_bias, grad_outer_scale,
    )


def solution(mesh):
    tokens_spec = P("scene", "frame", None)
    shard = P(None, ("scene", "frame"), None)
    in_specs = (tokens_spec, P("scene", "frame")) + (P(),) * 17 + (tokens_spec,)
    out_specs = (
        tokens_spec, tokens_spec, P(), P(), shard, P(), P(), P(), P(), shard,
        P(), P(), P(), P(), shard, P(), shard, P(), P(),
    )
    body = partial(local, mesh.shape["scene"], mesh.shape["frame"])
    return jax.shard_map(body, mesh=mesh, in_specs=in_specs, out_specs=out_specs, check_vma=False)
```

```python
from functools import partial

import jax
import jax.numpy as jnp
from jax import lax
from jax.experimental import pallas as pl
from jax.experimental.pallas import tpu as pltpu
from jax.sharding import PartitionSpec as P

SPECIAL = 5
CHUNK = 512
LANES = 128
SLAB = 256
SHARED_PIECES = 3
SWAP_EVERY = 3
AHEAD = 2
LAG = 3
VECTOR_LAG = 3
norm_eps = 1e-06
head_eps = 1e-05
closed_score = -10000.0
f32 = jnp.float32
bf16 = jnp.bfloat16


def nn(a, b):
    return lax.dot_general(a, b, (((1,), (0,)), ((), ())), preferred_element_type=f32)


def nt(a, b):
    return lax.dot_general(a, b, (((1,), (1,)), ((), ())), preferred_element_type=f32)


def tn(a, b):
    return lax.dot_general(a, b, (((0,), (0,)), ((), ())), preferred_element_type=f32)


def row(ref, index):
    return ref[...].astype(f32)[index : index + 1, :]


def col_sum(value):
    return jnp.sum(value, axis=0, keepdims=True)


def center_norm(value, eps):
    centered = value - jnp.mean(value, axis=-1, keepdims=True)
    spread = lax.rsqrt(jnp.mean(centered * centered, axis=-1, keepdims=True) + eps)
    return centered * spread, spread


def norm_back(grad_hat, hat, spread):
    mean_grad = jnp.mean(grad_hat, axis=-1, keepdims=True)
    mean_both = jnp.mean(grad_hat * hat, axis=-1, keepdims=True)
    return spread * (grad_hat - mean_grad - hat * mean_both)


def seg_matrix(width, head, value):
    shift = head.bit_length() - 1
    first = lax.shift_right_logical(lax.broadcasted_iota(jnp.int32, (width, width), 0), shift)
    second = lax.shift_right_logical(lax.broadcasted_iota(jnp.int32, (width, width), 1), shift)
    return jnp.where(first == second, value, 0.0).astype(bf16)


def repeated(ref, block):
    head = ref.shape[1]
    lane = lax.broadcasted_iota(jnp.int32, (head, SLAB), 1)
    place = lax.broadcasted_iota(jnp.int32, (head, SLAB), 0)
    copies = jnp.where(lax.rem(lane, head) == place, 1.0, 0.0).astype(bf16)
    return nn(ref[...], copies)[block : block + 1, :]


def seg_dot(value, matrix):
    high = value.astype(bf16)
    low = (value - high.astype(f32)).astype(bf16)
    return nn(high, matrix) + nn(low, matrix)


def seg_norm(value, mean_matrix):
    centered = value - seg_dot(value, mean_matrix)
    spread = lax.rsqrt(seg_dot(centered * centered, mean_matrix) + head_eps)
    return centered * spread, spread


def first_lanes(rows):
    return lax.broadcasted_iota(jnp.int32, (rows, LANES), 1) < LANES // 2


def turn(value):
    return pltpu.roll(value, LANES // 2, value.ndim - 1)


def pack_pair(slab):
    half = slab.shape[0] // 2
    top, bottom = slab[:half], slab[half:]
    low = first_lanes(half)
    return jnp.where(low, top, turn(bottom)), jnp.where(low, turn(top), bottom)


def unpack_pair(even, odd):
    low = first_lanes(even.shape[0])
    top = jnp.where(low, even, turn(odd))
    bottom = jnp.where(low, turn(even), odd)
    return jnp.concatenate([top, bottom], axis=0)


def erf(value):
    value = jnp.clip(value, -4.0, 4.0)
    square = value * value
    top = jnp.full_like(square, -2.72614225801306e-10)
    for coefficient in (
        2.77068142495902e-08,
        -2.10102402082508e-06,
        -5.69250639462346e-05,
        -7.34990630326855e-04,
        -2.95459980854025e-03,
        -1.60960333262415e-02,
    ):
        top = top * square + coefficient
    bottom = jnp.full_like(square, -1.45660718464996e-05)
    for coefficient in (
        -2.13374055278905e-04,
        -1.68282697438203e-03,
        -7.37332916720468e-03,
        -1.42647390514189e-02,
    ):
        bottom = bottom * square + coefficient
    return value * top / bottom


def full(shape):
    return pl.BlockSpec(shape, lambda *_: (0,) * len(shape))


def sds(shape, dtype):
    return jax.ShapeDtypeStruct(shape, dtype)


def call(body, name, grid, in_specs, out_specs, out_shape, scratch, flops, moved):
    return pl.pallas_call(
        body,
        name=name,
        out_shape=out_shape,
        grid_spec=pltpu.PrefetchScalarGridSpec(
            num_scalar_prefetch=1,
            grid=grid,
            in_specs=in_specs,
            out_specs=out_specs,
            scratch_shapes=scratch,
        ),
        cost_estimate=pl.CostEstimate(flops=flops, bytes_accessed=moved, transcendentals=0),
    )


def joint_body(
    block, packed, head, meta, x_ref, gain_ref, shift_ref, q_gain_ref, q_shift_ref, k_gain_ref, w_ref, b_ref,
    own_ref, other_ref, pre_ref, out_ref, normed_ref, *stage
):
    step = pl.program_id(0)
    rows, width = normed_ref.shape
    per_part = width // CHUNK
    half = rows // 2

    @pl.when(step == 0)
    def _():
        hat, _ = center_norm(x_ref[...].astype(f32), norm_eps)
        normed = (hat * row(gain_ref, block) + row(shift_ref, block)).astype(bf16)
        normed_ref[...] = normed

        scene = lax.axis_index("scene")

        @pl.when(scene == 0)
        def _():
            own_ref[...] = normed[:, : width // 2]
            other_ref[...] = normed[:, width // 2 :]

        @pl.when(scene != 0)
        def _():
            own_ref[...] = normed[:, width // 2 :]
            other_ref[...] = normed[:, : width // 2]

        if packed:
            count = jnp.full((8, LANES), meta[0], jnp.int32).astype(f32)
            for place in range(stage[0].shape[0]):
                stage[0][place, 3 * half : 3 * half + 8, :] = count

    joined = nn(normed_ref[...], w_ref[0]) + row(b_ref, block)

    def emit(part, values):
        if packed:
            base = (step - part * per_part) * (CHUNK // head)
            for slab in range(CHUNK // LANES):
                even, odd = pack_pair(values[:, slab * LANES : (slab + 1) * LANES])
                stage[0][base + 2 * slab, part * half : (part + 1) * half, :] = even
                stage[0][base + 2 * slab + 1, part * half : (part + 1) * half, :] = odd
        else:
            out_ref[...] = values.astype(bf16)

    def normed_heads(gain, shift):
        mean_matrix = seg_matrix(SLAB, head, 1.0 / head)
        pieces = []
        for slab in range(CHUNK // SLAB):
            hat, _ = seg_norm(joined[:, slab * SLAB : (slab + 1) * SLAB], mean_matrix)
            pieces.append(hat * gain if shift is None else hat * gain + shift)
        return jnp.concatenate(pieces, axis=1)

    scale = head ** (-0.5)

    @pl.when(step < per_part)
    def _():
        pre_ref[...] = joined
        emit(0, normed_heads(
            repeated(q_gain_ref, block) * scale,
            repeated(q_shift_ref, block) * scale,
        ))

    @pl.when((step >= per_part) & (step < 2 * per_part))
    def _():
        pre_ref[...] = joined
        emit(1, normed_heads(repeated(k_gain_ref, block), None))

    @pl.when(step >= 2 * per_part)
    def _():
        emit(2, joined)

    if packed:

        @pl.when(step == 3 * per_part - 1)
        def _():
            out_ref[...] = stage[0][...].astype(bf16)


def joint_forward(block, packed, head, meta, x, gain, shift, pattern, weight, bias):
    rows, width = x.shape
    per_part = width // CHUNK
    heads = width // head
    packed_rows = 3 * (rows // 2) + 8
    if packed:
        out_spec, out = full((heads, packed_rows, LANES)), sds((heads, packed_rows, LANES), bf16)
        extra = [pltpu.VMEM((heads, packed_rows, LANES), f32)]
    else:
        out_spec = pl.BlockSpec((rows, CHUNK), lambda j, m: (0, j))
        out = sds((rows, 3 * width), bf16)
        extra = []
    return call(
        partial(joint_body, block, packed, head),
        f"joint_forward_{block}",
        (3 * per_part,),
        [
            full((rows, width)),
            full(gain.shape),
            full(shift.shape),
            full(pattern[0].shape), full(pattern[1].shape), full(pattern[2].shape),
            pl.BlockSpec((1, width, CHUNK), lambda j, m: (block, 0, j)),
            pl.BlockSpec((2, CHUNK), lambda j, m: (0, j)),
        ],
        [
            full((rows, width // 2)),
            full((rows, width // 2)),
            pl.BlockSpec((rows, CHUNK), lambda j, m: (0, jnp.minimum(j, 2 * per_part - 1))),
            out_spec,
        ],
        [
            sds((rows, width // 2), bf16),
            sds((rows, width // 2), bf16),
            sds((rows, 2 * width), f32),
            out,
        ],
        [pltpu.VMEM((rows, width), bf16)] + extra,
        2 * rows * width * 3 * width,
        6 * width * width + 16 * rows * width,
    )(meta, x, gain, shift, *pattern, weight, bias)


def lane_picks():
    lane = lax.broadcasted_iota(jnp.int32, (1, LANES), 1)
    low = jnp.where(lane < LANES // 2, 1.0, 0.0)
    return low.astype(bf16), (1.0 - low).astype(bf16)


def open_row(meta, rows):
    place = lax.broadcasted_iota(jnp.int32, (1, rows), 1)
    return jnp.where(place < meta[0] + SPECIAL, 0.0, closed_score)


def frame_body(meta, qkv_ref, out_ref):
    rows, width = out_ref.shape
    bias = open_row(meta, rows)
    picks = lane_picks()
    low = first_lanes(rows)
    for slab in range(width // LANES):
        at = slab * LANES
        queries = qkv_ref[:, at : at + LANES]
        keys = qkv_ref[:, width + at : width + at + LANES]
        values = qkv_ref[:, 2 * width + at : 2 * width + at + LANES]
        results = []
        for pick in picks:
            power = jnp.exp(nt(queries * pick, keys) + bias)
            probs = power / jnp.sum(power, axis=-1, keepdims=True)
            results.append(nn(probs.astype(bf16), values))
        out_ref[:, at : at + LANES] = jnp.where(low, results[0], results[1]).astype(bf16)


def frame_forward(meta, qkv):
    rows = qkv.shape[0]
    width = qkv.shape[1] // 3
    return call(
        frame_body,
        "frame_forward",
        (1,),
        [full(qkv.shape)],
        full((rows, width)),
        sds((rows, width), bf16),
        [],
        4 * rows * rows * width,
        8 * rows * width,
    )(meta, qkv)


def frame_back_slab(at, meta, qkv_ref, grad_ref, out_ref):
    rows, width = grad_ref.shape
    bias = open_row(meta, rows)
    scale = (LANES // 2) ** (-0.5)

    def lanes(part):
        return pl.ds(pl.multiple_of(part * width + at, LANES), LANES)

    queries = qkv_ref[:, lanes(0)]
    keys = qkv_ref[:, lanes(1)]
    values = qkv_ref[:, lanes(2)]
    grads = grad_ref[:, lanes(0)]
    found = []
    for pick in lane_picks():
        power = jnp.exp(nt(queries * pick, keys) + bias)
        probs = power / jnp.sum(power, axis=-1, keepdims=True)
        grad_probs = nt(grads * pick, values)
        delta = jnp.sum(probs * grad_probs, axis=-1, keepdims=True)
        grad_scores = (probs * (grad_probs - delta)).astype(bf16)
        found.append((
            nn(grad_scores, keys) * scale,
            tn(grad_scores, queries),
            tn(probs.astype(bf16), grads),
        ))
    low = first_lanes(rows)
    for part in range(3):
        out_ref[:, lanes(part)] = jnp.where(low, found[0][part], found[1][part])


def packed_part(value, part, half):
    whole = value.astype(f32)
    return whole[:, part * half : (part + 1) * half, :].reshape(-1, LANES)


def open_slots(value, half):
    count = value.astype(f32)[:, 3 * half : 3 * half + 8, :]
    count = jnp.concatenate([count] * (half // 8), axis=1)
    place = lax.broadcasted_iota(jnp.int32, count.shape, 1).astype(f32)
    return (
        (place < count + SPECIAL).reshape(-1, LANES),
        (place + half < count + SPECIAL).reshape(-1, LANES),
    )


MESH = pl.DeviceIdType.MESH


def peers_of(frames):
    scene = lax.axis_index("scene")
    frame = lax.axis_index("frame")
    bits = []
    bit = 1
    while bit < frames:
        value = lax.rem(frame // bit, 2)
        bits.append((value, (scene, frame + bit * (1 - 2 * value))))
        bit *= 2
    core, core_peer = bits[0]
    scene_peer = (1 - scene, frame)
    cross_peer = (1 - scene, core_peer[1])
    return core, core_peer, scene_peer, cross_peer, bits[1:]


def greet(targets):
    barrier = pltpu.get_barrier_semaphore()
    for target in targets:
        pl.semaphore_signal(barrier, inc=1, device_id=target, device_id_type=MESH)


def enter_scene(frames):
    barrier = pltpu.get_barrier_semaphore()
    _, _, scene_peer, cross_peer, _ = peers_of(frames)
    scene = lax.axis_index("scene")
    frame = lax.axis_index("frame")
    for target in (scene_peer, cross_peer):
        pl.semaphore_signal(barrier, inc=1, device_id=target, device_id_type=MESH)

    @pl.loop(1, frames)
    def _(offset):
        pl.semaphore_signal(
            barrier, inc=1, device_id=(scene, lax.rem(frame + offset, frames)), device_id_type=MESH
        )

    pl.semaphore_wait(barrier, frames + 1)


def remote(source, target, send, recv, device):
    return pltpu.make_async_remote_copy(
        src_ref=source, dst_ref=target, send_sem=send, recv_sem=recv, device_id=device, device_id_type=MESH
    )


class Share:
    def __init__(self, frames, pairs, outs, send, recv):
        _, core_peer, scene_peer, _, _ = peers_of(frames)
        self.first, self.second = [], []
        for index, ((own, other), out) in enumerate(zip(pairs, outs)):
            self.first.append(remote(other, out.at[0], send.at[3 * index], recv.at[3 * index], scene_peer))
            self.first.append(remote(own, out.at[1], send.at[3 * index + 1], recv.at[3 * index + 1], core_peer))
            self.second.append(
                remote(out.at[0], out.at[2], send.at[3 * index + 2], recv.at[3 * index + 2], core_peer)
            )

    def start(self):
        for copy in self.first:
            copy.start()

    def relay(self):
        for index, copy in enumerate(self.second):
            self.first[2 * index].wait_recv()
            copy.start()

    def close(self):
        for index, copy in enumerate(self.second):
            self.first[2 * index].wait_send()
            self.first[2 * index + 1].wait()
            copy.wait()


def scene_body(
    frames, half, span, n_share, meta, pack_ref, *refs
):
    heads = pack_ref.shape[0]
    pairs = [(refs[2 * index], refs[2 * index + 1]) for index in range(n_share)]
    refs = refs[2 * n_share :]
    att_ref, kept_ref, out_ref, log_ref = refs[:4]
    outs, refs = refs[4 : 4 + n_share], refs[4 + n_share :]
    queries, keys, values, sent, a_send, a_recv, b_send, b_recv, s_send, s_recv, own_sem = refs
    n = queries.shape[0] // 2
    m = keys.shape[0] // 2
    scene = lax.axis_index("scene")
    frame = lax.axis_index("frame")
    part = frame // heads
    own = pltpu.make_async_copy(pack_ref.at[lax.rem(frame, heads)], kept_ref.at[frame], own_sem)
    own.start()
    share = Share(frames, pairs, outs, s_send, s_recv)
    enter_scene(frames)

    def to_head(offset):
        target = lax.rem(frame + offset, frames)
        return remote(
            pack_ref.at[lax.rem(target, heads)], kept_ref.at[frame], a_send.at[offset], a_recv.at[offset], (scene, target)
        )

    @pl.loop(1, frames)
    def _(offset):
        to_head(offset).start()

    share.start()
    own.wait()

    @pl.loop(1, frames)
    def _(offset):
        to_head(offset).wait_recv()

    first = pl.multiple_of(part * heads, heads)
    q = packed_part(kept_ref[pl.ds(first, heads)], 0, half)
    low_n, low_m = first_lanes(n), first_lanes(m)
    queries[:n, :] = jnp.where(low_n, q, 0.0).astype(bf16)
    queries[n:, :] = jnp.where(low_n, turn(q), 0.0).astype(bf16)
    k = packed_part(kept_ref[...], 1, half)
    keys[:m, :] = k.astype(bf16)
    keys[m:, :] = turn(k).astype(bf16)
    v = packed_part(kept_ref[...], 2, half)
    open_low, open_high = open_slots(kept_ref[...], half)
    values[:m, :] = jnp.where(open_low, jnp.where(low_m, v, 1.0), 0.0).astype(bf16)
    values[m:, :] = jnp.where(open_high, jnp.where(low_m, turn(v), 1.0), 0.0).astype(bf16)
    low = first_lanes(LANES)

    pair = 2 * half
    place = lax.rem(frame, heads)
    low = first_lanes(pair)
    pieces = heads // 2

    def from_head(target):
        return remote(
            sent.at[target], att_ref.at[place], b_send.at[target], b_recv.at[place], (scene, part * heads + target)
        )

    def turned(piece):
        return lax.rem(piece + place // 2 + 1, pieces)

    def send(piece):
        for index in range(2):
            target = 2 * turned(piece) + index

            @pl.when(target != place)
            def _():
                from_head(target).start()

    @pl.loop(0, pieces)
    def _(piece):
        @pl.when(piece > 0)
        def _():
            send(piece - 1)

        at = pl.multiple_of(turned(piece) * pair, pair)
        some = jnp.concatenate([queries[pl.ds(at, pair), :], queries[pl.ds(n + at, pair), :]], axis=0)
        total = jnp.zeros((2 * pair, LANES), f32)
        for start in range(0, 2 * m, span):
            power = jnp.exp(nt(some, keys[start : start + span, :])).astype(bf16)
            total = total + nn(power, values[start : start + span, :])
        first, second = total[:pair], total[pair:]
        bottom = jnp.where(low, turn(first), second)
        result = jnp.where(low, first, turn(second)) / bottom
        sent[pl.ds(2 * turned(piece), 2)] = result.reshape(2, half, LANES).astype(bf16)
        out_ref[pl.ds(at, pair), :] = result
        log_ref[pl.ds(at, pair), :] = jnp.log(bottom)

    share.relay()
    send(pieces - 1)
    att_ref[place] = sent[place]

    @pl.loop(1, frames)
    def _(offset):
        to_head(offset).wait_send()

    @pl.loop(1, heads)
    def _(offset):
        other = lax.rem(place + offset, heads)
        from_head(other).wait_send()
        remote(
            sent.at[other], att_ref.at[other], b_send.at[other], b_recv.at[other], (scene, part * heads + other)
        ).wait_recv()

    share.close()


any_space = pl.BlockSpec(memory_space=pl.ANY)
vmem_space = pl.BlockSpec(memory_space=pltpu.VMEM)
dma = pltpu.SemaphoreType.DMA


def scene_forward(frames, meta, pack, half, pairs):
    heads = pack.shape[0]
    n = heads * half
    m = frames * half
    span = m // 2
    while span > 640:
        span = span // 2
    flat = [value for pair in pairs for value in pair]
    results = pl.pallas_call(
        partial(scene_body, frames, half, span, len(pairs)),
        name="scene_forward",
        out_shape=[
            sds((heads, half, LANES), bf16),
            sds((frames,) + pack.shape[1:], bf16),
            sds((n, LANES), f32),
            sds((n, LANES), f32),
        ]
        + [sds((3,) + own.shape, bf16) for own, _ in pairs],
        grid_spec=pltpu.PrefetchScalarGridSpec(
            num_scalar_prefetch=1,
            grid=(1,),
            in_specs=[vmem_space] + [any_space] * len(flat),
            out_specs=[vmem_space] * 4 + [any_space] * len(pairs),
            scratch_shapes=[
                pltpu.VMEM((2 * n, LANES), bf16),
                pltpu.VMEM((2 * m, LANES), bf16),
                pltpu.VMEM((2 * m, LANES), bf16),
                pltpu.VMEM((heads, half, LANES), bf16),
                dma((frames,)),
                dma((frames,)),
                dma((heads,)),
                dma((heads,)),
                dma((3 * len(pairs),)),
                dma((3 * len(pairs),)),
                dma(()),
            ],
        ),
        compiler_params=pltpu.CompilerParams(collective_id=1, has_side_effects=True),
        cost_estimate=pl.CostEstimate(flops=16 * n * m * LANES, bytes_accessed=20 * n * LANES, transcendentals=0),
    )(meta, pack, *flat)
    return results[0], results[1], results[2], results[3], results[4:]


def three_lanes(value, closed):
    lane = lax.broadcasted_iota(jnp.int32, value.shape, 1)
    base = LANES // 2
    high = value.astype(bf16).astype(f32)
    rest = value - high
    middle = rest.astype(bf16).astype(f32)
    last = rest - middle
    result = jnp.where(lane == base, high, jnp.where(lane == base + 1, middle, last))
    return jnp.where(lane < base + 3, result, jnp.where(lane == base + 3, closed, 0.0))


def gradient_copies(frames, own, came, send, recv, lanes):
    core, core_peer, scene_peer, cross_peer, _ = peers_of(frames)
    targets = ((core, scene_peer), (1 - core, core_peer), (1 - core, cross_peer))
    return [
        remote(own.at[side, :, lanes], came.at[which, :, lanes], send.at[which], recv.at[which], peer)
        for which, (side, peer) in enumerate(targets)
    ]


def scene_back_body(frames, half, span, n_share, shared, meta, kept_ref, grad_ref, out_ref, log_ref, feed_ref, *refs):
    heads = grad_ref.shape[0]
    pairs = [(refs[2 * index], refs[2 * index + 1]) for index in range(n_share)]
    refs = refs[2 * n_share :]
    back_ref, feed_came, outs, refs = refs[0], refs[1], refs[2 : 2 + n_share], refs[2 + n_share :]
    queries, keys, values, grads, turned, came, sent_q, sent_kv = refs[:8]
    a_send, a_recv, b_send, b_recv, c_send, c_recv, s_send, s_recv, g_send, g_recv = refs[8:]
    n = queries.shape[0] // 2
    m = keys.shape[0] // 2
    scene = lax.axis_index("scene")
    frame = lax.axis_index("frame")
    part = frame // heads
    place = lax.rem(frame, heads)
    share = Share(frames, pairs, outs, s_send, s_recv)
    feed_copies = gradient_copies(frames, feed_ref, feed_came, g_send, g_recv, pl.ds(0, shared))
    enter_scene(frames)

    def to_head(offset):
        target = lax.rem(place + offset, heads)
        return remote(
            grad_ref.at[target], came.at[place], a_send.at[offset], a_recv.at[offset], (scene, part * heads + target)
        )

    @pl.loop(1, heads)
    def _(offset):
        to_head(offset).start()

    share.start()
    for copy in feed_copies:
        copy.start()
    came[place] = grad_ref[place]
    first = pl.multiple_of(part * heads, heads)
    low_n, low_m = first_lanes(n), first_lanes(m)
    base = LANES // 2
    q = packed_part(kept_ref[pl.ds(first, heads)], 0, half)
    log = -log_ref[...]
    queries[:n, :] = jnp.where(low_n, q, three_lanes(turn(log), closed_score)).astype(bf16)
    queries[n:, :] = jnp.where(low_n, turn(q), three_lanes(log, closed_score)).astype(bf16)
    lane = lax.broadcasted_iota(jnp.int32, (m, LANES), 1)
    ones = jnp.where(lane < base + 3, 1.0, 0.0)
    open_low, open_high = open_slots(kept_ref[...], half)
    k = packed_part(kept_ref[...], 1, half)
    for place_at, k_now, is_open in ((0, k, open_low), (m, turn(k), open_high)):
        tail = jnp.where((lane == base + 3) & jnp.logical_not(is_open), 1.0, ones)
        keys[place_at : place_at + m, :] = jnp.where(low_m, k_now, tail).astype(bf16)
    v = packed_part(kept_ref[...], 2, half)
    values[:m, :] = jnp.where(low_m, v, ones).astype(bf16)
    values[m:, :] = jnp.where(low_m, turn(v), ones).astype(bf16)
    turned[...] = jnp.zeros_like(turned)
    low = first_lanes(LANES)

    @pl.loop(1, heads)
    def _(offset):
        to_head(offset).wait_recv()

    g = came[...].astype(f32).reshape(n, LANES)
    delta = -seg_dot(g * out_ref[...], seg_matrix(LANES, base, 1.0))
    grads[:n, :] = jnp.where(low_n, g, three_lanes(turn(delta), 0.0)).astype(bf16)
    grads[n:, :] = jnp.where(low_n, turn(g), three_lanes(delta, 0.0)).astype(bf16)

    pair = 2 * half
    low_pair = first_lanes(pair)
    pieces = frames // 2

    def back_kv(target):
        return remote(
            sent_kv.at[target], back_ref.at[frame, pl.ds(1, 2)], b_send.at[target], b_recv.at[frame], (scene, target)
        )

    def turned_to(piece):
        return lax.rem(piece + frame // 2 + 1, pieces)

    def send(piece):
        for index in range(2):
            target = 2 * turned_to(piece) + index

            @pl.when(target != frame)
            def _():
                back_kv(target).start()

    @pl.loop(0, pieces)
    def _(piece):
        @pl.when(piece > 0)
        def _():
            send(piece - 1)

        at = pl.multiple_of(turned_to(piece) * pair, pair)
        key_part = jnp.concatenate([keys[pl.ds(at, pair), :], keys[pl.ds(m + at, pair), :]], axis=0)
        value_part = jnp.concatenate([values[pl.ds(at, pair), :], values[pl.ds(m + at, pair), :]], axis=0)
        key_turned = jnp.transpose(key_part.astype(f32)).astype(bf16)
        dk = jnp.zeros((2 * pair, LANES), f32)
        dv = jnp.zeros((2 * pair, LANES), f32)
        for start in range(0, 2 * n, span):
            some = queries[start : start + span, :]
            some_grads = grads[start : start + span, :]
            probs = jnp.exp(nt(key_part, some))
            grad_scores = (probs * nt(value_part, some_grads)).astype(bf16)
            dv = dv + nn(probs.astype(bf16), some_grads)
            dk = dk + nn(grad_scores, some)
            turned[:, start : start + span] += nn(key_turned, grad_scores)
        dk = jnp.where(low_pair, dk[:pair], turn(dk[pair:])).reshape(2, half, LANES)
        dv = jnp.where(low_pair, dv[:pair], turn(dv[pair:])).reshape(2, half, LANES)
        sent_kv[pl.ds(2 * turned_to(piece), 2), 0] = dk.astype(bf16)
        sent_kv[pl.ds(2 * turned_to(piece), 2), 1] = dv.astype(bf16)

    share.relay()
    send(pieces - 1)

    scale = base ** (-0.5)
    rows = []
    for at in range(0, n, LANES):
        first = jnp.transpose(turned[:, at : at + LANES])
        second = jnp.transpose(turned[:, n + at : n + at + LANES])
        rows.append(jnp.where(low, first, turn(second)) * scale)
    sent_q[...] = jnp.concatenate(rows, axis=0).reshape(heads, half, LANES).astype(bf16)

    def back_q(offset):
        target = lax.rem(place + offset, heads)
        return remote(
            sent_q.at[target], back_ref.at[frame, 0], c_send.at[offset], c_recv.at[offset], (scene, part * heads + target)
        )

    back_ref[frame, 1] = sent_kv[frame, 0]
    back_ref[frame, 2] = sent_kv[frame, 1]

    @pl.loop(1, heads)
    def _(offset):
        back_q(offset).start()

    back_ref[frame, 0] = sent_q[place]

    @pl.loop(1, heads)
    def _(offset):
        to_head(offset).wait_send()

    @pl.loop(1, frames)
    def _(offset):
        other = lax.rem(frame + offset, frames)
        back_kv(other).wait_send()
        remote(
            sent_kv.at[other], back_ref.at[other, pl.ds(1, 2)], b_send.at[other], b_recv.at[other], (scene, other)
        ).wait_recv()

    @pl.loop(1, heads)
    def _(offset):
        back_q(offset).wait()

    share.close()
    for copy in feed_copies:
        copy.wait()


def scene_backward(frames, meta, kept, grad, out, log, half, pairs, feed_grads, shared):
    heads = grad.shape[0]
    n = heads * half
    m = frames * half
    span = n // 2
    while span > 640:
        span = span // 2
    flat = [value for pair in pairs for value in pair]
    results = pl.pallas_call(
        partial(scene_back_body, frames, half, span, len(pairs), shared),
        name="scene_backward",
        out_shape=[sds((frames, 3, half, LANES), bf16), sds((3,) + feed_grads.shape[1:], bf16)]
        + [sds((3,) + own.shape, bf16) for own, _ in pairs],
        grid_spec=pltpu.PrefetchScalarGridSpec(
            num_scalar_prefetch=1,
            grid=(1,),
            in_specs=[vmem_space] * 4 + [any_space] * (1 + len(flat)),
            out_specs=[vmem_space] + [any_space] * (1 + len(pairs)),
            scratch_shapes=[
                pltpu.VMEM((2 * n, LANES), bf16),
                pltpu.VMEM((2 * m, LANES), bf16),
                pltpu.VMEM((2 * m, LANES), bf16),
                pltpu.VMEM((2 * n, LANES), bf16),
                pltpu.VMEM((LANES, 2 * n), f32),
                pltpu.VMEM((heads, half, LANES), bf16),
                pltpu.VMEM((heads, half, LANES), bf16),
                pltpu.VMEM((frames, 2, half, LANES), bf16),
                dma((heads,)),
                dma((heads,)),
                dma((frames,)),
                dma((frames,)),
                dma((heads,)),
                dma((heads,)),
                dma((3 * len(pairs),)),
                dma((3 * len(pairs),)),
                dma((3,)),
                dma((3,)),
            ],
        ),
        compiler_params=pltpu.CompilerParams(collective_id=2, has_side_effects=True),
        cost_estimate=pl.CostEstimate(flops=40 * n * m * LANES, bytes_accessed=30 * n * LANES, transcendentals=0),
    )(meta, kept, grad, out, log, feed_grads, *flat)
    back = results[0]
    if frames > heads:
        place = lax.axis_index("frame") // heads * heads
        dq = lax.dynamic_slice(back, (place, 0, 0, 0), (heads, 1, half, LANES))
        both = back.reshape(frames // heads, heads, 3, half, LANES)[:, :, 1:].astype(f32).sum(0)
        back = jnp.concatenate([dq, both.astype(bf16)], axis=1)
    return back, results[1], results[2:]


def feed_body(
    block, packed, meta, att_ref, x_ref, mixer_ref, mixer_bias, mixer_scale, gain_ref, shift_ref,
    inner_ref, inner_bias, outer_ref, outer_bias, outer_scale,
    own_ref, other_ref, middle_ref, branch_ref, feed_ref, slope_ref, out_ref, normed_ref, total_ref
):
    step = pl.program_id(0)
    steps = pl.num_programs(0)
    rows, width = middle_ref.shape
    hidden_half = own_ref.shape[1] - width
    half_steps = hidden_half // CHUNK
    mine = lax.axis_index("scene")

    def split(value, at):
        first, second = value[:, : width // 2], value[:, width // 2 :]

        @pl.when(mine == 0)
        def _():
            own_ref[:, at : at + width // 2] = first
            other_ref[:, at : at + width // 2] = second

        @pl.when(mine != 0)
        def _():
            own_ref[:, at : at + width // 2] = second
            other_ref[:, at : at + width // 2] = first

    @pl.when(step == 0)
    def _():
        if packed:
            pieces = []
            for pair in range(width // LANES):
                pieces.append(
                    unpack_pair(att_ref[2 * pair].astype(f32), att_ref[2 * pair + 1].astype(f32))
                )
            attended = jnp.concatenate(pieces, axis=1).astype(bf16)
        else:
            attended = att_ref[...]
        branch = nn(attended, mixer_ref[0]) + row(mixer_bias, block)
        middle = x_ref[...].astype(f32) + row(mixer_scale, block) * branch
        hat, _ = center_norm(middle, norm_eps)
        normed = (hat * row(gain_ref, block) + row(shift_ref, block)).astype(bf16)
        branch_ref[...] = branch
        middle_ref[...] = middle
        normed_ref[...] = normed
        split(normed, hidden_half)
        split(attended, hidden_half + width // 2)
        total_ref[...] = jnp.zeros_like(total_ref)

    pre = nn(normed_ref[...], inner_ref[0]) + row(inner_bias, block)
    share = 0.5 * (1.0 + erf(pre * (2.0 ** (-0.5))))
    slope_ref[...] = share + pre * jnp.exp(-0.5 * pre * pre) * 0.3989422804014327
    hidden = (pre * share).astype(bf16)
    place = pl.multiple_of(lax.rem(step, half_steps) * CHUNK, CHUNK)

    @pl.when(step // half_steps == mine)
    def _():
        own_ref[:, pl.ds(place, CHUNK)] = hidden

    @pl.when(step // half_steps != mine)
    def _():
        other_ref[:, pl.ds(place, CHUNK)] = hidden

    total_ref[...] += nn(hidden, outer_ref[0])

    @pl.when(step == steps - 1)
    def _():
        feed = total_ref[...] + row(outer_bias, block)
        feed_ref[...] = feed
        result = middle_ref[...] + row(outer_scale, block) * feed
        if packed:
            place = lax.broadcasted_iota(jnp.int32, result.shape, 0)
            result = jnp.where(place < meta[0] + SPECIAL, result, 0.0)
        out_ref[...] = result.astype(out_ref.dtype)


def feed_forward(block, packed, meta, att, x, mixer, mixer_bias, mixer_scale, gain, shift, inner, inner_bias, outer, outer_bias, outer_scale):
    rows, width = x.shape
    hidden = inner.shape[2]
    kept = hidden // 2 + width
    steps = hidden // CHUNK
    vector = full(gain.shape)
    return call(
        partial(feed_body, block, packed),
        f"feed_forward_{block}",
        (steps,),
        [
            full(att.shape),
            full((rows, width)),
            pl.BlockSpec((1, width, width), lambda j, m: (block, 0, 0)),
            vector, vector, vector, vector,
            pl.BlockSpec((1, width, CHUNK), lambda j, m: (block, 0, j)),
            pl.BlockSpec((2, CHUNK), lambda j, m: (0, j)),
            pl.BlockSpec((1, CHUNK, width), lambda j, m: (block, j, 0)),
            vector, vector,
        ],
        [full((rows, kept))] * 2
        + [full((rows, width))] * 3
        + [pl.BlockSpec((rows, CHUNK), lambda j, m: (0, j)), full((rows, width))],
        [sds((rows, kept), bf16)] * 2
        + [sds((rows, width), f32)] * 3
        + [sds((rows, hidden), f32), sds((rows, width), bf16 if packed else f32)],
        [pltpu.VMEM((rows, width), bf16), pltpu.VMEM((rows, width), f32)],
        2 * rows * width * (2 * hidden + width),
        4 * width * hidden + 4 * rows * hidden + 30 * rows * width,
    )(meta, att, x, mixer, mixer_bias, mixer_scale, gain, shift, inner, inner_bias, outer, outer_bias, outer_scale)


def feed_back_core(
    block, packed, step, steps, chunk, meta, g_ref, feed_ref, slope_ref, middle_ref, branch_ref,
    outer_scale, gain_ref, mixer_scale, outer_ref, inner_ref, mixer_ref,
    grads_ref, g_middle_ref, g_att_ref, vector_ref, g_feed_ref, total_ref
):
    rows, width = total_ref.shape
    half_steps = steps // 2
    at_branch = width // 2 + half_steps * CHUNK

    def incoming():
        g = g_ref[...].astype(f32)
        if packed:
            place = lax.broadcasted_iota(jnp.int32, g.shape, 0)
            g = jnp.where(place < meta[0] + SPECIAL, g, 0.0)
        return g

    @pl.when(step == 0)
    def _():
        g = incoming()
        g_feed = (g * row(outer_scale, block)).astype(bf16)
        g_feed_ref[...] = g_feed
        grads_ref[0, :, : width // 2] = g_feed[:, : width // 2]
        grads_ref[1, :, : width // 2] = g_feed[:, width // 2 :]
        vector_ref[0:1, :] = col_sum(g * feed_ref[...])
        vector_ref[1:2, :] = col_sum(g_feed.astype(f32))
        total_ref[...] = jnp.zeros_like(total_ref)

    g_pre = (nt(g_feed_ref[...], outer_ref[0]) * slope_ref[...]).astype(bf16)
    place = pl.multiple_of(width // 2 + lax.rem(chunk, half_steps) * CHUNK, CHUNK)
    grads_ref[chunk // half_steps, :, pl.ds(place, CHUNK)] = g_pre
    per_row = width // CHUNK
    lanes = pl.ds(pl.multiple_of(lax.rem(chunk, per_row) * CHUNK, CHUNK), CHUNK)
    vector_ref[pl.ds(6 + chunk // per_row, 1), lanes] = col_sum(g_pre.astype(f32))
    total_ref[...] += nt(g_pre, inner_ref[0])

    @pl.when(step == steps - 1)
    def _():
        hat, spread = center_norm(middle_ref[...], norm_eps)
        g_nm = total_ref[...]
        vector_ref[2:3, :] = col_sum(g_nm * hat)
        vector_ref[3:4, :] = col_sum(g_nm)
        g_middle = incoming() + norm_back(g_nm * row(gain_ref, block), hat, spread)
        g_middle_ref[...] = g_middle
        vector_ref[4:5, :] = col_sum(g_middle * branch_ref[...])
        g_branch = (g_middle * row(mixer_scale, block)).astype(bf16)
        vector_ref[5:6, :] = col_sum(g_branch.astype(f32))
        grads_ref[0, :, at_branch : at_branch + width // 2] = g_branch[:, : width // 2]
        grads_ref[1, :, at_branch : at_branch + width // 2] = g_branch[:, width // 2 :]
        g_att = nt(g_branch, mixer_ref[0])
        if packed:
            for pair in range(width // LANES):
                even, odd = pack_pair(g_att[:, pair * LANES : (pair + 1) * LANES])
                g_att_ref[2 * pair] = even.astype(bf16)
                g_att_ref[2 * pair + 1] = odd.astype(bf16)
        else:
            g_att_ref[...] = g_att.astype(bf16)


def feed_back_body(block, packed, meta, *refs):
    step = pl.program_id(0)
    feed_back_core(block, packed, step, pl.num_programs(0), step, meta, *refs)


def feed_backward(block, packed, heads, meta, g, feed, slope, middle, branch, outer_scale, gain, mixer_scale, outer, inner, mixer):
    rows, width = middle.shape
    hidden = inner.shape[2]
    steps = hidden // CHUNK
    vector = full(gain.shape)
    vector_rows = 6 + hidden // width
    att_shape = (heads, rows // 2, LANES) if packed else (rows, width)
    return call(
        partial(feed_back_body, block, packed),
        f"feed_backward_{block}",
        (steps,),
        [
            full((rows, width)),
            full((rows, width)),
            pl.BlockSpec((rows, CHUNK), lambda j, m: (0, j)),
            full((rows, width)),
            full((rows, width)),
            vector, vector, vector,
            pl.BlockSpec((1, CHUNK, width), lambda j, m: (block, j, 0)),
            pl.BlockSpec((1, width, CHUNK), lambda j, m: (block, 0, j)),
            pl.BlockSpec((1, width, width), lambda j, m: (block, 0, 0)),
        ],
        [
            full((2, rows, width + hidden // 2)),
            full((rows, width)),
            full(att_shape),
            full((vector_rows, width)),
        ],
        [
            sds((2, rows, width + hidden // 2), bf16),
            sds((rows, width), f32),
            sds(att_shape, bf16),
            sds((vector_rows, width), f32),
        ],
        [pltpu.VMEM((rows, width), bf16), pltpu.VMEM((rows, width), f32)],
        2 * rows * width * (2 * hidden + width),
        4 * width * hidden + 8 * rows * hidden + 20 * rows * width,
    )(meta, g, feed, slope, middle, branch, outer_scale, gain, mixer_scale, outer, inner, mixer)


def joint_back_core(
    block, head, step, steps, chunk, g, pre_ref, x_ref, g_middle_ref, gain_ref, q_gain_ref, k_gain_ref, w_ref,
    grads_ref, at_joined, out_ref, vector_ref, total_ref
):
    rows, width = total_ref.shape
    per_part = width // CHUNK
    half_steps = steps // 2

    @pl.when(step == 0)
    def _():
        total_ref[...] = jnp.zeros_like(total_ref)

    in_row = pl.ds(pl.multiple_of(lax.rem(chunk, per_part) * CHUNK, CHUNK), CHUNK)

    def finish(g_joined):
        rounded = g_joined.astype(bf16)
        place = pl.multiple_of(at_joined + lax.rem(chunk, half_steps) * CHUNK, CHUNK)
        grads_ref[chunk // half_steps, :, pl.ds(place, CHUNK)] = rounded
        vector_ref[pl.ds(2 + chunk // per_part, 1), in_row] = col_sum(rounded.astype(f32))
        total_ref[...] += nt(rounded, w_ref[0])

    def head_back(gain, gain_row, shift_row):
        mean_matrix = seg_matrix(SLAB, head, 1.0 / head)
        pieces = []
        for slab in range(CHUNK // SLAB):
            at = slab * SLAB
            g_now = g[:, at : at + SLAB]
            hat, spread = seg_norm(pre_ref[:, at : at + SLAB], mean_matrix)
            vector_ref[gain_row : gain_row + 1, at : at + SLAB] += col_sum(g_now * hat)
            if shift_row is not None:
                vector_ref[shift_row : shift_row + 1, at : at + SLAB] += col_sum(g_now)
            grad_hat = g_now * gain
            pieces.append(
                spread
                * (
                    grad_hat
                    - seg_dot(grad_hat, mean_matrix)
                    - hat * seg_dot(grad_hat * hat, mean_matrix)
                )
            )
        finish(jnp.concatenate(pieces, axis=1))

    @pl.when(chunk < per_part)
    def _():
        head_back(repeated(q_gain_ref, block), 5, 6)

    @pl.when((chunk >= per_part) & (chunk < 2 * per_part))
    def _():
        head_back(repeated(k_gain_ref, block), 7, None)

    @pl.when(chunk >= 2 * per_part)
    def _():
        finish(g)

    @pl.when(step == steps - 1)
    def _():
        hat, spread = center_norm(x_ref[...].astype(f32), norm_eps)
        g_normed = total_ref[...]
        vector_ref[0:1, :] = col_sum(g_normed * hat)
        vector_ref[1:2, :] = col_sum(g_normed)
        result = g_middle_ref[...] + norm_back(g_normed * row(gain_ref, block), hat, spread)
        out_ref[...] = result.astype(out_ref.dtype)


class Rows:
    def __init__(self, ref, lead, base):
        self.ref, self.lead, self.base = ref, lead, base

    def at(self, key):
        rows, lanes = key
        if isinstance(rows, slice):
            rows = slice(rows.start + self.base, rows.stop + self.base)
        else:
            rows = pl.ds(rows.start + self.base, rows.size)
        return self.lead, rows, lanes

    def __getitem__(self, key):
        return self.ref[self.at(key)]

    def __setitem__(self, key, value):
        self.ref[self.at(key)] = value


class Plan:
    def __init__(self, frames, rows, width, hidden):
        self.half = width // 2
        self.hidden_half = hidden // 2
        self.chips = frames // 2
        self.stages = self.chips.bit_length() - 1
        self.deep = self.half // self.chips // 2
        self.n_outer = CHUNK // LANES
        self.n_inner = self.hidden_half // CHUNK
        self.n_joint = 3 * self.half // CHUNK
        self.per_block = self.n_outer + self.n_inner + 1 + self.n_joint
        self.n_pieces = self.n_inner + self.n_joint + 2
        self.total = 2 * self.per_block
        self.joint_steps = 2 * self.n_joint
        self.feed_steps = 2 * self.n_inner
        self.slabs = 4
        self.frame_steps = width // LANES // self.slabs
        self.feed_at = self.joint_steps
        self.frame_at = self.feed_at + self.feed_steps
        self.joint_at = self.frame_at + self.frame_steps
        self.compute_end = self.joint_at + self.joint_steps
        self.leave = []
        for piece in range(SHARED_PIECES, 1 + self.n_inner + 1):
            self.leave.append((1 + piece - SHARED_PIECES, 0, piece))
        at_joined = 2 + self.n_inner
        for piece in range(self.n_joint):
            self.leave.append((2 + 2 * piece, 0, at_joined + piece))
        self.leave.append((self.feed_at + 1, 1, 0))
        for piece in range(self.n_inner):
            self.leave.append((self.feed_at + 2 + 2 * piece, 1, 1 + piece))
        self.leave.append((self.frame_at + 1, 1, 1 + self.n_inner))
        for piece in range(self.n_joint):
            self.leave.append((self.joint_at + 2 + 2 * piece, 1, at_joined + piece))
        first = 1
        for slot, block, piece in self.leave:
            unit = 0 if piece == 0 else piece + self.n_outer - 1
            first = max(first, slot + AHEAD - block * self.per_block - unit)
        self.first = first
        self.ring = 12
        self.lags = [LAG * (stage + 1) for stage in range(self.stages)]
        self.end_lag = self.lags[-1] + 2
        self.n_vector = 4 + self.stages
        self.vector_at = [self.compute_end]
        for wait in [1, 2] + [VECTOR_LAG] * self.stages + [1, 1]:
            self.vector_at.append(self.vector_at[-1] + wait)
        self.slots = max(self.first + self.total + self.end_lag, self.vector_at[-1] + 1)


def rear_body(plan, frames, head, meta, *refs):
    (
        back_ref, pre1_ref, x1_ref, g_middle1_ref, gain_ref, q_gain_ref, k_gain_ref, joint_ref,
        outer_scale, second_gain, mixer_scale, outer_ref, inner_ref, slope_ref, pre0_ref,
        mixer_in, feed_in, middle_in, branch_in, qkv_in, x0_in,
        feed_g, came_in, feed_x1, feed_three1, joint_x1, joint_three1, feed_x0, feed_three0, joint_x0, joint_three0,
        vector_in,
    ) = refs[:32]
    tokens_ref, outer_out, inner_out, mixer_out, joint_out, vector_out = refs[32:38]
    (
        own, came, acts, hids, act_turned, hid_turned, parts, last, sums, v_half, v_part,
        mixer, feed0, middle0, branch0, qkv0, x0,
        g1, g_middle0, g_att0, g_feed, g_qkv, total_sum,
    ) = refs[38:61]
    steps = refs[61 : 61 + plan.stages]
    load_sem, act_sem, hid_sem, g_send, g_recv, p_send, p_recv, f_send, f_recv, v_send, v_recv = refs[61 + plan.stages :]
    slot = pl.program_id(0)
    rows = own.shape[2]
    half, hidden_half, chips, total = plan.half, plan.hidden_half, plan.chips, plan.total
    width = 2 * half
    per_block, n_outer, n_inner = plan.per_block, plan.n_outer, plan.n_inner
    at_joined = (2 + n_inner) * CHUNK
    core, core_peer, scene_peer, cross_peer, bits = peers_of(frames)
    vector_rows = 6 + hidden_half * 2 // width
    section = vector_rows + 8

    sources = [
        (feed_g, own.at[0, :, :, pl.ds(0, at_joined)]),
        (came_in.at[:, :, pl.ds(0, SHARED_PIECES * CHUNK)], came.at[0, :, :, pl.ds(0, SHARED_PIECES * CHUNK)]),
        (feed_in, feed0),
        (mixer_in.at[pl.ds(0, 1)], mixer),
        (middle_in, middle0),
        (branch_in, branch0),
        (qkv_in, qkv0),
        (x0_in, x0),
    ]

    def load(index):
        return pltpu.make_async_copy(sources[index][0], sources[index][1], load_sem.at[index])

    def act_loads(block):
        feed_x, feed_three, joint_x, joint_three = (
            (feed_x1, feed_three1, joint_x1, joint_three1),
            (feed_x0, feed_three0, joint_x0, joint_three0),
        )[block]
        copies = []
        for place in range(4):
            feed_from = feed_x if place == 0 else feed_three.at[place - 1]
            joint_from = joint_x if place == 0 else joint_three.at[place - 1]
            copies.append(pltpu.make_async_copy(
                feed_from.at[:, pl.ds(hidden_half, width)], acts.at[place, :, pl.ds(0, width)], act_sem.at[2 * place]
            ))
            copies.append(pltpu.make_async_copy(
                joint_from, acts.at[place, :, pl.ds(width, half)], act_sem.at[2 * place + 1]
            ))
        return copies

    def hid_loads(block):
        feed_x, feed_three = ((feed_x1, feed_three1), (feed_x0, feed_three0))[block]
        return [
            pltpu.make_async_copy(
                (feed_x if place == 0 else feed_three.at[place - 1]).at[:, pl.ds(0, hidden_half)],
                hids.at[place],
                hid_sem.at[place],
            )
            for place in range(4)
        ]

    def piece_copy(block, piece, which):
        lanes = pl.ds(pl.multiple_of(piece * CHUNK, CHUNK), CHUNK)
        side = core if which == 0 else 1 - core
        return remote(
            own.at[block, side, :, lanes],
            came.at[block, which, :, lanes],
            g_send.at[block, which, piece],
            g_recv.at[block, which, piece],
            (scene_peer, core_peer, cross_peer)[which],
        )

    targets = [core_peer, scene_peer, cross_peer] + [peer for _, peer in bits]

    @pl.when(slot == 0)
    def _():
        load(0).start()
        for copy in hid_loads(0):
            copy.start()
        load(1).start()
        for copy in act_loads(0):
            copy.start()
        for index in range(2, len(sources)):
            load(index).start()
        sums[0] = jnp.zeros(sums.shape[1:], f32)
        for index in range(vector_rows):
            sums[0, section + index : section + index + 1, :] = vector_in[index : index + 1, :]
        greet(targets)

    def spread(step, steps_of):
        return lax.rem(step, 2) * (steps_of // 2) + step // 2

    @pl.when(slot < plan.joint_steps)
    def _():
        pieces = []
        for pair in range(CHUNK // LANES):
            pieces.append(
                unpack_pair(back_ref[2 * pair, 0].astype(f32), back_ref[2 * pair + 1, 0].astype(f32))
            )
        joint_back_core(
            1, head, slot, plan.joint_steps, spread(slot, plan.joint_steps), jnp.concatenate(pieces, axis=1),
            pre1_ref, x1_ref, g_middle1_ref, gain_ref, q_gain_ref, k_gain_ref, joint_ref,
            own.at[0], at_joined, g1, Rows(sums, 0, section + vector_rows), total_sum,
        )

    @pl.when(slot == plan.feed_at)
    def _():
        for index in range(2, len(sources)):
            load(index).wait()

    @pl.when((slot >= plan.feed_at) & (slot < plan.frame_at))
    def _():
        step = slot - plan.feed_at
        feed_back_core(
            0, False, step, plan.feed_steps, spread(step, plan.feed_steps), meta, g1, feed0, slope_ref, middle0, branch0,
            outer_scale, second_gain, mixer_scale, outer_ref, inner_ref, mixer,
            own.at[1], g_middle0, g_att0, Rows(sums, 0, 0), g_feed, total_sum,
        )

    @pl.when((slot >= plan.frame_at) & (slot < plan.joint_at))
    def _():
        @pl.loop(0, plan.slabs)
        def _(slab):
            at = ((slot - plan.frame_at) * plan.slabs + slab) * LANES
            frame_back_slab(at, meta, qkv0, g_att0, g_qkv)

    @pl.when((slot >= plan.joint_at) & (slot < plan.compute_end))
    def _():
        step = slot - plan.joint_at
        chunk = spread(step, plan.joint_steps)
        joint_back_core(
            0, head, step, plan.joint_steps, chunk,
            g_qkv[:, pl.ds(pl.multiple_of(chunk * CHUNK, CHUNK), CHUNK)],
            pre0_ref, x0, g_middle0, gain_ref, q_gain_ref, k_gain_ref, joint_ref,
            own.at[1], at_joined, tokens_ref, Rows(sums, 0, vector_rows), total_sum,
        )

    def swapped(index):
        return lax.rem(index, SWAP_EVERY) == 1

    def way(stage, index):
        value, peer = bits[stage]
        if stage > 1:
            return value, peer
        other_value, other_peer = bits[1 - stage]
        changed = swapped(index)
        return jnp.where(changed, other_value, value), (peer[0], jnp.where(changed, other_peer[1], peer[1]))

    def stage_start(stage, index):
        value, peer = way(stage, index)
        source = parts if stage == 0 else steps[stage - 1]
        held = lax.rem(index, plan.ring)
        for pair in range(chips >> (stage + 1)):
            remote(
                source.at[held, 2 * pair + 1 - value],
                steps[stage].at[held, pair],
                p_send.at[stage, held],
                p_recv.at[stage, held],
                peer,
            ).start()

    def stage_whole(stage, index):
        held = lax.rem(index, plan.ring)
        return remote(
            steps[stage].at[held], steps[stage].at[held], p_send.at[stage, held], p_recv.at[stage, held], way(stage, index)[1]
        )

    def last_copy(index):
        held = lax.rem(index, plan.ring)
        return remote(
            steps[-1].at[held, 0, 1 - core], last.at[held], f_send.at[held], f_recv.at[held], core_peer
        )

    def store(index, value):
        changed = swapped(index)
        held = lax.rem(index, plan.ring)

        @pl.when(jnp.logical_not(changed))
        def _():
            parts[held] = value.astype(bf16)

        @pl.when(changed)
        def _():
            pairs = value.reshape((chips // 4, 2, 2) + value.shape[1:])
            pairs = jnp.stack([pairs[:, :, place] for place in range(2)], axis=1)
            parts[held] = pairs.reshape(value.shape).astype(bf16)

    def multiply(index):
        block = index // per_block
        unit = lax.rem(index, per_block)

        def wait_piece(piece):
            @pl.when((block > 0) | (piece >= SHARED_PIECES))
            def _():
                for which in range(3):
                    piece_copy(block, piece, which).wait_recv()

        def gathered(lanes):
            return jnp.concatenate(
                [own[block, core, :, lanes]] + [came[block, which, :, lanes] for which in range(3)], axis=0
            )

        @pl.when(unit < n_outer)
        def _():
            @pl.when(unit == 0)
            def _():
                wait_piece(0)
                hid_turned[...] = jnp.transpose(jnp.concatenate([hids[place] for place in range(4)], axis=0))

            right = gathered(pl.ds(pl.multiple_of(unit * LANES, LANES), LANES))
            value = nn(hid_turned[...], right)
            value = value.reshape(chips, 2, 4, plan.deep, LANES)
            store(index, jnp.concatenate([value[:, :, place] for place in range(4)], axis=-1))

        @pl.when(unit >= n_outer)
        def _():
            piece = unit - (n_outer - 1)
            wait_piece(piece)

            for place, at in enumerate((n_outer, n_outer + n_inner, n_outer + n_inner + 1)):

                @pl.when(unit == at)
                def _():
                    left = [acts[source, :, place * half : (place + 1) * half] for source in range(4)]
                    act_turned[...] = jnp.transpose(jnp.concatenate(left, axis=0))

            value = nn(act_turned[...], gathered(pl.ds(pl.multiple_of(piece * CHUNK, CHUNK), CHUNK)))
            store(index, value.reshape(chips, 2, plan.deep, CHUNK))

    def put(index, side, value):
        block = 1 - index // per_block
        unit = lax.rem(index, per_block)

        @pl.when(unit < n_outer)
        def _():
            lanes = pl.ds(pl.multiple_of(side * half + unit * LANES, LANES), LANES)
            for place in range(4):
                outer_out[block, place * plan.deep : (place + 1) * plan.deep, lanes] = (
                    value[:, place * LANES : (place + 1) * LANES]
                )

        def wide(first, count, target):
            @pl.when((unit >= first) & (unit < first + count))
            def _():
                lanes = pl.ds(pl.multiple_of((side * count + unit - first) * CHUNK, CHUNK), CHUNK)
                target[block, :, lanes] = value

        wide(n_outer, n_inner, inner_out)
        wide(n_outer + n_inner, 1, mixer_out)
        wide(n_outer + n_inner + 1, plan.n_joint, joint_out)

    def add(stage, index):
        stage_whole(stage, index).wait()
        value = way(stage, index)[0]
        held = lax.rem(index, plan.ring)
        source = parts if stage == 0 else steps[stage - 1]
        for pair in range(chips >> (stage + 1)):
            result = source[held, 2 * pair + value].astype(f32) + steps[stage][held, pair].astype(f32)
            if stage + 1 == plan.stages:
                put(index, core, jnp.where(core == 0, result[0], result[1]))
            steps[stage][held, pair] = result.astype(bf16)

    def close(index):
        last_copy(index).wait()
        put(index, 1 - core, last[lax.rem(index, plan.ring)].astype(f32))

    def when_due(lag, action):
        index = slot - plan.first - lag

        @pl.when((index >= 0) & (index < total))
        def _():
            action(index)

    scene = lax.axis_index("scene")
    wide, narrow = width // 2, width // 4

    def lanes_of(side, size):
        return pl.ds(pl.multiple_of(side * size, size), size)

    n_chip = plan.stages
    vector_peers = [core_peer, scene_peer] + [peer for _, peer in bits] + [scene_peer, core_peer]

    def vector_copy(stage):
        if stage == 0:
            source, target = sums.at[0, :, lanes_of(1 - core, wide)], v_half.at[0]
        elif stage == 1:
            source, target = v_half.at[1, :, lanes_of(1 - scene, narrow)], v_part.at[0]
        elif stage < 2 + n_chip:
            source, target = v_part.at[2 * stage - 3], v_part.at[2 * stage - 2]
        elif stage == 2 + n_chip:
            source, target = v_part.at[2 * stage - 3], v_part.at[2 * stage - 2]
        else:
            source, target = v_half.at[2], v_half.at[3]
        return remote(source, target, v_send.at[stage], v_recv.at[stage], vector_peers[stage])

    def vector_step(stage):
        vector_copy(stage).wait()
        if stage == 0:
            v_half[1] = sums[0, :, lanes_of(core, wide)] + v_half[0]
        elif stage == 1:
            v_part[1] = v_half[1, :, lanes_of(scene, narrow)] + v_part[0]
        elif stage < 2 + n_chip:
            v_part[2 * stage - 1] = v_part[2 * stage - 3] + v_part[2 * stage - 2]
        elif stage == 2 + n_chip:
            v_half[2, :, lanes_of(scene, narrow)] = v_part[2 * stage - 3]
            v_half[2, :, lanes_of(1 - scene, narrow)] = v_part[2 * stage - 2]
        else:
            vector_out[:, lanes_of(core, wide)] = v_half[2]
            vector_out[:, lanes_of(1 - core, wide)] = v_half[3]

    @pl.when(slot == 0)
    def _():
        pl.semaphore_wait(pltpu.get_barrier_semaphore(), len(targets))
        load(0).wait()

    @pl.when(slot == plan.first)
    def _():
        load(1).wait()
        for copy in hid_loads(0):
            copy.wait()

    @pl.when(slot == plan.first + n_outer)
    def _():
        for copy in act_loads(0):
            copy.wait()

    when_due(0, multiply)
    for stage in range(plan.stages):
        when_due(plan.lags[stage], partial(add, stage))
    when_due(plan.end_lag, close)

    for stage in range(plan.n_vector):

        @pl.when(slot == plan.vector_at[stage + 1])
        def _():
            vector_step(stage)

    for stage in range(plan.stages - 1):
        when_due(plan.lags[stage], partial(stage_start, stage + 1))
    when_due(plan.lags[-1], lambda index: last_copy(index).start())
    when_due(0, partial(stage_start, 0))

    for at, block, piece in plan.leave:

        @pl.when(slot == at)
        def _():
            for which in range(3):
                piece_copy(block, piece, which).start()

    for stage in range(plan.n_vector):

        @pl.when(slot == plan.vector_at[stage])
        def _():
            vector_copy(stage).start()

    @pl.when(slot == plan.first + 1)
    def _():
        for copy in hid_loads(1):
            copy.start()

    @pl.when(slot == plan.first + per_block - 1)
    def _():
        for copy in hid_loads(1):
            copy.wait()

    @pl.when(slot == plan.first + n_outer + n_inner + 1)
    def _():
        for copy in act_loads(1):
            copy.start()

    @pl.when(slot == plan.first + per_block + n_outer - 1)
    def _():
        for copy in act_loads(1):
            copy.wait()

    @pl.when(slot == plan.slots - 1)
    def _():
        for at, block, piece in plan.leave:
            for which in range(3):
                piece_copy(block, piece, which).wait_send()


def rear(frames, head, meta, back, pre1, x1, g_middle1, gain, pattern, joint, outer_scale, second_gain, mixer_scale, outer, inner, slope0, pre0, mixer, feed0, middle0, branch0, qkv0, x0, feed_g1, came1, shares, vector1):
    rows, width = x1.shape
    hidden = inner.shape[2]
    half = width // 2
    plan = Plan(frames, rows, width, hidden)
    per_part = width // CHUNK
    vector_rows = vector1.shape[0]
    n_vector_rows = 2 * (vector_rows + 8)

    def clip(value, size):
        return jnp.minimum(jnp.maximum(value, 0), size - 1)

    def spread(step, steps):
        return lax.rem(step, 2) * (steps // 2) + step // 2

    def chunk1(slot):
        return spread(clip(slot, plan.joint_steps), plan.joint_steps)

    def chunk0(slot):
        return spread(clip(slot - plan.joint_at, plan.joint_steps), plan.joint_steps)

    def chunk_feed(slot):
        return spread(clip(slot - plan.feed_at, plan.feed_steps), plan.feed_steps)

    def back_map(slot, m):
        chunk = chunk1(slot)
        return (lax.rem(chunk, per_part), chunk // per_part, 0, 0)

    def joint_map(slot, m):
        late = slot >= plan.feed_at
        return (jnp.where(late, 0, 1), 0, jnp.where(late, chunk0(slot), chunk1(slot)))

    once = dict(pipeline_mode=pl.Buffered(1))
    single = lambda shape: pl.BlockSpec(shape, lambda *_: (0,) * len(shape), **once)
    out_shape = [
        sds((rows, width), bf16),
        sds((2, 4 * plan.deep, width), f32),
        sds((2, plan.deep, hidden), f32),
        sds((2, plan.deep, width), f32),
        sds((2, plan.deep, 3 * width), f32),
        sds((n_vector_rows, width), f32),
    ]
    container = (plan.ring, plan.chips, 2, plan.deep, CHUNK)
    return pl.pallas_call(
        partial(rear_body, plan, frames, head),
        name="rear",
        out_shape=out_shape,
        grid_spec=pltpu.PrefetchScalarGridSpec(
            num_scalar_prefetch=1,
            grid=(plan.slots,),
            in_specs=[
                pl.BlockSpec((CHUNK // head, 1, rows // 2, LANES), back_map),
                pl.BlockSpec((rows, CHUNK), lambda j, m: (0, jnp.minimum(chunk1(j), 2 * per_part - 1))),
                single(x1.shape),
                single(g_middle1.shape),
                single(gain.shape),
                single(pattern[0].shape), single(pattern[2].shape),
                pl.BlockSpec((1, width, CHUNK), joint_map),
                single(outer_scale.shape),
                single(second_gain.shape),
                single(mixer_scale.shape),
                pl.BlockSpec((1, CHUNK, width), lambda j, m: (0, chunk_feed(j), 0)),
                pl.BlockSpec((1, width, CHUNK), lambda j, m: (0, 0, chunk_feed(j))),
                pl.BlockSpec((rows, CHUNK), lambda j, m: (0, chunk_feed(j))),
                pl.BlockSpec((rows, CHUNK), lambda j, m: (0, jnp.minimum(chunk0(j), 2 * per_part - 1))),
            ]
            + [any_space] * 16
            + [single(vector1.shape)],
            out_specs=[vmem_space] * len(out_shape),
            scratch_shapes=[
                pltpu.VMEM((2, 2, rows, plan.n_pieces * CHUNK), bf16),
                pltpu.VMEM((2, 3, rows, plan.n_pieces * CHUNK), bf16),
                pltpu.VMEM((4, rows, 3 * half), bf16),
                pltpu.VMEM((4, rows, plan.hidden_half), bf16),
                pltpu.VMEM((half, 4 * rows), bf16),
                pltpu.VMEM((plan.hidden_half, 4 * rows), bf16),
                pltpu.VMEM(container, bf16),
                pltpu.VMEM((plan.ring, plan.deep, CHUNK), bf16),
                pltpu.VMEM((1, n_vector_rows, width), f32),
                pltpu.VMEM((4, n_vector_rows, half), f32),
                pltpu.VMEM((2 * plan.stages + 3, n_vector_rows, half // 2), f32),
                pltpu.VMEM((1, width, width), bf16),
                pltpu.VMEM((rows, width), f32),
                pltpu.VMEM((rows, width), f32),
                pltpu.VMEM((rows, width), f32),
                pltpu.VMEM((rows, 3 * width), bf16),
                pltpu.VMEM((rows, width), bf16),
                pltpu.VMEM((rows, width), f32),
                pltpu.VMEM((rows, width), f32),
                pltpu.VMEM((rows, width), bf16),
                pltpu.VMEM((rows, width), bf16),
                pltpu.VMEM((rows, 3 * width), f32),
                pltpu.VMEM((rows, width), f32),
            ]
            + [pltpu.VMEM((plan.ring, plan.chips >> (stage + 1)) + container[2:], bf16) for stage in range(plan.stages)]
            + [
                dma((8,)),
                dma((8,)),
                dma((4,)),
                dma((2, 3, plan.n_pieces)),
                dma((2, 3, plan.n_pieces)),
                dma((plan.stages, plan.ring)),
                dma((plan.stages, plan.ring)),
                dma((plan.ring,)),
                dma((plan.ring,)),
                dma((plan.n_vector,)),
                dma((plan.n_vector,)),
            ],
        ),
        compiler_params=pltpu.CompilerParams(
            collective_id=0, has_side_effects=True, vmem_limit_bytes=64 * 1024 * 1024 - 65536
        ),
        cost_estimate=pl.CostEstimate(flops=2 * rows * width * hidden * 20, bytes_accessed=60 * width * hidden, transcendentals=0),
    )(
        meta, back, pre1, x1, g_middle1, gain, pattern[0], pattern[2], joint, outer_scale, second_gain, mixer_scale, outer, inner, slope0, pre0,
        mixer, feed0, middle0, branch0, qkv0, x0, feed_g1, came1, *shares, vector1,
    )


def finish_body(heads, meta, vectors_ref, *refs):
    count = 5
    large_in, large_out = refs[:count], refs[count : 2 * count]
    (
        first_gain, first_shift, joint_bias, query_gain, query_shift, key_gain, mixer_bias, mixer_scale,
        second_gain, second_shift, inner_bias, outer_bias, outer_scale,
    ) = refs[2 * count : -1]
    sem = refs[-1]
    copies = [
        pltpu.make_async_copy(source, target, sem.at[index])
        for index, (source, target) in enumerate(zip(large_in, large_out))
    ]
    for copy in copies:
        copy.start()
    width = first_gain.shape[1]
    head = query_gain.shape[1]
    feed_rows = 6 + inner_bias.shape[1] // width
    for block in range(2):
        base = block * (feed_rows + 8)
        rows = vectors_ref[base : base + feed_rows + 8, :]

        def pick(index):
            return rows[index : index + 1, :]

        def at(index):
            return pick(feed_rows + index)

        def fold(value):
            total = value[:, :LANES]
            for place in range(1, width // LANES):
                total = total + value[:, place * LANES : (place + 1) * LANES]
            return (total + turn(total))[:, :head]

        here = slice(block, block + 1)
        for target, index in (
            (outer_scale, 0), (outer_bias, 1), (second_gain, 2), (second_shift, 3), (mixer_scale, 4), (mixer_bias, 5),
        ):
            target[here, :] = pick(index)
        for index in range(inner_bias.shape[1] // width):
            inner_bias[here, index * width : (index + 1) * width] = pick(6 + index)
        first_gain[here, :] = at(0)
        first_shift[here, :] = at(1)
        for index in range(3):
            joint_bias[here, index * width : (index + 1) * width] = at(2 + index)
        query_gain[here, :] = fold(at(5))
        query_shift[here, :] = fold(at(6))
        key_gain[here, :] = fold(at(7))
    for copy in copies:
        copy.wait()


def finish(heads, meta, vectors, large):
    width = vectors.shape[1]
    head = width // heads
    hidden = large[2].shape[2]
    sizes = [width, width, 3 * width, head, head, head, width, width, width, width, hidden, width, width]
    return pl.pallas_call(
        partial(finish_body, heads),
        name="finish",
        out_shape=[sds(value.shape, value.dtype) for value in large] + [sds((2, size), f32) for size in sizes],
        grid_spec=pltpu.PrefetchScalarGridSpec(
            num_scalar_prefetch=1,
            grid=(1,),
            in_specs=[vmem_space] * 6,
            out_specs=[any_space] * 5 + [full((2, size)) for size in sizes],
            scratch_shapes=[dma((5,))],
        ),
    )(meta, vectors, *large)


def local(scenes, frames, tokens, patch_counts, first_gain, first_shift, joint_weight, joint_bias, query_gain, query_shift, key_gain, mixer_weight, mixer_bias, mixer_scale, second_gain, second_shift, inner_weight, inner_bias, outer_weight, outer_bias, outer_scale, cotangent):
    rows, width = tokens.shape[1:]
    half = rows // 2
    head = query_gain.shape[1]
    heads = width // head
    hidden = inner_weight.shape[2]
    chips = frames // 2
    meta = patch_counts.reshape(1)
    pattern = (query_gain, query_shift, key_gain)

    x0 = tokens[0]
    feed_params = (mixer_weight, mixer_bias, mixer_scale, second_gain, second_shift, inner_weight, inner_bias, outer_weight, outer_bias, outer_scale)
    back_params = (outer_scale, second_gain, mixer_scale, outer_weight, inner_weight, mixer_weight)

    own0, other0, pre0, qkv0 = joint_forward(0, False, head, meta, x0, first_gain, first_shift, pattern, joint_weight, joint_bias)
    att0 = frame_forward(meta, qkv0)
    own_feed0, other_feed0, middle0, branch0, feed0, slope0, x1 = feed_forward(0, False, meta, att0, x0, *feed_params)
    own1, other1, pre1, pack1 = joint_forward(1, True, head, meta, x1, first_gain, first_shift, pattern, joint_weight, joint_bias)
    att1, kept1, att_full, att_log, (left_joint0, left_feed0, left_joint1) = scene_forward(
        frames, meta, pack1, half, [(own0, other0), (own_feed0, other_feed0), (own1, other1)]
    )
    own_feed1, other_feed1, middle1, branch1, feed1, slope1, layer_out = feed_forward(1, True, meta, att1, x1, *feed_params)

    g_feed1, g_middle1, g_att1, vector_feed1 = feed_backward(1, True, heads, meta, cotangent[0], feed1, slope1, middle1, branch1, *back_params)
    shared = SHARED_PIECES * CHUNK
    g_qkv1, came_feed1, (left_feed1,) = scene_backward(
        frames, meta, kept1, g_att1, att_full, att_log, half, [(own_feed1, other_feed1)], g_feed1, shared
    )
    g0, outer, inner, mixer, joint, vectors = rear(
        frames, head, meta, g_qkv1, pre1, x1, g_middle1, first_gain, pattern, joint_weight,
        outer_scale, second_gain, mixer_scale, outer_weight, inner_weight, slope0, pre0,
        mixer_weight, feed0, middle0, branch0, qkv0, x0, g_feed1, came_feed1,
        [own_feed1, left_feed1, own1, left_joint1, own_feed0, left_feed0, own0, left_joint0], vector_feed1,
    )
    (
        g0, outer, inner, mixer, joint,
        grad_first_gain, grad_first_shift, grad_joint_bias, grad_query_gain, grad_query_shift, grad_key_gain,
        grad_mixer_bias, grad_mixer_scale, grad_second_gain, grad_second_shift, grad_inner_bias, grad_outer_bias, grad_outer_scale,
    ) = finish(heads, meta, vectors, (g0, outer, inner, mixer, joint))
    return (
        layer_out[None], g0[None],
        grad_first_gain, grad_first_shift, joint, grad_joint_bias, grad_query_gain, grad_query_shift, grad_key_gain,
        mixer, grad_mixer_bias, grad_mixer_scale, grad_second_gain, grad_second_shift,
        inner, grad_inner_bias, outer, grad_outer_bias, grad_outer_scale,
    )


def solution(mesh):
    tokens_spec = P("scene", "frame", None)
    shard = P(None, ("scene", "frame"), None)
    in_specs = (tokens_spec, P("scene", "frame")) + (P(),) * 17 + (tokens_spec,)
    out_specs = (
        tokens_spec, tokens_spec, P(), P(), shard, P(), P(), P(), P(), shard,
        P(), P(), P(), P(), shard, P(), shard, P(), P(),
    )
    body = partial(local, mesh.shape["scene"], mesh.shape["frame"])
    return jax.shard_map(body, mesh=mesh, in_specs=in_specs, out_specs=out_specs, check_vma=False)
```

```python
from functools import partial

import jax
import jax.numpy as jnp
from jax import lax
from jax.experimental import pallas as pl
from jax.experimental.pallas import tpu as pltpu
from jax.sharding import PartitionSpec as P

SPECIAL = 5
CHUNK = 512
WIDE = 1024
LANES = 128
SLAB = 256
SHARED_PIECES = 3
SWAP_EVERY = 3
AHEAD = 2
LEAD = 6
DOUBLED = 0
LAG = 3
VECTOR_LAG = 3
norm_eps = 1e-06
head_eps = 1e-05
closed_score = -10000.0
f32 = jnp.float32
bf16 = jnp.bfloat16


def nn(a, b):
    return lax.dot_general(a, b, (((1,), (0,)), ((), ())), preferred_element_type=f32)


def nt(a, b):
    return lax.dot_general(a, b, (((1,), (1,)), ((), ())), preferred_element_type=f32)


def tn(a, b):
    return lax.dot_general(a, b, (((0,), (0,)), ((), ())), preferred_element_type=f32)


def row(ref, index):
    return ref[...].astype(f32)[index : index + 1, :]


def col_sum(value):
    return jnp.sum(value, axis=0, keepdims=True)


def center_norm(value, eps):
    centered = value - jnp.mean(value, axis=-1, keepdims=True)
    spread = lax.rsqrt(jnp.mean(centered * centered, axis=-1, keepdims=True) + eps)
    return centered * spread, spread


def norm_back(grad_hat, hat, spread):
    mean_grad = jnp.mean(grad_hat, axis=-1, keepdims=True)
    mean_both = jnp.mean(grad_hat * hat, axis=-1, keepdims=True)
    return spread * (grad_hat - mean_grad - hat * mean_both)


def seg_matrix(width, head, value):
    shift = head.bit_length() - 1
    first = lax.shift_right_logical(lax.broadcasted_iota(jnp.int32, (width, width), 0), shift)
    second = lax.shift_right_logical(lax.broadcasted_iota(jnp.int32, (width, width), 1), shift)
    return jnp.where(first == second, value, 0.0).astype(bf16)


def repeated(ref, block):
    head = ref.shape[1]
    lane = lax.broadcasted_iota(jnp.int32, (head, SLAB), 1)
    place = lax.broadcasted_iota(jnp.int32, (head, SLAB), 0)
    copies = jnp.where(lax.rem(lane, head) == place, 1.0, 0.0).astype(bf16)
    return nn(ref[...], copies)[block : block + 1, :]


def seg_dot(value, matrix):
    high = value.astype(bf16)
    low = (value - high.astype(f32)).astype(bf16)
    return nn(high, matrix) + nn(low, matrix)


def seg_norm(value, mean_matrix):
    centered = value - seg_dot(value, mean_matrix)
    spread = lax.rsqrt(seg_dot(centered * centered, mean_matrix) + head_eps)
    return centered * spread, spread


def first_lanes(rows):
    return lax.broadcasted_iota(jnp.int32, (rows, LANES), 1) < LANES // 2


def turn(value):
    return pltpu.roll(value, LANES // 2, value.ndim - 1)


def pack_pair(slab):
    half = slab.shape[0] // 2
    top, bottom = slab[:half], slab[half:]
    low = first_lanes(half)
    return jnp.where(low, top, turn(bottom)), jnp.where(low, turn(top), bottom)


def unpack_pair(even, odd):
    low = first_lanes(even.shape[0])
    top = jnp.where(low, even, turn(odd))
    bottom = jnp.where(low, turn(even), odd)
    return jnp.concatenate([top, bottom], axis=0)


def erf(value):
    value = jnp.clip(value, -4.0, 4.0)
    square = value * value
    top = jnp.full_like(square, -2.72614225801306e-10)
    for coefficient in (
        2.77068142495902e-08,
        -2.10102402082508e-06,
        -5.69250639462346e-05,
        -7.34990630326855e-04,
        -2.95459980854025e-03,
        -1.60960333262415e-02,
    ):
        top = top * square + coefficient
    bottom = jnp.full_like(square, -1.45660718464996e-05)
    for coefficient in (
        -2.13374055278905e-04,
        -1.68282697438203e-03,
        -7.37332916720468e-03,
        -1.42647390514189e-02,
    ):
        bottom = bottom * square + coefficient
    return value * top / bottom


def full(shape):
    return pl.BlockSpec(shape, lambda *_: (0,) * len(shape))


def sds(shape, dtype):
    return jax.ShapeDtypeStruct(shape, dtype)


def call(body, name, grid, in_specs, out_specs, out_shape, scratch, flops, moved):
    return pl.pallas_call(
        body,
        name=name,
        out_shape=out_shape,
        grid_spec=pltpu.PrefetchScalarGridSpec(
            num_scalar_prefetch=1,
            grid=grid,
            in_specs=in_specs,
            out_specs=out_specs,
            scratch_shapes=scratch,
        ),
        cost_estimate=pl.CostEstimate(flops=flops, bytes_accessed=moved, transcendentals=0),
    )


def joint_body(
    block, packed, head, meta, x_ref, gain_ref, shift_ref, q_gain_ref, q_shift_ref, k_gain_ref, w_ref, b_ref,
    own_ref, other_ref, pre_ref, out_ref, normed_ref, *stage
):
    step = pl.program_id(0)
    rows, width = normed_ref.shape
    per_part = width // WIDE
    half = rows // 2

    @pl.when(step == 0)
    def _():
        hat, _ = center_norm(x_ref[...].astype(f32), norm_eps)
        normed = (hat * row(gain_ref, block) + row(shift_ref, block)).astype(bf16)
        normed_ref[...] = normed

        scene = lax.axis_index("scene")

        @pl.when(scene == 0)
        def _():
            own_ref[...] = normed[:, : width // 2]
            other_ref[...] = normed[:, width // 2 :]

        @pl.when(scene != 0)
        def _():
            own_ref[...] = normed[:, width // 2 :]
            other_ref[...] = normed[:, : width // 2]

        if packed:
            count = jnp.full((8, LANES), meta[0], jnp.int32).astype(f32)
            for place in range(stage[0].shape[0]):
                stage[0][place, 3 * half : 3 * half + 8, :] = count

    joined = nn(normed_ref[...], w_ref[0]) + row(b_ref, block)

    def emit(part, values):
        if packed:
            base = (step - part * per_part) * (WIDE // head)
            for slab in range(WIDE // LANES):
                even, odd = pack_pair(values[:, slab * LANES : (slab + 1) * LANES])
                stage[0][base + 2 * slab, part * half : (part + 1) * half, :] = even
                stage[0][base + 2 * slab + 1, part * half : (part + 1) * half, :] = odd
        else:
            out_ref[...] = values.astype(bf16)

    def normed_heads(gain, shift):
        mean_matrix = seg_matrix(SLAB, head, 1.0 / head)
        pieces = []
        for slab in range(WIDE // SLAB):
            hat, _ = seg_norm(joined[:, slab * SLAB : (slab + 1) * SLAB], mean_matrix)
            pieces.append(hat * gain if shift is None else hat * gain + shift)
        return jnp.concatenate(pieces, axis=1)

    scale = head ** (-0.5)

    @pl.when(step < per_part)
    def _():
        pre_ref[...] = joined
        emit(0, normed_heads(
            repeated(q_gain_ref, block) * scale,
            repeated(q_shift_ref, block) * scale,
        ))

    @pl.when((step >= per_part) & (step < 2 * per_part))
    def _():
        pre_ref[...] = joined
        emit(1, normed_heads(repeated(k_gain_ref, block), None))

    @pl.when(step >= 2 * per_part)
    def _():
        emit(2, joined)

    if packed:

        @pl.when(step == 3 * per_part - 1)
        def _():
            out_ref[...] = stage[0][...].astype(bf16)


def joint_forward(block, packed, head, meta, x, gain, shift, pattern, weight, bias):
    rows, width = x.shape
    per_part = width // WIDE
    heads = width // head
    packed_rows = 3 * (rows // 2) + 8
    if packed:
        out_spec, out = full((heads, packed_rows, LANES)), sds((heads, packed_rows, LANES), bf16)
        extra = [pltpu.VMEM((heads, packed_rows, LANES), f32)]
    else:
        out_spec = pl.BlockSpec((rows, WIDE), lambda j, m: (0, j))
        out = sds((rows, 3 * width), bf16)
        extra = []
    return call(
        partial(joint_body, block, packed, head),
        f"joint_forward_{block}",
        (3 * per_part,),
        [
            full((rows, width)),
            full(gain.shape),
            full(shift.shape),
            full(pattern[0].shape), full(pattern[1].shape), full(pattern[2].shape),
            pl.BlockSpec((1, width, WIDE), lambda j, m: (block, 0, j)),
            pl.BlockSpec((2, WIDE), lambda j, m: (0, j)),
        ],
        [
            full((rows, width // 2)),
            full((rows, width // 2)),
            pl.BlockSpec((rows, WIDE), lambda j, m: (0, jnp.minimum(j, 2 * per_part - 1))),
            out_spec,
        ],
        [
            sds((rows, width // 2), bf16),
            sds((rows, width // 2), bf16),
            sds((rows, 2 * width), f32),
            out,
        ],
        [pltpu.VMEM((rows, width), bf16)] + extra,
        2 * rows * width * 3 * width,
        6 * width * width + 16 * rows * width,
    )(meta, x, gain, shift, *pattern, weight, bias)


def lane_picks():
    lane = lax.broadcasted_iota(jnp.int32, (1, LANES), 1)
    low = jnp.where(lane < LANES // 2, 1.0, 0.0)
    return low.astype(bf16), (1.0 - low).astype(bf16)


def open_row(meta, rows):
    place = lax.broadcasted_iota(jnp.int32, (1, rows), 1)
    return jnp.where(place < meta[0] + SPECIAL, 0.0, closed_score)


def frame_body(meta, qkv_ref, out_ref):
    rows, width = out_ref.shape
    bias = open_row(meta, rows)
    picks = lane_picks()
    low = first_lanes(rows)
    for slab in range(width // LANES):
        at = slab * LANES
        queries = qkv_ref[:, at : at + LANES]
        keys = qkv_ref[:, width + at : width + at + LANES]
        values = qkv_ref[:, 2 * width + at : 2 * width + at + LANES]
        results = []
        for pick in picks:
            power = jnp.exp(nt(queries * pick, keys) + bias)
            probs = power / jnp.sum(power, axis=-1, keepdims=True)
            results.append(nn(probs.astype(bf16), values))
        out_ref[:, at : at + LANES] = jnp.where(low, results[0], results[1]).astype(bf16)


def frame_forward(meta, qkv):
    rows = qkv.shape[0]
    width = qkv.shape[1] // 3
    return call(
        frame_body,
        "frame_forward",
        (1,),
        [full(qkv.shape)],
        full((rows, width)),
        sds((rows, width), bf16),
        [],
        4 * rows * rows * width,
        8 * rows * width,
    )(meta, qkv)


def frame_back_slab(at, meta, qkv_ref, grad_ref, out_ref):
    rows, width = grad_ref.shape
    bias = open_row(meta, rows)
    scale = (LANES // 2) ** (-0.5)

    def lanes(part):
        return pl.ds(pl.multiple_of(part * width + at, LANES), LANES)

    queries = qkv_ref[:, lanes(0)]
    keys = qkv_ref[:, lanes(1)]
    values = qkv_ref[:, lanes(2)]
    grads = grad_ref[:, lanes(0)]
    found = []
    for pick in lane_picks():
        power = jnp.exp(nt(queries * pick, keys) + bias)
        probs = power / jnp.sum(power, axis=-1, keepdims=True)
        grad_probs = nt(grads * pick, values)
        delta = jnp.sum(probs * grad_probs, axis=-1, keepdims=True)
        grad_scores = (probs * (grad_probs - delta)).astype(bf16)
        found.append((
            nn(grad_scores, keys) * scale,
            tn(grad_scores, queries),
            tn(probs.astype(bf16), grads),
        ))
    low = first_lanes(rows)
    for part in range(3):
        out_ref[:, lanes(part)] = jnp.where(low, found[0][part], found[1][part])


def packed_part(value, part, half):
    whole = value.astype(f32)
    return whole[:, part * half : (part + 1) * half, :].reshape(-1, LANES)


def open_slots(value, half):
    count = value.astype(f32)[:, 3 * half : 3 * half + 8, :]
    count = jnp.concatenate([count] * (half // 8), axis=1)
    place = lax.broadcasted_iota(jnp.int32, count.shape, 1).astype(f32)
    return (
        (place < count + SPECIAL).reshape(-1, LANES),
        (place + half < count + SPECIAL).reshape(-1, LANES),
    )


MESH = pl.DeviceIdType.MESH


def peers_of(frames):
    scene = lax.axis_index("scene")
    frame = lax.axis_index("frame")
    bits = []
    bit = 1
    while bit < frames:
        value = lax.rem(frame // bit, 2)
        bits.append((value, (scene, frame + bit * (1 - 2 * value))))
        bit *= 2
    core, core_peer = bits[0]
    scene_peer = (1 - scene, frame)
    cross_peer = (1 - scene, core_peer[1])
    return core, core_peer, scene_peer, cross_peer, bits[1:]


def greet(targets):
    barrier = pltpu.get_barrier_semaphore()
    for target in targets:
        pl.semaphore_signal(barrier, inc=1, device_id=target, device_id_type=MESH)


def enter_scene(frames):
    barrier = pltpu.get_barrier_semaphore()
    _, _, scene_peer, cross_peer, _ = peers_of(frames)
    scene = lax.axis_index("scene")
    frame = lax.axis_index("frame")
    for target in (scene_peer, cross_peer):
        pl.semaphore_signal(barrier, inc=1, device_id=target, device_id_type=MESH)

    @pl.loop(1, frames)
    def _(offset):
        pl.semaphore_signal(
            barrier, inc=1, device_id=(scene, lax.rem(frame + offset, frames)), device_id_type=MESH
        )

    pl.semaphore_wait(barrier, frames + 1)


def remote(source, target, send, recv, device):
    return pltpu.make_async_remote_copy(
        src_ref=source, dst_ref=target, send_sem=send, recv_sem=recv, device_id=device, device_id_type=MESH
    )


class Share:
    def __init__(self, frames, pairs, outs, send, recv):
        _, core_peer, scene_peer, _, _ = peers_of(frames)
        self.first, self.second = [], []
        for index, ((own, other), out) in enumerate(zip(pairs, outs)):
            self.first.append(remote(other, out.at[0], send.at[3 * index], recv.at[3 * index], scene_peer))
            self.first.append(remote(own, out.at[1], send.at[3 * index + 1], recv.at[3 * index + 1], core_peer))
            self.second.append(
                remote(out.at[0], out.at[2], send.at[3 * index + 2], recv.at[3 * index + 2], core_peer)
            )

    def start(self):
        for copy in self.first:
            copy.start()

    def relay(self):
        for index, copy in enumerate(self.second):
            self.first[2 * index].wait_recv()
            copy.start()

    def close(self):
        for index, copy in enumerate(self.second):
            self.first[2 * index].wait_send()
            self.first[2 * index + 1].wait()
            copy.wait()


def scene_body(
    frames, half, span, n_share, meta, pack_ref, *refs
):
    heads = pack_ref.shape[0]
    pairs = [(refs[2 * index], refs[2 * index + 1]) for index in range(n_share)]
    refs = refs[2 * n_share :]
    att_ref, kept_ref, out_ref, log_ref = refs[:4]
    outs, refs = refs[4 : 4 + n_share], refs[4 + n_share :]
    queries, keys, values, sent, a_send, a_recv, b_send, b_recv, s_send, s_recv, own_sem = refs
    n = queries.shape[0] // 2
    m = keys.shape[0] // 2
    scene = lax.axis_index("scene")
    frame = lax.axis_index("frame")
    part = frame // heads
    own = pltpu.make_async_copy(pack_ref.at[lax.rem(frame, heads)], kept_ref.at[frame], own_sem)
    own.start()
    share = Share(frames, pairs, outs, s_send, s_recv)
    enter_scene(frames)

    def to_head(offset):
        target = lax.rem(frame + offset, frames)
        return remote(
            pack_ref.at[lax.rem(target, heads)], kept_ref.at[frame], a_send.at[offset], a_recv.at[offset], (scene, target)
        )

    @pl.loop(1, frames)
    def _(offset):
        to_head(offset).start()

    share.start()
    own.wait()

    @pl.loop(1, frames)
    def _(offset):
        to_head(offset).wait_recv()

    first = pl.multiple_of(part * heads, heads)
    q = packed_part(kept_ref[pl.ds(first, heads)], 0, half)
    low_n, low_m = first_lanes(n), first_lanes(m)
    queries[:n, :] = jnp.where(low_n, q, 0.0).astype(bf16)
    queries[n:, :] = jnp.where(low_n, turn(q), 0.0).astype(bf16)
    k = packed_part(kept_ref[...], 1, half)
    keys[:m, :] = k.astype(bf16)
    keys[m:, :] = turn(k).astype(bf16)
    v = packed_part(kept_ref[...], 2, half)
    open_low, open_high = open_slots(kept_ref[...], half)
    values[:m, :] = jnp.where(open_low, jnp.where(low_m, v, 1.0), 0.0).astype(bf16)
    values[m:, :] = jnp.where(open_high, jnp.where(low_m, turn(v), 1.0), 0.0).astype(bf16)
    low = first_lanes(LANES)

    pair = 2 * half
    place = lax.rem(frame, heads)
    low = first_lanes(pair)
    pieces = heads // 2

    def from_head(target):
        return remote(
            sent.at[target], att_ref.at[place], b_send.at[target], b_recv.at[place], (scene, part * heads + target)
        )

    def turned(piece):
        return lax.rem(piece + place // 2 + 1, pieces)

    def send(piece):
        for index in range(2):
            target = 2 * turned(piece) + index

            @pl.when(target != place)
            def _():
                from_head(target).start()

    @pl.loop(0, pieces)
    def _(piece):
        @pl.when(piece > 0)
        def _():
            send(piece - 1)

        at = pl.multiple_of(turned(piece) * pair, pair)
        some = jnp.concatenate([queries[pl.ds(at, pair), :], queries[pl.ds(n + at, pair), :]], axis=0)
        total = jnp.zeros((2 * pair, LANES), f32)
        for start in range(0, 2 * m, span):
            power = jnp.exp(nt(some, keys[start : start + span, :])).astype(bf16)
            total = total + nn(power, values[start : start + span, :])
        first, second = total[:pair], total[pair:]
        bottom = jnp.where(low, turn(first), second)
        result = jnp.where(low, first, turn(second)) / bottom
        sent[pl.ds(2 * turned(piece), 2)] = result.reshape(2, half, LANES).astype(bf16)
        out_ref[pl.ds(at, pair), :] = result
        log_ref[pl.ds(at, pair), :] = jnp.log(bottom)

    share.relay()
    send(pieces - 1)
    att_ref[place] = sent[place]

    @pl.loop(1, frames)
    def _(offset):
        to_head(offset).wait_send()

    @pl.loop(1, heads)
    def _(offset):
        other = lax.rem(place + offset, heads)
        from_head(other).wait_send()
        remote(
            sent.at[other], att_ref.at[other], b_send.at[other], b_recv.at[other], (scene, part * heads + other)
        ).wait_recv()

    share.close()


any_space = pl.BlockSpec(memory_space=pl.ANY)
vmem_space = pl.BlockSpec(memory_space=pltpu.VMEM)
dma = pltpu.SemaphoreType.DMA


def scene_forward(frames, meta, pack, half, pairs):
    heads = pack.shape[0]
    n = heads * half
    m = frames * half
    span = m // 2
    while span > 640:
        span = span // 2
    flat = [value for pair in pairs for value in pair]
    results = pl.pallas_call(
        partial(scene_body, frames, half, span, len(pairs)),
        name="scene_forward",
        out_shape=[
            sds((heads, half, LANES), bf16),
            sds((frames,) + pack.shape[1:], bf16),
            sds((n, LANES), f32),
            sds((n, LANES), f32),
        ]
        + [sds((3,) + own.shape, bf16) for own, _ in pairs],
        grid_spec=pltpu.PrefetchScalarGridSpec(
            num_scalar_prefetch=1,
            grid=(1,),
            in_specs=[vmem_space] + [any_space] * len(flat),
            out_specs=[vmem_space] * 4 + [any_space] * len(pairs),
            scratch_shapes=[
                pltpu.VMEM((2 * n, LANES), bf16),
                pltpu.VMEM((2 * m, LANES), bf16),
                pltpu.VMEM((2 * m, LANES), bf16),
                pltpu.VMEM((heads, half, LANES), bf16),
                dma((frames,)),
                dma((frames,)),
                dma((heads,)),
                dma((heads,)),
                dma((3 * len(pairs),)),
                dma((3 * len(pairs),)),
                dma(()),
            ],
        ),
        compiler_params=pltpu.CompilerParams(collective_id=1, has_side_effects=True),
        cost_estimate=pl.CostEstimate(flops=16 * n * m * LANES, bytes_accessed=20 * n * LANES, transcendentals=0),
    )(meta, pack, *flat)
    return results[0], results[1], results[2], results[3], results[4:]


def three_lanes(value, closed):
    lane = lax.broadcasted_iota(jnp.int32, value.shape, 1)
    base = LANES // 2
    high = value.astype(bf16).astype(f32)
    rest = value - high
    middle = rest.astype(bf16).astype(f32)
    last = rest - middle
    result = jnp.where(lane == base, high, jnp.where(lane == base + 1, middle, last))
    return jnp.where(lane < base + 3, result, jnp.where(lane == base + 3, closed, 0.0))


def gradient_copies(frames, own, came, send, recv, lanes):
    core, core_peer, scene_peer, cross_peer, _ = peers_of(frames)
    targets = ((core, scene_peer), (1 - core, core_peer), (1 - core, cross_peer))
    return [
        remote(own.at[side, :, lanes], came.at[which, :, lanes], send.at[which], recv.at[which], peer)
        for which, (side, peer) in enumerate(targets)
    ]


def scene_back_body(frames, half, span, n_share, shared, meta, kept_ref, grad_ref, out_ref, log_ref, feed_ref, *refs):
    heads = grad_ref.shape[0]
    pairs = [(refs[2 * index], refs[2 * index + 1]) for index in range(n_share)]
    refs = refs[2 * n_share :]
    back_ref, feed_came, outs, refs = refs[0], refs[1], refs[2 : 2 + n_share], refs[2 + n_share :]
    queries, keys, values, grads, turned, came, sent_q, sent_kv = refs[:8]
    a_send, a_recv, b_send, b_recv, c_send, c_recv, s_send, s_recv, g_send, g_recv = refs[8:]
    n = queries.shape[0] // 2
    m = keys.shape[0] // 2
    scene = lax.axis_index("scene")
    frame = lax.axis_index("frame")
    part = frame // heads
    place = lax.rem(frame, heads)
    share = Share(frames, pairs, outs, s_send, s_recv)
    feed_copies = gradient_copies(frames, feed_ref, feed_came, g_send, g_recv, pl.ds(0, shared))
    enter_scene(frames)

    def to_head(offset):
        target = lax.rem(place + offset, heads)
        return remote(
            grad_ref.at[target], came.at[place], a_send.at[offset], a_recv.at[offset], (scene, part * heads + target)
        )

    @pl.loop(1, heads)
    def _(offset):
        to_head(offset).start()

    share.start()
    for copy in feed_copies:
        copy.start()
    came[place] = grad_ref[place]
    first = pl.multiple_of(part * heads, heads)
    low_n, low_m = first_lanes(n), first_lanes(m)
    base = LANES // 2
    q = packed_part(kept_ref[pl.ds(first, heads)], 0, half)
    log = -log_ref[...]
    queries[:n, :] = jnp.where(low_n, q, three_lanes(turn(log), closed_score)).astype(bf16)
    queries[n:, :] = jnp.where(low_n, turn(q), three_lanes(log, closed_score)).astype(bf16)
    lane = lax.broadcasted_iota(jnp.int32, (m, LANES), 1)
    ones = jnp.where(lane < base + 3, 1.0, 0.0)
    open_low, open_high = open_slots(kept_ref[...], half)
    k = packed_part(kept_ref[...], 1, half)
    for place_at, k_now, is_open in ((0, k, open_low), (m, turn(k), open_high)):
        tail = jnp.where((lane == base + 3) & jnp.logical_not(is_open), 1.0, ones)
        keys[place_at : place_at + m, :] = jnp.where(low_m, k_now, tail).astype(bf16)
    v = packed_part(kept_ref[...], 2, half)
    values[:m, :] = jnp.where(low_m, v, ones).astype(bf16)
    values[m:, :] = jnp.where(low_m, turn(v), ones).astype(bf16)
    turned[...] = jnp.zeros_like(turned)
    low = first_lanes(LANES)

    @pl.loop(1, heads)
    def _(offset):
        to_head(offset).wait_recv()

    g = came[...].astype(f32).reshape(n, LANES)
    delta = -seg_dot(g * out_ref[...], seg_matrix(LANES, base, 1.0))
    grads[:n, :] = jnp.where(low_n, g, three_lanes(turn(delta), 0.0)).astype(bf16)
    grads[n:, :] = jnp.where(low_n, turn(g), three_lanes(delta, 0.0)).astype(bf16)

    pair = 2 * half
    low_pair = first_lanes(pair)
    pieces = frames // 2

    def back_kv(target):
        return remote(
            sent_kv.at[target], back_ref.at[frame, pl.ds(1, 2)], b_send.at[target], b_recv.at[frame], (scene, target)
        )

    def turned_to(piece):
        return lax.rem(piece + frame // 2 + 1, pieces)

    def send(piece):
        for index in range(2):
            target = 2 * turned_to(piece) + index

            @pl.when(target != frame)
            def _():
                back_kv(target).start()

    @pl.loop(0, pieces)
    def _(piece):
        @pl.when(piece > 0)
        def _():
            send(piece - 1)

        at = pl.multiple_of(turned_to(piece) * pair, pair)
        key_part = jnp.concatenate([keys[pl.ds(at, pair), :], keys[pl.ds(m + at, pair), :]], axis=0)
        value_part = jnp.concatenate([values[pl.ds(at, pair), :], values[pl.ds(m + at, pair), :]], axis=0)
        key_turned = jnp.transpose(key_part.astype(f32)).astype(bf16)
        dk = jnp.zeros((2 * pair, LANES), f32)
        dv = jnp.zeros((2 * pair, LANES), f32)
        for start in range(0, 2 * n, span):
            some = queries[start : start + span, :]
            some_grads = grads[start : start + span, :]
            probs = jnp.exp(nt(key_part, some))
            grad_scores = (probs * nt(value_part, some_grads)).astype(bf16)
            dv = dv + nn(probs.astype(bf16), some_grads)
            dk = dk + nn(grad_scores, some)
            turned[:, start : start + span] += nn(key_turned, grad_scores)
        dk = jnp.where(low_pair, dk[:pair], turn(dk[pair:])).reshape(2, half, LANES)
        dv = jnp.where(low_pair, dv[:pair], turn(dv[pair:])).reshape(2, half, LANES)
        sent_kv[pl.ds(2 * turned_to(piece), 2), 0] = dk.astype(bf16)
        sent_kv[pl.ds(2 * turned_to(piece), 2), 1] = dv.astype(bf16)

    share.relay()
    send(pieces - 1)

    scale = base ** (-0.5)
    rows = []
    for at in range(0, n, LANES):
        first = jnp.transpose(turned[:, at : at + LANES])
        second = jnp.transpose(turned[:, n + at : n + at + LANES])
        rows.append(jnp.where(low, first, turn(second)) * scale)
    sent_q[...] = jnp.concatenate(rows, axis=0).reshape(heads, half, LANES).astype(bf16)

    def back_q(offset):
        target = lax.rem(place + offset, heads)
        return remote(
            sent_q.at[target], back_ref.at[frame, 0], c_send.at[offset], c_recv.at[offset], (scene, part * heads + target)
        )

    back_ref[frame, 1] = sent_kv[frame, 0]
    back_ref[frame, 2] = sent_kv[frame, 1]

    @pl.loop(1, heads)
    def _(offset):
        back_q(offset).start()

    back_ref[frame, 0] = sent_q[place]

    @pl.loop(1, heads)
    def _(offset):
        to_head(offset).wait_send()

    @pl.loop(1, frames)
    def _(offset):
        other = lax.rem(frame + offset, frames)
        back_kv(other).wait_send()
        remote(
            sent_kv.at[other], back_ref.at[other, pl.ds(1, 2)], b_send.at[other], b_recv.at[other], (scene, other)
        ).wait_recv()

    @pl.loop(1, heads)
    def _(offset):
        back_q(offset).wait()

    share.close()
    for copy in feed_copies:
        copy.wait()


def scene_backward(frames, meta, kept, grad, out, log, half, pairs, feed_grads, shared):
    heads = grad.shape[0]
    n = heads * half
    m = frames * half
    span = n // 2
    while span > 640:
        span = span // 2
    flat = [value for pair in pairs for value in pair]
    results = pl.pallas_call(
        partial(scene_back_body, frames, half, span, len(pairs), shared),
        name="scene_backward",
        out_shape=[sds((frames, 3, half, LANES), bf16), sds((3,) + feed_grads.shape[1:], bf16)]
        + [sds((3,) + own.shape, bf16) for own, _ in pairs],
        grid_spec=pltpu.PrefetchScalarGridSpec(
            num_scalar_prefetch=1,
            grid=(1,),
            in_specs=[vmem_space] * 4 + [any_space] * (1 + len(flat)),
            out_specs=[vmem_space] + [any_space] * (1 + len(pairs)),
            scratch_shapes=[
                pltpu.VMEM((2 * n, LANES), bf16),
                pltpu.VMEM((2 * m, LANES), bf16),
                pltpu.VMEM((2 * m, LANES), bf16),
                pltpu.VMEM((2 * n, LANES), bf16),
                pltpu.VMEM((LANES, 2 * n), f32),
                pltpu.VMEM((heads, half, LANES), bf16),
                pltpu.VMEM((heads, half, LANES), bf16),
                pltpu.VMEM((frames, 2, half, LANES), bf16),
                dma((heads,)),
                dma((heads,)),
                dma((frames,)),
                dma((frames,)),
                dma((heads,)),
                dma((heads,)),
                dma((3 * len(pairs),)),
                dma((3 * len(pairs),)),
                dma((3,)),
                dma((3,)),
            ],
        ),
        compiler_params=pltpu.CompilerParams(collective_id=2, has_side_effects=True),
        cost_estimate=pl.CostEstimate(flops=40 * n * m * LANES, bytes_accessed=30 * n * LANES, transcendentals=0),
    )(meta, kept, grad, out, log, feed_grads, *flat)
    back = results[0]
    if frames > heads:
        place = lax.axis_index("frame") // heads * heads
        dq = lax.dynamic_slice(back, (place, 0, 0, 0), (heads, 1, half, LANES))
        both = back.reshape(frames // heads, heads, 3, half, LANES)[:, :, 1:].astype(f32).sum(0)
        back = jnp.concatenate([dq, both.astype(bf16)], axis=1)
    return back, results[1], results[2:]


def feed_body(
    block, packed, meta, att_ref, x_ref, mixer_ref, mixer_bias, mixer_scale, gain_ref, shift_ref,
    inner_ref, inner_bias, outer_ref, outer_bias, outer_scale,
    own_ref, other_ref, middle_ref, branch_ref, feed_ref, slope_ref, out_ref, normed_ref, total_ref
):
    step = pl.program_id(0)
    steps = pl.num_programs(0)
    rows, width = middle_ref.shape
    hidden_half = own_ref.shape[1] - width
    half_steps = hidden_half // WIDE
    mine = lax.axis_index("scene")

    def split(value, at):
        first, second = value[:, : width // 2], value[:, width // 2 :]

        @pl.when(mine == 0)
        def _():
            own_ref[:, at : at + width // 2] = first
            other_ref[:, at : at + width // 2] = second

        @pl.when(mine != 0)
        def _():
            own_ref[:, at : at + width // 2] = second
            other_ref[:, at : at + width // 2] = first

    @pl.when(step == 0)
    def _():
        if packed:
            pieces = []
            for pair in range(width // LANES):
                pieces.append(
                    unpack_pair(att_ref[2 * pair].astype(f32), att_ref[2 * pair + 1].astype(f32))
                )
            attended = jnp.concatenate(pieces, axis=1).astype(bf16)
        else:
            attended = att_ref[...]
        branch = nn(attended, mixer_ref[0]) + row(mixer_bias, block)
        middle = x_ref[...].astype(f32) + row(mixer_scale, block) * branch
        hat, _ = center_norm(middle, norm_eps)
        normed = (hat * row(gain_ref, block) + row(shift_ref, block)).astype(bf16)
        branch_ref[...] = branch
        middle_ref[...] = middle
        normed_ref[...] = normed
        split(normed, hidden_half)
        split(attended, hidden_half + width // 2)
        total_ref[...] = jnp.zeros_like(total_ref)

    pre = nn(normed_ref[...], inner_ref[0]) + row(inner_bias, block)
    share = 0.5 * (1.0 + erf(pre * (2.0 ** (-0.5))))
    slope_ref[...] = share + pre * jnp.exp(-0.5 * pre * pre) * 0.3989422804014327
    hidden = (pre * share).astype(bf16)
    place = pl.multiple_of(lax.rem(step, half_steps) * WIDE, WIDE)

    @pl.when(step // half_steps == mine)
    def _():
        own_ref[:, pl.ds(place, WIDE)] = hidden

    @pl.when(step // half_steps != mine)
    def _():
        other_ref[:, pl.ds(place, WIDE)] = hidden

    total_ref[...] += nn(hidden, outer_ref[0])

    @pl.when(step == steps - 1)
    def _():
        feed = total_ref[...] + row(outer_bias, block)
        feed_ref[...] = feed
        result = middle_ref[...] + row(outer_scale, block) * feed
        if packed:
            place = lax.broadcasted_iota(jnp.int32, result.shape, 0)
            result = jnp.where(place < meta[0] + SPECIAL, result, 0.0)
        out_ref[...] = result.astype(out_ref.dtype)


def feed_forward(block, packed, meta, att, x, mixer, mixer_bias, mixer_scale, gain, shift, inner, inner_bias, outer, outer_bias, outer_scale):
    rows, width = x.shape
    hidden = inner.shape[2]
    kept = hidden // 2 + width
    steps = hidden // WIDE
    vector = full(gain.shape)
    return call(
        partial(feed_body, block, packed),
        f"feed_forward_{block}",
        (steps,),
        [
            full(att.shape),
            full((rows, width)),
            pl.BlockSpec((1, width, width), lambda j, m: (block, 0, 0)),
            vector, vector, vector, vector,
            pl.BlockSpec((1, width, WIDE), lambda j, m: (block, 0, j)),
            pl.BlockSpec((2, WIDE), lambda j, m: (0, j)),
            pl.BlockSpec((1, WIDE, width), lambda j, m: (block, j, 0)),
            vector, vector,
        ],
        [full((rows, kept))] * 2
        + [full((rows, width))] * 3
        + [pl.BlockSpec((rows, WIDE), lambda j, m: (0, j)), full((rows, width))],
        [sds((rows, kept), bf16)] * 2
        + [sds((rows, width), f32)] * 3
        + [sds((rows, hidden), f32), sds((rows, width), bf16 if packed else f32)],
        [pltpu.VMEM((rows, width), bf16), pltpu.VMEM((rows, width), f32)],
        2 * rows * width * (2 * hidden + width),
        4 * width * hidden + 4 * rows * hidden + 30 * rows * width,
    )(meta, att, x, mixer, mixer_bias, mixer_scale, gain, shift, inner, inner_bias, outer, outer_bias, outer_scale)


def feed_back_core(
    block, packed, step, steps, chunk, meta, g_ref, feed_ref, slope_ref, middle_ref, branch_ref,
    outer_scale, gain_ref, mixer_scale, outer_ref, inner_ref, mixer_ref,
    grads_ref, g_middle_ref, g_att_ref, vector_ref, g_feed_ref, total_ref
):
    rows, width = total_ref.shape
    size = inner_ref.shape[2]
    half_steps = steps // 2
    at_branch = width // 2 + half_steps * size

    def incoming():
        g = g_ref[...].astype(f32)
        if packed:
            place = lax.broadcasted_iota(jnp.int32, g.shape, 0)
            g = jnp.where(place < meta[0] + SPECIAL, g, 0.0)
        return g

    @pl.when(step == 0)
    def _():
        g = incoming()
        g_feed = (g * row(outer_scale, block)).astype(bf16)
        g_feed_ref[...] = g_feed
        grads_ref[0, :, : width // 2] = g_feed[:, : width // 2]
        grads_ref[1, :, : width // 2] = g_feed[:, width // 2 :]
        vector_ref[0:1, :] = col_sum(g * feed_ref[...])
        vector_ref[1:2, :] = col_sum(g_feed.astype(f32))
        total_ref[...] = jnp.zeros_like(total_ref)

    g_pre = (nt(g_feed_ref[...], outer_ref[0]) * slope_ref[...]).astype(bf16)
    place = pl.multiple_of(width // 2 + lax.rem(chunk, half_steps) * size, CHUNK)
    grads_ref[chunk // half_steps, :, pl.ds(place, size)] = g_pre
    per_row = width // size
    lanes = pl.ds(pl.multiple_of(lax.rem(chunk, per_row) * size, size), size)
    vector_ref[pl.ds(6 + chunk // per_row, 1), lanes] = col_sum(g_pre.astype(f32))
    total_ref[...] += nt(g_pre, inner_ref[0])

    @pl.when(step == steps - 1)
    def _():
        hat, spread = center_norm(middle_ref[...], norm_eps)
        g_nm = total_ref[...]
        vector_ref[2:3, :] = col_sum(g_nm * hat)
        vector_ref[3:4, :] = col_sum(g_nm)
        g_middle = incoming() + norm_back(g_nm * row(gain_ref, block), hat, spread)
        g_middle_ref[...] = g_middle
        vector_ref[4:5, :] = col_sum(g_middle * branch_ref[...])
        g_branch = (g_middle * row(mixer_scale, block)).astype(bf16)
        vector_ref[5:6, :] = col_sum(g_branch.astype(f32))
        grads_ref[0, :, at_branch : at_branch + width // 2] = g_branch[:, : width // 2]
        grads_ref[1, :, at_branch : at_branch + width // 2] = g_branch[:, width // 2 :]
        g_att = nt(g_branch, mixer_ref[0])
        if packed:
            for pair in range(width // LANES):
                even, odd = pack_pair(g_att[:, pair * LANES : (pair + 1) * LANES])
                g_att_ref[2 * pair] = even.astype(bf16)
                g_att_ref[2 * pair + 1] = odd.astype(bf16)
        else:
            g_att_ref[...] = g_att.astype(bf16)


def feed_back_body(block, packed, meta, *refs):
    step = pl.program_id(0)
    feed_back_core(block, packed, step, pl.num_programs(0), step, meta, *refs)


def feed_backward(block, packed, heads, meta, g, feed, slope, middle, branch, outer_scale, gain, mixer_scale, outer, inner, mixer):
    rows, width = middle.shape
    hidden = inner.shape[2]
    steps = hidden // WIDE
    vector = full(gain.shape)
    vector_rows = 6 + hidden // width
    att_shape = (heads, rows // 2, LANES) if packed else (rows, width)
    return call(
        partial(feed_back_body, block, packed),
        f"feed_backward_{block}",
        (steps,),
        [
            full((rows, width)),
            full((rows, width)),
            pl.BlockSpec((rows, WIDE), lambda j, m: (0, j)),
            full((rows, width)),
            full((rows, width)),
            vector, vector, vector,
            pl.BlockSpec((1, WIDE, width), lambda j, m: (block, j, 0)),
            pl.BlockSpec((1, width, WIDE), lambda j, m: (block, 0, j)),
            pl.BlockSpec((1, width, width), lambda j, m: (block, 0, 0)),
        ],
        [
            full((2, rows, width + hidden // 2)),
            full((rows, width)),
            full(att_shape),
            full((vector_rows, width)),
        ],
        [
            sds((2, rows, width + hidden // 2), bf16),
            sds((rows, width), f32),
            sds(att_shape, bf16),
            sds((vector_rows, width), f32),
        ],
        [pltpu.VMEM((rows, width), bf16), pltpu.VMEM((rows, width), f32)],
        2 * rows * width * (2 * hidden + width),
        4 * width * hidden + 8 * rows * hidden + 20 * rows * width,
    )(meta, g, feed, slope, middle, branch, outer_scale, gain, mixer_scale, outer, inner, mixer)


def joint_back_core(
    block, head, step, steps, chunk, g, pre_ref, x_ref, g_middle_ref, gain_ref, q_gain_ref, k_gain_ref, w_ref,
    grads_ref, at_joined, out_ref, vector_ref, total_ref
):
    rows, width = total_ref.shape
    per_part = width // CHUNK
    half_steps = steps // 2

    @pl.when(step == 0)
    def _():
        total_ref[...] = jnp.zeros_like(total_ref)

    in_row = pl.ds(pl.multiple_of(lax.rem(chunk, per_part) * CHUNK, CHUNK), CHUNK)

    def finish(g_joined):
        rounded = g_joined.astype(bf16)
        place = pl.multiple_of(at_joined + lax.rem(chunk, half_steps) * CHUNK, CHUNK)
        grads_ref[chunk // half_steps, :, pl.ds(place, CHUNK)] = rounded
        vector_ref[pl.ds(2 + chunk // per_part, 1), in_row] = col_sum(rounded.astype(f32))
        total_ref[...] += nt(rounded, w_ref[0])

    def head_back(gain, gain_row, shift_row):
        mean_matrix = seg_matrix(SLAB, head, 1.0 / head)
        pieces = []
        for slab in range(CHUNK // SLAB):
            at = slab * SLAB
            g_now = g[:, at : at + SLAB]
            hat, spread = seg_norm(pre_ref[:, at : at + SLAB], mean_matrix)
            vector_ref[gain_row : gain_row + 1, at : at + SLAB] += col_sum(g_now * hat)
            if shift_row is not None:
                vector_ref[shift_row : shift_row + 1, at : at + SLAB] += col_sum(g_now)
            grad_hat = g_now * gain
            pieces.append(
                spread
                * (
                    grad_hat
                    - seg_dot(grad_hat, mean_matrix)
                    - hat * seg_dot(grad_hat * hat, mean_matrix)
                )
            )
        finish(jnp.concatenate(pieces, axis=1))

    @pl.when(chunk < per_part)
    def _():
        head_back(repeated(q_gain_ref, block), 5, 6)

    @pl.when((chunk >= per_part) & (chunk < 2 * per_part))
    def _():
        head_back(repeated(k_gain_ref, block), 7, None)

    @pl.when(chunk >= 2 * per_part)
    def _():
        finish(g)

    @pl.when(step == steps - 1)
    def _():
        hat, spread = center_norm(x_ref[...].astype(f32), norm_eps)
        g_normed = total_ref[...]
        vector_ref[0:1, :] = col_sum(g_normed * hat)
        vector_ref[1:2, :] = col_sum(g_normed)
        result = g_middle_ref[...] + norm_back(g_normed * row(gain_ref, block), hat, spread)
        out_ref[...] = result.astype(out_ref.dtype)


class Rows:
    def __init__(self, ref, lead, base):
        self.ref, self.lead, self.base = ref, lead, base

    def at(self, key):
        rows, lanes = key
        if isinstance(rows, slice):
            rows = slice(rows.start + self.base, rows.stop + self.base)
        else:
            rows = pl.ds(rows.start + self.base, rows.size)
        return self.lead, rows, lanes

    def __getitem__(self, key):
        return self.ref[self.at(key)]

    def __setitem__(self, key, value):
        self.ref[self.at(key)] = value


class Plan:
    def __init__(self, frames, rows, width, hidden):
        self.half = width // 2
        self.hidden_half = hidden // 2
        self.chips = frames // 2
        self.stages = self.chips.bit_length() - 1
        self.deep = self.half // self.chips // 2
        self.n_outer = CHUNK // LANES
        self.n_inner = self.hidden_half // CHUNK
        self.n_joint = 3 * self.half // CHUNK
        self.per_block = self.n_outer + self.n_inner + 1 + self.n_joint
        self.n_pieces = self.n_inner + self.n_joint + 2
        self.total = 2 * self.per_block
        self.joint_steps = 2 * self.n_joint
        self.feed_steps = 2 * self.n_inner
        self.slabs = 4
        self.frame_steps = width // LANES // self.slabs
        self.feed_at = self.joint_steps
        self.frame_at = self.feed_at + self.feed_steps
        self.joint_at = self.frame_at + self.frame_steps
        self.compute_end = self.joint_at + self.joint_steps
        self.leave = []
        for piece in range(SHARED_PIECES, 1 + self.n_inner + 1):
            self.leave.append((1 + piece - SHARED_PIECES, 0, piece))
        at_joined = 2 + self.n_inner
        for piece in range(self.n_joint):
            self.leave.append((2 + 2 * piece, 0, at_joined + piece))
        self.leave.append((self.feed_at + 1, 1, 0))
        for piece in range(self.n_inner):
            self.leave.append((self.feed_at + 2 + 2 * piece, 1, 1 + piece))
        self.leave.append((self.frame_at + 1, 1, 1 + self.n_inner))
        for piece in range(self.n_joint):
            self.leave.append((self.joint_at + 2 + 2 * piece, 1, at_joined + piece))
        self.doubled = DOUBLED
        first = 0
        for slot, block, piece in self.leave:
            first = max(first, self.turn_of(slot) + AHEAD - self.index_of(block, piece))
        self.first = first
        self.leave = [
            (max(slot, self.slot_of(first + self.index_of(block, piece) - LEAD)), block, piece)
            for slot, block, piece in self.leave
        ]
        self.ring = 12
        self.lags = [LAG * (stage + 1) for stage in range(self.stages)]
        self.end_lag = self.lags[-1] + 2
        self.n_vector = 4 + self.stages
        self.vector_at = [self.compute_end]
        for wait in [1, 2] + [VECTOR_LAG] * self.stages + [1, 1]:
            self.vector_at.append(self.vector_at[-1] + wait)
        self.slots = max(self.slot_of(self.first + self.total + self.end_lag), self.vector_at[-1] + 1)

    def index_of(self, block, piece):
        return block * self.per_block + (0 if piece == 0 else piece + self.n_outer - 1)

    def turn_of(self, slot):
        return slot // 2 if slot < 2 * self.doubled else slot - self.doubled

    def slot_of(self, turn):
        return 2 * turn + 1 if turn < self.doubled else turn + self.doubled


def rear_body(plan, frames, head, meta, *refs):
    (
        back_ref, pre1_ref, x1_ref, g_middle1_ref, gain_ref, q_gain_ref, k_gain_ref, joint_ref,
        outer_scale, second_gain, mixer_scale, outer_ref, inner_ref, slope_ref, pre0_ref,
        mixer_in, feed_in, middle_in, branch_in, qkv_in, x0_in,
        feed_g, came_in, feed_x1, feed_three1, joint_x1, joint_three1, feed_x0, feed_three0, joint_x0, joint_three0,
        vector_in,
    ) = refs[:32]
    tokens_ref, outer_out, inner_out, mixer_out, joint_out, vector_out = refs[32:38]
    (
        own, came, acts, hids, act_turned, hid_turned, parts, last, sums, v_half, v_part,
        mixer, feed0, middle0, branch0, qkv0, x0,
        g1, g_middle0, g_att0, g_feed, g_qkv, total_sum,
    ) = refs[38:61]
    steps = refs[61 : 61 + plan.stages]
    load_sem, act_sem, hid_sem, g_send, g_recv, p_send, p_recv, f_send, f_recv, v_send, v_recv = refs[61 + plan.stages :]
    slot = pl.program_id(0)
    rows = own.shape[2]
    half, hidden_half, chips, total = plan.half, plan.hidden_half, plan.chips, plan.total
    width = 2 * half
    per_block, n_outer, n_inner = plan.per_block, plan.n_outer, plan.n_inner
    at_joined = (2 + n_inner) * CHUNK
    core, core_peer, scene_peer, cross_peer, bits = peers_of(frames)
    vector_rows = 6 + hidden_half * 2 // width
    section = vector_rows + 8

    sources = [
        (feed_g, own.at[0, :, :, pl.ds(0, at_joined)]),
        (came_in.at[:, :, pl.ds(0, SHARED_PIECES * CHUNK)], came.at[0, :, :, pl.ds(0, SHARED_PIECES * CHUNK)]),
        (feed_in, feed0),
        (mixer_in.at[pl.ds(0, 1)], mixer),
        (middle_in, middle0),
        (branch_in, branch0),
        (qkv_in, qkv0),
        (x0_in, x0),
    ]

    def load(index):
        return pltpu.make_async_copy(sources[index][0], sources[index][1], load_sem.at[index])

    def act_loads(block):
        feed_x, feed_three, joint_x, joint_three = (
            (feed_x1, feed_three1, joint_x1, joint_three1),
            (feed_x0, feed_three0, joint_x0, joint_three0),
        )[block]
        copies = []
        for place in range(4):
            feed_from = feed_x if place == 0 else feed_three.at[place - 1]
            joint_from = joint_x if place == 0 else joint_three.at[place - 1]
            copies.append(pltpu.make_async_copy(
                feed_from.at[:, pl.ds(hidden_half, width)], acts.at[place, :, pl.ds(0, width)], act_sem.at[2 * place]
            ))
            copies.append(pltpu.make_async_copy(
                joint_from, acts.at[place, :, pl.ds(width, half)], act_sem.at[2 * place + 1]
            ))
        return copies

    def hid_loads(block):
        feed_x, feed_three = ((feed_x1, feed_three1), (feed_x0, feed_three0))[block]
        return [
            pltpu.make_async_copy(
                (feed_x if place == 0 else feed_three.at[place - 1]).at[:, pl.ds(0, hidden_half)],
                hids.at[place],
                hid_sem.at[place],
            )
            for place in range(4)
        ]

    def piece_copy(block, piece, which):
        lanes = pl.ds(pl.multiple_of(piece * CHUNK, CHUNK), CHUNK)
        side = core if which == 0 else 1 - core
        return remote(
            own.at[block, side, :, lanes],
            came.at[block, which, :, lanes],
            g_send.at[block, which, piece],
            g_recv.at[block, which, piece],
            (scene_peer, core_peer, cross_peer)[which],
        )

    targets = [core_peer, scene_peer, cross_peer] + [peer for _, peer in bits]

    @pl.when(slot == 0)
    def _():
        load(0).start()
        for copy in hid_loads(0):
            copy.start()
        load(1).start()
        for copy in act_loads(0):
            copy.start()
        for index in range(2, len(sources)):
            load(index).start()
        sums[0] = jnp.zeros(sums.shape[1:], f32)
        for index in range(vector_rows):
            sums[0, section + index : section + index + 1, :] = vector_in[index : index + 1, :]
        greet(targets)

    def spread(step, steps_of):
        return lax.rem(step, 2) * (steps_of // 2) + step // 2

    @pl.when(slot < plan.joint_steps)
    def _():
        pieces = []
        for pair in range(CHUNK // LANES):
            pieces.append(
                unpack_pair(back_ref[2 * pair, 0].astype(f32), back_ref[2 * pair + 1, 0].astype(f32))
            )
        joint_back_core(
            1, head, slot, plan.joint_steps, spread(slot, plan.joint_steps), jnp.concatenate(pieces, axis=1),
            pre1_ref, x1_ref, g_middle1_ref, gain_ref, q_gain_ref, k_gain_ref, joint_ref,
            own.at[0], at_joined, g1, Rows(sums, 0, section + vector_rows), total_sum,
        )

    @pl.when(slot == plan.feed_at)
    def _():
        for index in range(2, len(sources)):
            load(index).wait()

    @pl.when((slot >= plan.feed_at) & (slot < plan.frame_at))
    def _():
        step = slot - plan.feed_at
        feed_back_core(
            0, False, step, plan.feed_steps, spread(step, plan.feed_steps), meta, g1, feed0, slope_ref, middle0, branch0,
            outer_scale, second_gain, mixer_scale, outer_ref, inner_ref, mixer,
            own.at[1], g_middle0, g_att0, Rows(sums, 0, 0), g_feed, total_sum,
        )

    @pl.when((slot >= plan.frame_at) & (slot < plan.joint_at))
    def _():
        @pl.loop(0, plan.slabs)
        def _(slab):
            at = ((slot - plan.frame_at) * plan.slabs + slab) * LANES
            frame_back_slab(at, meta, qkv0, g_att0, g_qkv)

    @pl.when((slot >= plan.joint_at) & (slot < plan.compute_end))
    def _():
        step = slot - plan.joint_at
        chunk = spread(step, plan.joint_steps)
        joint_back_core(
            0, head, step, plan.joint_steps, chunk,
            g_qkv[:, pl.ds(pl.multiple_of(chunk * CHUNK, CHUNK), CHUNK)],
            pre0_ref, x0, g_middle0, gain_ref, q_gain_ref, k_gain_ref, joint_ref,
            own.at[1], at_joined, tokens_ref, Rows(sums, 0, vector_rows), total_sum,
        )

    def swapped(index):
        return lax.rem(index, SWAP_EVERY) == 1

    def way(stage, index):
        value, peer = bits[stage]
        if stage > 1:
            return value, peer
        other_value, other_peer = bits[1 - stage]
        changed = swapped(index)
        return jnp.where(changed, other_value, value), (peer[0], jnp.where(changed, other_peer[1], peer[1]))

    def stage_start(stage, index):
        value, peer = way(stage, index)
        source = parts if stage == 0 else steps[stage - 1]
        held = lax.rem(index, plan.ring)
        for pair in range(chips >> (stage + 1)):
            remote(
                source.at[held, 2 * pair + 1 - value],
                steps[stage].at[held, pair],
                p_send.at[stage, held],
                p_recv.at[stage, held],
                peer,
            ).start()

    def stage_whole(stage, index):
        held = lax.rem(index, plan.ring)
        return remote(
            steps[stage].at[held], steps[stage].at[held], p_send.at[stage, held], p_recv.at[stage, held], way(stage, index)[1]
        )

    def last_copy(index):
        held = lax.rem(index, plan.ring)
        return remote(
            steps[-1].at[held, 0, 1 - core], last.at[held], f_send.at[held], f_recv.at[held], core_peer
        )

    def store(index, value):
        changed = swapped(index)
        held = lax.rem(index, plan.ring)

        @pl.when(jnp.logical_not(changed))
        def _():
            parts[held] = value.astype(bf16)

        @pl.when(changed)
        def _():
            pairs = value.reshape((chips // 4, 2, 2) + value.shape[1:])
            pairs = jnp.stack([pairs[:, :, place] for place in range(2)], axis=1)
            parts[held] = pairs.reshape(value.shape).astype(bf16)

    def multiply(index):
        block = index // per_block
        unit = lax.rem(index, per_block)

        def wait_piece(piece):
            @pl.when((block > 0) | (piece >= SHARED_PIECES))
            def _():
                for which in range(3):
                    piece_copy(block, piece, which).wait_recv()

        def gathered(lanes):
            return jnp.concatenate(
                [own[block, core, :, lanes]] + [came[block, which, :, lanes] for which in range(3)], axis=0
            )

        @pl.when(unit < n_outer)
        def _():
            @pl.when(unit == 0)
            def _():
                wait_piece(0)
                hid_turned[...] = jnp.transpose(jnp.concatenate([hids[place] for place in range(4)], axis=0))

            right = gathered(pl.ds(pl.multiple_of(unit * LANES, LANES), LANES))
            value = nn(hid_turned[...], right)
            value = value.reshape(chips, 2, 4, plan.deep, LANES)
            store(index, jnp.concatenate([value[:, :, place] for place in range(4)], axis=-1))

        @pl.when(unit >= n_outer)
        def _():
            piece = unit - (n_outer - 1)
            wait_piece(piece)

            for place, at in enumerate((n_outer, n_outer + n_inner, n_outer + n_inner + 1)):

                @pl.when(unit == at)
                def _():
                    left = [acts[source, :, place * half : (place + 1) * half] for source in range(4)]
                    act_turned[...] = jnp.transpose(jnp.concatenate(left, axis=0))

            value = nn(act_turned[...], gathered(pl.ds(pl.multiple_of(piece * CHUNK, CHUNK), CHUNK)))
            store(index, value.reshape(chips, 2, plan.deep, CHUNK))

    def put(index, side, value):
        block = 1 - index // per_block
        unit = lax.rem(index, per_block)

        @pl.when(unit < n_outer)
        def _():
            lanes = pl.ds(pl.multiple_of(side * half + unit * LANES, LANES), LANES)
            for place in range(4):
                outer_out[block, place * plan.deep : (place + 1) * plan.deep, lanes] = (
                    value[:, place * LANES : (place + 1) * LANES]
                )

        def wide(first, count, target):
            @pl.when((unit >= first) & (unit < first + count))
            def _():
                lanes = pl.ds(pl.multiple_of((side * count + unit - first) * CHUNK, CHUNK), CHUNK)
                target[block, :, lanes] = value

        wide(n_outer, n_inner, inner_out)
        wide(n_outer + n_inner, 1, mixer_out)
        wide(n_outer + n_inner + 1, plan.n_joint, joint_out)

    def add(stage, index):
        stage_whole(stage, index).wait()
        value = way(stage, index)[0]
        held = lax.rem(index, plan.ring)
        source = parts if stage == 0 else steps[stage - 1]
        for pair in range(chips >> (stage + 1)):
            result = source[held, 2 * pair + value].astype(f32) + steps[stage][held, pair].astype(f32)
            if stage + 1 == plan.stages:
                put(index, core, jnp.where(core == 0, result[0], result[1]))
            steps[stage][held, pair] = result.astype(bf16)

    def close(index):
        last_copy(index).wait()
        put(index, 1 - core, last[lax.rem(index, plan.ring)].astype(f32))

    early = slot < 2 * plan.doubled
    turn_now = jnp.where(early, slot // 2, slot - plan.doubled)
    active = jnp.logical_not(early) | (lax.rem(slot, 2) == 1)

    def when_turn(at):
        return pl.when(active & (turn_now == at))

    def when_due(lag, action):
        index = turn_now - plan.first - lag

        @pl.when(active & (index >= 0) & (index < total))
        def _():
            action(index)

    scene = lax.axis_index("scene")
    wide, narrow = width // 2, width // 4

    def lanes_of(side, size):
        return pl.ds(pl.multiple_of(side * size, size), size)

    n_chip = plan.stages
    vector_peers = [core_peer, scene_peer] + [peer for _, peer in bits] + [scene_peer, core_peer]

    def vector_copy(stage):
        if stage == 0:
            source, target = sums.at[0, :, lanes_of(1 - core, wide)], v_half.at[0]
        elif stage == 1:
            source, target = v_half.at[1, :, lanes_of(1 - scene, narrow)], v_part.at[0]
        elif stage < 2 + n_chip:
            source, target = v_part.at[2 * stage - 3], v_part.at[2 * stage - 2]
        elif stage == 2 + n_chip:
            source, target = v_part.at[2 * stage - 3], v_part.at[2 * stage - 2]
        else:
            source, target = v_half.at[2], v_half.at[3]
        return remote(source, target, v_send.at[stage], v_recv.at[stage], vector_peers[stage])

    def vector_step(stage):
        vector_copy(stage).wait()
        if stage == 0:
            v_half[1] = sums[0, :, lanes_of(core, wide)] + v_half[0]
        elif stage == 1:
            v_part[1] = v_half[1, :, lanes_of(scene, narrow)] + v_part[0]
        elif stage < 2 + n_chip:
            v_part[2 * stage - 1] = v_part[2 * stage - 3] + v_part[2 * stage - 2]
        elif stage == 2 + n_chip:
            v_half[2, :, lanes_of(scene, narrow)] = v_part[2 * stage - 3]
            v_half[2, :, lanes_of(1 - scene, narrow)] = v_part[2 * stage - 2]
        else:
            vector_out[:, lanes_of(core, wide)] = v_half[2]
            vector_out[:, lanes_of(1 - core, wide)] = v_half[3]

    @pl.when(slot == 0)
    def _():
        pl.semaphore_wait(pltpu.get_barrier_semaphore(), len(targets))
        load(0).wait()

    @when_turn(plan.first)
    def _():
        load(1).wait()
        for copy in hid_loads(0):
            copy.wait()

    @when_turn(plan.first + n_outer)
    def _():
        for copy in act_loads(0):
            copy.wait()

    when_due(0, multiply)
    for stage in range(plan.stages):
        when_due(plan.lags[stage], partial(add, stage))
    when_due(plan.end_lag, close)

    for stage in range(plan.n_vector):

        @pl.when(slot == plan.vector_at[stage + 1])
        def _():
            vector_step(stage)

    for stage in range(plan.stages - 1):
        when_due(plan.lags[stage], partial(stage_start, stage + 1))
    when_due(plan.lags[-1], lambda index: last_copy(index).start())
    when_due(0, partial(stage_start, 0))

    for at, block, piece in plan.leave:

        @pl.when(slot == at)
        def _():
            for which in range(3):
                piece_copy(block, piece, which).start()

    for stage in range(plan.n_vector):

        @pl.when(slot == plan.vector_at[stage])
        def _():
            vector_copy(stage).start()

    @when_turn(plan.first + 1)
    def _():
        for copy in hid_loads(1):
            copy.start()

    @when_turn(plan.first + per_block - 1)
    def _():
        for copy in hid_loads(1):
            copy.wait()

    @when_turn(plan.first + n_outer + n_inner + 1)
    def _():
        for copy in act_loads(1):
            copy.start()

    @when_turn(plan.first + per_block + n_outer - 1)
    def _():
        for copy in act_loads(1):
            copy.wait()

    @pl.when(slot == plan.slots - 1)
    def _():
        for at, block, piece in plan.leave:
            for which in range(3):
                piece_copy(block, piece, which).wait_send()


def rear(frames, head, meta, back, pre1, x1, g_middle1, gain, pattern, joint, outer_scale, second_gain, mixer_scale, outer, inner, slope0, pre0, mixer, feed0, middle0, branch0, qkv0, x0, feed_g1, came1, shares, vector1):
    rows, width = x1.shape
    hidden = inner.shape[2]
    half = width // 2
    plan = Plan(frames, rows, width, hidden)
    per_part = width // CHUNK
    vector_rows = vector1.shape[0]
    n_vector_rows = 2 * (vector_rows + 8)

    def clip(value, size):
        return jnp.minimum(jnp.maximum(value, 0), size - 1)

    def spread(step, steps):
        return lax.rem(step, 2) * (steps // 2) + step // 2

    def chunk1(slot):
        return spread(clip(slot, plan.joint_steps), plan.joint_steps)

    def chunk0(slot):
        return spread(clip(slot - plan.joint_at, plan.joint_steps), plan.joint_steps)

    def chunk_feed(slot):
        return spread(clip(slot - plan.feed_at, plan.feed_steps), plan.feed_steps)

    def back_map(slot, m):
        chunk = chunk1(slot)
        return (lax.rem(chunk, per_part), chunk // per_part, 0, 0)

    def joint_map(slot, m):
        late = slot >= plan.feed_at
        return (jnp.where(late, 0, 1), 0, jnp.where(late, chunk0(slot), chunk1(slot)))

    once = dict(pipeline_mode=pl.Buffered(1))
    single = lambda shape: pl.BlockSpec(shape, lambda *_: (0,) * len(shape), **once)
    out_shape = [
        sds((rows, width), bf16),
        sds((2, 4 * plan.deep, width), f32),
        sds((2, plan.deep, hidden), f32),
        sds((2, plan.deep, width), f32),
        sds((2, plan.deep, 3 * width), f32),
        sds((n_vector_rows, width), f32),
    ]
    container = (plan.ring, plan.chips, 2, plan.deep, CHUNK)
    return pl.pallas_call(
        partial(rear_body, plan, frames, head),
        name="rear",
        out_shape=out_shape,
        grid_spec=pltpu.PrefetchScalarGridSpec(
            num_scalar_prefetch=1,
            grid=(plan.slots,),
            in_specs=[
                pl.BlockSpec((CHUNK // head, 1, rows // 2, LANES), back_map),
                pl.BlockSpec((rows, CHUNK), lambda j, m: (0, jnp.minimum(chunk1(j), 2 * per_part - 1))),
                single(x1.shape),
                single(g_middle1.shape),
                single(gain.shape),
                single(pattern[0].shape), single(pattern[2].shape),
                pl.BlockSpec((1, width, CHUNK), joint_map),
                single(outer_scale.shape),
                single(second_gain.shape),
                single(mixer_scale.shape),
                pl.BlockSpec((1, CHUNK, width), lambda j, m: (0, chunk_feed(j), 0)),
                pl.BlockSpec((1, width, CHUNK), lambda j, m: (0, 0, chunk_feed(j))),
                pl.BlockSpec((rows, CHUNK), lambda j, m: (0, chunk_feed(j))),
                pl.BlockSpec((rows, CHUNK), lambda j, m: (0, jnp.minimum(chunk0(j), 2 * per_part - 1))),
            ]
            + [any_space] * 16
            + [single(vector1.shape)],
            out_specs=[vmem_space] * len(out_shape),
            scratch_shapes=[
                pltpu.VMEM((2, 2, rows, plan.n_pieces * CHUNK), bf16),
                pltpu.VMEM((2, 3, rows, plan.n_pieces * CHUNK), bf16),
                pltpu.VMEM((4, rows, 3 * half), bf16),
                pltpu.VMEM((4, rows, plan.hidden_half), bf16),
                pltpu.VMEM((half, 4 * rows), bf16),
                pltpu.VMEM((plan.hidden_half, 4 * rows), bf16),
                pltpu.VMEM(container, bf16),
                pltpu.VMEM((plan.ring, plan.deep, CHUNK), bf16),
                pltpu.VMEM((1, n_vector_rows, width), f32),
                pltpu.VMEM((4, n_vector_rows, half), f32),
                pltpu.VMEM((2 * plan.stages + 3, n_vector_rows, half // 2), f32),
                pltpu.VMEM((1, width, width), bf16),
                pltpu.VMEM((rows, width), f32),
                pltpu.VMEM((rows, width), f32),
                pltpu.VMEM((rows, width), f32),
                pltpu.VMEM((rows, 3 * width), bf16),
                pltpu.VMEM((rows, width), bf16),
                pltpu.VMEM((rows, width), f32),
                pltpu.VMEM((rows, width), f32),
                pltpu.VMEM((rows, width), bf16),
                pltpu.VMEM((rows, width), bf16),
                pltpu.VMEM((rows, 3 * width), f32),
                pltpu.VMEM((rows, width), f32),
            ]
            + [pltpu.VMEM((plan.ring, plan.chips >> (stage + 1)) + container[2:], bf16) for stage in range(plan.stages)]
            + [
                dma((8,)),
                dma((8,)),
                dma((4,)),
                dma((2, 3, plan.n_pieces)),
                dma((2, 3, plan.n_pieces)),
                dma((plan.stages, plan.ring)),
                dma((plan.stages, plan.ring)),
                dma((plan.ring,)),
                dma((plan.ring,)),
                dma((plan.n_vector,)),
                dma((plan.n_vector,)),
            ],
        ),
        compiler_params=pltpu.CompilerParams(
            collective_id=0, has_side_effects=True, vmem_limit_bytes=64 * 1024 * 1024 - 65536
        ),
        cost_estimate=pl.CostEstimate(flops=2 * rows * width * hidden * 20, bytes_accessed=60 * width * hidden, transcendentals=0),
    )(
        meta, back, pre1, x1, g_middle1, gain, pattern[0], pattern[2], joint, outer_scale, second_gain, mixer_scale, outer, inner, slope0, pre0,
        mixer, feed0, middle0, branch0, qkv0, x0, feed_g1, came1, *shares, vector1,
    )


def finish_body(heads, meta, vectors_ref, *refs):
    count = 5
    large_in, large_out = refs[:count], refs[count : 2 * count]
    (
        first_gain, first_shift, joint_bias, query_gain, query_shift, key_gain, mixer_bias, mixer_scale,
        second_gain, second_shift, inner_bias, outer_bias, outer_scale,
    ) = refs[2 * count : -1]
    sem = refs[-1]
    copies = [
        pltpu.make_async_copy(source, target, sem.at[index])
        for index, (source, target) in enumerate(zip(large_in, large_out))
    ]
    for copy in copies:
        copy.start()
    width = first_gain.shape[1]
    head = query_gain.shape[1]
    feed_rows = 6 + inner_bias.shape[1] // width
    for block in range(2):
        base = block * (feed_rows + 8)
        rows = vectors_ref[base : base + feed_rows + 8, :]

        def pick(index):
            return rows[index : index + 1, :]

        def at(index):
            return pick(feed_rows + index)

        def fold(value):
            total = value[:, :LANES]
            for place in range(1, width // LANES):
                total = total + value[:, place * LANES : (place + 1) * LANES]
            return (total + turn(total))[:, :head]

        here = slice(block, block + 1)
        for target, index in (
            (outer_scale, 0), (outer_bias, 1), (second_gain, 2), (second_shift, 3), (mixer_scale, 4), (mixer_bias, 5),
        ):
            target[here, :] = pick(index)
        for index in range(inner_bias.shape[1] // width):
            inner_bias[here, index * width : (index + 1) * width] = pick(6 + index)
        first_gain[here, :] = at(0)
        first_shift[here, :] = at(1)
        for index in range(3):
            joint_bias[here, index * width : (index + 1) * width] = at(2 + index)
        query_gain[here, :] = fold(at(5))
        query_shift[here, :] = fold(at(6))
        key_gain[here, :] = fold(at(7))
    for copy in copies:
        copy.wait()


def finish(heads, meta, vectors, large):
    width = vectors.shape[1]
    head = width // heads
    hidden = large[2].shape[2]
    sizes = [width, width, 3 * width, head, head, head, width, width, width, width, hidden, width, width]
    return pl.pallas_call(
        partial(finish_body, heads),
        name="finish",
        out_shape=[sds(value.shape, value.dtype) for value in large] + [sds((2, size), f32) for size in sizes],
        grid_spec=pltpu.PrefetchScalarGridSpec(
            num_scalar_prefetch=1,
            grid=(1,),
            in_specs=[vmem_space] * 6,
            out_specs=[any_space] * 5 + [full((2, size)) for size in sizes],
            scratch_shapes=[dma((5,))],
        ),
    )(meta, vectors, *large)


def local(scenes, frames, tokens, patch_counts, first_gain, first_shift, joint_weight, joint_bias, query_gain, query_shift, key_gain, mixer_weight, mixer_bias, mixer_scale, second_gain, second_shift, inner_weight, inner_bias, outer_weight, outer_bias, outer_scale, cotangent):
    rows, width = tokens.shape[1:]
    half = rows // 2
    head = query_gain.shape[1]
    heads = width // head
    hidden = inner_weight.shape[2]
    chips = frames // 2
    meta = patch_counts.reshape(1)
    pattern = (query_gain, query_shift, key_gain)

    x0 = tokens[0]
    feed_params = (mixer_weight, mixer_bias, mixer_scale, second_gain, second_shift, inner_weight, inner_bias, outer_weight, outer_bias, outer_scale)
    back_params = (outer_scale, second_gain, mixer_scale, outer_weight, inner_weight, mixer_weight)

    own0, other0, pre0, qkv0 = joint_forward(0, False, head, meta, x0, first_gain, first_shift, pattern, joint_weight, joint_bias)
    att0 = frame_forward(meta, qkv0)
    own_feed0, other_feed0, middle0, branch0, feed0, slope0, x1 = feed_forward(0, False, meta, att0, x0, *feed_params)
    own1, other1, pre1, pack1 = joint_forward(1, True, head, meta, x1, first_gain, first_shift, pattern, joint_weight, joint_bias)
    att1, kept1, att_full, att_log, (left_joint0, left_feed0, left_joint1) = scene_forward(
        frames, meta, pack1, half, [(own0, other0), (own_feed0, other_feed0), (own1, other1)]
    )
    own_feed1, other_feed1, middle1, branch1, feed1, slope1, layer_out = feed_forward(1, True, meta, att1, x1, *feed_params)

    g_feed1, g_middle1, g_att1, vector_feed1 = feed_backward(1, True, heads, meta, cotangent[0], feed1, slope1, middle1, branch1, *back_params)
    shared = SHARED_PIECES * CHUNK
    g_qkv1, came_feed1, (left_feed1,) = scene_backward(
        frames, meta, kept1, g_att1, att_full, att_log, half, [(own_feed1, other_feed1)], g_feed1, shared
    )
    g0, outer, inner, mixer, joint, vectors = rear(
        frames, head, meta, g_qkv1, pre1, x1, g_middle1, first_gain, pattern, joint_weight,
        outer_scale, second_gain, mixer_scale, outer_weight, inner_weight, slope0, pre0,
        mixer_weight, feed0, middle0, branch0, qkv0, x0, g_feed1, came_feed1,
        [own_feed1, left_feed1, own1, left_joint1, own_feed0, left_feed0, own0, left_joint0], vector_feed1,
    )
    (
        g0, outer, inner, mixer, joint,
        grad_first_gain, grad_first_shift, grad_joint_bias, grad_query_gain, grad_query_shift, grad_key_gain,
        grad_mixer_bias, grad_mixer_scale, grad_second_gain, grad_second_shift, grad_inner_bias, grad_outer_bias, grad_outer_scale,
    ) = finish(heads, meta, vectors, (g0, outer, inner, mixer, joint))
    return (
        layer_out[None], g0[None],
        grad_first_gain, grad_first_shift, joint, grad_joint_bias, grad_query_gain, grad_query_shift, grad_key_gain,
        mixer, grad_mixer_bias, grad_mixer_scale, grad_second_gain, grad_second_shift,
        inner, grad_inner_bias, outer, grad_outer_bias, grad_outer_scale,
    )


def solution(mesh):
    tokens_spec = P("scene", "frame", None)
    shard = P(None, ("scene", "frame"), None)
    in_specs = (tokens_spec, P("scene", "frame")) + (P(),) * 17 + (tokens_spec,)
    out_specs = (
        tokens_spec, tokens_spec, P(), P(), shard, P(), P(), P(), P(), shard,
        P(), P(), P(), P(), shard, P(), shard, P(), P(),
    )
    body = partial(local, mesh.shape["scene"], mesh.shape["frame"])
    return jax.shard_map(body, mesh=mesh, in_specs=in_specs, out_specs=out_specs, check_vma=False)
```
